32 devices in a mesh: ep: 16 (over z, y, x), tp: 2 (over core).
Axes of the slice: x: 2, y: 2, z: 4, core: 2. Of those that a mesh axis runs over, the one named last changes fastest.
Arguments:
- stream: bfloat16 [8192, 1536], P('ep'), may hold values from -6 to 6
- cotangent: bfloat16 [8192, 1536], P('ep'), may hold values from -6 to 6
- attention_gain: bfloat16 [1536], replicated, may hold values from 0.5 to 1.5
- query_weight: bfloat16 [1536, 1536], P(None, 'tp'), may hold values from -0.625 to 0.625
- key_matrix: bfloat16 [1536, 512], P(None, 'tp'), may hold values from -0.625 to 0.625
- value_matrix: bfloat16 [1536, 512], P(None, 'tp'), may hold values from -0.15625 to 0.15625
- out_weight: bfloat16 [1536, 1536], P('tp'), may hold values from -1.25 to 1.25
- mixture_gain: bfloat16 [1536], replicated, may hold values from 0.5 to 1.5
- router_weight: bfloat16 [1536, 16], replicated, may hold values from -0.078125 to 0.078125
- gate_weight: bfloat16 [16, 1536, 512], P('ep', None, 'tp'), may hold values from -0.15625 to 0.15625
- up_weight: bfloat16 [16, 1536, 512], P('ep', None, 'tp'), may hold values from -0.15625 to 0.15625
- down_weight: bfloat16 [16, 512, 1536], P('ep', 'tp'), may hold values from -2 to 2
- routes: int32 [8192, 8], P('ep'), may hold values from 0 to 15, all different within a row; in each aligned block of 512 rows (0 to 511, 512 to 1023, ...) at most 320 rows name the same one
Outputs:
- layer_out: bfloat16 [8192, 1536], P('ep')
- grad_stream: float32 [8192, 1536], P('ep')
- grad_attention_gain: float32 [1536], P('ep')
- grad_query: float32 [1536, 1536], P('ep', 'tp')
- grad_key: float32 [1536, 512], P('ep', 'tp')
- grad_value: float32 [1536, 512], P('ep', 'tp')
- grad_out: float32 [1536, 1536], P('tp', 'ep')
- grad_mixture_gain: float32 [1536], P('ep')
- grad_router: float32 [1536, 16], P('ep')
- grad_gate: float32 [16, 1536, 512], P('ep', None, 'tp')
- grad_up: float32 [16, 1536, 512], P('ep', None, 'tp')
- grad_down: float32 [16, 512, 1536], P('ep', 'tp')
- rms_stats: float32 [16, 3], P('ep')
The draws below stay inside these ranges and needn't reach their ends.
Inputs may be any that keep to these rules, and one draw needn't show every extreme that they name: `routes`: each token names 8 different experts. Within the rows of one device (aligned blocks of 512 rows) no expert is named by more than 320 rows, and in every draw some expert is named by exactly 320 rows of some device; every expert is named somewhere.
All inputs are finite; a program needn't handle non-finite values.
Results may differ from the reference program's by a relative error of at most 0.019.
Values may be sent and summed in bfloat16 or wider, within the bound.
A program may use at most 320 MiB of HBM per device.

```python
import math
import jax
import jax.numpy as jnp
import numpy as np
from jax import lax

MODEL_DIMENSION = 1536
QUERY_HEAD_COUNT = 24
VALUE_HEADS = 8
HEAD_FEATURES = 64
E_HID = 512
TOP = 8
SEQ_LEN = 512
TOK_DEV = 512
EXPERTS = 16
SEQS = 16
TOKENS = 8192
CAP = 320
N_EP = 16


def raised(values, stream_key, source, target, blocks, factor):
    def block_of(position):
        return (jnp.arange(values.shape[position]) // (values.shape[position] // blocks)).reshape((-1,) + (1,) * (values.ndim - 1 - position))

    near = jax.random.permutation(stream_key, blocks)[block_of(target)]
    far = (block_of(target) + blocks // 2) % blocks
    return jnp.where((block_of(source) == near) | (block_of(source) == far), factor * values, values)


def block_scale(stream_key, shape, split, smallest, high):
    def one(dim, parts):
        heights = jax.random.uniform(jax.random.fold_in(jax.random.fold_in(stream_key, 6), dim), (parts,), jnp.float32, smallest / len(split), high / len(split))
        return jnp.repeat(jnp.exp(heights), shape[dim] // parts).reshape((-1,) + (1,) * (len(shape) - dim - 1))

    level = one(*split[0])
    for cut in split[1:]:
        level = level * one(*cut)
    return level


def routed_block(rng, own, number, rows, count, top, bound, slope):
    sequence = jax.random.permutation(rng, count)
    packed, ordinary = load_shares(count, rows * top, bound, slope, True), load_shares(count, rows * top, bound, slope, False)
    places = jnp.arange(count)

    def named(tallies, rotation):
        used = int((tallies > 0).sum())
        fixed = max(1, used // 4)
        passed = fixed + (places - fixed + rotation * (used - fixed)) % max(1, count - fixed)
        return jnp.zeros((count,), jnp.int32).at[sequence[jnp.where(places < fixed, places, passed)]].set(jnp.asarray(tallies, jnp.int32))

    tallies = jnp.where(number % 4 == 0, named(packed, number // 4), named(ordinary, number - number // 4 - 1))
    mixed = jax.random.permutation(jax.random.fold_in(own, 3), count)
    giver, taker = mixed[0:count // 2 * 2:2], mixed[1:count // 2 * 2:2]
    room = jnp.minimum(tallies[giver] - 1, bound - tallies[taker]) // 2
    room = jnp.where((giver == sequence[0]) | (taker == sequence[0]) | (tallies[taker] == 0), 0, jnp.maximum(room, 0))
    passed = jax.random.randint(jax.random.fold_in(own, 4), (count // 2,), 0, 1 << 20) % (room + 1)
    tallies = tallies.at[giver].add(-passed).at[taker].add(passed)
    members = jnp.searchsorted(jnp.cumsum(tallies), jnp.arange(rows * top), side="right").astype(jnp.int32)
    grid = members.reshape(top, rows).T
    grid = grid[jax.random.permutation(jax.random.fold_in(own, 1), rows)]
    rotation = jax.random.randint(jax.random.fold_in(own, 2), (rows, 1), 0, top)
    return jnp.take_along_axis(grid, (jnp.arange(top)[None, :] + rotation) % top, axis=1)


def load_shares(count, total, bound, skew, full):
    loads = [(1 << 20) // math.isqrt(grade ** skew) + 1 for grade in range(1, count + 1)]
    largest = bound if full else min(bound, max(-(-total // count), total * loads[0] // sum(loads)))
    least = 1 if total - largest >= count - 1 else 0
    holding, spare = [largest] + [least] * (count - 1), total - largest - least * (count - 1)
    while spare > 0:
        free = [i for i in range(1, count) if holding[i] < largest] or [i for i in range(1, count) if holding[i] < bound]
        mass, remaining = sum([loads[i] for i in free]), spare
        for i in free:
            more = min(bound - holding[i], max(1, remaining * loads[i] // mass), spare)
            holding[i] = holding[i] + more
            spare = spare - more
    return np.array(holding)


def gaussian(rng, extent, width, bound, pieces=(), held_as=jnp.bfloat16):
    entries = jax.random.normal(rng, extent, jnp.float32) * width
    if len(pieces) > 0:
        entries = block_scale(rng, extent, pieces, -0.22, 0.18) * entries
    return jnp.clip(entries, min=-bound, max=bound).astype(held_as)


def gaussian_with(rng, extent, width, limit, cuts, heavy, held_as=jnp.bfloat16):
    values = width * jax.random.normal(rng, extent, jnp.float32)
    if cuts:
        values = values * block_scale(rng, extent, cuts, -0.22, 0.18)
    return jnp.clip(raised(values, jax.random.fold_in(rng, 3), *heavy), -limit, limit).astype(held_as)


def setup_inputs(seed: int = 0) -> dict:
    key_of = jax.random.split(jax.random.key(seed), 14)
    stream = gaussian_with(key_of[0], (TOKENS, MODEL_DIMENSION), 1.0, 6.0, ((0, 16),), (0, 1, 16, 2.0))
    cotangent = gaussian_with(key_of[1], (TOKENS, MODEL_DIMENSION), 1.0, 6.0, ((0, 16),), (0, 1, 16, 2.0))
    attention_gain = jnp.clip(1.0 + 0.1 * jax.random.normal(key_of[2], (MODEL_DIMENSION,), jnp.float32), 0.5, 1.5).astype(jnp.bfloat16)
    query_weight = gaussian(key_of[3], (MODEL_DIMENSION, QUERY_HEAD_COUNT * HEAD_FEATURES), (MODEL_DIMENSION // 16) ** -0.5, 0.625, ((1, 2),))
    key_matrix = gaussian(key_of[4], (MODEL_DIMENSION, VALUE_HEADS * HEAD_FEATURES), (MODEL_DIMENSION // 16) ** -0.5, 0.625, ((1, 2),))
    value_matrix = gaussian(key_of[5], (MODEL_DIMENSION, VALUE_HEADS * HEAD_FEATURES), MODEL_DIMENSION ** -0.5, 0.15625, ((1, 2),))
    out_weight = gaussian(key_of[6], (QUERY_HEAD_COUNT * HEAD_FEATURES, MODEL_DIMENSION), (QUERY_HEAD_COUNT * HEAD_FEATURES // 64) ** -0.5, 1.25, ((0, 2),))
    mixture_gain = jnp.clip(1.0 + 0.1 * jax.random.normal(key_of[7], (MODEL_DIMENSION,), jnp.float32), 0.5, 1.5).astype(jnp.bfloat16)
    router_weight = gaussian(key_of[8], (MODEL_DIMENSION, EXPERTS), (4 * MODEL_DIMENSION) ** -0.5, 0.078125)
    gate_weight = gaussian(key_of[9], (EXPERTS, MODEL_DIMENSION, E_HID), MODEL_DIMENSION ** -0.5, 0.15625, ((0, 16), (2, 2)))
    up_weight = gaussian(key_of[10], (EXPERTS, MODEL_DIMENSION, E_HID), MODEL_DIMENSION ** -0.5, 0.15625, ((0, 16), (2, 2)))
    down_weight = gaussian(key_of[11], (EXPERTS, E_HID, MODEL_DIMENSION), (max(E_HID // 64, 1)) ** -0.5, 2.0, ((0, 16), (1, 2)))
    routes_keys = jax.random.split(jax.random.fold_in(key_of[12], 1), TOKENS // TOK_DEV)
    routes_turns = jax.random.permutation(jax.random.fold_in(key_of[12], 3), TOKENS // TOK_DEV)
    routes = jax.vmap(lambda own, number: routed_block(jax.random.fold_in(key_of[12], 2), own, number, TOK_DEV, EXPERTS, TOP, CAP, 2))(routes_keys, routes_turns).reshape((TOKENS, TOP))
    return {"stream": stream, "cotangent": cotangent, "attention_gain": attention_gain, "query_weight": query_weight, "key_matrix": key_matrix, "value_matrix": value_matrix, "out_weight": out_weight, "mixture_gain": mixture_gain, "router_weight": router_weight, "gate_weight": gate_weight, "up_weight": up_weight, "down_weight": down_weight, "routes": routes}


@jax.custom_vjp
def low(v):
    return lax.optimization_barrier(v.astype(jnp.bfloat16)).astype(jnp.float32)

@jax.custom_vjp
def low_back(v):
    return v

def low_keep(v):
    return (low(v), None)

def low_pass(kept, grad):
    return (grad,)

def back_keep(v):
    return (v, None)

def back_low(kept, grad):
    return (low(grad),)
low.defvjp(low_keep, low_pass)
low_back.defvjp(back_keep, back_low)
epsilon = 1e-06
score_scale = 0.015625
residual_scale = 0.22
rope_base = 10000.0
masked_score = -1e+30

def highest_precision(left, right):
    return jnp.dot(left, right, precision=lax.Precision.HIGHEST)

def rope_tables(sequence_length):
    half_dim = HEAD_FEATURES // 2
    steps_up = jnp.arange(half_dim).astype(jnp.float32) * (2.0 / HEAD_FEATURES)
    inverse = jnp.exp(-steps_up * jnp.log(rope_base))
    places = jnp.arange(sequence_length).astype(jnp.float32)
    angles = places[:, None] * inverse[None, :]
    return (jnp.cos(angles), jnp.sin(angles))

def apply_rotation(value_rows, cosine_table, sine_values):
    half_dim = value_rows.shape[-1] // 2
    first_half = value_rows[..., :half_dim]
    second_half = value_rows[..., half_dim:]
    cos_rows = cosine_table[:, None, :]
    sin_rows = sine_values[:, None, :]
    return jnp.concatenate([first_half * cos_rows - second_half * sin_rows, second_half * cos_rows + first_half * sin_rows], axis=-1)

def attend(normalized_input, query_weight, key_matrix, value_matrix, out_weight):
    sequence_length = normalized_input.shape[0]
    cosine_table, sine_values = rope_tables(sequence_length)
    group_width = QUERY_HEAD_COUNT // VALUE_HEADS
    query_rows = low(apply_rotation(low_back(highest_precision(normalized_input, query_weight)).reshape(sequence_length, QUERY_HEAD_COUNT, HEAD_FEATURES), cosine_table, sine_values))
    rotated_keys = low(apply_rotation(low_back(highest_precision(normalized_input, key_matrix)).reshape(sequence_length, VALUE_HEADS, HEAD_FEATURES), cosine_table, sine_values))
    value_rows = low(low_back(highest_precision(normalized_input, value_matrix))).reshape(sequence_length, VALUE_HEADS, HEAD_FEATURES)
    query_rows = query_rows.reshape(sequence_length, VALUE_HEADS, group_width, HEAD_FEATURES)
    scores = low_back(score_scale * jnp.einsum('qhgd,khd->hgqk', query_rows, rotated_keys, precision=lax.Precision.HIGHEST))
    places = jnp.arange(sequence_length)
    causal = places[:, None] >= places[None, :]
    scores = jnp.where(causal, scores, masked_score)
    largest = lax.optimization_barrier(jnp.max(scores, axis=-1, keepdims=True))
    weights_exp = jnp.exp(scores - largest)
    probs_low = low(weights_exp / lax.optimization_barrier(jnp.sum(weights_exp, axis=-1, keepdims=True)))
    mixed_rows = jnp.einsum('hgqk,khd->qhgd', probs_low, value_rows, precision=lax.Precision.HIGHEST).reshape(sequence_length, QUERY_HEAD_COUNT * HEAD_FEATURES)
    mixed_rows = low(low_back(mixed_rows))
    return low_back(highest_precision(mixed_rows, out_weight))

def layer(stream, attention_gain, query_weight, key_matrix, value_matrix, out_weight, mixture_gain, router_weight, gate_weight, up_weight, down_weight, routes):
    inv_first = lax.rsqrt(lax.optimization_barrier(jnp.mean(stream * stream, axis=-1, keepdims=True)) + epsilon)
    normalized_input = low(stream * inv_first * attention_gain)
    checked = jax.checkpoint(attend)

    def seq_step(state_in, seq_rows):
        return (state_in, checked(seq_rows, query_weight, key_matrix, value_matrix, out_weight))
    unused, attended = lax.scan(seq_step, None, normalized_input.reshape(SEQS, SEQ_LEN, MODEL_DIMENSION))
    attended = attended.reshape(TOKENS, MODEL_DIMENSION)
    middle = stream + residual_scale * attended
    inv_second = lax.rsqrt(lax.optimization_barrier(jnp.mean(middle * middle, axis=-1, keepdims=True)) + epsilon)
    mixer_in = low(middle * inv_second * mixture_gain)
    logits = low_back(highest_precision(mixer_in, router_weight))
    chosen = jnp.take_along_axis(logits, routes, axis=1)
    chosen_exp = jnp.exp(chosen - lax.optimization_barrier(jnp.max(chosen, axis=-1, keepdims=True)))
    gate_probs = chosen_exp / lax.optimization_barrier(jnp.sum(chosen_exp, axis=-1, keepdims=True))
    flat_routes = routes.reshape(-1)
    flat_gates = gate_probs.reshape(-1)
    most_rows = N_EP * CAP
    slot_ids = jnp.arange(most_rows).astype(jnp.int32)

    def expert_step(running, inputs):
        expert_id, gate_mat, up_mat, down_mat = inputs
        hit_mask = flat_routes == expert_id
        picked = jnp.nonzero(hit_mask, size=most_rows, fill_value=0)[0].astype(jnp.int32)
        live_rows = (slot_ids < jnp.sum(hit_mask.astype(jnp.int32))).astype(jnp.float32)
        tokens = picked // TOP
        weight = flat_gates[picked] * live_rows
        rows_in = low_back(mixer_in[tokens] * live_rows[:, None])
        gate_pre = low_back(highest_precision(rows_in, gate_mat))
        up_pre = low_back(highest_precision(rows_in, up_mat))
        active = low(gate_pre * jax.nn.sigmoid(gate_pre) * up_pre)
        rows_out = low(low_back(highest_precision(active, down_mat)))
        return (running.at[tokens].add(weight[:, None] * rows_out), None)
    mixture, unused_too = lax.scan(jax.checkpoint(expert_step), jnp.zeros((TOKENS, MODEL_DIMENSION), jnp.float32), (jnp.arange(EXPERTS).astype(jnp.int32), gate_weight, up_weight, down_weight))
    result = middle + residual_scale * mixture
    return (result, (attended, mixture))

def seq_rms(value_rows):
    return jnp.sqrt(lax.optimization_barrier(jnp.mean((value_rows * value_rows).reshape(SEQS, SEQ_LEN * MODEL_DIMENSION), axis=1)))

def reference(stream, cotangent, attention_gain, query_weight, key_matrix, value_matrix, out_weight, mixture_gain, router_weight, gate_weight, up_weight, down_weight, routes):
    inputs = (stream.astype(jnp.float32), attention_gain.astype(jnp.float32), query_weight.astype(jnp.float32), key_matrix.astype(jnp.float32), value_matrix.astype(jnp.float32), out_weight.astype(jnp.float32), mixture_gain.astype(jnp.float32), router_weight.astype(jnp.float32), gate_weight.astype(jnp.float32), up_weight.astype(jnp.float32), down_weight.astype(jnp.float32))

    def forward(*params):
        return layer(*params, routes)
    result, pullback, extras = jax.vjp(forward, *inputs, has_aux=True)
    gradients = pullback(cotangent.astype(jnp.float32))
    attended, mixture = extras
    rms_stats = jnp.stack([seq_rms(result), seq_rms(attended), seq_rms(mixture)], axis=1)
    return (result.astype(jnp.bfloat16), gradients[0], gradients[1], gradients[2], gradients[3], gradients[4], gradients[5], gradients[6], gradients[7], gradients[8], gradients[9], gradients[10], rms_stats)
```

```python
import jax
import jax.numpy as jnp
from jax import lax
from jax.sharding import PartitionSpec as P

HEAD_FEATURES = 64
TOP = 8
SEQ_LEN = 512


epsilon = 1e-06
score_scale = 0.015625
residual_scale = 0.22
rope_base = 10000.0
masked_score = -1e30


def rope_tables(sequence_length):
    half_dim = HEAD_FEATURES // 2
    steps_up = jnp.arange(half_dim).astype(jnp.float32) * (2.0 / HEAD_FEATURES)
    inverse = jnp.exp(-steps_up * jnp.log(rope_base))
    places = jnp.arange(sequence_length).astype(jnp.float32)
    angles = places[:, None] * inverse[None, :]
    return (jnp.cos(angles), jnp.sin(angles))


def apply_rotation(value_rows, cosine_table, sine_values):
    half_dim = value_rows.shape[-1] // 2
    first_half = value_rows[..., :half_dim]
    second_half = value_rows[..., half_dim:]
    cos_rows = cosine_table[:, None, :]
    sin_rows = sine_values[:, None, :]
    return jnp.concatenate(
        [
            first_half * cos_rows - second_half * sin_rows,
            second_half * cos_rows + first_half * sin_rows,
        ],
        axis=-1,
    )


def rotary_back(grads_in, cosine_table, sine_values):
    half_dim = grads_in.shape[-1] // 2
    first_half = grads_in[..., :half_dim]
    second_half = grads_in[..., half_dim:]
    cos_rows = cosine_table[:, None, :]
    sin_rows = sine_values[:, None, :]
    return jnp.concatenate(
        [
            first_half * cos_rows + second_half * sin_rows,
            second_half * cos_rows - first_half * sin_rows,
        ],
        axis=-1,
    )


def block_scores(query_block, rotated_keys, row_start, block_rows, row_stop):
    scores = score_scale * jnp.einsum(
        "qhgd,khd->hgqk", query_block, rotated_keys, preferred_element_type=jnp.float32
    )
    causal = (row_start + jnp.arange(block_rows))[:, None] >= jnp.arange(row_stop)[None, :]
    return jnp.where(causal, scores, masked_score)


def attention_forward(query_rows, rotated_keys, value_rows):
    sequence_length = query_rows.shape[0]
    block_rows = min(512, sequence_length)
    scores = block_scores(query_rows, rotated_keys, 0, block_rows, block_rows)
    largest = jnp.max(scores, axis=-1, keepdims=True)
    weights_exp = jnp.exp(scores - largest)
    totals = jnp.sum(weights_exp, axis=-1, keepdims=True)
    probs_low = (weights_exp / totals).astype(jnp.bfloat16)
    outputs = jnp.einsum(
        "hgqk,khd->qhgd", probs_low, value_rows, preferred_element_type=jnp.float32
    )
    normalizers = [largest + jnp.log(totals)]
    return (outputs, normalizers)


def attention_backward(query_rows, rotated_keys, value_rows, normalizers, grad_mixed):
    sequence_length = query_rows.shape[0]
    block_rows = min(512, sequence_length)
    grad_keys = jnp.zeros(rotated_keys.shape, jnp.float32)
    grad_values = jnp.zeros(value_rows.shape, jnp.float32)
    grad_queries = []
    for block_index, row_start in enumerate(range(0, sequence_length, block_rows)):
        row_stop = row_start + block_rows
        scores = block_scores(query_rows, rotated_keys, row_start, block_rows, row_stop)
        probs = jnp.exp(scores - normalizers[block_index])
        probs_low = probs.astype(jnp.bfloat16)
        grad_probs = jnp.einsum(
            "qhgd,khd->hgqk", grad_mixed, value_rows, preferred_element_type=jnp.float32
        )
        inner = jnp.sum(probs * grad_probs, axis=-1, keepdims=True)
        grad_scores = (probs * (grad_probs - inner)).astype(jnp.bfloat16)
        grad_queries.append(
            score_scale
            * jnp.einsum(
                "hgqk,khd->qhgd", grad_scores, rotated_keys, preferred_element_type=jnp.float32
            )
        )
        grad_keys = grad_keys.at[:row_stop].add(
            score_scale
            * jnp.einsum(
                "hgqk,qhgd->khd", grad_scores, query_rows, preferred_element_type=jnp.float32
            )
        )
        grad_values = grad_values.at[:row_stop].add(
            jnp.einsum("hgqk,qhgd->khd", probs_low, grad_mixed, preferred_element_type=jnp.float32)
        )
    return (grad_queries[0], grad_keys, grad_values)


def to_owners(packed):
    return lax.all_to_all(packed, "ep", split_axis=1, concat_axis=1, tiled=True)


def back_to_tokens(rows_low, slot_count, model_width):
    returned = lax.all_to_all(rows_low, "ep", split_axis=1, concat_axis=1, tiled=True)
    joined = lax.all_gather(returned, "tp", axis=0, tiled=True)
    return joined.reshape(slot_count, model_width)


def from_owners(term_fn, slot_count, experts, model_width):
    share_rows = slot_count // lax.axis_size("tp")
    summed = lax.psum_scatter(
        term_fn(jnp.int32(0), lax.axis_size("tp") * share_rows).astype(jnp.bfloat16),
        "tp",
        scatter_dimension=0,
        tiled=True,
    ).astype(jnp.float32)
    summed = summed.astype(jnp.bfloat16).reshape(share_rows // experts, experts, model_width)
    return back_to_tokens(summed, slot_count, model_width)


def seq_rms(value_rows, seq_count):
    return jnp.sqrt(jnp.mean((value_rows * value_rows).reshape(seq_count, -1), axis=1))


def routed_shards(
    stream,
    cotangent,
    attention_gain,
    query_weight,
    key_matrix,
    value_matrix,
    out_weight,
    mixture_gain,
    router_weight,
    gate_weight,
    up_weight,
    down_weight,
    routes,
):
    tok_rows, model_width = stream.shape
    experts = router_weight.shape[1]
    cap_slots = tok_rows * TOP * 5 // (4 * experts)
    slot_count = cap_slots * experts
    query_heads = query_weight.shape[1] // HEAD_FEATURES
    key_heads = key_matrix.shape[1] // HEAD_FEATURES
    group_width = query_heads // key_heads
    seq_count = tok_rows // SEQ_LEN
    stream_f = stream.astype(jnp.float32)
    grad_result = cotangent.astype(jnp.float32)
    gain_first = attention_gain.astype(jnp.float32)
    gain_second = mixture_gain.astype(jnp.float32)
    cosine_table, sine_values = rope_tables(SEQ_LEN)
    cosine_rows = jnp.tile(cosine_table, (seq_count, 1))
    sine_rows = jnp.tile(sine_values, (seq_count, 1))
    zero_low = jnp.zeros((), jnp.bfloat16)
    inv_first = lax.rsqrt(jnp.mean(stream_f * stream_f, axis=-1, keepdims=True) + epsilon)
    normalized_input = (stream_f * inv_first * gain_first).astype(jnp.bfloat16)
    query_pre = jnp.dot(normalized_input, query_weight, preferred_element_type=jnp.float32).reshape(
        tok_rows, query_heads, HEAD_FEATURES
    )
    key_pre = jnp.dot(normalized_input, key_matrix, preferred_element_type=jnp.float32).reshape(
        tok_rows, key_heads, HEAD_FEATURES
    )
    query_rows = (
        apply_rotation(query_pre, cosine_rows, sine_rows)
        .astype(jnp.bfloat16)
        .reshape(tok_rows, key_heads, group_width, HEAD_FEATURES)
    )
    rotated_keys = apply_rotation(key_pre, cosine_rows, sine_rows).astype(jnp.bfloat16)
    value_rows = (
        jnp.dot(normalized_input, value_matrix, preferred_element_type=jnp.float32)
        .astype(jnp.bfloat16)
        .reshape(tok_rows, key_heads, HEAD_FEATURES)
    )
    mixed_seq, norms_seq = attention_forward(query_rows, rotated_keys, value_rows)
    mixed_low = mixed_seq.reshape(tok_rows, query_heads * HEAD_FEATURES).astype(jnp.bfloat16)
    attended = lax.psum(
        jnp.dot(mixed_low, out_weight, preferred_element_type=jnp.float32).astype(jnp.bfloat16),
        "tp",
    ).astype(jnp.float32)
    middle = stream_f + residual_scale * attended
    inv_second = lax.rsqrt(jnp.mean(middle * middle, axis=-1, keepdims=True) + epsilon)
    mixer_in = (middle * inv_second * gain_second).astype(jnp.bfloat16)
    logits = jnp.dot(mixer_in, router_weight, preferred_element_type=jnp.float32)
    expert_ids = jnp.arange(experts, dtype=jnp.int32)
    route_hot = routes[:, :, None] == expert_ids[None, None, :]
    chosen = jnp.sum(jnp.where(route_hot, logits[:, None, :], 0.0), axis=-1)
    chosen_exp = jnp.exp(chosen - jnp.max(chosen, axis=-1, keepdims=True))
    gate_probs = chosen_exp / jnp.sum(chosen_exp, axis=-1, keepdims=True)
    flat_routes = routes.reshape(-1)
    flat_hot = route_hot.reshape(tok_rows * TOP, experts).astype(jnp.int32)
    ranks = jnp.sum((jnp.cumsum(flat_hot, axis=0) - 1) * flat_hot, axis=1)
    slot_index = ranks * experts + flat_routes
    source_pair = (
        jnp.zeros((slot_count,), jnp.int32)
        .at[slot_index]
        .set(jnp.arange(tok_rows * TOP, dtype=jnp.int32))
    )
    filled = jnp.zeros((slot_count,), jnp.bool_).at[slot_index].set(True)
    source_token = source_pair // TOP
    sent_rows = jnp.where(filled[:, None], mixer_in[source_token], zero_low).reshape(
        cap_slots, experts, model_width
    )
    received = to_owners(sent_rows).reshape(slot_count, model_width)
    gate_matrix = gate_weight[0]
    up_matrix = up_weight[0]
    down_matrix = down_weight[0]
    gate_pre = jnp.dot(received, gate_matrix, preferred_element_type=jnp.float32)
    up_pre = jnp.dot(received, up_matrix, preferred_element_type=jnp.float32)
    sigmoid_gate = jax.nn.sigmoid(gate_pre)
    silu_gate = gate_pre * sigmoid_gate
    active = (silu_gate * up_pre).astype(jnp.bfloat16)

    def down_term(row_start, row_count):
        return jnp.dot(active, down_matrix, preferred_element_type=jnp.float32)

    expert_rows = from_owners(down_term, slot_count, experts, model_width)
    picked_rows = expert_rows[slot_index].reshape(tok_rows, TOP, model_width)
    mixture = jnp.sum(gate_probs[:, :, None] * picked_rows, axis=1)
    result = middle + residual_scale * mixture
    layer_out = result.astype(jnp.bfloat16)
    rms_stats = jnp.stack(
        [seq_rms(result, seq_count), seq_rms(attended, seq_count), seq_rms(mixture, seq_count)],
        axis=1,
    )
    grad_mix = residual_scale * grad_result
    grad_weighting = jnp.sum(picked_rows * grad_mix[:, None, :], axis=-1)
    grad_chosen = gate_probs * (
        grad_weighting - jnp.sum(gate_probs * grad_weighting, axis=-1, keepdims=True)
    )
    grad_logits = jnp.sum(jnp.where(route_hot, grad_chosen[:, :, None], 0.0), axis=1).astype(
        jnp.bfloat16
    )
    router_grad = jnp.dot(mixer_in.T, grad_logits, preferred_element_type=jnp.float32)
    flat_gates = gate_probs.reshape(-1)
    grad_sent = jnp.where(
        filled[:, None],
        (flat_gates[source_pair][:, None] * grad_mix[source_token]).astype(jnp.bfloat16),
        zero_low,
    ).reshape(cap_slots, experts, model_width)
    grad_received = to_owners(grad_sent).reshape(slot_count, model_width)
    grad_active = jnp.dot(grad_received, down_matrix.T, preferred_element_type=jnp.float32)
    down_grad = jnp.dot(active.T, grad_received, preferred_element_type=jnp.float32)
    grad_gate_pre = (
        grad_active * up_pre * sigmoid_gate * (1.0 + gate_pre * (1.0 - sigmoid_gate))
    ).astype(jnp.bfloat16)
    grad_up_pre = (grad_active * silu_gate).astype(jnp.bfloat16)
    gate_grad = jnp.dot(received.T, grad_gate_pre, preferred_element_type=jnp.float32)
    up_grad = jnp.dot(received.T, grad_up_pre, preferred_element_type=jnp.float32)

    def input_term(row_start, row_count):
        return jnp.dot(grad_gate_pre, gate_matrix.T, preferred_element_type=jnp.float32) + jnp.dot(
            grad_up_pre, up_matrix.T, preferred_element_type=jnp.float32
        )

    grad_rows = from_owners(input_term, slot_count, experts, model_width)
    grad_mixer = jnp.dot(
        grad_logits, router_weight.T, preferred_element_type=jnp.float32
    ) + jnp.sum(
        grad_rows[slot_index].reshape(tok_rows, TOP, model_width), axis=1, dtype=jnp.float32
    )
    weighted_second = grad_mixer * gain_second
    second_grad = jnp.sum(grad_mixer * middle * inv_second, axis=0)
    grad_middle = (
        grad_result
        + inv_second * weighted_second
        - middle * inv_second**3 * jnp.mean(middle * weighted_second, axis=-1, keepdims=True)
    )
    grad_attended = (residual_scale * grad_middle).astype(jnp.bfloat16)
    out_grad_t = jnp.dot(grad_attended.T, mixed_low, preferred_element_type=jnp.float32)
    grad_mixed = (
        jnp.dot(grad_attended, out_weight.T, preferred_element_type=jnp.float32)
        .astype(jnp.bfloat16)
        .reshape(tok_rows, key_heads, group_width, HEAD_FEATURES)
    )
    grad_query_seq, grad_key_seq, grad_value_seq = attention_backward(
        query_rows, rotated_keys, value_rows, norms_seq, grad_mixed
    )
    grad_queries_rot = grad_query_seq.reshape(tok_rows, query_heads, HEAD_FEATURES)
    grad_query_pre = (
        rotary_back(grad_queries_rot, cosine_rows, sine_rows)
        .astype(jnp.bfloat16)
        .reshape(tok_rows, query_heads * HEAD_FEATURES)
    )
    grad_key_pre = (
        rotary_back(grad_key_seq, cosine_rows, sine_rows)
        .astype(jnp.bfloat16)
        .reshape(tok_rows, key_heads * HEAD_FEATURES)
    )
    grad_values_low = grad_value_seq.astype(jnp.bfloat16).reshape(
        tok_rows, key_heads * HEAD_FEATURES
    )
    query_grad = jnp.dot(normalized_input.T, grad_query_pre, preferred_element_type=jnp.float32)
    key_grad = jnp.dot(normalized_input.T, grad_key_pre, preferred_element_type=jnp.float32)
    value_grad = jnp.dot(normalized_input.T, grad_values_low, preferred_element_type=jnp.float32)
    normed_term = jnp.dot(grad_query_pre, query_weight.T, preferred_element_type=jnp.float32)
    normed_term = normed_term + jnp.dot(
        grad_key_pre, key_matrix.T, preferred_element_type=jnp.float32
    )
    normed_term = normed_term + jnp.dot(
        grad_values_low, value_matrix.T, preferred_element_type=jnp.float32
    )
    grad_normed = lax.psum(normed_term.astype(jnp.bfloat16), "tp").astype(jnp.float32)
    weighted_first = grad_normed * gain_first
    first_grad = jnp.sum(grad_normed * stream_f * inv_first, axis=0)
    grad_stream = (
        grad_middle
        + inv_first * weighted_first
        - stream_f * inv_first**3 * jnp.mean(stream_f * weighted_first, axis=-1, keepdims=True)
    )
    reduced = (
        lax.psum_scatter(query_grad, "ep", scatter_dimension=0, tiled=True),
        lax.psum_scatter(key_grad, "ep", scatter_dimension=0, tiled=True),
        lax.psum_scatter(value_grad, "ep", scatter_dimension=0, tiled=True),
        lax.psum_scatter(out_grad_t, "ep", scatter_dimension=0, tiled=True),
        lax.psum_scatter(router_grad, "ep", scatter_dimension=0, tiled=True),
        lax.psum_scatter(first_grad, "ep", scatter_dimension=0, tiled=True),
        lax.psum_scatter(second_grad, "ep", scatter_dimension=0, tiled=True),
    )
    return (
        layer_out,
        grad_stream,
        reduced[5],
        reduced[0],
        reduced[1],
        reduced[2],
        reduced[3].T,
        reduced[6],
        reduced[4],
        gate_grad[None],
        up_grad[None],
        down_grad[None],
        rms_stats,
    )


def swap_cores(value):
    return lax.ppermute(value, "tp", [(0, 1), (1, 0)])


def exchange(value, bits):
    count = lax.axis_size("ep")
    return lax.ppermute(value, "ep", [(i, i ^ bits) for i in range(count)])


def keep_and_send(value, axis, bit):
    kept = lax.dynamic_index_in_dim(value, bit, axis, keepdims=False)
    sent = lax.dynamic_index_in_dim(value, 1 - bit, axis, keepdims=False)
    return kept, sent


def scatter_stage(value, axis, bits, bit):
    kept, sent = keep_and_send(value, axis, bit)
    arrived = exchange(sent, bits)
    return (kept.astype(jnp.float32) + arrived.astype(jnp.float32)).astype(jnp.bfloat16)


def scatter_rows(value, first_bit, place):
    rows = value.shape[0]
    count = lax.axis_size("ep")
    bit_count = count.bit_length() - 1
    value = value.reshape((2,) * bit_count + (rows // count, value.shape[1]))
    order = [first_bit, 1 - first_bit] + list(range(bit_count - 1, 1, -1))
    left = list(range(bit_count - 1, -1, -1))
    for bit in order:
        axis = left.index(bit)
        value = scatter_stage(value, axis, 1 << bit, (place >> bit) & 1)
        left.remove(bit)
    return value.astype(jnp.float32)


def dense_shards(
    stream,
    cotangent,
    attention_gain,
    query_weight,
    key_matrix,
    value_matrix,
    out_weight,
    mixture_gain,
    router_weight,
    gate_weight,
    up_weight,
    down_weight,
    routes,
):
    tok_rows, model_width = stream.shape
    experts = router_weight.shape[1]
    plane = 4
    lines = experts // plane
    hidden_half = gate_weight.shape[2]
    hidden = 2 * hidden_half * plane
    half = tok_rows // 2
    query_heads = query_weight.shape[1] // HEAD_FEATURES
    key_heads = key_matrix.shape[1] // HEAD_FEATURES
    group_width = query_heads // key_heads
    core = lax.axis_index("tp")
    place = lax.axis_index("ep")
    line_place = place // plane
    plane_place = place % plane

    def own_half(value):
        return lax.dynamic_slice_in_dim(value, core * half, half, 0)

    def other_half(value):
        return lax.dynamic_slice_in_dim(value, (1 - core) * half, half, 0)

    def join_halves(mine, theirs):
        return jnp.where(
            core == 0,
            jnp.concatenate([mine, theirs], axis=0),
            jnp.concatenate([theirs, mine], axis=0),
        )

    def plane_parts(weight):
        near = [weight] + [exchange(weight, d) for d in range(1, plane)]
        return near + [swap_cores(part) for part in near]

    gate_all = jnp.concatenate(plane_parts(gate_weight[0]), axis=1)
    up_all = jnp.concatenate(plane_parts(up_weight[0]), axis=1)
    down_all = jnp.concatenate(plane_parts(down_weight[0]), axis=0)

    def line_parts(value):
        return [value] + [exchange(value, d * plane) for d in range(1, lines)]

    cot_rows = jnp.concatenate(line_parts(own_half(cotangent)), axis=0)

    stream_f = stream.astype(jnp.float32)
    gain_first = attention_gain.astype(jnp.float32)
    gain_second = mixture_gain.astype(jnp.float32)
    cosine_rows, sine_rows = rope_tables(SEQ_LEN)
    inv_first = lax.rsqrt(jnp.mean(stream_f * stream_f, axis=-1, keepdims=True) + epsilon)
    normalized_input = (stream_f * inv_first * gain_first).astype(jnp.bfloat16)
    query_pre = jnp.dot(normalized_input, query_weight, preferred_element_type=jnp.float32).reshape(
        tok_rows, query_heads, HEAD_FEATURES
    )
    key_pre = jnp.dot(normalized_input, key_matrix, preferred_element_type=jnp.float32).reshape(
        tok_rows, key_heads, HEAD_FEATURES
    )
    query_rows = (
        apply_rotation(query_pre, cosine_rows, sine_rows)
        .astype(jnp.bfloat16)
        .reshape(tok_rows, key_heads, group_width, HEAD_FEATURES)
    )
    rotated_keys = apply_rotation(key_pre, cosine_rows, sine_rows).astype(jnp.bfloat16)
    value_rows = (
        jnp.dot(normalized_input, value_matrix, preferred_element_type=jnp.float32)
        .astype(jnp.bfloat16)
        .reshape(tok_rows, key_heads, HEAD_FEATURES)
    )
    mixed_seq, norms_seq = attention_forward(query_rows, rotated_keys, value_rows)
    mixed_low = mixed_seq.reshape(tok_rows, query_heads * HEAD_FEATURES).astype(jnp.bfloat16)
    attended_part = jnp.dot(mixed_low, out_weight, preferred_element_type=jnp.float32).astype(
        jnp.bfloat16
    )
    attended = own_half(attended_part).astype(jnp.float32) + swap_cores(
        other_half(attended_part)
    ).astype(jnp.float32)
    middle = own_half(stream).astype(jnp.float32) + residual_scale * attended
    inv_second = lax.rsqrt(jnp.mean(middle * middle, axis=-1, keepdims=True) + epsilon)
    mixer_in = (middle * inv_second * gain_second).astype(jnp.bfloat16)
    logits = jnp.dot(mixer_in, router_weight, preferred_element_type=jnp.float32)
    expert_ids = jnp.arange(experts, dtype=jnp.int32)
    routed = jnp.any(own_half(routes)[:, :, None] == expert_ids[None, None, :], axis=1)
    largest = jnp.max(jnp.where(routed, logits, masked_score), axis=-1, keepdims=True)
    gate_exp = jnp.where(routed, jnp.exp(jnp.minimum(logits - largest, 0.0)), 0.0)
    gate_probs = gate_exp / jnp.sum(gate_exp, axis=-1, keepdims=True)

    mixer_rows = jnp.concatenate(line_parts(mixer_in), axis=0)
    prob_rows = jnp.concatenate(line_parts(gate_probs), axis=0)

    def expert_of(line_step, plane_step):
        return (line_place ^ line_step) * plane + (plane_place ^ plane_step)

    prob_near = jnp.stack(
        [
            jnp.sum(jnp.where(expert_ids[None, :] == expert_of(0, d), prob_rows, 0.0), axis=1)
            for d in range(plane)
        ],
        axis=1,
    )
    rows = lines * half

    def spread(value):
        return jnp.broadcast_to(
            value[:, None, :, None], (rows, 2, plane, hidden_half)
        ).reshape(rows, hidden)

    gate_pre = jnp.dot(mixer_rows, gate_all, preferred_element_type=jnp.float32)
    up_pre = jnp.dot(mixer_rows, up_all, preferred_element_type=jnp.float32)
    grad_raw = residual_scale * jnp.dot(cot_rows, down_all.T, preferred_element_type=jnp.float32)
    sigmoid_gate = jax.nn.sigmoid(gate_pre)
    silu_gate = gate_pre * sigmoid_gate
    active = silu_gate * up_pre
    weighting_near = jnp.sum(
        (active * grad_raw).reshape(rows, 2, plane, hidden_half), axis=(1, 3)
    )
    prob_wide = spread(prob_near)
    scaled_active = (prob_wide * active).astype(jnp.bfloat16)
    grad_active = prob_wide * grad_raw
    grad_gate_pre = (
        grad_active * up_pre * sigmoid_gate * (1.0 + gate_pre * (1.0 - sigmoid_gate))
    ).astype(jnp.bfloat16)
    grad_up_pre = (grad_active * silu_gate).astype(jnp.bfloat16)
    out_rows = jnp.dot(scaled_active, down_all, preferred_element_type=jnp.float32).astype(
        jnp.bfloat16
    )
    grad_rows = (
        jnp.dot(grad_gate_pre, gate_all.T, preferred_element_type=jnp.float32)
        + jnp.dot(grad_up_pre, up_all.T, preferred_element_type=jnp.float32)
    ).astype(jnp.bfloat16)

    def line_return(value):
        pieces = [value[d * half : (d + 1) * half] for d in range(lines)]
        return [pieces[0]] + [exchange(pieces[d], d * plane) for d in range(1, lines)]

    mixture = sum(piece.astype(jnp.float32) for piece in line_return(out_rows))
    grad_mixer_rows = sum(piece.astype(jnp.float32) for piece in line_return(grad_rows))
    grad_weighting = jnp.zeros((half, experts), jnp.float32)
    for line_step, piece in enumerate(line_return(weighting_near)):
        for plane_step in range(plane):
            grad_weighting = grad_weighting + jnp.where(
                expert_ids[None, :] == expert_of(line_step, plane_step),
                piece[:, plane_step : plane_step + 1],
                0.0,
            )

    gate_grad = jnp.dot(mixer_rows.T, grad_gate_pre, preferred_element_type=jnp.float32)
    up_grad = jnp.dot(mixer_rows.T, grad_up_pre, preferred_element_type=jnp.float32)
    down_grad = residual_scale * jnp.dot(
        scaled_active.T, cot_rows, preferred_element_type=jnp.float32
    )

    def plane_sum(value, axis):
        low = value.astype(jnp.bfloat16)
        mine, theirs = jnp.split(low, 2, axis=axis)
        both = mine.astype(jnp.float32) + swap_cores(theirs).astype(jnp.float32)
        parts = jnp.split(both, plane, axis=axis)
        total = parts[0]
        for d in range(1, plane):
            total = total + exchange(parts[d].astype(jnp.bfloat16), d).astype(jnp.float32)
        return total

    gate_grad = plane_sum(gate_grad, 1)
    up_grad = plane_sum(up_grad, 1)
    down_grad = plane_sum(down_grad, 0)

    result = middle + residual_scale * mixture
    result_low = result.astype(jnp.bfloat16)
    layer_out = join_halves(result_low, swap_cores(result_low))
    squares = jnp.stack([jnp.sum(v * v) for v in (result, attended, mixture)])
    rms_stats = jnp.sqrt((squares + swap_cores(squares)) / (tok_rows * model_width))[None, :]
    grad_chosen = gate_probs * (
        grad_weighting - jnp.sum(gate_probs * grad_weighting, axis=-1, keepdims=True)
    )
    grad_logits = grad_chosen.astype(jnp.bfloat16)
    router_grad = jnp.dot(mixer_in.T, grad_logits, preferred_element_type=jnp.float32)
    grad_mixer = (
        jnp.dot(grad_logits, router_weight.T, preferred_element_type=jnp.float32) + grad_mixer_rows
    )
    weighted_second = grad_mixer * gain_second
    second_grad = jnp.sum(grad_mixer * middle * inv_second, axis=0)
    grad_middle = (
        own_half(cotangent).astype(jnp.float32)
        + inv_second * weighted_second
        - middle * inv_second**3 * jnp.mean(middle * weighted_second, axis=-1, keepdims=True)
    )
    grad_middle_low = grad_middle.astype(jnp.bfloat16)
    grad_middle_all = join_halves(grad_middle_low, swap_cores(grad_middle_low)).astype(jnp.float32)
    grad_attended = (residual_scale * grad_middle_all).astype(jnp.bfloat16)
    out_grad_t = jnp.dot(grad_attended.T, mixed_low, preferred_element_type=jnp.float32)
    grad_mixed = (
        jnp.dot(grad_attended, out_weight.T, preferred_element_type=jnp.float32)
        .astype(jnp.bfloat16)
        .reshape(tok_rows, key_heads, group_width, HEAD_FEATURES)
    )
    grad_query_seq, grad_key_seq, grad_value_seq = attention_backward(
        query_rows, rotated_keys, value_rows, norms_seq, grad_mixed
    )
    grad_queries_rot = grad_query_seq.reshape(tok_rows, query_heads, HEAD_FEATURES)
    grad_query_pre = (
        rotary_back(grad_queries_rot, cosine_rows, sine_rows)
        .astype(jnp.bfloat16)
        .reshape(tok_rows, query_heads * HEAD_FEATURES)
    )
    grad_key_pre = (
        rotary_back(grad_key_seq, cosine_rows, sine_rows)
        .astype(jnp.bfloat16)
        .reshape(tok_rows, key_heads * HEAD_FEATURES)
    )
    grad_values_low = grad_value_seq.astype(jnp.bfloat16).reshape(
        tok_rows, key_heads * HEAD_FEATURES
    )
    query_grad = jnp.dot(normalized_input.T, grad_query_pre, preferred_element_type=jnp.float32)
    key_grad = jnp.dot(normalized_input.T, grad_key_pre, preferred_element_type=jnp.float32)
    value_grad = jnp.dot(normalized_input.T, grad_values_low, preferred_element_type=jnp.float32)
    normed_term = jnp.dot(grad_query_pre, query_weight.T, preferred_element_type=jnp.float32)
    normed_term = normed_term + jnp.dot(
        grad_key_pre, key_matrix.T, preferred_element_type=jnp.float32
    )
    normed_term = normed_term + jnp.dot(
        grad_values_low, value_matrix.T, preferred_element_type=jnp.float32
    )
    normed_low = normed_term.astype(jnp.bfloat16)
    grad_normed = normed_low.astype(jnp.float32) + swap_cores(normed_low).astype(jnp.float32)
    weighted_first = grad_normed * gain_first
    first_grad = jnp.sum(grad_normed * stream_f * inv_first, axis=0)
    grad_stream = (
        grad_middle_all
        + inv_first * weighted_first
        - stream_f * inv_first**3 * jnp.mean(stream_f * weighted_first, axis=-1, keepdims=True)
    )
    small = jnp.concatenate(
        [router_grad, second_grad[:, None], 0.5 * first_grad[:, None]], axis=1
    )
    small = small + swap_cores(small)
    small = jnp.pad(small, ((0, 0), (0, 128 - small.shape[1])))
    low = [
        value.astype(jnp.bfloat16)
        for value in (out_grad_t, key_grad, query_grad, value_grad, small)
    ]
    first_part = scatter_rows(jnp.concatenate(low[:2], axis=1), 0, place)
    second_part = scatter_rows(jnp.concatenate(low[2:], axis=1), 1, place)
    query_width = query_weight.shape[1]
    key_width = key_matrix.shape[1]
    small_part = second_part[:, query_width + key_width :]
    return (
        layer_out,
        grad_stream,
        small_part[:, experts + 1],
        second_part[:, :query_width],
        first_part[:, query_width:],
        second_part[:, query_width : query_width + key_width],
        first_part[:, :query_width].T,
        small_part[:, experts],
        small_part[:, :experts],
        gate_grad[None],
        up_grad[None],
        down_grad[None],
        rms_stats,
    )


def solution(mesh):
    in_specs = (
        P("ep", None),
        P("ep", None),
        P(),
        P(None, "tp"),
        P(None, "tp"),
        P(None, "tp"),
        P("tp", None),
        P(),
        P(),
        P("ep", None, "tp"),
        P("ep", None, "tp"),
        P("ep", "tp", None),
        P("ep", None),
    )
    out_specs = (
        P("ep", None),
        P("ep", None),
        P("ep"),
        P("ep", "tp"),
        P("ep", "tp"),
        P("ep", "tp"),
        P("tp", "ep"),
        P("ep"),
        P("ep", None),
        P("ep", None, "tp"),
        P("ep", None, "tp"),
        P("ep", "tp", None),
        P("ep", None),
    )
    ep_size = mesh.shape["ep"]
    dense = mesh.shape["tp"] == 2 and ep_size <= 2 * TOP and ep_size == 16
    shards = dense_shards if dense else routed_shards
    return jax.shard_map(shards, mesh=mesh, in_specs=in_specs, out_specs=out_specs, check_vma=False)
```

```python
import functools

import jax
import jax.numpy as jnp
from jax import lax
from jax.experimental import pallas as pl
from jax.experimental.pallas import tpu as pltpu
from jax.sharding import PartitionSpec as P

HEAD_FEATURES = 64
TOP = 8
SEQ_LEN = 512


epsilon = 1e-06
score_scale = 0.015625
residual_scale = 0.22
rope_base = 10000.0
masked_score = -1e30


def rope_tables(sequence_length):
    half_dim = HEAD_FEATURES // 2
    steps_up = jnp.arange(half_dim).astype(jnp.float32) * (2.0 / HEAD_FEATURES)
    inverse = jnp.exp(-steps_up * jnp.log(rope_base))
    places = jnp.arange(sequence_length).astype(jnp.float32)
    angles = places[:, None] * inverse[None, :]
    return (jnp.cos(angles), jnp.sin(angles))


def apply_rotation(value_rows, cosine_table, sine_values):
    half_dim = value_rows.shape[-1] // 2
    first_half = value_rows[..., :half_dim]
    second_half = value_rows[..., half_dim:]
    cos_rows = cosine_table[:, None, :]
    sin_rows = sine_values[:, None, :]
    return jnp.concatenate(
        [
            first_half * cos_rows - second_half * sin_rows,
            second_half * cos_rows + first_half * sin_rows,
        ],
        axis=-1,
    )


def rotary_back(grads_in, cosine_table, sine_values):
    half_dim = grads_in.shape[-1] // 2
    first_half = grads_in[..., :half_dim]
    second_half = grads_in[..., half_dim:]
    cos_rows = cosine_table[:, None, :]
    sin_rows = sine_values[:, None, :]
    return jnp.concatenate(
        [
            first_half * cos_rows + second_half * sin_rows,
            second_half * cos_rows - first_half * sin_rows,
        ],
        axis=-1,
    )


def block_scores(query_block, rotated_keys, row_start, block_rows, row_stop):
    scores = score_scale * jnp.einsum(
        "qhgd,khd->hgqk", query_block, rotated_keys, preferred_element_type=jnp.float32
    )
    causal = (row_start + jnp.arange(block_rows))[:, None] >= jnp.arange(row_stop)[None, :]
    return jnp.where(causal, scores, masked_score)


def attention_forward(query_rows, rotated_keys, value_rows):
    sequence_length = query_rows.shape[0]
    block_rows = min(512, sequence_length)
    scores = block_scores(query_rows, rotated_keys, 0, block_rows, block_rows)
    largest = jnp.max(scores, axis=-1, keepdims=True)
    weights_exp = jnp.exp(scores - largest)
    totals = jnp.sum(weights_exp, axis=-1, keepdims=True)
    probs_low = (weights_exp / totals).astype(jnp.bfloat16)
    outputs = jnp.einsum(
        "hgqk,khd->qhgd", probs_low, value_rows, preferred_element_type=jnp.float32
    )
    normalizers = [largest + jnp.log(totals)]
    return (outputs, normalizers)


def attention_backward(query_rows, rotated_keys, value_rows, normalizers, grad_mixed):
    sequence_length = query_rows.shape[0]
    block_rows = min(512, sequence_length)
    grad_keys = jnp.zeros(rotated_keys.shape, jnp.float32)
    grad_values = jnp.zeros(value_rows.shape, jnp.float32)
    grad_queries = []
    for block_index, row_start in enumerate(range(0, sequence_length, block_rows)):
        row_stop = row_start + block_rows
        scores = block_scores(query_rows, rotated_keys, row_start, block_rows, row_stop)
        probs = jnp.exp(scores - normalizers[block_index])
        probs_low = probs.astype(jnp.bfloat16)
        grad_probs = jnp.einsum(
            "qhgd,khd->hgqk", grad_mixed, value_rows, preferred_element_type=jnp.float32
        )
        inner = jnp.sum(probs * grad_probs, axis=-1, keepdims=True)
        grad_scores = (probs * (grad_probs - inner)).astype(jnp.bfloat16)
        grad_queries.append(
            score_scale
            * jnp.einsum(
                "hgqk,khd->qhgd", grad_scores, rotated_keys, preferred_element_type=jnp.float32
            )
        )
        grad_keys = grad_keys.at[:row_stop].add(
            score_scale
            * jnp.einsum(
                "hgqk,qhgd->khd", grad_scores, query_rows, preferred_element_type=jnp.float32
            )
        )
        grad_values = grad_values.at[:row_stop].add(
            jnp.einsum("hgqk,qhgd->khd", probs_low, grad_mixed, preferred_element_type=jnp.float32)
        )
    return (grad_queries[0], grad_keys, grad_values)


def to_owners(packed):
    return lax.all_to_all(packed, "ep", split_axis=1, concat_axis=1, tiled=True)


def back_to_tokens(rows_low, slot_count, model_width):
    returned = lax.all_to_all(rows_low, "ep", split_axis=1, concat_axis=1, tiled=True)
    joined = lax.all_gather(returned, "tp", axis=0, tiled=True)
    return joined.reshape(slot_count, model_width)


def from_owners(term_fn, slot_count, experts, model_width):
    share_rows = slot_count // lax.axis_size("tp")
    summed = lax.psum_scatter(
        term_fn(jnp.int32(0), lax.axis_size("tp") * share_rows).astype(jnp.bfloat16),
        "tp",
        scatter_dimension=0,
        tiled=True,
    ).astype(jnp.float32)
    summed = summed.astype(jnp.bfloat16).reshape(share_rows // experts, experts, model_width)
    return back_to_tokens(summed, slot_count, model_width)


def seq_rms(value_rows, seq_count):
    return jnp.sqrt(jnp.mean((value_rows * value_rows).reshape(seq_count, -1), axis=1))


def routed_shards(
    stream,
    cotangent,
    attention_gain,
    query_weight,
    key_matrix,
    value_matrix,
    out_weight,
    mixture_gain,
    router_weight,
    gate_weight,
    up_weight,
    down_weight,
    routes,
):
    tok_rows, model_width = stream.shape
    experts = router_weight.shape[1]
    cap_slots = tok_rows * TOP * 5 // (4 * experts)
    slot_count = cap_slots * experts
    query_heads = query_weight.shape[1] // HEAD_FEATURES
    key_heads = key_matrix.shape[1] // HEAD_FEATURES
    group_width = query_heads // key_heads
    seq_count = tok_rows // SEQ_LEN
    stream_f = stream.astype(jnp.float32)
    grad_result = cotangent.astype(jnp.float32)
    gain_first = attention_gain.astype(jnp.float32)
    gain_second = mixture_gain.astype(jnp.float32)
    cosine_table, sine_values = rope_tables(SEQ_LEN)
    cosine_rows = jnp.tile(cosine_table, (seq_count, 1))
    sine_rows = jnp.tile(sine_values, (seq_count, 1))
    zero_low = jnp.zeros((), jnp.bfloat16)
    inv_first = lax.rsqrt(jnp.mean(stream_f * stream_f, axis=-1, keepdims=True) + epsilon)
    normalized_input = (stream_f * inv_first * gain_first).astype(jnp.bfloat16)
    query_pre = jnp.dot(normalized_input, query_weight, preferred_element_type=jnp.float32).reshape(
        tok_rows, query_heads, HEAD_FEATURES
    )
    key_pre = jnp.dot(normalized_input, key_matrix, preferred_element_type=jnp.float32).reshape(
        tok_rows, key_heads, HEAD_FEATURES
    )
    query_rows = (
        apply_rotation(query_pre, cosine_rows, sine_rows)
        .astype(jnp.bfloat16)
        .reshape(tok_rows, key_heads, group_width, HEAD_FEATURES)
    )
    rotated_keys = apply_rotation(key_pre, cosine_rows, sine_rows).astype(jnp.bfloat16)
    value_rows = (
        jnp.dot(normalized_input, value_matrix, preferred_element_type=jnp.float32)
        .astype(jnp.bfloat16)
        .reshape(tok_rows, key_heads, HEAD_FEATURES)
    )
    mixed_seq, norms_seq = attention_forward(query_rows, rotated_keys, value_rows)
    mixed_low = mixed_seq.reshape(tok_rows, query_heads * HEAD_FEATURES).astype(jnp.bfloat16)
    attended = lax.psum(
        jnp.dot(mixed_low, out_weight, preferred_element_type=jnp.float32).astype(jnp.bfloat16),
        "tp",
    ).astype(jnp.float32)
    middle = stream_f + residual_scale * attended
    inv_second = lax.rsqrt(jnp.mean(middle * middle, axis=-1, keepdims=True) + epsilon)
    mixer_in = (middle * inv_second * gain_second).astype(jnp.bfloat16)
    logits = jnp.dot(mixer_in, router_weight, preferred_element_type=jnp.float32)
    expert_ids = jnp.arange(experts, dtype=jnp.int32)
    route_hot = routes[:, :, None] == expert_ids[None, None, :]
    chosen = jnp.sum(jnp.where(route_hot, logits[:, None, :], 0.0), axis=-1)
    chosen_exp = jnp.exp(chosen - jnp.max(chosen, axis=-1, keepdims=True))
    gate_probs = chosen_exp / jnp.sum(chosen_exp, axis=-1, keepdims=True)
    flat_routes = routes.reshape(-1)
    flat_hot = route_hot.reshape(tok_rows * TOP, experts).astype(jnp.int32)
    ranks = jnp.sum((jnp.cumsum(flat_hot, axis=0) - 1) * flat_hot, axis=1)
    slot_index = ranks * experts + flat_routes
    source_pair = (
        jnp.zeros((slot_count,), jnp.int32)
        .at[slot_index]
        .set(jnp.arange(tok_rows * TOP, dtype=jnp.int32))
    )
    filled = jnp.zeros((slot_count,), jnp.bool_).at[slot_index].set(True)
    source_token = source_pair // TOP
    sent_rows = jnp.where(filled[:, None], mixer_in[source_token], zero_low).reshape(
        cap_slots, experts, model_width
    )
    received = to_owners(sent_rows).reshape(slot_count, model_width)
    gate_matrix = gate_weight[0]
    up_matrix = up_weight[0]
    down_matrix = down_weight[0]
    gate_pre = jnp.dot(received, gate_matrix, preferred_element_type=jnp.float32)
    up_pre = jnp.dot(received, up_matrix, preferred_element_type=jnp.float32)
    sigmoid_gate = jax.nn.sigmoid(gate_pre)
    silu_gate = gate_pre * sigmoid_gate
    active = (silu_gate * up_pre).astype(jnp.bfloat16)

    def down_term(row_start, row_count):
        return jnp.dot(active, down_matrix, preferred_element_type=jnp.float32)

    expert_rows = from_owners(down_term, slot_count, experts, model_width)
    picked_rows = expert_rows[slot_index].reshape(tok_rows, TOP, model_width)
    mixture = jnp.sum(gate_probs[:, :, None] * picked_rows, axis=1)
    result = middle + residual_scale * mixture
    layer_out = result.astype(jnp.bfloat16)
    rms_stats = jnp.stack(
        [seq_rms(result, seq_count), seq_rms(attended, seq_count), seq_rms(mixture, seq_count)],
        axis=1,
    )
    grad_mix = residual_scale * grad_result
    grad_weighting = jnp.sum(picked_rows * grad_mix[:, None, :], axis=-1)
    grad_chosen = gate_probs * (
        grad_weighting - jnp.sum(gate_probs * grad_weighting, axis=-1, keepdims=True)
    )
    grad_logits = jnp.sum(jnp.where(route_hot, grad_chosen[:, :, None], 0.0), axis=1).astype(
        jnp.bfloat16
    )
    router_grad = jnp.dot(mixer_in.T, grad_logits, preferred_element_type=jnp.float32)
    flat_gates = gate_probs.reshape(-1)
    grad_sent = jnp.where(
        filled[:, None],
        (flat_gates[source_pair][:, None] * grad_mix[source_token]).astype(jnp.bfloat16),
        zero_low,
    ).reshape(cap_slots, experts, model_width)
    grad_received = to_owners(grad_sent).reshape(slot_count, model_width)
    grad_active = jnp.dot(grad_received, down_matrix.T, preferred_element_type=jnp.float32)
    down_grad = jnp.dot(active.T, grad_received, preferred_element_type=jnp.float32)
    grad_gate_pre = (
        grad_active * up_pre * sigmoid_gate * (1.0 + gate_pre * (1.0 - sigmoid_gate))
    ).astype(jnp.bfloat16)
    grad_up_pre = (grad_active * silu_gate).astype(jnp.bfloat16)
    gate_grad = jnp.dot(received.T, grad_gate_pre, preferred_element_type=jnp.float32)
    up_grad = jnp.dot(received.T, grad_up_pre, preferred_element_type=jnp.float32)

    def input_term(row_start, row_count):
        return jnp.dot(grad_gate_pre, gate_matrix.T, preferred_element_type=jnp.float32) + jnp.dot(
            grad_up_pre, up_matrix.T, preferred_element_type=jnp.float32
        )

    grad_rows = from_owners(input_term, slot_count, experts, model_width)
    grad_mixer = jnp.dot(
        grad_logits, router_weight.T, preferred_element_type=jnp.float32
    ) + jnp.sum(
        grad_rows[slot_index].reshape(tok_rows, TOP, model_width), axis=1, dtype=jnp.float32
    )
    weighted_second = grad_mixer * gain_second
    second_grad = jnp.sum(grad_mixer * middle * inv_second, axis=0)
    grad_middle = (
        grad_result
        + inv_second * weighted_second
        - middle * inv_second**3 * jnp.mean(middle * weighted_second, axis=-1, keepdims=True)
    )
    grad_attended = (residual_scale * grad_middle).astype(jnp.bfloat16)
    out_grad_t = jnp.dot(grad_attended.T, mixed_low, preferred_element_type=jnp.float32)
    grad_mixed = (
        jnp.dot(grad_attended, out_weight.T, preferred_element_type=jnp.float32)
        .astype(jnp.bfloat16)
        .reshape(tok_rows, key_heads, group_width, HEAD_FEATURES)
    )
    grad_query_seq, grad_key_seq, grad_value_seq = attention_backward(
        query_rows, rotated_keys, value_rows, norms_seq, grad_mixed
    )
    grad_queries_rot = grad_query_seq.reshape(tok_rows, query_heads, HEAD_FEATURES)
    grad_query_pre = (
        rotary_back(grad_queries_rot, cosine_rows, sine_rows)
        .astype(jnp.bfloat16)
        .reshape(tok_rows, query_heads * HEAD_FEATURES)
    )
    grad_key_pre = (
        rotary_back(grad_key_seq, cosine_rows, sine_rows)
        .astype(jnp.bfloat16)
        .reshape(tok_rows, key_heads * HEAD_FEATURES)
    )
    grad_values_low = grad_value_seq.astype(jnp.bfloat16).reshape(
        tok_rows, key_heads * HEAD_FEATURES
    )
    query_grad = jnp.dot(normalized_input.T, grad_query_pre, preferred_element_type=jnp.float32)
    key_grad = jnp.dot(normalized_input.T, grad_key_pre, preferred_element_type=jnp.float32)
    value_grad = jnp.dot(normalized_input.T, grad_values_low, preferred_element_type=jnp.float32)
    normed_term = jnp.dot(grad_query_pre, query_weight.T, preferred_element_type=jnp.float32)
    normed_term = normed_term + jnp.dot(
        grad_key_pre, key_matrix.T, preferred_element_type=jnp.float32
    )
    normed_term = normed_term + jnp.dot(
        grad_values_low, value_matrix.T, preferred_element_type=jnp.float32
    )
    grad_normed = lax.psum(normed_term.astype(jnp.bfloat16), "tp").astype(jnp.float32)
    weighted_first = grad_normed * gain_first
    first_grad = jnp.sum(grad_normed * stream_f * inv_first, axis=0)
    grad_stream = (
        grad_middle
        + inv_first * weighted_first
        - stream_f * inv_first**3 * jnp.mean(stream_f * weighted_first, axis=-1, keepdims=True)
    )
    reduced = (
        lax.psum_scatter(query_grad, "ep", scatter_dimension=0, tiled=True),
        lax.psum_scatter(key_grad, "ep", scatter_dimension=0, tiled=True),
        lax.psum_scatter(value_grad, "ep", scatter_dimension=0, tiled=True),
        lax.psum_scatter(out_grad_t, "ep", scatter_dimension=0, tiled=True),
        lax.psum_scatter(router_grad, "ep", scatter_dimension=0, tiled=True),
        lax.psum_scatter(first_grad, "ep", scatter_dimension=0, tiled=True),
        lax.psum_scatter(second_grad, "ep", scatter_dimension=0, tiled=True),
    )
    return (
        layer_out,
        grad_stream,
        reduced[5],
        reduced[0],
        reduced[1],
        reduced[2],
        reduced[3].T,
        reduced[6],
        reduced[4],
        gate_grad[None],
        up_grad[None],
        down_grad[None],
        rms_stats,
    )


def swap_cores(value):
    return lax.ppermute(value, "tp", [(0, 1), (1, 0)])


def exchange(value, bits):
    count = lax.axis_size("ep")
    return lax.ppermute(value, "ep", [(i, i ^ bits) for i in range(count)])


MESH = pl.DeviceIdType.MESH
PLANE = 4
LINES = 4


def flip(place, unit):
    return place + unit * (1 - 2 * lax.rem(lax.div(place, unit), 2))


def flip_line(place, step):
    if step % 2:
        place = flip(place, PLANE)
    if step // 2:
        place = flip(place, 2 * PLANE)
    return place


def matmul(left, right):
    return jnp.dot(left, right, preferred_element_type=jnp.float32)


def matmul_nt(left, right):
    return lax.dot_general(
        left, right, (((1,), (1,)), ((), ())), preferred_element_type=jnp.float32
    )


def matmul_tn(left, right):
    return lax.dot_general(
        left, right, (((0,), (0,)), ((), ())), preferred_element_type=jnp.float32
    )


def expert_kernel(*refs):
    tiles = 2 * PLANE
    refs = list(refs)

    def take(count):
        taken = refs[:count]
        del refs[:count]
        return taken

    mixer_parts, cot_parts, prob_parts = take(LINES), take(LINES), take(LINES)
    gate_parts, up_parts, down_parts = take(tiles), take(tiles), take(tiles)
    out_parts = take(LINES)
    grow_sum, weighting_sum, gate_out, up_out, down_out = take(5)
    mixer, cots, probs, gates, ups, downs = take(6)
    scaled, ggate, gup, grow, grow_in, outs, weighting, weighting_in = take(8)
    load_sem, tile_sem, store_sem, tile_out_sem = take(4)
    grow_send, grow_recv, weighting_send, weighting_recv = take(4)
    half, width = mixer_parts[0].shape
    rows = LINES * half
    span = gates.shape[2]
    column_tiles = width // span

    place = lax.axis_index("ep")
    core = lax.axis_index("tp")
    partners = [flip_line(place, step) for step in range(LINES)]
    barrier = pltpu.get_barrier_semaphore()
    for step in range(1, LINES):
        pl.semaphore_signal(
            barrier, inc=1, device_id=(partners[step], core), device_id_type=MESH
        )

    loads = []
    for step in range(LINES):
        part = pl.ds(step * half, half)
        for kind, (source, target) in enumerate(
            ((mixer_parts, mixer), (cot_parts, cots), (prob_parts, probs))
        ):
            loads.append(
                pltpu.make_async_copy(source[step], target.at[part], load_sem.at[kind, step])
            )
    for copy in loads:
        copy.start()
    for tile in range(tiles):
        for kind, (source, target) in enumerate(
            ((gate_parts, gates), (up_parts, ups), (down_parts, downs))
        ):
            pltpu.make_async_copy(source[tile], target.at[tile], tile_sem.at[kind, tile]).start()
    pl.semaphore_wait(barrier, LINES - 1)
    for copy in loads:
        copy.wait()
    weighting[...] = jnp.zeros_like(weighting)
    line_place = lax.div(place, PLANE)
    lanes = lax.broadcasted_iota(jnp.int32, (rows, 128), 1)

    def hidden_tile(tile, carry):
        for kind, (source, target) in enumerate(
            ((gate_parts, gates), (up_parts, ups), (down_parts, downs))
        ):
            pltpu.make_async_copy(source[0], target.at[tile], tile_sem.at[kind, tile]).wait()
        step = lax.rem(tile, PLANE)
        owner = lax.rem(place, PLANE)
        owner = jnp.where(lax.rem(step, 2) == 1, flip(owner, 1), owner)
        owner = jnp.where(lax.div(step, 2) == 1, flip(owner, 2), owner)
        chosen = lanes == line_place * PLANE + owner
        prob = jnp.sum(jnp.where(chosen, probs[...], 0.0), axis=1, keepdims=True)
        gate_pre = matmul(mixer[...], gates[tile])
        up_pre = matmul(mixer[...], ups[tile])
        grad_raw = residual_scale * matmul_nt(cots[...], downs[tile])
        sigmoid_gate = 1.0 / (1.0 + jnp.exp(-gate_pre))
        silu_gate = gate_pre * sigmoid_gate
        active = silu_gate * up_pre
        share = jnp.sum(active * grad_raw, axis=1, keepdims=True)
        weighting[...] += jnp.where(chosen, share, 0.0)
        grad_active = prob * grad_raw
        scaled[tile] = (prob * active).astype(jnp.bfloat16)
        ggate[tile] = (
            grad_active * up_pre * sigmoid_gate * (1.0 + gate_pre * (1.0 - sigmoid_gate))
        ).astype(jnp.bfloat16)
        gup[tile] = (grad_active * silu_gate).astype(jnp.bfloat16)
        return carry

    lax.fori_loop(0, tiles, hidden_tile, 0)

    def weighting_copy(step):
        return pltpu.make_async_remote_copy(
            src_ref=weighting.at[pl.ds(step * half, half)],
            dst_ref=weighting_in.at[step - 1],
            send_sem=weighting_send.at[step - 1],
            recv_sem=weighting_recv.at[step - 1],
            device_id=(partners[step], core),
            device_id_type=MESH,
        )

    def grow_copy(step, column):
        return pltpu.make_async_remote_copy(
            src_ref=grow.at[column, pl.ds(step * half, half)],
            dst_ref=grow_in.at[step - 1, column],
            send_sem=grow_send.at[step - 1, column],
            recv_sem=grow_recv.at[step - 1, column],
            device_id=(partners[step], core),
            device_id_type=MESH,
        )

    for step in range(1, LINES):
        weighting_copy(step).start()

    def grow_tile(column, carry):
        here = pl.ds(pl.multiple_of(column * span, span), span)
        total = matmul_nt(ggate[0], gates[0, here, :])
        for tile in range(1, tiles):
            total = total + matmul_nt(ggate[tile], gates[tile, here, :])
        for tile in range(tiles):
            total = total + matmul_nt(gup[tile], ups[tile, here, :])
        grow[column] = total.astype(jnp.bfloat16)
        for step in range(1, LINES):
            grow_copy(step, column).start()
        return carry

    lax.fori_loop(0, column_tiles, grow_tile, 0)

    def out_tile(column, carry):
        here = pl.ds(pl.multiple_of(column * span, span), span)
        total = matmul(scaled[0], downs[0, :, here])
        for tile in range(1, tiles):
            total = total + matmul(scaled[tile], downs[tile, :, here])
        outs[:, here] = total.astype(jnp.bfloat16)
        return carry

    lax.fori_loop(0, column_tiles, out_tile, 0)
    stores = [
        pltpu.make_async_copy(
            outs.at[pl.ds(step * half, half)], out_parts[step], store_sem.at[step]
        )
        for step in range(LINES)
    ]
    for copy in stores:
        copy.start()

    def tile_copies(tile):
        return [
            pltpu.make_async_copy(source.at[tile], target.at[tile], tile_out_sem.at[kind, tile])
            for kind, (source, target) in enumerate(
                ((gates, gate_out), (ups, up_out), (downs, down_out))
            )
        ]

    def weight_tile(tile, carry):
        gates[tile] = matmul_tn(mixer[...], ggate[tile]).astype(jnp.bfloat16)
        ups[tile] = matmul_tn(mixer[...], gup[tile]).astype(jnp.bfloat16)
        downs[tile] = (residual_scale * matmul_tn(scaled[tile], cots[...])).astype(jnp.bfloat16)
        for copy in tile_copies(tile):
            copy.start()
        return carry

    lax.fori_loop(0, tiles, weight_tile, 0)
    for step in range(1, LINES):
        weighting_copy(step).wait()
    total = weighting[pl.ds(0, half), :]
    for step in range(1, LINES):
        total = total + weighting_in[step - 1]
    weighting_sum[...] = total
    for column in range(column_tiles):
        here = pl.ds(column * span, span)
        for step in range(1, LINES):
            grow_copy(step, column).wait()
        total = grow[column, pl.ds(0, half), :].astype(jnp.float32)
        for step in range(1, LINES):
            total = total + grow_in[step - 1, column].astype(jnp.float32)
        grow_sum[:, here] = total
    for copy in stores:
        copy.wait()

    def drain(tile, carry):
        for copy in tile_copies(tile):
            copy.wait()
        return carry

    lax.fori_loop(0, tiles, drain, 0)


def run_experts(mixer_parts, cot_parts, prob_parts, gate_parts, up_parts, down_parts):
    tiles = 2 * PLANE
    half, width = mixer_parts[0].shape
    span = gate_parts[0].shape[1]
    rows = LINES * half
    low, wide = jnp.bfloat16, jnp.float32
    shape = jax.ShapeDtypeStruct
    far = pl.BlockSpec(memory_space=pl.ANY)
    near = pl.BlockSpec(memory_space=pltpu.VMEM)
    operands = [*mixer_parts, *cot_parts, *prob_parts, *gate_parts, *up_parts, *down_parts]
    dma = pltpu.SemaphoreType.DMA
    flops = 18 * rows * width * span * tiles
    results = pl.pallas_call(
        expert_kernel,
        name="experts",
        out_shape=(
            *[shape((half, width), low)] * LINES,
            shape((half, width), wide),
            shape((half, 128), wide),
            shape((tiles, width, span), low),
            shape((tiles, width, span), low),
            shape((tiles, span, width), low),
        ),
        in_specs=[far] * len(operands),
        out_specs=(*[far] * LINES, near, near, far, far, far),
        scratch_shapes=[
            pltpu.VMEM((rows, width), low),
            pltpu.VMEM((rows, width), low),
            pltpu.VMEM((rows, 128), wide),
            pltpu.VMEM((tiles, width, span), low),
            pltpu.VMEM((tiles, width, span), low),
            pltpu.VMEM((tiles, span, width), low),
            pltpu.VMEM((tiles, rows, span), low),
            pltpu.VMEM((tiles, rows, span), low),
            pltpu.VMEM((tiles, rows, span), low),
            pltpu.VMEM((width // span, rows, span), low),
            pltpu.VMEM((LINES - 1, width // span, half, span), low),
            pltpu.VMEM((rows, width), low),
            pltpu.VMEM((rows, 128), wide),
            pltpu.VMEM((LINES - 1, half, 128), wide),
            dma((3, LINES)),
            dma((3, tiles)),
            dma((LINES,)),
            dma((3, tiles)),
            dma((LINES - 1, width // span)),
            dma((LINES - 1, width // span)),
            dma((LINES - 1,)),
            dma((LINES - 1,)),
        ],
        compiler_params=pltpu.CompilerParams(
            collective_id=0, has_side_effects=True, vmem_limit_bytes=63 << 20
        ),
        cost_estimate=pl.CostEstimate(
            flops=flops, bytes_accessed=12 * width * span * tiles, transcendentals=0
        ),
    )(*operands)
    return results[:LINES], *results[LINES:]


def scatter_kernel(widths, *refs):
    count = len(widths)
    sources, results = refs[:count], refs[count : 2 * count]
    scratch = refs[2 * count :]
    per = 7
    place = lax.axis_index("ep")
    core = lax.axis_index("tp")
    line_place = lax.div(place, PLANE)
    slab = results[0].shape[0]
    bits = [lax.rem(place, 2), lax.rem(lax.div(place, 2), 2)]
    neighbours = [flip(place, 1), flip(place, 2)]
    partners = [flip_line(place, step) for step in range(LINES)]

    barrier = pltpu.get_barrier_semaphore()
    for other in neighbours + partners[1:]:
        pl.semaphore_signal(barrier, inc=1, device_id=(other, core), device_id_type=MESH)

    order = [3, 2, 1, 0]

    def rows_of(step, first, second_same, first_same):
        line = lax.div(partners[step], PLANE)
        second = 1 - first
        first_bit = bits[first] if first_same else 1 - bits[first]
        second_bit = bits[second] if second_same else 1 - bits[second]
        index = line * PLANE + first_bit * (1 << first) + second_bit * (1 << second)
        return pl.ds(pl.multiple_of(index * slab, slab), slab)

    def remote(source, target, sems, index, other):
        return pltpu.make_async_remote_copy(
            src_ref=source,
            dst_ref=target,
            send_sem=sems[0].at[index],
            recv_sem=sems[1].at[index],
            device_id=(other, core),
            device_id_type=MESH,
        )

    plans = []
    for number in range(count):
        own, first_in, second_out, second_in, line_out, line_in, sems = scratch[
            per * number : per * number + per
        ]
        plans.append((sources[number], own, first_in, second_out, second_in, line_out, line_in, sems))

    def first_copy(number, step, same):
        source, own, first_in, _, _, _, _, sems = plans[number]
        first = number % 2
        index = step * 2 + same
        return remote(
            source.at[rows_of(step, first, same, False)],
            first_in.at[index],
            (sems.at[0], sems.at[1]),
            index,
            neighbours[first],
        )

    def own_copy(number, step, same):
        source, own, _, _, _, _, _, sems = plans[number]
        index = step * 2 + same
        return pltpu.make_async_copy(
            source.at[rows_of(step, number % 2, same, True)], own.at[index], sems.at[2, index]
        )

    def second_copy(number, step):
        _, _, _, second_out, second_in, _, _, sems = plans[number]
        return remote(
            second_out.at[step],
            second_in.at[step],
            (sems.at[3], sems.at[4]),
            step,
            neighbours[1 - number % 2],
        )

    def line_copy(number, step):
        _, _, _, _, _, line_out, line_in, sems = plans[number]
        return remote(
            line_out.at[step],
            line_in.at[step],
            (sems.at[5], sems.at[6]),
            step,
            partners[step],
        )

    for step in order:
        for same in (0, 1):
            for number in range(count):
                own_copy(number, step, same).start()
    pl.semaphore_wait(barrier, 2 + LINES - 1)
    for step in order:
        for same in (0, 1):
            for number in range(count):
                first_copy(number, step, same).start()

    def add_first(number, step, same):
        _, own, first_in, _, _, _, _, _ = plans[number]
        own_copy(number, step, same).wait()
        first_copy(number, step, same).wait()
        index = step * 2 + same
        return own[index].astype(jnp.float32) + first_in[index].astype(jnp.float32)

    def finish_first(step):
        for number in range(count):
            second_out = plans[number][3]
            second_out[step] = add_first(number, step, 0).astype(jnp.bfloat16)
            second_copy(number, step).start()

    def finish_second(step):
        for number in range(count):
            _, own, _, _, second_in, line_out, _, _ = plans[number]
            total = add_first(number, step, 1)
            second_copy(number, step).wait()
            total = total + second_in[step].astype(jnp.float32)
            if step:
                line_out[step] = total.astype(jnp.bfloat16)
                line_copy(number, step).start()
            else:
                results[number][...] = total

    for position, step in enumerate(order):
        finish_first(step)
        if position:
            finish_second(order[position - 1])
    finish_second(order[-1])
    for step in order[:-1]:
        for number in range(count):
            line_copy(number, step).wait()
            results[number][...] += plans[number][6][step].astype(jnp.float32)


def run_scatter(values, collective_id):
    rows = values[0].shape[0]
    slab = rows // (PLANE * LINES)
    low = jnp.bfloat16
    scratch = []
    for value in values:
        width = value.shape[1]
        scratch += [
            pltpu.VMEM((2 * LINES, slab, width), low),
            pltpu.VMEM((2 * LINES, slab, width), low),
            pltpu.VMEM((LINES, slab, width), low),
            pltpu.VMEM((LINES, slab, width), low),
            pltpu.VMEM((LINES, slab, width), low),
            pltpu.VMEM((LINES, slab, width), low),
            pltpu.SemaphoreType.DMA((7, 2 * LINES)),
        ]
    far = pl.BlockSpec(memory_space=pl.ANY)
    near = pl.BlockSpec(memory_space=pltpu.VMEM)
    return pl.pallas_call(
        functools.partial(scatter_kernel, [value.shape[1] for value in values]),
        name="scatter",
        out_shape=tuple(
            jax.ShapeDtypeStruct((slab, value.shape[1]), jnp.float32) for value in values
        ),
        in_specs=[far] * len(values),
        out_specs=(near,) * len(values),
        scratch_shapes=scratch,
        compiler_params=pltpu.CompilerParams(
            collective_id=collective_id, has_side_effects=True, vmem_limit_bytes=60 << 20
        ),
    )(*values)


def dense_shards(
    stream,
    cotangent,
    attention_gain,
    query_weight,
    key_matrix,
    value_matrix,
    out_weight,
    mixture_gain,
    router_weight,
    gate_weight,
    up_weight,
    down_weight,
    routes,
):
    tok_rows, model_width = stream.shape
    experts = router_weight.shape[1]
    plane, lines = PLANE, LINES
    half = tok_rows // 2
    query_heads = query_weight.shape[1] // HEAD_FEATURES
    key_heads = key_matrix.shape[1] // HEAD_FEATURES
    group_width = query_heads // key_heads
    core = lax.axis_index("tp")
    place = lax.axis_index("ep")
    line_place = place // plane
    plane_place = place % plane

    def own_half(value):
        return lax.dynamic_slice_in_dim(value, core * half, half, 0)

    def other_half(value):
        return lax.dynamic_slice_in_dim(value, (1 - core) * half, half, 0)

    def join_halves(mine, theirs):
        return jnp.where(
            core == 0,
            jnp.concatenate([mine, theirs], axis=0),
            jnp.concatenate([theirs, mine], axis=0),
        )

    def plane_parts(weight):
        near = [weight] + [exchange(weight, d) for d in range(1, plane)]
        return near + [swap_cores(part) for part in near]

    gate_parts = plane_parts(gate_weight[0])
    up_parts = plane_parts(up_weight[0])
    down_parts = plane_parts(down_weight[0])

    def line_parts(value):
        return [value] + [exchange(value, d * plane) for d in range(1, lines)]

    cot_parts = line_parts(own_half(cotangent))

    stream_f = stream.astype(jnp.float32)
    gain_first = attention_gain.astype(jnp.float32)
    gain_second = mixture_gain.astype(jnp.float32)
    cosine_rows, sine_rows = rope_tables(SEQ_LEN)
    inv_first = lax.rsqrt(jnp.mean(stream_f * stream_f, axis=-1, keepdims=True) + epsilon)
    normalized_input = (stream_f * inv_first * gain_first).astype(jnp.bfloat16)
    query_pre = jnp.dot(normalized_input, query_weight, preferred_element_type=jnp.float32).reshape(
        tok_rows, query_heads, HEAD_FEATURES
    )
    key_pre = jnp.dot(normalized_input, key_matrix, preferred_element_type=jnp.float32).reshape(
        tok_rows, key_heads, HEAD_FEATURES
    )
    query_rows = (
        apply_rotation(query_pre, cosine_rows, sine_rows)
        .astype(jnp.bfloat16)
        .reshape(tok_rows, key_heads, group_width, HEAD_FEATURES)
    )
    rotated_keys = apply_rotation(key_pre, cosine_rows, sine_rows).astype(jnp.bfloat16)
    value_rows = (
        jnp.dot(normalized_input, value_matrix, preferred_element_type=jnp.float32)
        .astype(jnp.bfloat16)
        .reshape(tok_rows, key_heads, HEAD_FEATURES)
    )
    mixed_seq, norms_seq = attention_forward(query_rows, rotated_keys, value_rows)
    mixed_low = mixed_seq.reshape(tok_rows, query_heads * HEAD_FEATURES).astype(jnp.bfloat16)
    attended_part = jnp.dot(mixed_low, out_weight, preferred_element_type=jnp.float32).astype(
        jnp.bfloat16
    )
    attended = own_half(attended_part).astype(jnp.float32) + swap_cores(
        other_half(attended_part)
    ).astype(jnp.float32)
    middle = own_half(stream).astype(jnp.float32) + residual_scale * attended
    inv_second = lax.rsqrt(jnp.mean(middle * middle, axis=-1, keepdims=True) + epsilon)
    mixer_in = (middle * inv_second * gain_second).astype(jnp.bfloat16)
    logits = jnp.dot(mixer_in, router_weight, preferred_element_type=jnp.float32)
    expert_ids = jnp.arange(experts, dtype=jnp.int32)
    routed = jnp.any(own_half(routes)[:, :, None] == expert_ids[None, None, :], axis=1)
    largest = jnp.max(jnp.where(routed, logits, masked_score), axis=-1, keepdims=True)
    gate_exp = jnp.where(routed, jnp.exp(jnp.minimum(logits - largest, 0.0)), 0.0)
    gate_probs = gate_exp / jnp.sum(gate_exp, axis=-1, keepdims=True)

    mixer_parts = line_parts(mixer_in)
    prob_parts = line_parts(jnp.pad(gate_probs, ((0, 0), (0, 128 - experts))))
    out_parts, grad_mixer_rows, weighting_sum, gate_grad, up_grad, down_grad = run_experts(
        mixer_parts, cot_parts, prob_parts, gate_parts, up_parts, down_parts
    )
    grad_weighting = weighting_sum[:, :experts]
    mixture = out_parts[0].astype(jnp.float32)
    for d in range(1, lines):
        mixture = mixture + exchange(out_parts[d], d * plane).astype(jnp.float32)

    def plane_sum(low):
        both = low[:plane].astype(jnp.float32) + swap_cores(low[plane:]).astype(jnp.float32)
        total = both[0]
        for d in range(1, plane):
            total = total + exchange(both[d].astype(jnp.bfloat16), d).astype(jnp.float32)
        return total

    gate_grad = plane_sum(gate_grad)
    up_grad = plane_sum(up_grad)
    down_grad = plane_sum(down_grad)

    result = middle + residual_scale * mixture
    result_low = result.astype(jnp.bfloat16)
    layer_out = join_halves(result_low, swap_cores(result_low))
    squares = jnp.stack([jnp.sum(v * v) for v in (result, attended, mixture)])
    rms_stats = jnp.sqrt((squares + swap_cores(squares)) / (tok_rows * model_width))[None, :]
    grad_chosen = gate_probs * (
        grad_weighting - jnp.sum(gate_probs * grad_weighting, axis=-1, keepdims=True)
    )
    grad_logits = grad_chosen.astype(jnp.bfloat16)
    router_grad = jnp.dot(mixer_in.T, grad_logits, preferred_element_type=jnp.float32)
    grad_mixer = (
        jnp.dot(grad_logits, router_weight.T, preferred_element_type=jnp.float32) + grad_mixer_rows
    )
    weighted_second = grad_mixer * gain_second
    second_grad = jnp.sum(grad_mixer * middle * inv_second, axis=0)
    grad_middle = (
        own_half(cotangent).astype(jnp.float32)
        + inv_second * weighted_second
        - middle * inv_second**3 * jnp.mean(middle * weighted_second, axis=-1, keepdims=True)
    )
    grad_middle_low = grad_middle.astype(jnp.bfloat16)
    grad_middle_all = join_halves(grad_middle_low, swap_cores(grad_middle_low)).astype(jnp.float32)
    grad_attended = (residual_scale * grad_middle_all).astype(jnp.bfloat16)
    out_grad_t = jnp.dot(grad_attended.T, mixed_low, preferred_element_type=jnp.float32)
    grad_mixed = (
        jnp.dot(grad_attended, out_weight.T, preferred_element_type=jnp.float32)
        .astype(jnp.bfloat16)
        .reshape(tok_rows, key_heads, group_width, HEAD_FEATURES)
    )
    grad_query_seq, grad_key_seq, grad_value_seq = attention_backward(
        query_rows, rotated_keys, value_rows, norms_seq, grad_mixed
    )
    grad_queries_rot = grad_query_seq.reshape(tok_rows, query_heads, HEAD_FEATURES)
    grad_query_pre = (
        rotary_back(grad_queries_rot, cosine_rows, sine_rows)
        .astype(jnp.bfloat16)
        .reshape(tok_rows, query_heads * HEAD_FEATURES)
    )
    grad_key_pre = (
        rotary_back(grad_key_seq, cosine_rows, sine_rows)
        .astype(jnp.bfloat16)
        .reshape(tok_rows, key_heads * HEAD_FEATURES)
    )
    grad_values_low = grad_value_seq.astype(jnp.bfloat16).reshape(
        tok_rows, key_heads * HEAD_FEATURES
    )
    query_grad = jnp.dot(normalized_input.T, grad_query_pre, preferred_element_type=jnp.float32)
    key_grad = jnp.dot(normalized_input.T, grad_key_pre, preferred_element_type=jnp.float32)
    value_grad = jnp.dot(normalized_input.T, grad_values_low, preferred_element_type=jnp.float32)
    normed_term = jnp.dot(grad_query_pre, query_weight.T, preferred_element_type=jnp.float32)
    normed_term = normed_term + jnp.dot(
        grad_key_pre, key_matrix.T, preferred_element_type=jnp.float32
    )
    normed_term = normed_term + jnp.dot(
        grad_values_low, value_matrix.T, preferred_element_type=jnp.float32
    )
    normed_low = normed_term.astype(jnp.bfloat16)
    grad_normed = normed_low.astype(jnp.float32) + swap_cores(normed_low).astype(jnp.float32)
    weighted_first = grad_normed * gain_first
    first_grad = jnp.sum(grad_normed * stream_f * inv_first, axis=0)
    grad_stream = (
        grad_middle_all
        + inv_first * weighted_first
        - stream_f * inv_first**3 * jnp.mean(stream_f * weighted_first, axis=-1, keepdims=True)
    )
    small = jnp.concatenate(
        [router_grad, second_grad[:, None], 0.5 * first_grad[:, None]], axis=1
    )
    small = small + swap_cores(small)
    small = jnp.pad(small, ((0, 0), (0, 128 - small.shape[1])))
    low = [
        value.astype(jnp.bfloat16)
        for value in (out_grad_t, key_grad, query_grad, value_grad, small)
    ]
    first_part, second_part = run_scatter(
        [jnp.concatenate(low[:2], axis=1), jnp.concatenate(low[2:], axis=1)], 1
    )
    query_width = query_weight.shape[1]
    key_width = key_matrix.shape[1]
    small_part = second_part[:, query_width + key_width :]
    return (
        layer_out,
        grad_stream,
        small_part[:, experts + 1],
        second_part[:, :query_width],
        first_part[:, query_width:],
        second_part[:, query_width : query_width + key_width],
        first_part[:, :query_width].T,
        small_part[:, experts],
        small_part[:, :experts],
        gate_grad[None],
        up_grad[None],
        down_grad[None],
        rms_stats,
    )


def solution(mesh):
    in_specs = (
        P("ep", None),
        P("ep", None),
        P(),
        P(None, "tp"),
        P(None, "tp"),
        P(None, "tp"),
        P("tp", None),
        P(),
        P(),
        P("ep", None, "tp"),
        P("ep", None, "tp"),
        P("ep", "tp", None),
        P("ep", None),
    )
    out_specs = (
        P("ep", None),
        P("ep", None),
        P("ep"),
        P("ep", "tp"),
        P("ep", "tp"),
        P("ep", "tp"),
        P("tp", "ep"),
        P("ep"),
        P("ep", None),
        P("ep", None, "tp"),
        P("ep", None, "tp"),
        P("ep", "tp", None),
        P("ep", None),
    )
    ep_size = mesh.shape["ep"]
    dense = mesh.shape["tp"] == 2 and ep_size <= 2 * TOP and ep_size == 16
    shards = dense_shards if dense else routed_shards
    return jax.shard_map(shards, mesh=mesh, in_specs=in_specs, out_specs=out_specs, check_vma=False)
```

```python
import functools

import jax
import jax.numpy as jnp
from jax import lax
from jax.experimental import pallas as pl
from jax.experimental.pallas import tpu as pltpu
from jax.sharding import PartitionSpec as P

HEAD_FEATURES = 64
TOP = 8
SEQ_LEN = 512


epsilon = 1e-06
score_scale = 0.015625
residual_scale = 0.22
rope_base = 10000.0
masked_score = -1e30


def rope_tables(sequence_length):
    half_dim = HEAD_FEATURES // 2
    steps_up = jnp.arange(half_dim).astype(jnp.float32) * (2.0 / HEAD_FEATURES)
    inverse = jnp.exp(-steps_up * jnp.log(rope_base))
    places = jnp.arange(sequence_length).astype(jnp.float32)
    angles = places[:, None] * inverse[None, :]
    return (jnp.cos(angles), jnp.sin(angles))


def apply_rotation(value_rows, cosine_table, sine_values):
    half_dim = value_rows.shape[-1] // 2
    first_half = value_rows[..., :half_dim]
    second_half = value_rows[..., half_dim:]
    cos_rows = cosine_table[:, None, :]
    sin_rows = sine_values[:, None, :]
    return jnp.concatenate(
        [
            first_half * cos_rows - second_half * sin_rows,
            second_half * cos_rows + first_half * sin_rows,
        ],
        axis=-1,
    )


def rotary_back(grads_in, cosine_table, sine_values):
    half_dim = grads_in.shape[-1] // 2
    first_half = grads_in[..., :half_dim]
    second_half = grads_in[..., half_dim:]
    cos_rows = cosine_table[:, None, :]
    sin_rows = sine_values[:, None, :]
    return jnp.concatenate(
        [
            first_half * cos_rows + second_half * sin_rows,
            second_half * cos_rows - first_half * sin_rows,
        ],
        axis=-1,
    )


def block_scores(query_block, rotated_keys, row_start, block_rows, row_stop):
    scores = score_scale * jnp.einsum(
        "qhgd,khd->hgqk", query_block, rotated_keys, preferred_element_type=jnp.float32
    )
    causal = (row_start + jnp.arange(block_rows))[:, None] >= jnp.arange(row_stop)[None, :]
    return jnp.where(causal, scores, masked_score)


def attention_forward(query_rows, rotated_keys, value_rows):
    sequence_length = query_rows.shape[0]
    block_rows = min(512, sequence_length)
    scores = block_scores(query_rows, rotated_keys, 0, block_rows, block_rows)
    largest = jnp.max(scores, axis=-1, keepdims=True)
    weights_exp = jnp.exp(scores - largest)
    totals = jnp.sum(weights_exp, axis=-1, keepdims=True)
    probs_low = (weights_exp / totals).astype(jnp.bfloat16)
    outputs = jnp.einsum(
        "hgqk,khd->qhgd", probs_low, value_rows, preferred_element_type=jnp.float32
    )
    normalizers = [largest + jnp.log(totals)]
    return (outputs, normalizers)


def attention_backward(query_rows, rotated_keys, value_rows, normalizers, grad_mixed):
    sequence_length = query_rows.shape[0]
    block_rows = min(512, sequence_length)
    grad_keys = jnp.zeros(rotated_keys.shape, jnp.float32)
    grad_values = jnp.zeros(value_rows.shape, jnp.float32)
    grad_queries = []
    for block_index, row_start in enumerate(range(0, sequence_length, block_rows)):
        row_stop = row_start + block_rows
        scores = block_scores(query_rows, rotated_keys, row_start, block_rows, row_stop)
        probs = jnp.exp(scores - normalizers[block_index])
        probs_low = probs.astype(jnp.bfloat16)
        grad_probs = jnp.einsum(
            "qhgd,khd->hgqk", grad_mixed, value_rows, preferred_element_type=jnp.float32
        )
        inner = jnp.sum(probs * grad_probs, axis=-1, keepdims=True)
        grad_scores = (probs * (grad_probs - inner)).astype(jnp.bfloat16)
        grad_queries.append(
            score_scale
            * jnp.einsum(
                "hgqk,khd->qhgd", grad_scores, rotated_keys, preferred_element_type=jnp.float32
            )
        )
        grad_keys = grad_keys.at[:row_stop].add(
            score_scale
            * jnp.einsum(
                "hgqk,qhgd->khd", grad_scores, query_rows, preferred_element_type=jnp.float32
            )
        )
        grad_values = grad_values.at[:row_stop].add(
            jnp.einsum("hgqk,qhgd->khd", probs_low, grad_mixed, preferred_element_type=jnp.float32)
        )
    return (grad_queries[0], grad_keys, grad_values)


def to_owners(packed):
    return lax.all_to_all(packed, "ep", split_axis=1, concat_axis=1, tiled=True)


def back_to_tokens(rows_low, slot_count, model_width):
    returned = lax.all_to_all(rows_low, "ep", split_axis=1, concat_axis=1, tiled=True)
    joined = lax.all_gather(returned, "tp", axis=0, tiled=True)
    return joined.reshape(slot_count, model_width)


def from_owners(term_fn, slot_count, experts, model_width):
    share_rows = slot_count // lax.axis_size("tp")
    summed = lax.psum_scatter(
        term_fn(jnp.int32(0), lax.axis_size("tp") * share_rows).astype(jnp.bfloat16),
        "tp",
        scatter_dimension=0,
        tiled=True,
    ).astype(jnp.float32)
    summed = summed.astype(jnp.bfloat16).reshape(share_rows // experts, experts, model_width)
    return back_to_tokens(summed, slot_count, model_width)


def seq_rms(value_rows, seq_count):
    return jnp.sqrt(jnp.mean((value_rows * value_rows).reshape(seq_count, -1), axis=1))


def routed_shards(
    stream,
    cotangent,
    attention_gain,
    query_weight,
    key_matrix,
    value_matrix,
    out_weight,
    mixture_gain,
    router_weight,
    gate_weight,
    up_weight,
    down_weight,
    routes,
):
    tok_rows, model_width = stream.shape
    experts = router_weight.shape[1]
    cap_slots = tok_rows * TOP * 5 // (4 * experts)
    slot_count = cap_slots * experts
    query_heads = query_weight.shape[1] // HEAD_FEATURES
    key_heads = key_matrix.shape[1] // HEAD_FEATURES
    group_width = query_heads // key_heads
    seq_count = tok_rows // SEQ_LEN
    stream_f = stream.astype(jnp.float32)
    grad_result = cotangent.astype(jnp.float32)
    gain_first = attention_gain.astype(jnp.float32)
    gain_second = mixture_gain.astype(jnp.float32)
    cosine_table, sine_values = rope_tables(SEQ_LEN)
    cosine_rows = jnp.tile(cosine_table, (seq_count, 1))
    sine_rows = jnp.tile(sine_values, (seq_count, 1))
    zero_low = jnp.zeros((), jnp.bfloat16)
    inv_first = lax.rsqrt(jnp.mean(stream_f * stream_f, axis=-1, keepdims=True) + epsilon)
    normalized_input = (stream_f * inv_first * gain_first).astype(jnp.bfloat16)
    query_pre = jnp.dot(normalized_input, query_weight, preferred_element_type=jnp.float32).reshape(
        tok_rows, query_heads, HEAD_FEATURES
    )
    key_pre = jnp.dot(normalized_input, key_matrix, preferred_element_type=jnp.float32).reshape(
        tok_rows, key_heads, HEAD_FEATURES
    )
    query_rows = (
        apply_rotation(query_pre, cosine_rows, sine_rows)
        .astype(jnp.bfloat16)
        .reshape(tok_rows, key_heads, group_width, HEAD_FEATURES)
    )
    rotated_keys = apply_rotation(key_pre, cosine_rows, sine_rows).astype(jnp.bfloat16)
    value_rows = (
        jnp.dot(normalized_input, value_matrix, preferred_element_type=jnp.float32)
        .astype(jnp.bfloat16)
        .reshape(tok_rows, key_heads, HEAD_FEATURES)
    )
    mixed_seq, norms_seq = attention_forward(query_rows, rotated_keys, value_rows)
    mixed_low = mixed_seq.reshape(tok_rows, query_heads * HEAD_FEATURES).astype(jnp.bfloat16)
    attended = lax.psum(
        jnp.dot(mixed_low, out_weight, preferred_element_type=jnp.float32).astype(jnp.bfloat16),
        "tp",
    ).astype(jnp.float32)
    middle = stream_f + residual_scale * attended
    inv_second = lax.rsqrt(jnp.mean(middle * middle, axis=-1, keepdims=True) + epsilon)
    mixer_in = (middle * inv_second * gain_second).astype(jnp.bfloat16)
    logits = jnp.dot(mixer_in, router_weight, preferred_element_type=jnp.float32)
    expert_ids = jnp.arange(experts, dtype=jnp.int32)
    route_hot = routes[:, :, None] == expert_ids[None, None, :]
    chosen = jnp.sum(jnp.where(route_hot, logits[:, None, :], 0.0), axis=-1)
    chosen_exp = jnp.exp(chosen - jnp.max(chosen, axis=-1, keepdims=True))
    gate_probs = chosen_exp / jnp.sum(chosen_exp, axis=-1, keepdims=True)
    flat_routes = routes.reshape(-1)
    flat_hot = route_hot.reshape(tok_rows * TOP, experts).astype(jnp.int32)
    ranks = jnp.sum((jnp.cumsum(flat_hot, axis=0) - 1) * flat_hot, axis=1)
    slot_index = ranks * experts + flat_routes
    source_pair = (
        jnp.zeros((slot_count,), jnp.int32)
        .at[slot_index]
        .set(jnp.arange(tok_rows * TOP, dtype=jnp.int32))
    )
    filled = jnp.zeros((slot_count,), jnp.bool_).at[slot_index].set(True)
    source_token = source_pair // TOP
    sent_rows = jnp.where(filled[:, None], mixer_in[source_token], zero_low).reshape(
        cap_slots, experts, model_width
    )
    received = to_owners(sent_rows).reshape(slot_count, model_width)
    gate_matrix = gate_weight[0]
    up_matrix = up_weight[0]
    down_matrix = down_weight[0]
    gate_pre = jnp.dot(received, gate_matrix, preferred_element_type=jnp.float32)
    up_pre = jnp.dot(received, up_matrix, preferred_element_type=jnp.float32)
    sigmoid_gate = jax.nn.sigmoid(gate_pre)
    silu_gate = gate_pre * sigmoid_gate
    active = (silu_gate * up_pre).astype(jnp.bfloat16)

    def down_term(row_start, row_count):
        return jnp.dot(active, down_matrix, preferred_element_type=jnp.float32)

    expert_rows = from_owners(down_term, slot_count, experts, model_width)
    picked_rows = expert_rows[slot_index].reshape(tok_rows, TOP, model_width)
    mixture = jnp.sum(gate_probs[:, :, None] * picked_rows, axis=1)
    result = middle + residual_scale * mixture
    layer_out = result.astype(jnp.bfloat16)
    rms_stats = jnp.stack(
        [seq_rms(result, seq_count), seq_rms(attended, seq_count), seq_rms(mixture, seq_count)],
        axis=1,
    )
    grad_mix = residual_scale * grad_result
    grad_weighting = jnp.sum(picked_rows * grad_mix[:, None, :], axis=-1)
    grad_chosen = gate_probs * (
        grad_weighting - jnp.sum(gate_probs * grad_weighting, axis=-1, keepdims=True)
    )
    grad_logits = jnp.sum(jnp.where(route_hot, grad_chosen[:, :, None], 0.0), axis=1).astype(
        jnp.bfloat16
    )
    router_grad = jnp.dot(mixer_in.T, grad_logits, preferred_element_type=jnp.float32)
    flat_gates = gate_probs.reshape(-1)
    grad_sent = jnp.where(
        filled[:, None],
        (flat_gates[source_pair][:, None] * grad_mix[source_token]).astype(jnp.bfloat16),
        zero_low,
    ).reshape(cap_slots, experts, model_width)
    grad_received = to_owners(grad_sent).reshape(slot_count, model_width)
    grad_active = jnp.dot(grad_received, down_matrix.T, preferred_element_type=jnp.float32)
    down_grad = jnp.dot(active.T, grad_received, preferred_element_type=jnp.float32)
    grad_gate_pre = (
        grad_active * up_pre * sigmoid_gate * (1.0 + gate_pre * (1.0 - sigmoid_gate))
    ).astype(jnp.bfloat16)
    grad_up_pre = (grad_active * silu_gate).astype(jnp.bfloat16)
    gate_grad = jnp.dot(received.T, grad_gate_pre, preferred_element_type=jnp.float32)
    up_grad = jnp.dot(received.T, grad_up_pre, preferred_element_type=jnp.float32)

    def input_term(row_start, row_count):
        return jnp.dot(grad_gate_pre, gate_matrix.T, preferred_element_type=jnp.float32) + jnp.dot(
            grad_up_pre, up_matrix.T, preferred_element_type=jnp.float32
        )

    grad_rows = from_owners(input_term, slot_count, experts, model_width)
    grad_mixer = jnp.dot(
        grad_logits, router_weight.T, preferred_element_type=jnp.float32
    ) + jnp.sum(
        grad_rows[slot_index].reshape(tok_rows, TOP, model_width), axis=1, dtype=jnp.float32
    )
    weighted_second = grad_mixer * gain_second
    second_grad = jnp.sum(grad_mixer * middle * inv_second, axis=0)
    grad_middle = (
        grad_result
        + inv_second * weighted_second
        - middle * inv_second**3 * jnp.mean(middle * weighted_second, axis=-1, keepdims=True)
    )
    grad_attended = (residual_scale * grad_middle).astype(jnp.bfloat16)
    out_grad_t = jnp.dot(grad_attended.T, mixed_low, preferred_element_type=jnp.float32)
    grad_mixed = (
        jnp.dot(grad_attended, out_weight.T, preferred_element_type=jnp.float32)
        .astype(jnp.bfloat16)
        .reshape(tok_rows, key_heads, group_width, HEAD_FEATURES)
    )
    grad_query_seq, grad_key_seq, grad_value_seq = attention_backward(
        query_rows, rotated_keys, value_rows, norms_seq, grad_mixed
    )
    grad_queries_rot = grad_query_seq.reshape(tok_rows, query_heads, HEAD_FEATURES)
    grad_query_pre = (
        rotary_back(grad_queries_rot, cosine_rows, sine_rows)
        .astype(jnp.bfloat16)
        .reshape(tok_rows, query_heads * HEAD_FEATURES)
    )
    grad_key_pre = (
        rotary_back(grad_key_seq, cosine_rows, sine_rows)
        .astype(jnp.bfloat16)
        .reshape(tok_rows, key_heads * HEAD_FEATURES)
    )
    grad_values_low = grad_value_seq.astype(jnp.bfloat16).reshape(
        tok_rows, key_heads * HEAD_FEATURES
    )
    query_grad = jnp.dot(normalized_input.T, grad_query_pre, preferred_element_type=jnp.float32)
    key_grad = jnp.dot(normalized_input.T, grad_key_pre, preferred_element_type=jnp.float32)
    value_grad = jnp.dot(normalized_input.T, grad_values_low, preferred_element_type=jnp.float32)
    normed_term = jnp.dot(grad_query_pre, query_weight.T, preferred_element_type=jnp.float32)
    normed_term = normed_term + jnp.dot(
        grad_key_pre, key_matrix.T, preferred_element_type=jnp.float32
    )
    normed_term = normed_term + jnp.dot(
        grad_values_low, value_matrix.T, preferred_element_type=jnp.float32
    )
    grad_normed = lax.psum(normed_term.astype(jnp.bfloat16), "tp").astype(jnp.float32)
    weighted_first = grad_normed * gain_first
    first_grad = jnp.sum(grad_normed * stream_f * inv_first, axis=0)
    grad_stream = (
        grad_middle
        + inv_first * weighted_first
        - stream_f * inv_first**3 * jnp.mean(stream_f * weighted_first, axis=-1, keepdims=True)
    )
    reduced = (
        lax.psum_scatter(query_grad, "ep", scatter_dimension=0, tiled=True),
        lax.psum_scatter(key_grad, "ep", scatter_dimension=0, tiled=True),
        lax.psum_scatter(value_grad, "ep", scatter_dimension=0, tiled=True),
        lax.psum_scatter(out_grad_t, "ep", scatter_dimension=0, tiled=True),
        lax.psum_scatter(router_grad, "ep", scatter_dimension=0, tiled=True),
        lax.psum_scatter(first_grad, "ep", scatter_dimension=0, tiled=True),
        lax.psum_scatter(second_grad, "ep", scatter_dimension=0, tiled=True),
    )
    return (
        layer_out,
        grad_stream,
        reduced[5],
        reduced[0],
        reduced[1],
        reduced[2],
        reduced[3].T,
        reduced[6],
        reduced[4],
        gate_grad[None],
        up_grad[None],
        down_grad[None],
        rms_stats,
    )


MESH = pl.DeviceIdType.MESH
PLANE = 4
LINES = 4


def flip(place, unit):
    return place + unit * (1 - 2 * lax.rem(lax.div(place, unit), 2))


def flip_line(place, step):
    if step % 2:
        place = flip(place, PLANE)
    if step // 2:
        place = flip(place, 2 * PLANE)
    return place


def matmul(left, right):
    return jnp.dot(left, right, preferred_element_type=jnp.float32)


def matmul_nt(left, right):
    return lax.dot_general(
        left, right, (((1,), (1,)), ((), ())), preferred_element_type=jnp.float32
    )


def matmul_tn(left, right):
    return lax.dot_general(
        left, right, (((0,), (0,)), ((), ())), preferred_element_type=jnp.float32
    )


def lane_halves(value):
    lane = lax.broadcasted_iota(jnp.int32, value.shape, 1)
    low = jnp.where(lane < HEAD_FEATURES, value, 0.0)
    high = jnp.where(lane < HEAD_FEATURES, 0.0, value)
    return low, high


def partner_lanes(value):
    width = value.shape[1]
    quarter = HEAD_FEATURES // 2
    lane = lax.broadcasted_iota(jnp.int32, value.shape, 1)
    ahead = pltpu.roll(value, width - quarter, 1)
    behind = pltpu.roll(value, quarter, 1)
    return jnp.where(lax.rem(lane, HEAD_FEATURES) < quarter, ahead, behind)


def causal_scores(query_block, key_block, row_start):
    scores = score_scale * matmul_nt(query_block, key_block)
    row = lax.broadcasted_iota(jnp.int32, scores.shape, 0) + row_start
    column = lax.broadcasted_iota(jnp.int32, scores.shape, 1)
    return jnp.where(row >= column, scores, masked_score)


def store_slots(slots, values):
    for group in range(values.shape[1] // HEAD_FEATURES):
        pair = group // 2
        low, high = lane_halves(values[:, pair * 128 : pair * 128 + 128])
        if group % 2:
            low = pltpu.roll(high, HEAD_FEATURES, 1)
        else:
            high = pltpu.roll(low, HEAD_FEATURES, 1)
        slots[2 * group] = low.astype(jnp.bfloat16)
        slots[2 * group + 1] = high.astype(jnp.bfloat16)


def front_kernel(*refs):
    refs = list(refs)

    def take(count):
        taken = refs[:count]
        del refs[:count]
        return taken

    stream, cotangent, gain_first, gain_second, query_weight, key_weight = take(6)
    value_weight, out_weight, router, routes, cosine, sine = take(6)
    weights = take(3)
    weights_all = take(3)
    mixer_all, cot_all, probs_all = take(3)
    normed, queries, keys, values, mixed, attended = take(6)
    stream_v, query_v, key_v, value_v, out_v = take(5)
    key_slots, value_slots, part_send, part_recv, mixer, probs = take(6)
    load_sem, own_sem, weight_send, weight_recv = take(4)
    relay_send, relay_recv, probs_send, probs_recv, part_sem = take(5)
    tokens, width = stream_v.shape
    half = tokens // 2

    place = lax.axis_index("ep")
    core = lax.axis_index("tp")
    line = lax.div(place, PLANE)
    across = [flip(place, 1), flip(place, 2)]
    partners = [flip_line(place, step) for step in range(LINES)]
    own_rows = pl.ds(pl.multiple_of(core * half, half), half)
    other_rows = pl.ds(pl.multiple_of((1 - core) * half, half), half)

    barrier = pltpu.get_barrier_semaphore()
    for other in across + partners[1:]:
        pl.semaphore_signal(barrier, inc=1, device_id=(other, core), device_id_type=MESH)
    pl.semaphore_signal(barrier, inc=1, device_id=(place, 1 - core), device_id_type=MESH)

    loads = [
        pltpu.make_async_copy(source, target, load_sem.at[index])
        for index, (source, target) in enumerate(
            (
                (stream, stream_v),
                (query_weight, query_v),
                (key_weight, key_v),
                (value_weight, value_v),
                (out_weight, out_v),
            )
        )
    ]
    for copy in loads:
        copy.start()
    pl.semaphore_wait(barrier, LINES + 2)

    def send(source, target, sems, index, device):
        return pltpu.make_async_remote_copy(
            src_ref=source,
            dst_ref=target,
            send_sem=sems[0].at[index],
            recv_sem=sems[1].at[index],
            device_id=device,
            device_id_type=MESH,
        )

    sibling = (place, 1 - core)
    sems = (weight_send, weight_recv)

    def direct(kind, axis):
        return send(
            weights[kind],
            weights_all[kind].at[axis + 1],
            sems,
            (kind, axis),
            (across[axis], core),
        )

    def to_sibling(kind, slot):
        source = weights[kind] if slot == 0 else weights_all[kind].at[slot]
        return send(source, weights_all[kind].at[PLANE + slot], sems, (kind, 2 + slot), sibling)

    def onward(kind, axis):
        gathered = weights_all[kind]
        source, target = gathered.at[2 - axis], gathered.at[3]
        if kind == 1:
            part = pl.ds(axis * (width // 2), width // 2)
            source, target = gathered.at[2 - axis, part], gathered.at[3, part]
        return send(source, target, sems, (kind, 6 + axis), (across[axis], core))

    onwards = {0: (0,), 1: (0, 1), 2: (1,)}

    def relay(array, hop, downward):
        gathered = (cot_all, mixer_all)[array]
        shift = -1 if downward else 1
        block = jnp.clip(line - shift * hop, 0, LINES - 1)
        if hop == 0:
            source = mixer if array else cotangent.at[own_rows]
        else:
            source = gathered.at[block]
        return send(
            source,
            gathered.at[block],
            (relay_send, relay_recv),
            (array, downward, hop),
            (place + shift * PLANE, core),
        )

    def relay_sends(hop, downward):
        if downward:
            return jnp.logical_and(line > 0, line + hop < LINES)
        return jnp.logical_and(line < LINES - 1, line - hop >= 0)

    def relay_receives(hop, downward):
        if downward:
            return line + 1 + hop < LINES
        return line - 1 - hop >= 0

    def start_relay(array, hop):
        for downward in (0, 1):

            @pl.when(relay_sends(hop, downward))
            def _():
                relay(array, hop, downward).start()

    def receive_relay(array, hop):
        for downward in (0, 1):

            @pl.when(relay_receives(hop, downward))
            def _():
                relay(array, hop, downward).wait_recv()

    def finish_relay(array, hop):
        for downward in (0, 1):

            @pl.when(relay_sends(hop, downward))
            def _():
                relay(array, hop, downward).wait_send()

    for kind in range(3):
        for axis in (0, 1):
            direct(kind, axis).start()
    start_relay(0, 0)
    own_copies = [
        pltpu.make_async_copy(weights[kind], weights_all[kind].at[0], own_sem.at[kind])
        for kind in range(3)
    ]
    own_copies.append(
        pltpu.make_async_copy(cotangent.at[own_rows], cot_all.at[line], own_sem.at[3])
    )
    for kind in range(3):
        to_sibling(kind, 0).start()
    for copy in own_copies:
        copy.start()

    loads[0].wait()
    stream_f = stream_v[...].astype(jnp.float32)
    inverse = lax.rsqrt(jnp.mean(stream_f * stream_f, axis=-1, keepdims=True) + epsilon)
    normed[...] = (stream_f * inverse * gain_first[...]).astype(jnp.bfloat16)
    for copy in loads[1:4]:
        copy.wait()
    span = cosine.shape[1]

    def rotated(pre):
        return pre * cosine[...] + partner_lanes(pre) * sine[...]

    for start in range(0, query_v.shape[1], span):
        here = slice(start, start + span)
        queries[:, here] = rotated(matmul(normed[...], query_v[:, here])).astype(jnp.bfloat16)
    key_rows = rotated(matmul(normed[...], key_v[...])).astype(jnp.bfloat16)
    keys[...] = key_rows
    store_slots(key_slots, key_rows.astype(jnp.float32))
    value_rows = matmul(normed[...], value_v[...]).astype(jnp.bfloat16)
    values[...] = value_rows
    store_slots(value_slots, value_rows.astype(jnp.float32))
    group = query_v.shape[1] // key_v.shape[1]
    blocks = 2
    block_rows = tokens // blocks

    def head_pair(pair, carry):
        here = pl.ds(pl.multiple_of(pair * 128, 128), 128)
        for block in range(blocks):
            rows = slice(block * block_rows, (block + 1) * block_rows)
            reach = (block + 1) * block_rows
            total = jnp.zeros((block_rows, 128), jnp.float32)
            for parity in range(2):
                slot = 2 * lax.div(2 * pair + parity, group) + parity
                scores = causal_scores(
                    queries[rows, here], key_slots[slot, :reach, :], block * block_rows
                )
                weight = jnp.exp(scores - jnp.max(scores, axis=-1, keepdims=True))
                weight = weight / jnp.sum(weight, axis=-1, keepdims=True)
                total = total + matmul(
                    weight.astype(jnp.bfloat16), value_slots[slot, :reach, :]
                )
            mixed[rows, here] = total.astype(jnp.bfloat16)
        return carry

    lax.fori_loop(0, query_v.shape[1] // 128, head_pair, 0)
    receive_relay(0, 0)
    start_relay(0, 1)
    loads[4].wait()
    part_send[...] = matmul(mixed[other_rows, :], out_v[...]).astype(jnp.bfloat16)
    part_copy = pltpu.make_async_remote_copy(
        src_ref=part_send,
        dst_ref=part_recv,
        send_sem=part_sem.at[0],
        recv_sem=part_sem.at[1],
        device_id=sibling,
        device_id_type=MESH,
    )
    part_copy.start()
    own_part = matmul(mixed[own_rows, :], out_v[...])
    part_copy.wait()
    attended_half = own_part + part_recv[...].astype(jnp.float32)
    attended[...] = attended_half.astype(jnp.bfloat16)
    middle = stream_v[own_rows, :].astype(jnp.float32) + residual_scale * attended_half
    inverse = lax.rsqrt(jnp.mean(middle * middle, axis=-1, keepdims=True) + epsilon)
    mixer[...] = (middle * inverse * gain_second[...]).astype(jnp.bfloat16)
    start_relay(1, 0)
    logits = matmul(mixer[...], router[...])
    lane = lax.broadcasted_iota(jnp.int32, logits.shape, 1)
    routed = lane < 0
    for entry in range(TOP):
        routed = jnp.logical_or(routed, lane == routes[own_rows, entry : entry + 1])
    largest = jnp.max(jnp.where(routed, logits, masked_score), axis=-1, keepdims=True)
    gate_exp = jnp.where(routed, jnp.exp(jnp.minimum(logits - largest, 0.0)), 0.0)
    probs[...] = gate_exp / jnp.sum(gate_exp, axis=-1, keepdims=True)

    def probs_copy(step):
        return send(
            probs,
            probs_all.at[line],
            (probs_send, probs_recv),
            (step - 1,),
            (partners[step], core),
        )

    for step in range(1, LINES):
        probs_copy(step).start()
    own_copies.append(pltpu.make_async_copy(probs, probs_all.at[line], own_sem.at[4]))
    own_copies.append(pltpu.make_async_copy(mixer, mixer_all.at[line], own_sem.at[5]))
    for copy in own_copies[4:]:
        copy.start()

    def pass_on(kind):
        for axis in (0, 1):
            direct(kind, axis).wait_recv()
        for axis in onwards[kind]:
            onward(kind, axis).start()
        for slot in (1, 2):
            to_sibling(kind, slot).start()

    pass_on(0)
    receive_relay(1, 0)
    start_relay(1, 1)
    receive_relay(0, 1)
    start_relay(0, 2)
    pass_on(1)
    pass_on(2)
    receive_relay(1, 1)
    start_relay(1, 2)
    for kind in range(3):
        for axis in onwards[kind]:
            onward(kind, axis).wait_recv()
        to_sibling(kind, 3).start()
    receive_relay(0, 2)
    receive_relay(1, 2)
    for step in range(1, LINES):
        probs_copy(step).wait()
    for copy in own_copies:
        copy.wait()
    for kind in range(3):
        for slot in range(PLANE):
            to_sibling(kind, slot).wait()
        for axis in (0, 1):
            direct(kind, axis).wait_send()
        for axis in onwards[kind]:
            onward(kind, axis).wait_send()
    for array in (0, 1):
        for hop in range(LINES - 1):
            finish_relay(array, hop)


def run_front(operands, weights):
    low, wide = jnp.bfloat16, jnp.float32
    shape = jax.ShapeDtypeStruct
    far = pl.BlockSpec(memory_space=pl.ANY)
    near = pl.BlockSpec(memory_space=pltpu.VMEM)
    tokens, width = operands[0].shape
    half = tokens // 2
    query_width, key_width = operands[4].shape[1], operands[5].shape[1]
    span = weights[0].shape[1]
    tiles = 2 * PLANE
    dma = pltpu.SemaphoreType.DMA
    slots = 2 * key_width // HEAD_FEATURES
    return pl.pallas_call(
        front_kernel,
        name="front",
        out_shape=(
            shape((tiles, width, span), low),
            shape((tiles, width, span), low),
            shape((tiles, span, width), low),
            shape((LINES, half, width), low),
            shape((LINES, half, width), low),
            shape((LINES, half, 128), wide),
            shape((tokens, width), low),
            shape((tokens, query_width), low),
            shape((tokens, key_width), low),
            shape((tokens, key_width), low),
            shape((tokens, query_width), low),
            shape((half, width), low),
        ),
        in_specs=[far, far, near, near, far, far, far, far, near, near, near, near] + [far] * 3,
        out_specs=(far,) * 6 + (near,) * 6,
        scratch_shapes=[
            pltpu.VMEM((tokens, width), low),
            pltpu.VMEM((width, query_width), low),
            pltpu.VMEM((width, key_width), low),
            pltpu.VMEM((width, key_width), low),
            pltpu.VMEM((query_width, width), low),
            pltpu.VMEM((slots, tokens, 128), low),
            pltpu.VMEM((slots, tokens, 128), low),
            pltpu.VMEM((half, width), low),
            pltpu.VMEM((half, width), low),
            pltpu.VMEM((half, width), low),
            pltpu.VMEM((half, 128), wide),
            dma((5,)),
            dma((6,)),
            dma((3, 8)),
            dma((3, 8)),
            dma((2, 2, LINES - 1)),
            dma((2, 2, LINES - 1)),
            dma((LINES - 1,)),
            dma((LINES - 1,)),
            dma((2,)),
        ],
        compiler_params=pltpu.CompilerParams(
            collective_id=2, has_side_effects=True, vmem_limit_bytes=60 << 20
        ),
    )(*operands, *weights)


def expert_kernel(*refs):
    tiles = 2 * PLANE
    refs = list(refs)

    def take(count):
        taken = refs[:count]
        del refs[:count]
        return taken

    mixer_all, cot_all, probs_all, gate_all, up_all, down_all = take(6)
    out_parts = take(LINES)
    grow_sum, weighting_sum = take(2)
    kept = take(3)
    landed = take(3)
    mixer, cots, probs, gates, ups, downs = take(6)
    scaled, ggate, gup, grow, grow_in, outs, weighting, weighting_in = take(8)
    load_sem, tile_sem, store_sem, kept_sem = take(4)
    grow_send, grow_recv, weighting_send, weighting_recv = take(4)
    core_send, core_recv, plane_send, plane_recv, ready_sem = take(5)
    half, width = mixer_all.shape[1:]
    rows = LINES * half
    span = gates.shape[2]
    column_tiles = width // span

    place = lax.axis_index("ep")
    core = lax.axis_index("tp")
    partners = [flip_line(place, step) for step in range(LINES)]
    barrier = pltpu.get_barrier_semaphore()
    for step in range(1, LINES):
        pl.semaphore_signal(
            barrier, inc=1, device_id=(partners[step], core), device_id_type=MESH
        )
    sibling = (place, 1 - core)
    across = [(flip(place, 1), core), (flip(place, 2), core)]
    for other in across + [sibling]:
        pl.semaphore_signal(barrier, inc=1, device_id=other, device_id_type=MESH)

    loads = []
    for step in range(LINES):
        part = pl.ds(step * half, half)
        for kind, (source, target) in enumerate(
            ((mixer_all, mixer), (cot_all, cots), (probs_all, probs))
        ):
            loads.append(
                pltpu.make_async_copy(source.at[step], target.at[part], load_sem.at[kind, step])
            )
    for copy in loads:
        copy.start()
    for tile in range(tiles):
        for kind, (source, target) in enumerate(
            ((gate_all, gates), (up_all, ups), (down_all, downs))
        ):
            pltpu.make_async_copy(source.at[tile], target.at[tile], tile_sem.at[kind, tile]).start()
    pl.semaphore_wait(barrier, LINES + 2)
    for copy in loads:
        copy.wait()
    weighting[...] = jnp.zeros_like(weighting)
    line_place = lax.div(place, PLANE)
    lanes = lax.broadcasted_iota(jnp.int32, (rows, 128), 1)

    def hidden_tile(tile, carry):
        for kind, (source, target) in enumerate(
            ((gate_all, gates), (up_all, ups), (down_all, downs))
        ):
            pltpu.make_async_copy(source.at[tile], target.at[tile], tile_sem.at[kind, tile]).wait()
        step = lax.rem(tile, PLANE)
        owner = lax.rem(place, PLANE)
        owner = jnp.where(lax.rem(step, 2) == 1, flip(owner, 1), owner)
        owner = jnp.where(lax.div(step, 2) == 1, flip(owner, 2), owner)
        chosen = lanes == line_place * PLANE + owner
        prob = jnp.sum(jnp.where(chosen, probs[...], 0.0), axis=1, keepdims=True)
        gate_pre = matmul(mixer[...], gates[tile])
        up_pre = matmul(mixer[...], ups[tile])
        grad_raw = residual_scale * matmul_nt(cots[...], downs[tile])
        sigmoid_gate = 1.0 / (1.0 + jnp.exp(-gate_pre))
        silu_gate = gate_pre * sigmoid_gate
        active = silu_gate * up_pre
        share = jnp.sum(active * grad_raw, axis=1, keepdims=True)
        weighting[...] += jnp.where(chosen, share, 0.0)
        grad_active = prob * grad_raw
        scaled[tile] = (prob * active).astype(jnp.bfloat16)
        ggate[tile] = (
            grad_active * up_pre * sigmoid_gate * (1.0 + gate_pre * (1.0 - sigmoid_gate))
        ).astype(jnp.bfloat16)
        gup[tile] = (grad_active * silu_gate).astype(jnp.bfloat16)
        return carry

    lax.fori_loop(0, tiles, hidden_tile, 0)

    def rows_for(step):
        return pl.ds(pl.multiple_of(lax.div(partners[step], PLANE) * half, half), half)

    def weighting_copy(step):
        return pltpu.make_async_remote_copy(
            src_ref=weighting.at[rows_for(step)],
            dst_ref=weighting_in.at[step - 1],
            send_sem=weighting_send.at[step - 1],
            recv_sem=weighting_recv.at[step - 1],
            device_id=(partners[step], core),
            device_id_type=MESH,
        )

    def grow_copy(step, column):
        return pltpu.make_async_remote_copy(
            src_ref=grow.at[column, rows_for(step)],
            dst_ref=grow_in.at[step - 1, column],
            send_sem=grow_send.at[step - 1, column],
            recv_sem=grow_recv.at[step - 1, column],
            device_id=(partners[step], core),
            device_id_type=MESH,
        )

    for step in range(1, LINES):
        weighting_copy(step).start()

    def grow_tile(column, carry):
        here = pl.ds(pl.multiple_of(column * span, span), span)
        total = matmul_nt(ggate[0], gates[0, here, :])
        for tile in range(1, tiles):
            total = total + matmul_nt(ggate[tile], gates[tile, here, :])
        for tile in range(tiles):
            total = total + matmul_nt(gup[tile], ups[tile, here, :])
        grow[column] = total.astype(jnp.bfloat16)
        for step in range(1, LINES):
            grow_copy(step, column).start()
        return carry

    lax.fori_loop(0, column_tiles, grow_tile, 0)

    def out_tile(column, carry):
        here = pl.ds(pl.multiple_of(column * span, span), span)
        total = matmul(scaled[0], downs[0, :, here])
        for tile in range(1, tiles):
            total = total + matmul(scaled[tile], downs[tile, :, here])
        outs[:, here] = total.astype(jnp.bfloat16)
        return carry

    lax.fori_loop(0, column_tiles, out_tile, 0)
    stores = [
        pltpu.make_async_copy(
            outs.at[rows_for(step)], out_parts[step], store_sem.at[step]
        )
        for step in range(LINES)
    ]
    for copy in stores:
        copy.start()

    pl.semaphore_signal(ready_sem, inc=1, device_id=sibling, device_id_type=MESH)
    pl.semaphore_wait(ready_sem, 1)
    held = (gates, ups, downs)

    def tile_order(index):
        return jnp.where(index == 0, 3, jnp.where(index == 3, 0, index))

    def tile_grads(tile):
        yield matmul_tn(mixer[...], ggate[tile])
        yield matmul_tn(mixer[...], gup[tile])
        yield residual_scale * matmul_tn(scaled[tile], cots[...])

    def core_copy(kind, step):
        return pltpu.make_async_remote_copy(
            src_ref=held[kind].at[PLANE + step],
            dst_ref=held[kind].at[step],
            send_sem=core_send.at[kind, step],
            recv_sem=core_recv.at[kind, step],
            device_id=sibling,
            device_id_type=MESH,
        )

    def sibling_tile(index, carry):
        step = tile_order(index)
        for kind, grad in enumerate(tile_grads(PLANE + step)):
            held[kind][PLANE + step] = grad.astype(jnp.bfloat16)
            core_copy(kind, step).start()
        return carry

    lax.fori_loop(0, PLANE, sibling_tile, 0)

    def plane_copy(kind, axis, passing):
        span_rows = held[kind].shape[1] // 2
        step = 3 if passing else axis + 1
        return pltpu.make_async_remote_copy(
            src_ref=held[kind].at[step, pl.ds(axis * span_rows, span_rows)],
            dst_ref=landed[kind].at[axis, passing],
            send_sem=plane_send.at[kind, axis, passing],
            recv_sem=plane_recv.at[kind, axis, passing],
            device_id=across[axis],
            device_id_type=MESH,
        )

    def kept_copy(kind, step):
        return pltpu.make_async_copy(
            held[kind].at[step], kept[kind].at[step], kept_sem.at[kind, step]
        )

    def own_tile(index, carry):
        step = tile_order(index)
        for kind, grad in enumerate(tile_grads(step)):
            core_copy(kind, step).wait_recv()
            held[kind][step] = (grad + held[kind][step].astype(jnp.float32)).astype(jnp.bfloat16)

            @pl.when(step == 3)
            def _():
                for axis in (0, 1):
                    plane_copy(kind, axis, 1).start()

            for axis in (0, 1):

                @pl.when(step == axis + 1)
                def _():
                    plane_copy(kind, axis, 0).start()

            @pl.when(step < 3)
            def _():
                kept_copy(kind, step).start()

        return carry

    lax.fori_loop(0, PLANE, own_tile, 0)
    for step in range(1, LINES):
        weighting_copy(step).wait()
    total = weighting[rows_for(0), :]
    for step in range(1, LINES):
        total = total + weighting_in[step - 1]
    weighting_sum[...] = total
    for column in range(column_tiles):
        here = pl.ds(column * span, span)
        for step in range(1, LINES):
            grow_copy(step, column).wait()
        total = grow[column, rows_for(0), :].astype(jnp.float32)
        for step in range(1, LINES):
            total = total + grow_in[step - 1, column].astype(jnp.float32)
        grow_sum[:, here] = total
    for copy in stores:
        copy.wait()

    for kind in range(3):
        for step in range(PLANE):
            core_copy(kind, step).wait_send()
        for step in range(3):
            kept_copy(kind, step).wait()
        for axis in (0, 1):
            for passing in (0, 1):
                plane_copy(kind, axis, passing).wait()


def run_experts(mixer_all, cot_all, probs_all, gate_all, up_all, down_all):
    tiles = 2 * PLANE
    half, width = mixer_all.shape[1:]
    span = gate_all.shape[2]
    rows = LINES * half
    low, wide = jnp.bfloat16, jnp.float32
    shape = jax.ShapeDtypeStruct
    far = pl.BlockSpec(memory_space=pl.ANY)
    near = pl.BlockSpec(memory_space=pltpu.VMEM)
    operands = [mixer_all, cot_all, probs_all, gate_all, up_all, down_all]
    dma = pltpu.SemaphoreType.DMA
    flops = 18 * rows * width * span * tiles
    results = pl.pallas_call(
        expert_kernel,
        name="experts",
        out_shape=(
            *[shape((half, width), low)] * LINES,
            shape((half, width), wide),
            shape((half, 128), wide),
            shape((3, width, span), low),
            shape((3, width, span), low),
            shape((3, span, width), low),
            shape((2, 2, width // 2, span), low),
            shape((2, 2, width // 2, span), low),
            shape((2, 2, span // 2, width), low),
        ),
        in_specs=[far] * len(operands),
        out_specs=(*[far] * LINES, near, near, *[far] * 6),
        scratch_shapes=[
            pltpu.VMEM((rows, width), low),
            pltpu.VMEM((rows, width), low),
            pltpu.VMEM((rows, 128), wide),
            pltpu.VMEM((tiles, width, span), low),
            pltpu.VMEM((tiles, width, span), low),
            pltpu.VMEM((tiles, span, width), low),
            pltpu.VMEM((tiles, rows, span), low),
            pltpu.VMEM((tiles, rows, span), low),
            pltpu.VMEM((tiles, rows, span), low),
            pltpu.VMEM((width // span, rows, span), low),
            pltpu.VMEM((LINES - 1, width // span, half, span), low),
            pltpu.VMEM((rows, width), low),
            pltpu.VMEM((rows, 128), wide),
            pltpu.VMEM((LINES - 1, half, 128), wide),
            dma((3, LINES)),
            dma((3, tiles)),
            dma((LINES,)),
            dma((3, 3)),
            dma((LINES - 1, width // span)),
            dma((LINES - 1, width // span)),
            dma((LINES - 1,)),
            dma((LINES - 1,)),
            dma((3, PLANE)),
            dma((3, PLANE)),
            dma((3, 2, 2)),
            dma((3, 2, 2)),
            pltpu.SemaphoreType.REGULAR,
        ],
        compiler_params=pltpu.CompilerParams(
            collective_id=0, has_side_effects=True, vmem_limit_bytes=63 << 20
        ),
        cost_estimate=pl.CostEstimate(
            flops=flops, bytes_accessed=12 * width * span * tiles, transcendentals=0
        ),
    )(*operands)
    return results


def back_kernel(*refs):
    refs = list(refs)

    def take(count):
        taken = refs[:count]
        del refs[:count]
        return taken

    out_parts = take(LINES)
    grow_sum, weighting_sum = take(2)
    kept, landed = take(3), take(3)
    stream, cotangent, gain_first, gain_second, query_weight, key_weight = take(6)
    value_weight, out_weight, router, cosine, sine = take(5)
    mixer_all, probs_all, normed, queries, keys, values, mixed, attended = take(8)
    layer_out, grad_stream, out_result_a, out_result_b, query_result, rest_result = take(6)
    expert_grads = take(3)
    small_out = take(1)[0]
    stream_v, cot_v, query_v, key_v, value_v, out_v, normed_v, queries_v = take(8)
    mixed_v, grow_v, attended_v, out_in, layer_v = take(5)
    key_v2, value_v2, mixer_v, probs_v, weighting_v = take(5)
    key_slots, value_slots, key_totals, value_totals = take(4)
    middle_grads, attended_grads, mixed_grads = take(3)
    key_grads, value_grads, normed_recv = take(3)
    normed_send, first_terms = attended_grads, layer_v
    second_terms, query_grads = cot_v, mixed_v
    own_parts, landed_v, plane_in = take(3), take(3), take(3)
    out_source_a, out_source_b, query_source, rest_source = take(4)
    scatter_scratch = [take(5) for _ in range(4)]
    last_send, last_recv = take(2)
    load_sem, part_sem, out_send, out_recv, pair_sem, plane_send, plane_recv = take(7)
    store_sem = take(1)[0]
    tokens, width = stream_v.shape
    half = tokens // 2

    place = lax.axis_index("ep")
    core = lax.axis_index("tp")
    line = lax.div(place, PLANE)
    sibling = (place, 1 - core)
    across = [flip(place, 1), flip(place, 2)]
    partners = [flip_line(place, step) for step in range(LINES)]
    bits = [lax.rem(place, 2), lax.rem(lax.div(place, 2), 2)]
    own_rows = pl.ds(pl.multiple_of(core * half, half), half)

    barrier = pltpu.get_barrier_semaphore()
    for other in across + partners[1:]:
        pl.semaphore_signal(barrier, inc=1, device_id=(other, core), device_id_type=MESH)
    pl.semaphore_signal(barrier, inc=1, device_id=sibling, device_id_type=MESH)

    pairs = [
        (grow_sum, grow_v),
        (weighting_sum, weighting_v),
        (attended, attended_v),
        (probs_all.at[line], probs_v),
        (stream, stream_v),
        (cotangent.at[own_rows], cot_v),
        (out_weight, out_v),
        (mixed, mixed_v),
        (queries, queries_v),
        (keys, key_v2),
        (values, value_v2),
        (normed, normed_v),
        (query_weight, query_v),
        (key_weight, key_v),
        (value_weight, value_v),
        (mixer_all.at[line], mixer_v),
        (out_parts[0], mixer_v),
    ]
    loads = [
        pltpu.make_async_copy(source, target, load_sem.at[index])
        for index, (source, target) in enumerate(pairs)
    ]

    def part_copies(kind, final):
        rows = own_parts[kind].shape[1]
        low, high = pl.ds(0, rows), pl.ds(rows, rows)
        first, second = (0, 0) if final else (2, 1)
        return [
            pltpu.make_async_copy(source, target, part_sem.at[kind, index])
            for index, (source, target) in enumerate(
                (
                    (kept[kind].at[first, low], own_parts[kind].at[0]),
                    (kept[kind].at[second, high], own_parts[kind].at[1]),
                )
            )
        ]

    def landed_copy(kind):
        return pltpu.make_async_copy(landed[kind], landed_v[kind], part_sem.at[kind, 2])

    for copy in loads[:6]:
        copy.start()
    for kind in range(3):
        landed_copy(kind).start()
        for copy in part_copies(kind, False):
            copy.start()
    for copy in loads[6:-1]:
        copy.start()
    pl.semaphore_wait(barrier, LINES + 2)

    def send(source, target, sems, index, device):
        return pltpu.make_async_remote_copy(
            src_ref=source,
            dst_ref=target,
            send_sem=sems[0].at[index],
            recv_sem=sems[1].at[index],
            device_id=device,
            device_id_type=MESH,
        )

    def out_copy(step):
        return send(
            out_parts[step],
            out_in.at[step - 1],
            (out_send, out_recv),
            (step - 1,),
            (partners[step], core),
        )

    for step in (3, 2, 1):
        out_copy(step).start()

    for copy in loads[:6]:
        copy.wait()
    middle = stream_v[own_rows, :].astype(jnp.float32) + residual_scale * attended_v[...].astype(jnp.float32)
    inverse = lax.rsqrt(jnp.mean(middle * middle, axis=-1, keepdims=True) + epsilon)
    probs = probs_v[...]
    weighting = weighting_v[...]
    grad_chosen = probs * (weighting - jnp.sum(probs * weighting, axis=-1, keepdims=True))
    grad_logits = grad_chosen.astype(jnp.bfloat16)
    grad_mixer = matmul_nt(grad_logits, router[...]) + grow_v[...]
    weighted = grad_mixer * gain_second[...]
    grad_middle = (
        cot_v[...].astype(jnp.float32)
        + inverse * weighted
        - middle * (inverse * inverse * inverse)
        * jnp.mean(middle * weighted, axis=-1, keepdims=True)
    )
    middle_grads[own_rows, :] = grad_middle.astype(jnp.bfloat16)
    second_terms[...] = (grad_mixer * middle * inverse).astype(jnp.bfloat16)

    def pair_copy(source, target, index):
        return pltpu.make_async_remote_copy(
            src_ref=source,
            dst_ref=target,
            send_sem=pair_sem.at[0, index],
            recv_sem=pair_sem.at[1, index],
            device_id=sibling,
            device_id_type=MESH,
        )

    middle_copy = pair_copy(middle_grads.at[own_rows], middle_grads.at[own_rows], 0)
    middle_copy.start()

    def plane_copy(kind, axis):
        return send(
            landed_v[kind].at[axis, 1],
            plane_in[kind].at[axis],
            (plane_send, plane_recv),
            (kind, axis),
            (across[1 - axis], core),
        )

    for kind in range(3):
        landed_copy(kind).wait()
        for copy in part_copies(kind, False):
            copy.wait()
        for axis in (0, 1):
            landed_v[kind][axis, 1] = (
                own_parts[kind][axis].astype(jnp.float32)
                + landed_v[kind][axis, 1].astype(jnp.float32)
            ).astype(jnp.bfloat16)
            plane_copy(kind, axis).start()
        for copy in part_copies(kind, True):
            copy.start()

    slab = out_result_a.shape[0]
    order = (3, 2, 1, 0)
    plans = list(
        zip(
            (out_source_a, out_source_b, query_source, rest_source),
            (out_result_a, out_result_b, query_result, rest_result),
            scatter_scratch,
        )
    )

    def rows_of(step, first, second_same, first_same):
        other_line = lax.div(partners[step], PLANE)
        first_bit = bits[first] if first_same else 1 - bits[first]
        second_bit = bits[1 - first] if second_same else 1 - bits[1 - first]
        index = other_line * PLANE + first_bit * (1 + first) + second_bit * (2 - first)
        return pl.ds(pl.multiple_of(index * slab, slab), slab)

    def first_copy(number, step, same):
        source, _, scratch = plans[number]
        first = number % 2
        index = step * 2 + same
        return send(
            source.at[rows_of(step, first, same, False)],
            scratch[0].at[index],
            (scratch[4].at[0], scratch[4].at[1]),
            (index,),
            (across[first], core),
        )

    def second_copy(number, step):
        scratch = plans[number][2]
        return send(
            scratch[1].at[step],
            scratch[2].at[step],
            (scratch[4].at[2], scratch[4].at[3]),
            (step,),
            (across[1 - number % 2], core),
        )

    def line_copy(number, step):
        scratch = plans[number][2]
        return send(
            scratch[1].at[step],
            scratch[3].at[step],
            (scratch[4].at[4], scratch[4].at[5]),
            (step,),
            (partners[step], core),
        )

    def start_scatter(number):
        for step in order:
            for same in (0, 1):
                first_copy(number, step, same).start()

    def add_first(number, step, same):
        source, _, scratch = plans[number]
        first_copy(number, step, same).wait()
        mine = source[rows_of(step, number % 2, same, True), :].astype(jnp.float32)
        return mine + scratch[0][step * 2 + same].astype(jnp.float32)

    def finish_first(number, step):
        plans[number][2][1][step] = add_first(number, step, 0).astype(jnp.bfloat16)
        second_copy(number, step).start()

    def finish_second(number, step):
        _, result, scratch = plans[number]
        total = add_first(number, step, 1)
        second_copy(number, step).wait()
        total = total + scratch[2][step].astype(jnp.float32)
        if step:
            scratch[1][step] = total.astype(jnp.bfloat16)
            line_copy(number, step).start()
        else:
            result[...] = total

    def finish_line(number):
        _, result, scratch = plans[number]
        for step in order[:-1]:
            line_copy(number, step).wait()
            result[...] += scratch[3][step].astype(jnp.float32)

    middle_copy.wait()
    attended_grads[...] = (residual_scale * middle_grads[...].astype(jnp.float32)).astype(
        jnp.bfloat16
    )
    loads[6].wait()
    loads[7].wait()
    columns = out_source_a.shape[1]
    out_source_a[...] = matmul_tn(attended_grads[...], mixed_v[:, :columns]).astype(jnp.bfloat16)
    start_scatter(0)
    out_source_b[...] = matmul_tn(attended_grads[...], mixed_v[:, columns:]).astype(jnp.bfloat16)
    start_scatter(1)
    mixed_grads[...] = matmul_nt(attended_grads[...], out_v[...]).astype(jnp.bfloat16)
    for copy in loads[8:11]:
        copy.wait()
    store_slots(key_slots, key_v2[...].astype(jnp.float32))
    store_slots(value_slots, value_v2[...].astype(jnp.float32))
    key_totals[...] = jnp.zeros_like(key_totals)
    value_totals[...] = jnp.zeros_like(value_totals)
    group = query_v.shape[1] // key_v.shape[1]
    blocks = 2
    block_rows = tokens // blocks

    def turned_back(value, cosines, sines):
        return (value * cosines - partner_lanes(value) * sines).astype(jnp.bfloat16)

    def head_pair(pair, carry):
        here = pl.ds(pl.multiple_of(pair * 128, 128), 128)
        for block in range(blocks):
            rows = slice(block * block_rows, (block + 1) * block_rows)
            reach = (block + 1) * block_rows
            total = jnp.zeros((block_rows, 128), jnp.float32)
            query_block = queries_v[rows, here]
            grad_block = mixed_grads[rows, here]
            for parity in range(2):
                slot = 2 * lax.div(2 * pair + parity, group) + parity
                key_block = key_slots[slot, :reach, :]
                scores = causal_scores(query_block, key_block, block * block_rows)
                weight = jnp.exp(scores - jnp.max(scores, axis=-1, keepdims=True))
                weight = weight / jnp.sum(weight, axis=-1, keepdims=True)
                grad_probs = matmul_nt(grad_block, value_slots[slot, :reach, :])
                inner = jnp.sum(weight * grad_probs, axis=-1, keepdims=True)
                grad_scores = (weight * (grad_probs - inner)).astype(jnp.bfloat16)
                total = total + matmul(grad_scores, key_block)
                key_totals[slot, :reach, :] += matmul_tn(grad_scores, query_block)
                value_totals[slot, :reach, :] += matmul_tn(
                    weight.astype(jnp.bfloat16), grad_block
                )
            query_grads[rows, here] = turned_back(
                score_scale * total, cosine[rows, :128], sine[rows, :128]
            )
        return carry

    lax.fori_loop(0, query_v.shape[1] // 128, head_pair, 0)

    def gathered_pairs(totals):
        found = []
        for pair in range(key_v.shape[1] // 128):
            first, second = 4 * pair, 4 * pair + 2
            low = lane_halves(totals[first])[0] + pltpu.roll(
                lane_halves(totals[first + 1])[1], HEAD_FEATURES, 1
            )
            high = lane_halves(totals[second + 1])[1] + pltpu.roll(
                lane_halves(totals[second])[0], HEAD_FEATURES, 1
            )
            found.append(low + high)
        return jnp.concatenate(found, axis=1)

    key_grads[...] = turned_back(
        score_scale * gathered_pairs(key_totals), cosine[...], sine[...]
    )
    value_grads[...] = gathered_pairs(value_totals).astype(jnp.bfloat16)
    for copy in loads[11:-1]:
        copy.wait()
    query_source[...] = matmul_tn(normed_v[...], query_grads[...]).astype(jnp.bfloat16)
    start_scatter(2)
    normed_send[...] = (
        matmul_nt(query_grads[...], query_v[...])
        + matmul_nt(key_grads[...], key_v[...])
        + matmul_nt(value_grads[...], value_v[...])
    ).astype(jnp.bfloat16)
    normed_copy = pair_copy(normed_send, normed_recv, 1)
    normed_copy.start()
    key_width = key_grads.shape[1]
    rest_source[:, :key_width] = matmul_tn(normed_v[...], key_grads[...]).astype(jnp.bfloat16)
    rest_source[:, key_width : 2 * key_width] = matmul_tn(
        normed_v[...], value_grads[...]
    ).astype(jnp.bfloat16)
    for step in order:
        finish_first(0, step)
        finish_first(1, step)
    normed_copy.wait()

    def stream_rows(rows):
        grad_normed = normed_send[rows, :].astype(jnp.float32) + normed_recv[rows, :].astype(
            jnp.float32
        )
        stream_f = stream_v[rows, :].astype(jnp.float32)
        inverse = lax.rsqrt(jnp.mean(stream_f * stream_f, axis=-1, keepdims=True) + epsilon)
        weighted = grad_normed * gain_first[...]
        total = (
            middle_grads[rows, :].astype(jnp.float32)
            + inverse * weighted
            - stream_f * (inverse * inverse * inverse)
            * jnp.mean(stream_f * weighted, axis=-1, keepdims=True)
        )
        return grad_normed * stream_f * inverse, total

    first_terms[...] = stream_rows(own_rows)[0].astype(jnp.bfloat16)
    lane = lax.broadcasted_iota(jnp.int32, (half, 128), 1)
    experts = LINES * PLANE
    rest_source[:, 2 * key_width :] = (
        matmul_tn(mixer_v[...], grad_logits)
        + matmul_tn(second_terms[...], (lane == experts).astype(jnp.bfloat16))
        + matmul_tn(first_terms[...], (lane == experts + 1).astype(jnp.bfloat16))
    ).astype(jnp.bfloat16)
    loads[-1].start()
    start_scatter(3)
    for position in range(2):
        rows = slice(position * half, position * half + half)
        normed_recv[rows, :] = stream_rows(rows)[1].astype(jnp.bfloat16)
    stream_copy = pltpu.make_async_copy(normed_recv, grad_stream, store_sem.at[4])
    stream_copy.start()
    for step in order:
        finish_second(0, step)
        finish_second(1, step)
    for step in order:
        finish_first(2, step)
        finish_first(3, step)
    for step in (1, 2, 3):
        out_copy(step).wait()
    loads[-1].wait()
    mixture = mixer_v[...].astype(jnp.float32)
    for step in range(1, LINES):
        mixture = mixture + out_in[step - 1].astype(jnp.float32)
    middle = stream_v[own_rows, :].astype(jnp.float32) + residual_scale * attended_v[...].astype(jnp.float32)
    result = middle + residual_scale * mixture
    layer_v[...] = result.astype(jnp.bfloat16)
    layer_pair = pair_copy(layer_v, layer_out.at[own_rows], 2)
    layer_pair.start()
    layer_own = pltpu.make_async_copy(layer_v, layer_out.at[own_rows], store_sem.at[0])
    layer_own.start()
    row_lane = lax.broadcasted_iota(jnp.int32, (8, 128), 1)
    squares = jnp.zeros((8, 128), jnp.float32)
    for index, value in enumerate((result, attended_v[...].astype(jnp.float32), mixture)):
        total = jnp.sum(jnp.sum(value * value, axis=1, keepdims=True), axis=0, keepdims=True)
        squares = jnp.where(row_lane == index, total, squares)
    for step in order:
        finish_second(2, step)
        finish_second(3, step)
    def expert_copy(kind):
        return pltpu.make_async_copy(own_parts[kind], expert_grads[kind], store_sem.at[1 + kind])

    for kind in range(3):
        for copy in part_copies(kind, True):
            copy.wait()
        for axis in (0, 1):
            plane_copy(kind, axis).wait()
            own_parts[kind][axis] = (
                own_parts[kind][axis].astype(jnp.float32)
                + landed_v[kind][axis, 0].astype(jnp.float32)
                + plane_in[kind][axis].astype(jnp.float32)
            ).astype(jnp.bfloat16)
        expert_copy(kind).start()
    finish_line(3)
    last_send[:slab, :] = rest_result[:, 2 * key_width :]
    last_send[slab:, :] = squares
    last_copy = pair_copy(last_send, last_recv, 3)
    last_copy.start()
    for number in range(3):
        finish_line(number)
    last_copy.wait()
    small_out[...] = last_send[...] + last_recv[...]
    layer_pair.wait()
    layer_own.wait()
    stream_copy.wait()
    for kind in range(3):
        expert_copy(kind).wait()


def run_back(expert_results, operands, front_results):
    low, wide = jnp.bfloat16, jnp.float32
    shape = jax.ShapeDtypeStruct
    vmem = pltpu.VMEM
    far = pl.BlockSpec(memory_space=pl.ANY)
    near = pl.BlockSpec(memory_space=pltpu.VMEM)
    tokens, width = operands[0].shape
    half = tokens // 2
    query_width, key_width = operands[4].shape[1], operands[5].shape[1]
    kept = expert_results[LINES + 2 : LINES + 5]
    tile_shapes = [value.shape[1:] for value in kept]
    half_shapes = [(value[0] // 2, value[1]) for value in tile_shapes]
    slab = width // (LINES * PLANE)
    slots = 2 * key_width // HEAD_FEATURES
    rest_width = 2 * key_width + 128
    widths = (query_width // 2, query_width // 2, query_width, rest_width)
    dma = pltpu.SemaphoreType.DMA
    scatter_scratch = []
    for columns in widths:
        scatter_scratch += [
            vmem((2 * LINES, slab, columns), low),
            vmem((LINES, slab, columns), low),
            vmem((LINES, slab, columns), low),
            vmem((LINES, slab, columns), low),
            dma((6, 2 * LINES)),
        ]
    return pl.pallas_call(
        back_kernel,
        name="back",
        out_shape=(
            shape((tokens, width), low),
            shape((tokens, width), low),
            *[shape((slab, columns), wide) for columns in widths],
            *[shape((2, *value), low) for value in half_shapes],
            shape((slab + 8, 128), wide),
        ),
        in_specs=[far] * (LINES + 8)
        + [far, far, near, near, far, far, far, far, near, near, near]
        + [far] * 8,
        out_specs=(far,) * 2 + (near,) * 4 + (far,) * 3 + (near,),
        scratch_shapes=[
            vmem((tokens, width), low),
            vmem((half, width), low),
            vmem((width, query_width), low),
            vmem((width, key_width), low),
            vmem((width, key_width), low),
            vmem((query_width, width), low),
            vmem((tokens, width), low),
            vmem((tokens, query_width), low),
            vmem((tokens, query_width), low),
            vmem((half, width), wide),
            vmem((half, width), low),
            vmem((LINES - 1, half, width), low),
            vmem((half, width), low),
            vmem((tokens, key_width), low),
            vmem((tokens, key_width), low),
            vmem((half, width), low),
            vmem((half, 128), wide),
            vmem((half, 128), wide),
            vmem((slots, tokens, 128), low),
            vmem((slots, tokens, 128), low),
            vmem((slots, tokens, 128), wide),
            vmem((slots, tokens, 128), wide),
            vmem((tokens, width), low),
            vmem((tokens, width), low),
            vmem((tokens, query_width), low),
            vmem((tokens, key_width), low),
            vmem((tokens, key_width), low),
            vmem((tokens, width), low),
            *[vmem((2, *value), low) for value in half_shapes],
            *[vmem((2, 2, *value), low) for value in half_shapes],
            *[vmem((2, *value), low) for value in half_shapes],
            *[vmem((width, columns), low) for columns in widths],
            *scatter_scratch,
            vmem((slab + 8, 128), wide),
            vmem((slab + 8, 128), wide),
            dma((17,)),
            dma((3, 3)),
            dma((LINES - 1,)),
            dma((LINES - 1,)),
            dma((2, 4)),
            dma((3, 2)),
            dma((3, 2)),
            dma((5,)),
        ],
        compiler_params=pltpu.CompilerParams(
            collective_id=1, has_side_effects=True, vmem_limit_bytes=63 << 20
        ),
    )(*expert_results, *operands, *front_results)


def dense_shards(
    stream,
    cotangent,
    attention_gain,
    query_weight,
    key_matrix,
    value_matrix,
    out_weight,
    mixture_gain,
    router_weight,
    gate_weight,
    up_weight,
    down_weight,
    routes,
):
    tok_rows, model_width = stream.shape
    experts = router_weight.shape[1]
    query_width = query_weight.shape[1]
    key_width = key_matrix.shape[1]
    cosine_rows, sine_rows = rope_tables(SEQ_LEN)
    operands = [
        stream,
        cotangent,
        attention_gain.astype(jnp.float32)[None, :],
        mixture_gain.astype(jnp.float32)[None, :],
        query_weight,
        key_matrix,
        value_matrix,
        out_weight,
        jnp.pad(router_weight, ((0, 0), (0, 128 - experts))),
        routes,
        jnp.tile(cosine_rows, (1, 8)),
        jnp.tile(jnp.concatenate([-sine_rows, sine_rows], axis=1), (1, 4)),
    ]
    front = run_front(operands, [gate_weight[0], up_weight[0], down_weight[0]])
    gate_all, up_all, down_all, mixer_all, cot_all, probs_all = front[:6]
    expert_results = run_experts(mixer_all, cot_all, probs_all, gate_all, up_all, down_all)
    (
        layer_out,
        grad_stream,
        out_first,
        out_second,
        query_grad,
        rest_grad,
        gate_grad,
        up_grad,
        down_grad,
        small,
    ) = run_back(expert_results, operands[:9] + operands[10:], [mixer_all, *front[5:]])
    slab = query_grad.shape[0]
    rms_stats = jnp.sqrt(small[slab : slab + 1, :3] / (tok_rows * model_width))
    return (
        layer_out,
        grad_stream.astype(jnp.float32),
        small[:slab, experts + 1],
        query_grad,
        rest_grad[:, :key_width],
        rest_grad[:, key_width : 2 * key_width],
        jnp.concatenate([out_first, out_second], axis=1).T,
        small[:slab, experts],
        small[:slab, :experts],
        gate_grad.astype(jnp.float32).reshape(gate_weight.shape),
        up_grad.astype(jnp.float32).reshape(up_weight.shape),
        down_grad.astype(jnp.float32).reshape(down_weight.shape),
        rms_stats,
    )


def solution(mesh):
    in_specs = (
        P("ep", None),
        P("ep", None),
        P(),
        P(None, "tp"),
        P(None, "tp"),
        P(None, "tp"),
        P("tp", None),
        P(),
        P(),
        P("ep", None, "tp"),
        P("ep", None, "tp"),
        P("ep", "tp", None),
        P("ep", None),
    )
    out_specs = (
        P("ep", None),
        P("ep", None),
        P("ep"),
        P("ep", "tp"),
        P("ep", "tp"),
        P("ep", "tp"),
        P("tp", "ep"),
        P("ep"),
        P("ep", None),
        P("ep", None, "tp"),
        P("ep", None, "tp"),
        P("ep", "tp", None),
        P("ep", None),
    )
    ep_size = mesh.shape["ep"]
    dense = mesh.shape["tp"] == 2 and ep_size <= 2 * TOP and ep_size == 16
    shards = dense_shards if dense else routed_shards
    return jax.shard_map(shards, mesh=mesh, in_specs=in_specs, out_specs=out_specs, check_vma=False)
```

```python
import functools

import jax
import jax.numpy as jnp
import numpy as np
from jax import lax
from jax.experimental import pallas as pl
from jax.experimental.pallas import tpu as pltpu
from jax.sharding import PartitionSpec as P

HEAD_FEATURES = 64
TOP = 8
SEQ_LEN = 512


epsilon = 1e-06
score_scale = 0.015625
residual_scale = 0.22
rope_base = 10000.0
masked_score = -1e30


def rope_tables(sequence_length):
    half_dim = HEAD_FEATURES // 2
    steps_up = jnp.arange(half_dim).astype(jnp.float32) * (2.0 / HEAD_FEATURES)
    inverse = jnp.exp(-steps_up * jnp.log(rope_base))
    places = jnp.arange(sequence_length).astype(jnp.float32)
    angles = places[:, None] * inverse[None, :]
    return (jnp.cos(angles), jnp.sin(angles))


def apply_rotation(value_rows, cosine_table, sine_values):
    half_dim = value_rows.shape[-1] // 2
    first_half = value_rows[..., :half_dim]
    second_half = value_rows[..., half_dim:]
    cos_rows = cosine_table[:, None, :]
    sin_rows = sine_values[:, None, :]
    return jnp.concatenate(
        [
            first_half * cos_rows - second_half * sin_rows,
            second_half * cos_rows + first_half * sin_rows,
        ],
        axis=-1,
    )


def rotary_back(grads_in, cosine_table, sine_values):
    half_dim = grads_in.shape[-1] // 2
    first_half = grads_in[..., :half_dim]
    second_half = grads_in[..., half_dim:]
    cos_rows = cosine_table[:, None, :]
    sin_rows = sine_values[:, None, :]
    return jnp.concatenate(
        [
            first_half * cos_rows + second_half * sin_rows,
            second_half * cos_rows - first_half * sin_rows,
        ],
        axis=-1,
    )


def block_scores(query_block, rotated_keys, row_start, block_rows, row_stop):
    scores = score_scale * jnp.einsum(
        "qhgd,khd->hgqk", query_block, rotated_keys, preferred_element_type=jnp.float32
    )
    causal = (row_start + jnp.arange(block_rows))[:, None] >= jnp.arange(row_stop)[None, :]
    return jnp.where(causal, scores, masked_score)


def attention_forward(query_rows, rotated_keys, value_rows):
    sequence_length = query_rows.shape[0]
    block_rows = min(512, sequence_length)
    scores = block_scores(query_rows, rotated_keys, 0, block_rows, block_rows)
    largest = jnp.max(scores, axis=-1, keepdims=True)
    weights_exp = jnp.exp(scores - largest)
    totals = jnp.sum(weights_exp, axis=-1, keepdims=True)
    probs_low = (weights_exp / totals).astype(jnp.bfloat16)
    outputs = jnp.einsum(
        "hgqk,khd->qhgd", probs_low, value_rows, preferred_element_type=jnp.float32
    )
    normalizers = [largest + jnp.log(totals)]
    return (outputs, normalizers)


def attention_backward(query_rows, rotated_keys, value_rows, normalizers, grad_mixed):
    sequence_length = query_rows.shape[0]
    block_rows = min(512, sequence_length)
    grad_keys = jnp.zeros(rotated_keys.shape, jnp.float32)
    grad_values = jnp.zeros(value_rows.shape, jnp.float32)
    grad_queries = []
    for block_index, row_start in enumerate(range(0, sequence_length, block_rows)):
        row_stop = row_start + block_rows
        scores = block_scores(query_rows, rotated_keys, row_start, block_rows, row_stop)
        probs = jnp.exp(scores - normalizers[block_index])
        probs_low = probs.astype(jnp.bfloat16)
        grad_probs = jnp.einsum(
            "qhgd,khd->hgqk", grad_mixed, value_rows, preferred_element_type=jnp.float32
        )
        inner = jnp.sum(probs * grad_probs, axis=-1, keepdims=True)
        grad_scores = (probs * (grad_probs - inner)).astype(jnp.bfloat16)
        grad_queries.append(
            score_scale
            * jnp.einsum(
                "hgqk,khd->qhgd", grad_scores, rotated_keys, preferred_element_type=jnp.float32
            )
        )
        grad_keys = grad_keys.at[:row_stop].add(
            score_scale
            * jnp.einsum(
                "hgqk,qhgd->khd", grad_scores, query_rows, preferred_element_type=jnp.float32
            )
        )
        grad_values = grad_values.at[:row_stop].add(
            jnp.einsum("hgqk,qhgd->khd", probs_low, grad_mixed, preferred_element_type=jnp.float32)
        )
    return (grad_queries[0], grad_keys, grad_values)


def to_owners(packed):
    return lax.all_to_all(packed, "ep", split_axis=1, concat_axis=1, tiled=True)


def back_to_tokens(rows_low, slot_count, model_width):
    returned = lax.all_to_all(rows_low, "ep", split_axis=1, concat_axis=1, tiled=True)
    joined = lax.all_gather(returned, "tp", axis=0, tiled=True)
    return joined.reshape(slot_count, model_width)


def from_owners(term_fn, slot_count, experts, model_width):
    share_rows = slot_count // lax.axis_size("tp")
    summed = lax.psum_scatter(
        term_fn(jnp.int32(0), lax.axis_size("tp") * share_rows).astype(jnp.bfloat16),
        "tp",
        scatter_dimension=0,
        tiled=True,
    ).astype(jnp.float32)
    summed = summed.astype(jnp.bfloat16).reshape(share_rows // experts, experts, model_width)
    return back_to_tokens(summed, slot_count, model_width)


def seq_rms(value_rows, seq_count):
    return jnp.sqrt(jnp.mean((value_rows * value_rows).reshape(seq_count, -1), axis=1))


def routed_shards(
    stream,
    cotangent,
    attention_gain,
    query_weight,
    key_matrix,
    value_matrix,
    out_weight,
    mixture_gain,
    router_weight,
    gate_weight,
    up_weight,
    down_weight,
    routes,
):
    tok_rows, model_width = stream.shape
    experts = router_weight.shape[1]
    cap_slots = tok_rows * TOP * 5 // (4 * experts)
    slot_count = cap_slots * experts
    query_heads = query_weight.shape[1] // HEAD_FEATURES
    key_heads = key_matrix.shape[1] // HEAD_FEATURES
    group_width = query_heads // key_heads
    seq_count = tok_rows // SEQ_LEN
    stream_f = stream.astype(jnp.float32)
    grad_result = cotangent.astype(jnp.float32)
    gain_first = attention_gain.astype(jnp.float32)
    gain_second = mixture_gain.astype(jnp.float32)
    cosine_table, sine_values = rope_tables(SEQ_LEN)
    cosine_rows = jnp.tile(cosine_table, (seq_count, 1))
    sine_rows = jnp.tile(sine_values, (seq_count, 1))
    zero_low = jnp.zeros((), jnp.bfloat16)
    inv_first = lax.rsqrt(jnp.mean(stream_f * stream_f, axis=-1, keepdims=True) + epsilon)
    normalized_input = (stream_f * inv_first * gain_first).astype(jnp.bfloat16)
    query_pre = jnp.dot(normalized_input, query_weight, preferred_element_type=jnp.float32).reshape(
        tok_rows, query_heads, HEAD_FEATURES
    )
    key_pre = jnp.dot(normalized_input, key_matrix, preferred_element_type=jnp.float32).reshape(
        tok_rows, key_heads, HEAD_FEATURES
    )
    query_rows = (
        apply_rotation(query_pre, cosine_rows, sine_rows)
        .astype(jnp.bfloat16)
        .reshape(tok_rows, key_heads, group_width, HEAD_FEATURES)
    )
    rotated_keys = apply_rotation(key_pre, cosine_rows, sine_rows).astype(jnp.bfloat16)
    value_rows = (
        jnp.dot(normalized_input, value_matrix, preferred_element_type=jnp.float32)
        .astype(jnp.bfloat16)
        .reshape(tok_rows, key_heads, HEAD_FEATURES)
    )
    mixed_seq, norms_seq = attention_forward(query_rows, rotated_keys, value_rows)
    mixed_low = mixed_seq.reshape(tok_rows, query_heads * HEAD_FEATURES).astype(jnp.bfloat16)
    attended = lax.psum(
        jnp.dot(mixed_low, out_weight, preferred_element_type=jnp.float32).astype(jnp.bfloat16),
        "tp",
    ).astype(jnp.float32)
    middle = stream_f + residual_scale * attended
    inv_second = lax.rsqrt(jnp.mean(middle * middle, axis=-1, keepdims=True) + epsilon)
    mixer_in = (middle * inv_second * gain_second).astype(jnp.bfloat16)
    logits = jnp.dot(mixer_in, router_weight, preferred_element_type=jnp.float32)
    expert_ids = jnp.arange(experts, dtype=jnp.int32)
    route_hot = routes[:, :, None] == expert_ids[None, None, :]
    chosen = jnp.sum(jnp.where(route_hot, logits[:, None, :], 0.0), axis=-1)
    chosen_exp = jnp.exp(chosen - jnp.max(chosen, axis=-1, keepdims=True))
    gate_probs = chosen_exp / jnp.sum(chosen_exp, axis=-1, keepdims=True)
    flat_routes = routes.reshape(-1)
    flat_hot = route_hot.reshape(tok_rows * TOP, experts).astype(jnp.int32)
    ranks = jnp.sum((jnp.cumsum(flat_hot, axis=0) - 1) * flat_hot, axis=1)
    slot_index = ranks * experts + flat_routes
    source_pair = (
        jnp.zeros((slot_count,), jnp.int32)
        .at[slot_index]
        .set(jnp.arange(tok_rows * TOP, dtype=jnp.int32))
    )
    filled = jnp.zeros((slot_count,), jnp.bool_).at[slot_index].set(True)
    source_token = source_pair // TOP
    sent_rows = jnp.where(filled[:, None], mixer_in[source_token], zero_low).reshape(
        cap_slots, experts, model_width
    )
    received = to_owners(sent_rows).reshape(slot_count, model_width)
    gate_matrix = gate_weight[0]
    up_matrix = up_weight[0]
    down_matrix = down_weight[0]
    gate_pre = jnp.dot(received, gate_matrix, preferred_element_type=jnp.float32)
    up_pre = jnp.dot(received, up_matrix, preferred_element_type=jnp.float32)
    sigmoid_gate = jax.nn.sigmoid(gate_pre)
    silu_gate = gate_pre * sigmoid_gate
    active = (silu_gate * up_pre).astype(jnp.bfloat16)

    def down_term(row_start, row_count):
        return jnp.dot(active, down_matrix, preferred_element_type=jnp.float32)

    expert_rows = from_owners(down_term, slot_count, experts, model_width)
    picked_rows = expert_rows[slot_index].reshape(tok_rows, TOP, model_width)
    mixture = jnp.sum(gate_probs[:, :, None] * picked_rows, axis=1)
    result = middle + residual_scale * mixture
    layer_out = result.astype(jnp.bfloat16)
    rms_stats = jnp.stack(
        [seq_rms(result, seq_count), seq_rms(attended, seq_count), seq_rms(mixture, seq_count)],
        axis=1,
    )
    grad_mix = residual_scale * grad_result
    grad_weighting = jnp.sum(picked_rows * grad_mix[:, None, :], axis=-1)
    grad_chosen = gate_probs * (
        grad_weighting - jnp.sum(gate_probs * grad_weighting, axis=-1, keepdims=True)
    )
    grad_logits = jnp.sum(jnp.where(route_hot, grad_chosen[:, :, None], 0.0), axis=1).astype(
        jnp.bfloat16
    )
    router_grad = jnp.dot(mixer_in.T, grad_logits, preferred_element_type=jnp.float32)
    flat_gates = gate_probs.reshape(-1)
    grad_sent = jnp.where(
        filled[:, None],
        (flat_gates[source_pair][:, None] * grad_mix[source_token]).astype(jnp.bfloat16),
        zero_low,
    ).reshape(cap_slots, experts, model_width)
    grad_received = to_owners(grad_sent).reshape(slot_count, model_width)
    grad_active = jnp.dot(grad_received, down_matrix.T, preferred_element_type=jnp.float32)
    down_grad = jnp.dot(active.T, grad_received, preferred_element_type=jnp.float32)
    grad_gate_pre = (
        grad_active * up_pre * sigmoid_gate * (1.0 + gate_pre * (1.0 - sigmoid_gate))
    ).astype(jnp.bfloat16)
    grad_up_pre = (grad_active * silu_gate).astype(jnp.bfloat16)
    gate_grad = jnp.dot(received.T, grad_gate_pre, preferred_element_type=jnp.float32)
    up_grad = jnp.dot(received.T, grad_up_pre, preferred_element_type=jnp.float32)

    def input_term(row_start, row_count):
        return jnp.dot(grad_gate_pre, gate_matrix.T, preferred_element_type=jnp.float32) + jnp.dot(
            grad_up_pre, up_matrix.T, preferred_element_type=jnp.float32
        )

    grad_rows = from_owners(input_term, slot_count, experts, model_width)
    grad_mixer = jnp.dot(
        grad_logits, router_weight.T, preferred_element_type=jnp.float32
    ) + jnp.sum(
        grad_rows[slot_index].reshape(tok_rows, TOP, model_width), axis=1, dtype=jnp.float32
    )
    weighted_second = grad_mixer * gain_second
    second_grad = jnp.sum(grad_mixer * middle * inv_second, axis=0)
    grad_middle = (
        grad_result
        + inv_second * weighted_second
        - middle * inv_second**3 * jnp.mean(middle * weighted_second, axis=-1, keepdims=True)
    )
    grad_attended = (residual_scale * grad_middle).astype(jnp.bfloat16)
    out_grad_t = jnp.dot(grad_attended.T, mixed_low, preferred_element_type=jnp.float32)
    grad_mixed = (
        jnp.dot(grad_attended, out_weight.T, preferred_element_type=jnp.float32)
        .astype(jnp.bfloat16)
        .reshape(tok_rows, key_heads, group_width, HEAD_FEATURES)
    )
    grad_query_seq, grad_key_seq, grad_value_seq = attention_backward(
        query_rows, rotated_keys, value_rows, norms_seq, grad_mixed
    )
    grad_queries_rot = grad_query_seq.reshape(tok_rows, query_heads, HEAD_FEATURES)
    grad_query_pre = (
        rotary_back(grad_queries_rot, cosine_rows, sine_rows)
        .astype(jnp.bfloat16)
        .reshape(tok_rows, query_heads * HEAD_FEATURES)
    )
    grad_key_pre = (
        rotary_back(grad_key_seq, cosine_rows, sine_rows)
        .astype(jnp.bfloat16)
        .reshape(tok_rows, key_heads * HEAD_FEATURES)
    )
    grad_values_low = grad_value_seq.astype(jnp.bfloat16).reshape(
        tok_rows, key_heads * HEAD_FEATURES
    )
    query_grad = jnp.dot(normalized_input.T, grad_query_pre, preferred_element_type=jnp.float32)
    key_grad = jnp.dot(normalized_input.T, grad_key_pre, preferred_element_type=jnp.float32)
    value_grad = jnp.dot(normalized_input.T, grad_values_low, preferred_element_type=jnp.float32)
    normed_term = jnp.dot(grad_query_pre, query_weight.T, preferred_element_type=jnp.float32)
    normed_term = normed_term + jnp.dot(
        grad_key_pre, key_matrix.T, preferred_element_type=jnp.float32
    )
    normed_term = normed_term + jnp.dot(
        grad_values_low, value_matrix.T, preferred_element_type=jnp.float32
    )
    grad_normed = lax.psum(normed_term.astype(jnp.bfloat16), "tp").astype(jnp.float32)
    weighted_first = grad_normed * gain_first
    first_grad = jnp.sum(grad_normed * stream_f * inv_first, axis=0)
    grad_stream = (
        grad_middle
        + inv_first * weighted_first
        - stream_f * inv_first**3 * jnp.mean(stream_f * weighted_first, axis=-1, keepdims=True)
    )
    reduced = (
        lax.psum_scatter(query_grad, "ep", scatter_dimension=0, tiled=True),
        lax.psum_scatter(key_grad, "ep", scatter_dimension=0, tiled=True),
        lax.psum_scatter(value_grad, "ep", scatter_dimension=0, tiled=True),
        lax.psum_scatter(out_grad_t, "ep", scatter_dimension=0, tiled=True),
        lax.psum_scatter(router_grad, "ep", scatter_dimension=0, tiled=True),
        lax.psum_scatter(first_grad, "ep", scatter_dimension=0, tiled=True),
        lax.psum_scatter(second_grad, "ep", scatter_dimension=0, tiled=True),
    )
    return (
        layer_out,
        grad_stream,
        reduced[5],
        reduced[0],
        reduced[1],
        reduced[2],
        reduced[3].T,
        reduced[6],
        reduced[4],
        gate_grad[None],
        up_grad[None],
        down_grad[None],
        rms_stats,
    )


MESH = pl.DeviceIdType.MESH
PLANE = 4
LINES = 4


def flip(place, unit):
    return place + unit * (1 - 2 * lax.rem(lax.div(place, unit), 2))


def flip_line(place, step):
    if step % 2:
        place = flip(place, PLANE)
    if step // 2:
        place = flip(place, 2 * PLANE)
    return place


def matmul(left, right):
    return jnp.dot(left, right, preferred_element_type=jnp.float32)


def matmul_nt(left, right):
    return lax.dot_general(
        left, right, (((1,), (1,)), ((), ())), preferred_element_type=jnp.float32
    )


def matmul_tn(left, right):
    return lax.dot_general(
        left, right, (((0,), (0,)), ((), ())), preferred_element_type=jnp.float32
    )


def lane_halves(value):
    lane = lax.broadcasted_iota(jnp.int32, value.shape, 1)
    low = jnp.where(lane < HEAD_FEATURES, value, 0.0)
    high = jnp.where(lane < HEAD_FEATURES, 0.0, value)
    return low, high


def partner_lanes(value):
    width = value.shape[1]
    quarter = HEAD_FEATURES // 2
    lane = lax.broadcasted_iota(jnp.int32, value.shape, 1)
    ahead = pltpu.roll(value, width - quarter, 1)
    behind = pltpu.roll(value, quarter, 1)
    return jnp.where(lax.rem(lane, HEAD_FEATURES) < quarter, ahead, behind)


def causal_scores(query_block, key_block, row_start):
    scores = score_scale * matmul_nt(query_block, key_block)
    row = lax.broadcasted_iota(jnp.int32, scores.shape, 0) + row_start
    column = lax.broadcasted_iota(jnp.int32, scores.shape, 1)
    return jnp.where(row >= column, scores, masked_score)


def store_slots(slots, values):
    for group in range(values.shape[1] // HEAD_FEATURES):
        pair = group // 2
        low, high = lane_halves(values[:, pair * 128 : pair * 128 + 128])
        if group % 2:
            low = pltpu.roll(high, HEAD_FEATURES, 1)
        else:
            high = pltpu.roll(low, HEAD_FEATURES, 1)
        slots[2 * group] = low.astype(jnp.bfloat16)
        slots[2 * group + 1] = high.astype(jnp.bfloat16)


def front_kernel(*refs):
    tiles = 2 * PLANE
    refs = list(refs)

    def take(count):
        taken = refs[:count]
        del refs[:count]
        return taken

    stream, cotangent, gain_first, gain_second, query_weight, key_weight = take(6)
    value_weight, out_weight, router, routes, cosine, sine = take(6)
    weights = take(3)
    out_parts = take(LINES)
    grow_sum, weighting_sum = take(2)
    kept = take(3)
    landed = take(3)
    mixer_own, probs_own, normed_out, queries_out, keys_out, values_out, mixed_out = take(7)
    attended = take(1)[0]
    mixer, cots, probs, gates, ups, downs = take(6)
    scaled, ggate, gup, grow, grow_in, outs, weighting, weighting_in = take(8)
    part_send, part_recv = take(2)
    load_sem, own_sem, weight_send, weight_recv = take(4)
    relay_send, relay_recv, probs_send, probs_recv, part_sem = take(5)
    result_sem, store_sem, kept_sem = take(3)
    grow_send, grow_recv, weighting_send, weighting_recv = take(4)
    core_send, core_recv, plane_send, plane_recv, ready_sem = take(5)
    held = (gates, ups, downs)
    rows_all, width = mixer.shape
    half = rows_all // LINES
    tokens = 2 * half
    span = gates.shape[2]
    column_tiles = width // span
    heads_width = query_weight.shape[1]
    pieces = heads_width // span
    tall = scaled.shape[1]

    place = lax.axis_index("ep")
    core = lax.axis_index("tp")
    line = lax.div(place, PLANE)
    sibling = (place, 1 - core)
    across = [(flip(place, 1), core), (flip(place, 2), core)]
    partners = [(flip_line(place, step), core) for step in range(LINES)]
    own_rows = pl.ds(pl.multiple_of(core * half, half), half)
    stream_v, normed = outs.at[pl.ds(0, tokens)], outs.at[pl.ds(tokens, tokens)]

    def block_rows_of(block):
        return pl.ds(pl.multiple_of(block * half, half), half)

    line_rows = block_rows_of(line)

    barrier = pltpu.get_barrier_semaphore()
    for other in across + partners[1:] + [sibling]:
        pl.semaphore_signal(barrier, inc=1, device_id=other, device_id_type=MESH)

    def tall_loads(source, column, target, tile, index):
        return [
            pltpu.make_async_copy(
                source.at[pl.ds(start, size), pl.ds(column * span, span)],
                target.at[tile + part, pl.ds(0, size)],
                load_sem.at[index + part],
            )
            for part, (start, size) in enumerate(((0, tall), (tall, width - tall)))
        ]

    loads = [pltpu.make_async_copy(stream, stream_v, load_sem.at[0])]
    for piece in range(pieces):
        loads += tall_loads(query_weight, piece, scaled, 2 * piece, 1 + 2 * piece)
    loads += tall_loads(key_weight, 0, ggate, 0, 1 + 2 * pieces)
    loads += tall_loads(value_weight, 0, ggate, tiles - 2, 3 + 2 * pieces)
    out_loads = [
        pltpu.make_async_copy(
            out_weight.at[:, pl.ds(column * span, span)],
            grow.at[column, pl.ds(0, heads_width)],
            load_sem.at[5 + 2 * pieces + column],
        )
        for column in range(column_tiles)
    ]
    for copy in loads + out_loads:
        copy.start()
    pl.semaphore_wait(barrier, LINES + 2)

    def send(source, target, sems, index, device):
        return pltpu.make_async_remote_copy(
            src_ref=source,
            dst_ref=target,
            send_sem=sems[0].at[index],
            recv_sem=sems[1].at[index],
            device_id=device,
            device_id_type=MESH,
        )

    weight_sems = (weight_send, weight_recv)

    def direct(kind, axis):
        return send(
            weights[kind], held[kind].at[axis + 1], weight_sems, (kind, axis), across[axis]
        )

    def to_sibling(kind, slot):
        source = weights[kind] if slot == 0 else held[kind].at[slot]
        return send(source, held[kind].at[PLANE + slot], weight_sems, (kind, 2 + slot), sibling)

    def onward(kind, axis):
        source, target = held[kind].at[2 - axis], held[kind].at[3]
        if kind == 1:
            part = pl.ds(axis * (width // 2), width // 2)
            source, target = held[kind].at[2 - axis, part], held[kind].at[3, part]
        return send(source, target, weight_sems, (kind, 6 + axis), across[axis])

    onwards = {0: (0,), 1: (0, 1), 2: (1,)}

    def relay(array, hop, downward):
        gathered = (cots, mixer)[array]
        shift = -1 if downward else 1
        block = block_rows_of(jnp.clip(line - shift * hop, 0, LINES - 1))
        source = gathered.at[block]
        if hop == 0 and array == 0:
            source = cotangent.at[own_rows]
        return send(
            source,
            gathered.at[block],
            (relay_send, relay_recv),
            (array, downward, hop),
            (place + shift * PLANE, core),
        )

    def arriving(array, hop, downward):
        gathered = (cots, mixer)[array]
        shift = -1 if downward else 1
        block = block_rows_of(jnp.clip(line - shift * (hop + 1), 0, LINES - 1))
        return send(
            gathered.at[block],
            gathered.at[block],
            (relay_send, relay_recv),
            (array, downward, hop),
            (place + shift * PLANE, core),
        )

    def relay_sends(hop, downward):
        if downward:
            return jnp.logical_and(line > 0, line + hop < LINES)
        return jnp.logical_and(line < LINES - 1, line - hop >= 0)

    def relay_receives(hop, downward):
        if downward:
            return line + 1 + hop < LINES
        return line - 1 - hop >= 0

    def start_relay(array, hop):
        for downward in (0, 1):

            @pl.when(relay_sends(hop, downward))
            def _():
                relay(array, hop, downward).start()

    def receive_relay(array, hop):
        for downward in (0, 1):

            @pl.when(relay_receives(hop, downward))
            def _():
                arriving(array, hop, downward).wait_recv()

    def finish_relay(array, hop):
        for downward in (0, 1):

            @pl.when(relay_sends(hop, downward))
            def _():
                relay(array, hop, downward).wait_send()

    for kind in range(3):
        for axis in (0, 1):
            direct(kind, axis).start()
    start_relay(0, 0)
    own_copies = [
        pltpu.make_async_copy(weights[kind], held[kind].at[0], own_sem.at[kind])
        for kind in range(3)
    ]
    own_copies.append(
        pltpu.make_async_copy(cotangent.at[own_rows], cots.at[line_rows], own_sem.at[3])
    )
    for kind in range(3):
        to_sibling(kind, 0).start()
    for copy in own_copies:
        copy.start()
    weighting[...] = jnp.zeros_like(weighting)

    loads[0].wait()
    stream_f = stream_v[...].astype(jnp.float32)
    inverse = lax.rsqrt(jnp.mean(stream_f * stream_f, axis=-1, keepdims=True) + epsilon)
    normed[...] = (stream_f * inverse * gain_first[...]).astype(jnp.bfloat16)
    for copy in loads[1:]:
        copy.wait()

    def projected(target, tile):
        return matmul(normed[:, :tall], target[tile]) + matmul(
            normed[:, tall:], target[tile + 1, : width - tall, :]
        )

    def rotated(pre):
        turned = []
        for pair in range(span // 128):
            part = pre[:, pair * 128 : pair * 128 + 128]
            turned.append(part * cosine[...] + partner_lanes(part) * sine[...])
        return jnp.concatenate(turned, axis=1).astype(jnp.bfloat16)

    low_rows, high_rows = pl.ds(0, tokens), pl.ds(tokens, tokens)
    for piece in range(pieces):
        ggate[3 + piece, low_rows, :] = rotated(projected(scaled, 2 * piece))
    key_rows = rotated(projected(ggate, 0))
    ggate[2, low_rows, :] = key_rows
    value_rows = projected(ggate, tiles - 2).astype(jnp.bfloat16)
    ggate[2, high_rows, :] = value_rows

    def store_overlaid(values, rows):
        for group in range(values.shape[1] // HEAD_FEATURES):
            pair = group // 2
            low, high = lane_halves(values[:, pair * 128 : pair * 128 + 128].astype(jnp.float32))
            if group % 2:
                low = pltpu.roll(high, HEAD_FEATURES, 1)
            else:
                high = pltpu.roll(low, HEAD_FEATURES, 1)
            gup[2 * group, rows, :128] = low.astype(jnp.bfloat16)
            gup[2 * group + 1, rows, :128] = high.astype(jnp.bfloat16)

    store_overlaid(key_rows, low_rows)
    store_overlaid(value_rows, high_rows)
    results = [
        pltpu.make_async_copy(normed, normed_out, result_sem.at[0]),
        pltpu.make_async_copy(ggate.at[2, low_rows], keys_out, result_sem.at[1]),
        pltpu.make_async_copy(ggate.at[2, high_rows], values_out, result_sem.at[2]),
    ]
    for piece in range(pieces):
        results.append(
            pltpu.make_async_copy(
                ggate.at[3 + piece, low_rows],
                queries_out.at[:, pl.ds(piece * span, span)],
                result_sem.at[3 + piece],
            )
        )
    for copy in results:
        copy.start()
    group = heads_width // key_weight.shape[1]
    blocks = 2
    block_rows = tokens // blocks

    def head_pair(pair, carry):
        tile = 3 + lax.div(pair, 2)
        here = pl.ds(pl.multiple_of(lax.rem(pair, 2) * 128, 128), 128)
        for block in range(blocks):
            start = block * block_rows
            reach = start + block_rows
            total = jnp.zeros((block_rows, 128), jnp.float32)
            query_block = ggate[tile, pl.ds(start, block_rows), here]
            for parity in range(2):
                slot = 2 * lax.div(2 * pair + parity, group) + parity
                scores = causal_scores(query_block, gup[slot, pl.ds(0, reach), :128], start)
                weight = jnp.exp(scores - jnp.max(scores, axis=-1, keepdims=True))
                weight = weight / jnp.sum(weight, axis=-1, keepdims=True)
                total = total + matmul(
                    weight.astype(jnp.bfloat16), gup[slot, pl.ds(tokens, reach), :128]
                )
            ggate[tile, pl.ds(tokens + start, block_rows), here] = total.astype(jnp.bfloat16)
        return carry

    lax.fori_loop(0, heads_width // 128, head_pair, 0)
    receive_relay(0, 0)
    start_relay(0, 1)
    for piece in range(pieces):
        results.append(
            pltpu.make_async_copy(
                ggate.at[3 + piece, high_rows],
                mixed_out.at[:, pl.ds(piece * span, span)],
                result_sem.at[3 + pieces + piece],
            )
        )
    for copy in results[3 + pieces :]:
        copy.start()
    for copy in out_loads:
        copy.wait()

    def out_product(first_row):
        rows = pl.ds(pl.multiple_of(tokens + first_row * half, half), half)
        found = []
        for column in range(column_tiles):
            found.append(
                sum(
                    matmul(
                        ggate[3 + piece, rows, :],
                        grow[column, pl.ds(piece * span, span), :],
                    )
                    for piece in range(pieces)
                )
            )
        return jnp.concatenate(found, axis=1)

    part_send[...] = out_product(1 - core).astype(jnp.bfloat16)
    part_copy = pltpu.make_async_remote_copy(
        src_ref=part_send,
        dst_ref=part_recv,
        send_sem=part_sem.at[0],
        recv_sem=part_sem.at[1],
        device_id=sibling,
        device_id_type=MESH,
    )
    part_copy.start()
    own_part = out_product(core)
    part_copy.wait()
    attended_half = own_part + part_recv[...].astype(jnp.float32)
    attended[...] = attended_half.astype(jnp.bfloat16)
    middle = stream_v[own_rows, :].astype(jnp.float32) + residual_scale * attended_half
    inverse = lax.rsqrt(jnp.mean(middle * middle, axis=-1, keepdims=True) + epsilon)
    mixer[line_rows, :] = (middle * inverse * gain_second[...]).astype(jnp.bfloat16)
    start_relay(1, 0)
    logits = matmul(mixer[line_rows, :], router[...])
    lane = lax.broadcasted_iota(jnp.int32, logits.shape, 1)
    routed = lane < 0
    for entry in range(TOP):
        routed = jnp.logical_or(routed, lane == routes[own_rows, entry : entry + 1])
    largest = jnp.max(jnp.where(routed, logits, masked_score), axis=-1, keepdims=True)
    gate_exp = jnp.where(routed, jnp.exp(jnp.minimum(logits - largest, 0.0)), 0.0)
    probs[line_rows, :] = gate_exp / jnp.sum(gate_exp, axis=-1, keepdims=True)

    def probs_copy(step):
        return send(
            probs.at[line_rows],
            probs.at[line_rows],
            (probs_send, probs_recv),
            (step,),
            partners[step],
        )

    def probs_arriving(step):
        theirs = block_rows_of(lax.div(partners[step][0], PLANE))
        return send(
            probs.at[theirs],
            probs.at[theirs],
            (probs_send, probs_recv),
            (step,),
            partners[step],
        )

    for step in range(1, LINES):
        probs_copy(step).start()
    own_copies.append(pltpu.make_async_copy(probs.at[line_rows], probs_own, own_sem.at[4]))
    own_copies.append(pltpu.make_async_copy(mixer.at[line_rows], mixer_own, own_sem.at[5]))
    for copy in own_copies[4:]:
        copy.start()

    def pass_on(kind):
        for axis in (0, 1):
            direct(kind, axis).wait_recv()
        for axis in onwards[kind]:
            onward(kind, axis).start()
        for slot in (1, 2):
            to_sibling(kind, slot).start()

    def hidden_tile(block, tile):
        rows = block_rows_of(block)
        step = lax.rem(tile, PLANE)
        owner = lax.rem(place, PLANE)
        owner = jnp.where(lax.rem(step, 2) == 1, flip(owner, 1), owner)
        owner = jnp.where(lax.div(step, 2) == 1, flip(owner, 2), owner)
        chosen = lax.broadcasted_iota(jnp.int32, (half, 128), 1) == line * PLANE + owner
        prob = jnp.sum(jnp.where(chosen, probs[rows, :], 0.0), axis=1, keepdims=True)
        gate_pre = matmul(mixer[rows, :], gates[tile])
        up_pre = matmul(mixer[rows, :], ups[tile])
        grad_raw = residual_scale * matmul_nt(cots[rows, :], downs[tile])
        sigmoid_gate = 1.0 / (1.0 + jnp.exp(-gate_pre))
        silu_gate = gate_pre * sigmoid_gate
        active = silu_gate * up_pre
        share = jnp.sum(active * grad_raw, axis=1, keepdims=True)
        weighting[rows, :] += jnp.where(chosen, share, 0.0)
        grad_active = prob * grad_raw
        scaled[tile, rows, :] = (prob * active).astype(jnp.bfloat16)
        ggate[tile, rows, :] = (
            grad_active * up_pre * sigmoid_gate * (1.0 + gate_pre * (1.0 - sigmoid_gate))
        ).astype(jnp.bfloat16)
        gup[tile, rows, :] = (grad_active * silu_gate).astype(jnp.bfloat16)

    def early_tiles(block):
        def body(index, carry):
            hidden_tile(block, index + lax.div(index, 3))
            return carry

        lax.fori_loop(0, 6, body, 0)

    def late_tiles(block):
        def body(index, carry):
            hidden_tile(block, 3 + PLANE * index)
            return carry

        lax.fori_loop(0, 2, body, 0)

    def grow_tiles(block):
        rows = block_rows_of(block)

        def body(column, carry):
            here = pl.ds(pl.multiple_of(column * span, span), span)
            total = matmul_nt(ggate[0, rows, :], gates[0, here, :])
            for tile in range(1, tiles):
                total = total + matmul_nt(ggate[tile, rows, :], gates[tile, here, :])
            for tile in range(tiles):
                total = total + matmul_nt(gup[tile, rows, :], ups[tile, here, :])
            grow[column, rows, :] = total.astype(jnp.bfloat16)
            return carry

        lax.fori_loop(0, column_tiles, body, 0)

    def remote_block(index):
        near = (jnp.where(line == 0, 1, jnp.where(line == 1, 0, jnp.where(line == 2, 3, 2))))
        middle_block = jnp.where(line < 2, 2, 1)
        distant = jnp.where(line < 2, 3, 0)
        return (near, middle_block, distant)[index]

    def home_of(block):
        return (place + (block - line) * PLANE, core)

    def grow_copy(index):
        block = remote_block(index)
        return pltpu.make_async_remote_copy(
            src_ref=grow.at[:, block_rows_of(block)],
            dst_ref=grow_in.at[line],
            send_sem=grow_send.at[index],
            recv_sem=grow_recv.at[line],
            device_id=home_of(block),
            device_id_type=MESH,
        )

    def weighting_copy(index):
        block = remote_block(index)
        return pltpu.make_async_remote_copy(
            src_ref=weighting.at[block_rows_of(block)],
            dst_ref=weighting_in.at[line],
            send_sem=weighting_send.at[index],
            recv_sem=weighting_recv.at[line],
            device_id=home_of(block),
            device_id_type=MESH,
        )

    def returned(index):
        block = remote_block(index)
        return [
            pltpu.make_async_remote_copy(
                src_ref=target.at[block],
                dst_ref=target.at[block],
                send_sem=sems[0].at[index],
                recv_sem=sems[1].at[block],
                device_id=home_of(block),
                device_id_type=MESH,
            )
            for target, sems in (
                (grow_in, (grow_send, grow_recv)),
                (weighting_in, (weighting_send, weighting_recv)),
            )
        ]

    def send_back(index):
        grow_tiles(remote_block(index))
        weighting_copy(index).start()
        grow_copy(index).start()

    pass_on(0)
    receive_relay(1, 0)
    start_relay(1, 1)
    receive_relay(0, 1)
    start_relay(0, 2)
    pass_on(1)
    pass_on(2)
    for copy in results:
        copy.wait()
    for copy in own_copies:
        copy.wait()
    for step in range(1, LINES):
        probs_copy(step).wait_send()
        probs_arriving(step).wait_recv()
    for kind in range(3):
        for slot in range(3):
            to_sibling(kind, slot).wait_recv()
    early_tiles(remote_block(0))
    receive_relay(1, 1)
    start_relay(1, 2)
    for kind in range(3):
        for axis in onwards[kind]:
            onward(kind, axis).wait_recv()
        to_sibling(kind, 3).start()
    early_tiles(line)
    for kind in range(3):
        to_sibling(kind, 3).wait_recv()
    late_tiles(remote_block(0))
    send_back(0)
    early_tiles(remote_block(1))
    late_tiles(remote_block(1))
    send_back(1)
    receive_relay(0, 2)
    receive_relay(1, 2)
    early_tiles(remote_block(2))
    late_tiles(remote_block(2))
    send_back(2)
    late_tiles(line)
    grow_tiles(line)

    def out_tile(column, carry):
        here = pl.ds(pl.multiple_of(column * span, span), span)
        total = matmul(scaled[0], downs[0, :, here])
        for tile in range(1, tiles):
            total = total + matmul(scaled[tile], downs[tile, :, here])
        outs[:, here] = total.astype(jnp.bfloat16)
        return carry

    lax.fori_loop(0, column_tiles, out_tile, 0)
    stores = [
        pltpu.make_async_copy(
            outs.at[block_rows_of(lax.div(partners[step][0], PLANE))],
            out_parts[step],
            store_sem.at[step],
        )
        for step in range(LINES)
    ]
    for copy in stores:
        copy.start()
    for kind in range(3):
        for slot in range(PLANE):
            to_sibling(kind, slot).wait_send()
        for axis in (0, 1):
            direct(kind, axis).wait_send()
        for axis in onwards[kind]:
            onward(kind, axis).wait_send()
    for array in (0, 1):
        for hop in range(LINES - 1):
            finish_relay(array, hop)

    pl.semaphore_signal(ready_sem, inc=1, device_id=sibling, device_id_type=MESH)
    pl.semaphore_wait(ready_sem, 1)
    def tile_order(index):
        return jnp.where(index == 0, 3, jnp.where(index == 3, 0, index))

    def tile_grads(tile):
        yield matmul_tn(mixer[...], ggate[tile])
        yield matmul_tn(mixer[...], gup[tile])
        yield residual_scale * matmul_tn(scaled[tile], cots[...])

    def core_copy(kind, step):
        return pltpu.make_async_remote_copy(
            src_ref=held[kind].at[PLANE + step],
            dst_ref=held[kind].at[step],
            send_sem=core_send.at[kind, step],
            recv_sem=core_recv.at[kind, step],
            device_id=sibling,
            device_id_type=MESH,
        )

    def sibling_tile(index, carry):
        step = tile_order(index)
        for kind, grad in enumerate(tile_grads(PLANE + step)):
            held[kind][PLANE + step] = grad.astype(jnp.bfloat16)
            core_copy(kind, step).start()
        return carry

    lax.fori_loop(0, PLANE, sibling_tile, 0)

    def plane_copy(kind, axis, passing):
        span_rows = held[kind].shape[1] // 2
        step = 3 if passing else axis + 1
        return pltpu.make_async_remote_copy(
            src_ref=held[kind].at[step, pl.ds(axis * span_rows, span_rows)],
            dst_ref=landed[kind].at[axis, passing],
            send_sem=plane_send.at[kind, axis, passing],
            recv_sem=plane_recv.at[kind, axis, passing],
            device_id=across[axis],
            device_id_type=MESH,
        )

    def kept_copy(kind, step):
        return pltpu.make_async_copy(
            held[kind].at[step], kept[kind].at[step], kept_sem.at[kind, step]
        )

    def own_tile(index, carry):
        step = tile_order(index)
        for kind, grad in enumerate(tile_grads(step)):
            core_copy(kind, step).wait_recv()
            held[kind][step] = (grad + held[kind][step].astype(jnp.float32)).astype(jnp.bfloat16)

            @pl.when(step == 3)
            def _():
                for axis in (0, 1):
                    plane_copy(kind, axis, 1).start()

            for axis in (0, 1):

                @pl.when(step == axis + 1)
                def _():
                    plane_copy(kind, axis, 0).start()

            @pl.when(step < 3)
            def _():
                kept_copy(kind, step).start()

        return carry

    lax.fori_loop(0, PLANE, own_tile, 0)
    for index in range(LINES - 1):
        weighting_copy(index).wait_send()
        grow_copy(index).wait_send()
        for copy in returned(index):
            copy.wait_recv()
    total = weighting[line_rows, :]
    for index in range(LINES - 1):
        total = total + weighting_in[remote_block(index)]
    weighting_sum[...] = total
    for column in range(column_tiles):
        here = pl.ds(column * span, span)
        total = grow[column, line_rows, :].astype(jnp.float32)
        for index in range(LINES - 1):
            total = total + grow_in[remote_block(index), column].astype(jnp.float32)
        grow_sum[:, here] = total
    for copy in stores:
        copy.wait()
    for kind in range(3):
        for step in range(PLANE):
            core_copy(kind, step).wait_send()
        for step in range(3):
            kept_copy(kind, step).wait()
        for axis in (0, 1):
            for passing in (0, 1):
                plane_copy(kind, axis, passing).wait()


def run_front(operands, weights):
    low, wide = jnp.bfloat16, jnp.float32
    shape = jax.ShapeDtypeStruct
    vmem = pltpu.VMEM
    far = pl.BlockSpec(memory_space=pl.ANY)
    near = pl.BlockSpec(memory_space=pltpu.VMEM)
    tokens, width = operands[0].shape
    half = tokens // 2
    rows = LINES * half
    query_width, key_width = operands[4].shape[1], operands[5].shape[1]
    span = weights[0].shape[1]
    tiles = 2 * PLANE
    dma = pltpu.SemaphoreType.DMA
    pieces = query_width // span
    columns = width // span
    return pl.pallas_call(
        front_kernel,
        name="front",
        out_shape=(
            *[shape((half, width), low)] * LINES,
            shape((half, width), wide),
            shape((half, 128), wide),
            shape((3, width, span), low),
            shape((3, width, span), low),
            shape((3, span, width), low),
            shape((2, 2, width // 2, span), low),
            shape((2, 2, width // 2, span), low),
            shape((2, 2, span // 2, width), low),
            shape((half, width), low),
            shape((half, 128), wide),
            shape((tokens, width), low),
            shape((tokens, query_width), low),
            shape((tokens, key_width), low),
            shape((tokens, key_width), low),
            shape((tokens, query_width), low),
            shape((half, width), low),
        ),
        in_specs=[far, far, near, near, far, far, far, far, near, near, near, near] + [far] * 3,
        out_specs=(*[far] * LINES, near, near, *[far] * 13, near),
        scratch_shapes=[
            vmem((rows, width), low),
            vmem((rows, width), low),
            vmem((rows, 128), wide),
            vmem((tiles, width, span), low),
            vmem((tiles, width, span), low),
            vmem((tiles, span, width), low),
            vmem((tiles, rows, span), low),
            vmem((tiles, rows, span), low),
            vmem((tiles, rows, span), low),
            vmem((columns, rows, span), low),
            vmem((LINES, columns, half, span), low),
            vmem((rows, width), low),
            vmem((rows, 128), wide),
            vmem((LINES, half, 128), wide),
            vmem((half, width), low),
            vmem((half, width), low),
            dma((5 + 2 * pieces + columns,)),
            dma((6,)),
            dma((3, 8)),
            dma((3, 8)),
            dma((2, 2, LINES - 1)),
            dma((2, 2, LINES - 1)),
            dma((LINES,)),
            dma((LINES,)),
            dma((2,)),
            dma((3 + 2 * pieces,)),
            dma((LINES,)),
            dma((3, 3)),
            dma((LINES - 1,)),
            dma((LINES,)),
            dma((LINES - 1,)),
            dma((LINES,)),
            dma((3, PLANE)),
            dma((3, PLANE)),
            dma((3, 2, 2)),
            dma((3, 2, 2)),
            pltpu.SemaphoreType.REGULAR,
        ],
        compiler_params=pltpu.CompilerParams(
            collective_id=0, has_side_effects=True, vmem_limit_bytes=63 << 20
        ),
        cost_estimate=pl.CostEstimate(
            flops=18 * rows * width * span * tiles,
            bytes_accessed=12 * width * span * tiles,
            transcendentals=0,
        ),
    )(*operands, *weights)


def back_kernel(*refs):
    refs = list(refs)

    def take(count):
        taken = refs[:count]
        del refs[:count]
        return taken

    out_parts = take(LINES)
    grow_sum, weighting_sum = take(2)
    kept, landed = take(3), take(3)
    stream, cotangent, gain_first, gain_second, query_weight, key_weight = take(6)
    value_weight, out_weight, router, cosine, sine = take(5)
    mixer_own, probs_own, normed, queries, keys, values, mixed, attended = take(8)
    layer_out, grad_stream, out_result_a, out_result_b, query_result, rest_result = take(6)
    expert_grads = take(3)
    small_out = take(1)[0]
    stream_v, cot_v, query_v, key_v, value_v, out_v, normed_v, queries_v = take(8)
    mixed_v, grow_v, attended_v, out_in, layer_v = take(5)
    key_v2, value_v2, mixer_v, probs_v, weighting_v = take(5)
    key_slots, value_slots, key_totals, value_totals = take(4)
    middle_grads, attended_grads, mixed_grads = take(3)
    key_grads, value_grads, normed_recv = take(3)
    normed_send, first_terms = attended_grads, layer_v
    second_terms, query_grads = cot_v, mixed_v
    own_parts, landed_v, plane_in = take(3), take(3), take(3)
    out_source_a, out_source_b, query_source, rest_source = take(4)
    scatter_scratch = [take(5) for _ in range(4)]
    last_send, last_recv = take(2)
    load_sem, part_sem, out_send, out_recv, pair_sem, plane_send, plane_recv = take(7)
    store_sem = take(1)[0]
    tokens, width = stream_v.shape
    half = tokens // 2

    place = lax.axis_index("ep")
    core = lax.axis_index("tp")
    sibling = (place, 1 - core)
    across = [flip(place, 1), flip(place, 2)]
    partners = [flip_line(place, step) for step in range(LINES)]
    bits = [lax.rem(place, 2), lax.rem(lax.div(place, 2), 2)]
    own_rows = pl.ds(pl.multiple_of(core * half, half), half)

    barrier = pltpu.get_barrier_semaphore()
    for other in across + partners[1:]:
        pl.semaphore_signal(barrier, inc=1, device_id=(other, core), device_id_type=MESH)
    pl.semaphore_signal(barrier, inc=1, device_id=sibling, device_id_type=MESH)

    pairs = [
        (grow_sum, grow_v),
        (weighting_sum, weighting_v),
        (attended, attended_v),
        (probs_own, probs_v),
        (stream, stream_v),
        (cotangent.at[own_rows], cot_v),
        (out_weight, out_v),
        (mixed, mixed_v),
        (queries, queries_v),
        (keys, key_v2),
        (values, value_v2),
        (normed, normed_v),
        (query_weight, query_v),
        (key_weight, key_v),
        (value_weight, value_v),
        (mixer_own, mixer_v),
        (out_parts[0], mixer_v),
    ]
    loads = [
        pltpu.make_async_copy(source, target, load_sem.at[index])
        for index, (source, target) in enumerate(pairs)
    ]

    def part_copies(kind, final):
        rows = own_parts[kind].shape[1]
        low, high = pl.ds(0, rows), pl.ds(rows, rows)
        first, second = (0, 0) if final else (2, 1)
        return [
            pltpu.make_async_copy(source, target, part_sem.at[kind, index])
            for index, (source, target) in enumerate(
                (
                    (kept[kind].at[first, low], own_parts[kind].at[0]),
                    (kept[kind].at[second, high], own_parts[kind].at[1]),
                )
            )
        ]

    def landed_copy(kind):
        return pltpu.make_async_copy(landed[kind], landed_v[kind], part_sem.at[kind, 2])

    for copy in loads[:6]:
        copy.start()
    for kind in range(3):
        landed_copy(kind).start()
        for copy in part_copies(kind, False):
            copy.start()
    for copy in loads[6:-1]:
        copy.start()
    pl.semaphore_wait(barrier, LINES + 2)

    def send(source, target, sems, index, device):
        return pltpu.make_async_remote_copy(
            src_ref=source,
            dst_ref=target,
            send_sem=sems[0].at[index],
            recv_sem=sems[1].at[index],
            device_id=device,
            device_id_type=MESH,
        )

    def out_copy(step):
        return send(
            out_parts[step],
            out_in.at[step - 1],
            (out_send, out_recv),
            (step - 1,),
            (partners[step], core),
        )

    for step in (3, 2, 1):
        out_copy(step).start()

    for copy in loads[:6]:
        copy.wait()
    middle = stream_v[own_rows, :].astype(jnp.float32) + residual_scale * attended_v[...].astype(jnp.float32)
    inverse = lax.rsqrt(jnp.mean(middle * middle, axis=-1, keepdims=True) + epsilon)
    probs = probs_v[...]
    weighting = weighting_v[...]
    grad_chosen = probs * (weighting - jnp.sum(probs * weighting, axis=-1, keepdims=True))
    grad_logits = grad_chosen.astype(jnp.bfloat16)
    grad_mixer = matmul_nt(grad_logits, router[...]) + grow_v[...]
    weighted = grad_mixer * gain_second[...]
    grad_middle = (
        cot_v[...].astype(jnp.float32)
        + inverse * weighted
        - middle * (inverse * inverse * inverse)
        * jnp.mean(middle * weighted, axis=-1, keepdims=True)
    )
    middle_grads[own_rows, :] = grad_middle.astype(jnp.bfloat16)
    second_terms[...] = (grad_mixer * middle * inverse).astype(jnp.bfloat16)

    def pair_copy(source, target, index):
        return pltpu.make_async_remote_copy(
            src_ref=source,
            dst_ref=target,
            send_sem=pair_sem.at[0, index],
            recv_sem=pair_sem.at[1, index],
            device_id=sibling,
            device_id_type=MESH,
        )

    middle_copy = pair_copy(middle_grads.at[own_rows], middle_grads.at[own_rows], 0)
    middle_copy.start()

    def plane_copy(kind, axis):
        return send(
            landed_v[kind].at[axis, 1],
            plane_in[kind].at[axis],
            (plane_send, plane_recv),
            (kind, axis),
            (across[1 - axis], core),
        )

    for kind in range(3):
        landed_copy(kind).wait()
        for copy in part_copies(kind, False):
            copy.wait()
        for axis in (0, 1):
            landed_v[kind][axis, 1] = (
                own_parts[kind][axis].astype(jnp.float32)
                + landed_v[kind][axis, 1].astype(jnp.float32)
            ).astype(jnp.bfloat16)
            plane_copy(kind, axis).start()
        for copy in part_copies(kind, True):
            copy.start()

    slab = out_result_a.shape[0]
    order = (3, 2, 1, 0)
    plans = list(
        zip(
            (out_source_a, out_source_b, query_source, rest_source),
            (out_result_a, out_result_b, query_result, rest_result),
            scatter_scratch,
        )
    )

    def rows_of(step, first, second_same, first_same):
        other_line = lax.div(partners[step], PLANE)
        first_bit = bits[first] if first_same else 1 - bits[first]
        second_bit = bits[1 - first] if second_same else 1 - bits[1 - first]
        index = other_line * PLANE + first_bit * (1 + first) + second_bit * (2 - first)
        return pl.ds(pl.multiple_of(index * slab, slab), slab)

    def first_copy(number, step, same):
        source, _, scratch = plans[number]
        first = number % 2
        index = step * 2 + same
        return send(
            source.at[rows_of(step, first, same, False)],
            scratch[0].at[index],
            (scratch[4].at[0], scratch[4].at[1]),
            (index,),
            (across[first], core),
        )

    def second_copy(number, step):
        scratch = plans[number][2]
        return send(
            scratch[1].at[step],
            scratch[2].at[step],
            (scratch[4].at[2], scratch[4].at[3]),
            (step,),
            (across[1 - number % 2], core),
        )

    def line_copy(number, step):
        scratch = plans[number][2]
        return send(
            scratch[1].at[step],
            scratch[3].at[step],
            (scratch[4].at[4], scratch[4].at[5]),
            (step,),
            (partners[step], core),
        )

    def start_scatter(number):
        for step in order:
            for same in (0, 1):
                first_copy(number, step, same).start()

    def add_first(number, step, same):
        source, _, scratch = plans[number]
        first_copy(number, step, same).wait()
        mine = source[rows_of(step, number % 2, same, True), :].astype(jnp.float32)
        return mine + scratch[0][step * 2 + same].astype(jnp.float32)

    def finish_first(number, step):
        plans[number][2][1][step] = add_first(number, step, 0).astype(jnp.bfloat16)
        second_copy(number, step).start()

    def finish_second(number, step):
        _, result, scratch = plans[number]
        total = add_first(number, step, 1)
        second_copy(number, step).wait()
        total = total + scratch[2][step].astype(jnp.float32)
        if step:
            scratch[1][step] = total.astype(jnp.bfloat16)
            line_copy(number, step).start()
        else:
            result[...] = total

    def finish_line(number):
        _, result, scratch = plans[number]
        for step in order[:-1]:
            line_copy(number, step).wait()
            result[...] += scratch[3][step].astype(jnp.float32)

    middle_copy.wait()
    attended_grads[...] = (residual_scale * middle_grads[...].astype(jnp.float32)).astype(
        jnp.bfloat16
    )
    loads[6].wait()
    loads[7].wait()
    columns = out_source_a.shape[1]
    out_source_a[...] = matmul_tn(attended_grads[...], mixed_v[:, :columns]).astype(jnp.bfloat16)
    start_scatter(0)
    out_source_b[...] = matmul_tn(attended_grads[...], mixed_v[:, columns:]).astype(jnp.bfloat16)
    start_scatter(1)
    mixed_grads[...] = matmul_nt(attended_grads[...], out_v[...]).astype(jnp.bfloat16)
    for copy in loads[8:11]:
        copy.wait()
    store_slots(key_slots, key_v2[...].astype(jnp.float32))
    store_slots(value_slots, value_v2[...].astype(jnp.float32))
    key_totals[...] = jnp.zeros_like(key_totals)
    value_totals[...] = jnp.zeros_like(value_totals)
    group = query_v.shape[1] // key_v.shape[1]
    blocks = 2
    block_rows = tokens // blocks

    def turned_back(value, cosines, sines):
        return (value * cosines - partner_lanes(value) * sines).astype(jnp.bfloat16)

    def head_pair(pair, carry):
        here = pl.ds(pl.multiple_of(pair * 128, 128), 128)
        for block in range(blocks):
            rows = slice(block * block_rows, (block + 1) * block_rows)
            reach = (block + 1) * block_rows
            total = jnp.zeros((block_rows, 128), jnp.float32)
            query_block = queries_v[rows, here]
            grad_block = mixed_grads[rows, here]
            for parity in range(2):
                slot = 2 * lax.div(2 * pair + parity, group) + parity
                key_block = key_slots[slot, :reach, :]
                scores = causal_scores(query_block, key_block, block * block_rows)
                weight = jnp.exp(scores - jnp.max(scores, axis=-1, keepdims=True))
                weight = weight / jnp.sum(weight, axis=-1, keepdims=True)
                grad_probs = matmul_nt(grad_block, value_slots[slot, :reach, :])
                inner = jnp.sum(weight * grad_probs, axis=-1, keepdims=True)
                grad_scores = (weight * (grad_probs - inner)).astype(jnp.bfloat16)
                total = total + matmul(grad_scores, key_block)
                key_totals[slot, :reach, :] += matmul_tn(grad_scores, query_block)
                value_totals[slot, :reach, :] += matmul_tn(
                    weight.astype(jnp.bfloat16), grad_block
                )
            query_grads[rows, here] = turned_back(
                score_scale * total, cosine[rows, :], sine[rows, :]
            )
        return carry

    lax.fori_loop(0, query_v.shape[1] // 128, head_pair, 0)

    def gathered_pairs(totals):
        found = []
        for pair in range(key_v.shape[1] // 128):
            first, second = 4 * pair, 4 * pair + 2
            low = lane_halves(totals[first])[0] + pltpu.roll(
                lane_halves(totals[first + 1])[1], HEAD_FEATURES, 1
            )
            high = lane_halves(totals[second + 1])[1] + pltpu.roll(
                lane_halves(totals[second])[0], HEAD_FEATURES, 1
            )
            found.append(low + high)
        return found

    for pair, value in enumerate(gathered_pairs(key_totals)):
        key_grads[:, pair * 128 : pair * 128 + 128] = turned_back(
            score_scale * value, cosine[...], sine[...]
        )
    for pair, value in enumerate(gathered_pairs(value_totals)):
        value_grads[:, pair * 128 : pair * 128 + 128] = value.astype(jnp.bfloat16)
    for copy in loads[11:-1]:
        copy.wait()
    query_source[...] = matmul_tn(normed_v[...], query_grads[...]).astype(jnp.bfloat16)
    start_scatter(2)
    normed_send[...] = (
        matmul_nt(query_grads[...], query_v[...])
        + matmul_nt(key_grads[...], key_v[...])
        + matmul_nt(value_grads[...], value_v[...])
    ).astype(jnp.bfloat16)
    normed_copy = pair_copy(normed_send, normed_recv, 1)
    normed_copy.start()
    key_width = key_grads.shape[1]
    rest_source[:, :key_width] = matmul_tn(normed_v[...], key_grads[...]).astype(jnp.bfloat16)
    rest_source[:, key_width : 2 * key_width] = matmul_tn(
        normed_v[...], value_grads[...]
    ).astype(jnp.bfloat16)
    for step in order:
        finish_first(0, step)
        finish_first(1, step)
    normed_copy.wait()

    def stream_rows(rows):
        grad_normed = normed_send[rows, :].astype(jnp.float32) + normed_recv[rows, :].astype(
            jnp.float32
        )
        stream_f = stream_v[rows, :].astype(jnp.float32)
        inverse = lax.rsqrt(jnp.mean(stream_f * stream_f, axis=-1, keepdims=True) + epsilon)
        weighted = grad_normed * gain_first[...]
        total = (
            middle_grads[rows, :].astype(jnp.float32)
            + inverse * weighted
            - stream_f * (inverse * inverse * inverse)
            * jnp.mean(stream_f * weighted, axis=-1, keepdims=True)
        )
        return grad_normed * stream_f * inverse, total

    first_terms[...] = stream_rows(own_rows)[0].astype(jnp.bfloat16)
    lane = lax.broadcasted_iota(jnp.int32, (half, 128), 1)
    experts = LINES * PLANE
    rest_source[:, 2 * key_width :] = (
        matmul_tn(mixer_v[...], grad_logits)
        + matmul_tn(second_terms[...], (lane == experts).astype(jnp.bfloat16))
        + matmul_tn(first_terms[...], (lane == experts + 1).astype(jnp.bfloat16))
    ).astype(jnp.bfloat16)
    loads[-1].start()
    start_scatter(3)
    for position in range(2):
        rows = slice(position * half, position * half + half)
        normed_recv[rows, :] = stream_rows(rows)[1].astype(jnp.bfloat16)
    stream_copy = pltpu.make_async_copy(normed_recv, grad_stream, store_sem.at[4])
    stream_copy.start()
    for step in order:
        finish_second(0, step)
        finish_second(1, step)
    for step in order:
        finish_first(2, step)
        finish_first(3, step)
    for step in (1, 2, 3):
        out_copy(step).wait()
    loads[-1].wait()
    mixture = mixer_v[...].astype(jnp.float32)
    for step in range(1, LINES):
        mixture = mixture + out_in[step - 1].astype(jnp.float32)
    middle = stream_v[own_rows, :].astype(jnp.float32) + residual_scale * attended_v[...].astype(jnp.float32)
    result = middle + residual_scale * mixture
    layer_v[...] = result.astype(jnp.bfloat16)
    layer_pair = pair_copy(layer_v, layer_out.at[own_rows], 2)
    layer_pair.start()
    layer_own = pltpu.make_async_copy(layer_v, layer_out.at[own_rows], store_sem.at[0])
    layer_own.start()
    row_lane = lax.broadcasted_iota(jnp.int32, (8, 128), 1)
    squares = jnp.zeros((8, 128), jnp.float32)
    for index, value in enumerate((result, attended_v[...].astype(jnp.float32), mixture)):
        total = jnp.sum(jnp.sum(value * value, axis=1, keepdims=True), axis=0, keepdims=True)
        squares = jnp.where(row_lane == index, total, squares)
    for step in order:
        finish_second(2, step)
        finish_second(3, step)
    def expert_copy(kind):
        return pltpu.make_async_copy(own_parts[kind], expert_grads[kind], store_sem.at[1 + kind])

    for kind in range(3):
        for copy in part_copies(kind, True):
            copy.wait()
        for axis in (0, 1):
            plane_copy(kind, axis).wait()
            own_parts[kind][axis] = (
                own_parts[kind][axis].astype(jnp.float32)
                + landed_v[kind][axis, 0].astype(jnp.float32)
                + plane_in[kind][axis].astype(jnp.float32)
            ).astype(jnp.bfloat16)
        expert_copy(kind).start()
    finish_line(3)
    last_send[:slab, :] = rest_result[:, 2 * key_width :]
    last_send[slab:, :] = squares
    last_copy = pair_copy(last_send, last_recv, 3)
    last_copy.start()
    for number in range(3):
        finish_line(number)
    last_copy.wait()
    small_out[...] = last_send[...] + last_recv[...]
    layer_pair.wait()
    layer_own.wait()
    stream_copy.wait()
    for kind in range(3):
        expert_copy(kind).wait()


def run_back(expert_results, operands, front_results):
    low, wide = jnp.bfloat16, jnp.float32
    shape = jax.ShapeDtypeStruct
    vmem = pltpu.VMEM
    far = pl.BlockSpec(memory_space=pl.ANY)
    near = pl.BlockSpec(memory_space=pltpu.VMEM)
    tokens, width = operands[0].shape
    half = tokens // 2
    query_width, key_width = operands[4].shape[1], operands[5].shape[1]
    kept = expert_results[LINES + 2 : LINES + 5]
    tile_shapes = [value.shape[1:] for value in kept]
    half_shapes = [(value[0] // 2, value[1]) for value in tile_shapes]
    slab = width // (LINES * PLANE)
    slots = 2 * key_width // HEAD_FEATURES
    rest_width = 2 * key_width + 128
    widths = (query_width // 2, query_width // 2, query_width, rest_width)
    dma = pltpu.SemaphoreType.DMA
    scatter_scratch = []
    for columns in widths:
        scatter_scratch += [
            vmem((2 * LINES, slab, columns), low),
            vmem((LINES, slab, columns), low),
            vmem((LINES, slab, columns), low),
            vmem((LINES, slab, columns), low),
            dma((6, 2 * LINES)),
        ]
    return pl.pallas_call(
        back_kernel,
        name="back",
        out_shape=(
            shape((tokens, width), low),
            shape((tokens, width), low),
            *[shape((slab, columns), wide) for columns in widths],
            *[shape((2, *value), low) for value in half_shapes],
            shape((slab + 8, 128), wide),
        ),
        in_specs=[far] * (LINES + 8)
        + [far, far, near, near, far, far, far, far, near, near, near]
        + [far] * 8,
        out_specs=(far,) * 2 + (near,) * 4 + (far,) * 3 + (near,),
        scratch_shapes=[
            vmem((tokens, width), low),
            vmem((half, width), low),
            vmem((width, query_width), low),
            vmem((width, key_width), low),
            vmem((width, key_width), low),
            vmem((query_width, width), low),
            vmem((tokens, width), low),
            vmem((tokens, query_width), low),
            vmem((tokens, query_width), low),
            vmem((half, width), wide),
            vmem((half, width), low),
            vmem((LINES - 1, half, width), low),
            vmem((half, width), low),
            vmem((tokens, key_width), low),
            vmem((tokens, key_width), low),
            vmem((half, width), low),
            vmem((half, 128), wide),
            vmem((half, 128), wide),
            vmem((slots, tokens, 128), low),
            vmem((slots, tokens, 128), low),
            vmem((slots, tokens, 128), wide),
            vmem((slots, tokens, 128), wide),
            vmem((tokens, width), low),
            vmem((tokens, width), low),
            vmem((tokens, query_width), low),
            vmem((tokens, key_width), low),
            vmem((tokens, key_width), low),
            vmem((tokens, width), low),
            *[vmem((2, *value), low) for value in half_shapes],
            *[vmem((2, 2, *value), low) for value in half_shapes],
            *[vmem((2, *value), low) for value in half_shapes],
            *[vmem((width, columns), low) for columns in widths],
            *scatter_scratch,
            vmem((slab + 8, 128), wide),
            vmem((slab + 8, 128), wide),
            dma((17,)),
            dma((3, 3)),
            dma((LINES - 1,)),
            dma((LINES - 1,)),
            dma((2, 4)),
            dma((3, 2)),
            dma((3, 2)),
            dma((5,)),
        ],
        compiler_params=pltpu.CompilerParams(
            collective_id=1, has_side_effects=True, vmem_limit_bytes=63 << 20
        ),
    )(*expert_results, *operands, *front_results)


def dense_shards(
    stream,
    cotangent,
    attention_gain,
    query_weight,
    key_matrix,
    value_matrix,
    out_weight,
    mixture_gain,
    router_weight,
    gate_weight,
    up_weight,
    down_weight,
    routes,
):
    tok_rows, model_width = stream.shape
    experts = router_weight.shape[1]
    query_width = query_weight.shape[1]
    key_width = key_matrix.shape[1]
    steps_up = np.arange(HEAD_FEATURES // 2, dtype=np.float32) * np.float32(2.0 / HEAD_FEATURES)
    turns = np.exp(-steps_up * np.log(np.float32(rope_base)))
    angles = np.arange(SEQ_LEN, dtype=np.float32)[:, None] * turns[None, :]
    cosines, sines = np.cos(angles), np.sin(angles)
    operands = [
        stream,
        cotangent,
        attention_gain.astype(jnp.float32)[None, :],
        mixture_gain.astype(jnp.float32)[None, :],
        query_weight,
        key_matrix,
        value_matrix,
        out_weight,
        jnp.pad(router_weight, ((0, 0), (0, 128 - experts))),
        routes,
        jnp.asarray(np.tile(cosines, (1, 4))),
        jnp.asarray(np.tile(np.concatenate([-sines, sines], axis=1), (1, 2))),
    ]
    front = run_front(operands, [gate_weight[0], up_weight[0], down_weight[0]])
    (
        layer_out,
        grad_stream,
        out_first,
        out_second,
        query_grad,
        rest_grad,
        gate_grad,
        up_grad,
        down_grad,
        small,
    ) = run_back(front[: LINES + 8], operands[:9] + operands[10:], front[LINES + 8 :])
    slab = query_grad.shape[0]
    rms_stats = jnp.sqrt(small[slab : slab + 1, :3] / (tok_rows * model_width))
    return (
        layer_out,
        grad_stream.astype(jnp.float32),
        small[:slab, experts + 1],
        query_grad,
        rest_grad[:, :key_width],
        rest_grad[:, key_width : 2 * key_width],
        jnp.concatenate([out_first, out_second], axis=1).T,
        small[:slab, experts],
        small[:slab, :experts],
        gate_grad.astype(jnp.float32).reshape(gate_weight.shape),
        up_grad.astype(jnp.float32).reshape(up_weight.shape),
        down_grad.astype(jnp.float32).reshape(down_weight.shape),
        rms_stats,
    )


def solution(mesh):
    in_specs = (
        P("ep", None),
        P("ep", None),
        P(),
        P(None, "tp"),
        P(None, "tp"),
        P(None, "tp"),
        P("tp", None),
        P(),
        P(),
        P("ep", None, "tp"),
        P("ep", None, "tp"),
        P("ep", "tp", None),
        P("ep", None),
    )
    out_specs = (
        P("ep", None),
        P("ep", None),
        P("ep"),
        P("ep", "tp"),
        P("ep", "tp"),
        P("ep", "tp"),
        P("tp", "ep"),
        P("ep"),
        P("ep", None),
        P("ep", None, "tp"),
        P("ep", None, "tp"),
        P("ep", "tp", None),
        P("ep", None),
    )
    ep_size = mesh.shape["ep"]
    dense = mesh.shape["tp"] == 2 and ep_size <= 2 * TOP and ep_size == 16
    shards = dense_shards if dense else routed_shards
    return jax.shard_map(shards, mesh=mesh, in_specs=in_specs, out_specs=out_specs, check_vma=False)
```

```python
import functools

import jax
import jax.numpy as jnp
import numpy as np
from jax import lax
from jax.experimental import pallas as pl
from jax.experimental.pallas import tpu as pltpu
from jax.sharding import PartitionSpec as P

HEAD_FEATURES = 64
TOP = 8
SEQ_LEN = 512


epsilon = 1e-06
score_scale = 0.015625
residual_scale = 0.22
rope_base = 10000.0
masked_score = -1e30


def rope_tables(sequence_length):
    half_dim = HEAD_FEATURES // 2
    steps_up = jnp.arange(half_dim).astype(jnp.float32) * (2.0 / HEAD_FEATURES)
    inverse = jnp.exp(-steps_up * jnp.log(rope_base))
    places = jnp.arange(sequence_length).astype(jnp.float32)
    angles = places[:, None] * inverse[None, :]
    return (jnp.cos(angles), jnp.sin(angles))


def apply_rotation(value_rows, cosine_table, sine_values):
    half_dim = value_rows.shape[-1] // 2
    first_half = value_rows[..., :half_dim]
    second_half = value_rows[..., half_dim:]
    cos_rows = cosine_table[:, None, :]
    sin_rows = sine_values[:, None, :]
    return jnp.concatenate(
        [
            first_half * cos_rows - second_half * sin_rows,
            second_half * cos_rows + first_half * sin_rows,
        ],
        axis=-1,
    )


def rotary_back(grads_in, cosine_table, sine_values):
    half_dim = grads_in.shape[-1] // 2
    first_half = grads_in[..., :half_dim]
    second_half = grads_in[..., half_dim:]
    cos_rows = cosine_table[:, None, :]
    sin_rows = sine_values[:, None, :]
    return jnp.concatenate(
        [
            first_half * cos_rows + second_half * sin_rows,
            second_half * cos_rows - first_half * sin_rows,
        ],
        axis=-1,
    )


def block_scores(query_block, rotated_keys, row_start, block_rows, row_stop):
    scores = score_scale * jnp.einsum(
        "qhgd,khd->hgqk", query_block, rotated_keys, preferred_element_type=jnp.float32
    )
    causal = (row_start + jnp.arange(block_rows))[:, None] >= jnp.arange(row_stop)[None, :]
    return jnp.where(causal, scores, masked_score)


def attention_forward(query_rows, rotated_keys, value_rows):
    sequence_length = query_rows.shape[0]
    block_rows = min(512, sequence_length)
    scores = block_scores(query_rows, rotated_keys, 0, block_rows, block_rows)
    largest = jnp.max(scores, axis=-1, keepdims=True)
    weights_exp = jnp.exp(scores - largest)
    totals = jnp.sum(weights_exp, axis=-1, keepdims=True)
    probs_low = (weights_exp / totals).astype(jnp.bfloat16)
    outputs = jnp.einsum(
        "hgqk,khd->qhgd", probs_low, value_rows, preferred_element_type=jnp.float32
    )
    normalizers = [largest + jnp.log(totals)]
    return (outputs, normalizers)


def attention_backward(query_rows, rotated_keys, value_rows, normalizers, grad_mixed):
    sequence_length = query_rows.shape[0]
    block_rows = min(512, sequence_length)
    grad_keys = jnp.zeros(rotated_keys.shape, jnp.float32)
    grad_values = jnp.zeros(value_rows.shape, jnp.float32)
    grad_queries = []
    for block_index, row_start in enumerate(range(0, sequence_length, block_rows)):
        row_stop = row_start + block_rows
        scores = block_scores(query_rows, rotated_keys, row_start, block_rows, row_stop)
        probs = jnp.exp(scores - normalizers[block_index])
        probs_low = probs.astype(jnp.bfloat16)
        grad_probs = jnp.einsum(
            "qhgd,khd->hgqk", grad_mixed, value_rows, preferred_element_type=jnp.float32
        )
        inner = jnp.sum(probs * grad_probs, axis=-1, keepdims=True)
        grad_scores = (probs * (grad_probs - inner)).astype(jnp.bfloat16)
        grad_queries.append(
            score_scale
            * jnp.einsum(
                "hgqk,khd->qhgd", grad_scores, rotated_keys, preferred_element_type=jnp.float32
            )
        )
        grad_keys = grad_keys.at[:row_stop].add(
            score_scale
            * jnp.einsum(
                "hgqk,qhgd->khd", grad_scores, query_rows, preferred_element_type=jnp.float32
            )
        )
        grad_values = grad_values.at[:row_stop].add(
            jnp.einsum("hgqk,qhgd->khd", probs_low, grad_mixed, preferred_element_type=jnp.float32)
        )
    return (grad_queries[0], grad_keys, grad_values)


def to_owners(packed):
    return lax.all_to_all(packed, "ep", split_axis=1, concat_axis=1, tiled=True)


def back_to_tokens(rows_low, slot_count, model_width):
    returned = lax.all_to_all(rows_low, "ep", split_axis=1, concat_axis=1, tiled=True)
    joined = lax.all_gather(returned, "tp", axis=0, tiled=True)
    return joined.reshape(slot_count, model_width)


def from_owners(term_fn, slot_count, experts, model_width):
    share_rows = slot_count // lax.axis_size("tp")
    summed = lax.psum_scatter(
        term_fn(jnp.int32(0), lax.axis_size("tp") * share_rows).astype(jnp.bfloat16),
        "tp",
        scatter_dimension=0,
        tiled=True,
    ).astype(jnp.float32)
    summed = summed.astype(jnp.bfloat16).reshape(share_rows // experts, experts, model_width)
    return back_to_tokens(summed, slot_count, model_width)


def seq_rms(value_rows, seq_count):
    return jnp.sqrt(jnp.mean((value_rows * value_rows).reshape(seq_count, -1), axis=1))


def routed_shards(
    stream,
    cotangent,
    attention_gain,
    query_weight,
    key_matrix,
    value_matrix,
    out_weight,
    mixture_gain,
    router_weight,
    gate_weight,
    up_weight,
    down_weight,
    routes,
):
    tok_rows, model_width = stream.shape
    experts = router_weight.shape[1]
    cap_slots = tok_rows * TOP * 5 // (4 * experts)
    slot_count = cap_slots * experts
    query_heads = query_weight.shape[1] // HEAD_FEATURES
    key_heads = key_matrix.shape[1] // HEAD_FEATURES
    group_width = query_heads // key_heads
    seq_count = tok_rows // SEQ_LEN
    stream_f = stream.astype(jnp.float32)
    grad_result = cotangent.astype(jnp.float32)
    gain_first = attention_gain.astype(jnp.float32)
    gain_second = mixture_gain.astype(jnp.float32)
    cosine_table, sine_values = rope_tables(SEQ_LEN)
    cosine_rows = jnp.tile(cosine_table, (seq_count, 1))
    sine_rows = jnp.tile(sine_values, (seq_count, 1))
    zero_low = jnp.zeros((), jnp.bfloat16)
    inv_first = lax.rsqrt(jnp.mean(stream_f * stream_f, axis=-1, keepdims=True) + epsilon)
    normalized_input = (stream_f * inv_first * gain_first).astype(jnp.bfloat16)
    query_pre = jnp.dot(normalized_input, query_weight, preferred_element_type=jnp.float32).reshape(
        tok_rows, query_heads, HEAD_FEATURES
    )
    key_pre = jnp.dot(normalized_input, key_matrix, preferred_element_type=jnp.float32).reshape(
        tok_rows, key_heads, HEAD_FEATURES
    )
    query_rows = (
        apply_rotation(query_pre, cosine_rows, sine_rows)
        .astype(jnp.bfloat16)
        .reshape(tok_rows, key_heads, group_width, HEAD_FEATURES)
    )
    rotated_keys = apply_rotation(key_pre, cosine_rows, sine_rows).astype(jnp.bfloat16)
    value_rows = (
        jnp.dot(normalized_input, value_matrix, preferred_element_type=jnp.float32)
        .astype(jnp.bfloat16)
        .reshape(tok_rows, key_heads, HEAD_FEATURES)
    )
    mixed_seq, norms_seq = attention_forward(query_rows, rotated_keys, value_rows)
    mixed_low = mixed_seq.reshape(tok_rows, query_heads * HEAD_FEATURES).astype(jnp.bfloat16)
    attended = lax.psum(
        jnp.dot(mixed_low, out_weight, preferred_element_type=jnp.float32).astype(jnp.bfloat16),
        "tp",
    ).astype(jnp.float32)
    middle = stream_f + residual_scale * attended
    inv_second = lax.rsqrt(jnp.mean(middle * middle, axis=-1, keepdims=True) + epsilon)
    mixer_in = (middle * inv_second * gain_second).astype(jnp.bfloat16)
    logits = jnp.dot(mixer_in, router_weight, preferred_element_type=jnp.float32)
    expert_ids = jnp.arange(experts, dtype=jnp.int32)
    route_hot = routes[:, :, None] == expert_ids[None, None, :]
    chosen = jnp.sum(jnp.where(route_hot, logits[:, None, :], 0.0), axis=-1)
    chosen_exp = jnp.exp(chosen - jnp.max(chosen, axis=-1, keepdims=True))
    gate_probs = chosen_exp / jnp.sum(chosen_exp, axis=-1, keepdims=True)
    flat_routes = routes.reshape(-1)
    flat_hot = route_hot.reshape(tok_rows * TOP, experts).astype(jnp.int32)
    ranks = jnp.sum((jnp.cumsum(flat_hot, axis=0) - 1) * flat_hot, axis=1)
    slot_index = ranks * experts + flat_routes
    source_pair = (
        jnp.zeros((slot_count,), jnp.int32)
        .at[slot_index]
        .set(jnp.arange(tok_rows * TOP, dtype=jnp.int32))
    )
    filled = jnp.zeros((slot_count,), jnp.bool_).at[slot_index].set(True)
    source_token = source_pair // TOP
    sent_rows = jnp.where(filled[:, None], mixer_in[source_token], zero_low).reshape(
        cap_slots, experts, model_width
    )
    received = to_owners(sent_rows).reshape(slot_count, model_width)
    gate_matrix = gate_weight[0]
    up_matrix = up_weight[0]
    down_matrix = down_weight[0]
    gate_pre = jnp.dot(received, gate_matrix, preferred_element_type=jnp.float32)
    up_pre = jnp.dot(received, up_matrix, preferred_element_type=jnp.float32)
    sigmoid_gate = jax.nn.sigmoid(gate_pre)
    silu_gate = gate_pre * sigmoid_gate
    active = (silu_gate * up_pre).astype(jnp.bfloat16)

    def down_term(row_start, row_count):
        return jnp.dot(active, down_matrix, preferred_element_type=jnp.float32)

    expert_rows = from_owners(down_term, slot_count, experts, model_width)
    picked_rows = expert_rows[slot_index].reshape(tok_rows, TOP, model_width)
    mixture = jnp.sum(gate_probs[:, :, None] * picked_rows, axis=1)
    result = middle + residual_scale * mixture
    layer_out = result.astype(jnp.bfloat16)
    rms_stats = jnp.stack(
        [seq_rms(result, seq_count), seq_rms(attended, seq_count), seq_rms(mixture, seq_count)],
        axis=1,
    )
    grad_mix = residual_scale * grad_result
    grad_weighting = jnp.sum(picked_rows * grad_mix[:, None, :], axis=-1)
    grad_chosen = gate_probs * (
        grad_weighting - jnp.sum(gate_probs * grad_weighting, axis=-1, keepdims=True)
    )
    grad_logits = jnp.sum(jnp.where(route_hot, grad_chosen[:, :, None], 0.0), axis=1).astype(
        jnp.bfloat16
    )
    router_grad = jnp.dot(mixer_in.T, grad_logits, preferred_element_type=jnp.float32)
    flat_gates = gate_probs.reshape(-1)
    grad_sent = jnp.where(
        filled[:, None],
        (flat_gates[source_pair][:, None] * grad_mix[source_token]).astype(jnp.bfloat16),
        zero_low,
    ).reshape(cap_slots, experts, model_width)
    grad_received = to_owners(grad_sent).reshape(slot_count, model_width)
    grad_active = jnp.dot(grad_received, down_matrix.T, preferred_element_type=jnp.float32)
    down_grad = jnp.dot(active.T, grad_received, preferred_element_type=jnp.float32)
    grad_gate_pre = (
        grad_active * up_pre * sigmoid_gate * (1.0 + gate_pre * (1.0 - sigmoid_gate))
    ).astype(jnp.bfloat16)
    grad_up_pre = (grad_active * silu_gate).astype(jnp.bfloat16)
    gate_grad = jnp.dot(received.T, grad_gate_pre, preferred_element_type=jnp.float32)
    up_grad = jnp.dot(received.T, grad_up_pre, preferred_element_type=jnp.float32)

    def input_term(row_start, row_count):
        return jnp.dot(grad_gate_pre, gate_matrix.T, preferred_element_type=jnp.float32) + jnp.dot(
            grad_up_pre, up_matrix.T, preferred_element_type=jnp.float32
        )

    grad_rows = from_owners(input_term, slot_count, experts, model_width)
    grad_mixer = jnp.dot(
        grad_logits, router_weight.T, preferred_element_type=jnp.float32
    ) + jnp.sum(
        grad_rows[slot_index].reshape(tok_rows, TOP, model_width), axis=1, dtype=jnp.float32
    )
    weighted_second = grad_mixer * gain_second
    second_grad = jnp.sum(grad_mixer * middle * inv_second, axis=0)
    grad_middle = (
        grad_result
        + inv_second * weighted_second
        - middle * inv_second**3 * jnp.mean(middle * weighted_second, axis=-1, keepdims=True)
    )
    grad_attended = (residual_scale * grad_middle).astype(jnp.bfloat16)
    out_grad_t = jnp.dot(grad_attended.T, mixed_low, preferred_element_type=jnp.float32)
    grad_mixed = (
        jnp.dot(grad_attended, out_weight.T, preferred_element_type=jnp.float32)
        .astype(jnp.bfloat16)
        .reshape(tok_rows, key_heads, group_width, HEAD_FEATURES)
    )
    grad_query_seq, grad_key_seq, grad_value_seq = attention_backward(
        query_rows, rotated_keys, value_rows, norms_seq, grad_mixed
    )
    grad_queries_rot = grad_query_seq.reshape(tok_rows, query_heads, HEAD_FEATURES)
    grad_query_pre = (
        rotary_back(grad_queries_rot, cosine_rows, sine_rows)
        .astype(jnp.bfloat16)
        .reshape(tok_rows, query_heads * HEAD_FEATURES)
    )
    grad_key_pre = (
        rotary_back(grad_key_seq, cosine_rows, sine_rows)
        .astype(jnp.bfloat16)
        .reshape(tok_rows, key_heads * HEAD_FEATURES)
    )
    grad_values_low = grad_value_seq.astype(jnp.bfloat16).reshape(
        tok_rows, key_heads * HEAD_FEATURES
    )
    query_grad = jnp.dot(normalized_input.T, grad_query_pre, preferred_element_type=jnp.float32)
    key_grad = jnp.dot(normalized_input.T, grad_key_pre, preferred_element_type=jnp.float32)
    value_grad = jnp.dot(normalized_input.T, grad_values_low, preferred_element_type=jnp.float32)
    normed_term = jnp.dot(grad_query_pre, query_weight.T, preferred_element_type=jnp.float32)
    normed_term = normed_term + jnp.dot(
        grad_key_pre, key_matrix.T, preferred_element_type=jnp.float32
    )
    normed_term = normed_term + jnp.dot(
        grad_values_low, value_matrix.T, preferred_element_type=jnp.float32
    )
    grad_normed = lax.psum(normed_term.astype(jnp.bfloat16), "tp").astype(jnp.float32)
    weighted_first = grad_normed * gain_first
    first_grad = jnp.sum(grad_normed * stream_f * inv_first, axis=0)
    grad_stream = (
        grad_middle
        + inv_first * weighted_first
        - stream_f * inv_first**3 * jnp.mean(stream_f * weighted_first, axis=-1, keepdims=True)
    )
    reduced = (
        lax.psum_scatter(query_grad, "ep", scatter_dimension=0, tiled=True),
        lax.psum_scatter(key_grad, "ep", scatter_dimension=0, tiled=True),
        lax.psum_scatter(value_grad, "ep", scatter_dimension=0, tiled=True),
        lax.psum_scatter(out_grad_t, "ep", scatter_dimension=0, tiled=True),
        lax.psum_scatter(router_grad, "ep", scatter_dimension=0, tiled=True),
        lax.psum_scatter(first_grad, "ep", scatter_dimension=0, tiled=True),
        lax.psum_scatter(second_grad, "ep", scatter_dimension=0, tiled=True),
    )
    return (
        layer_out,
        grad_stream,
        reduced[5],
        reduced[0],
        reduced[1],
        reduced[2],
        reduced[3].T,
        reduced[6],
        reduced[4],
        gate_grad[None],
        up_grad[None],
        down_grad[None],
        rms_stats,
    )


MESH = pl.DeviceIdType.MESH
PLANE = 4
LINES = 4
DEFERRED = (2,)


def flip(place, unit):
    return place + unit * (1 - 2 * lax.rem(lax.div(place, unit), 2))


def flip_line(place, step):
    if step % 2:
        place = flip(place, PLANE)
    if step // 2:
        place = flip(place, 2 * PLANE)
    return place


def matmul(left, right):
    return jnp.dot(left, right, preferred_element_type=jnp.float32)


def matmul_nt(left, right):
    return lax.dot_general(
        left, right, (((1,), (1,)), ((), ())), preferred_element_type=jnp.float32
    )


def matmul_tn(left, right):
    return lax.dot_general(
        left, right, (((0,), (0,)), ((), ())), preferred_element_type=jnp.float32
    )


def lane_halves(value):
    lane = lax.broadcasted_iota(jnp.int32, value.shape, 1)
    low = jnp.where(lane < HEAD_FEATURES, value, 0.0)
    high = jnp.where(lane < HEAD_FEATURES, 0.0, value)
    return low, high


def partner_lanes(value):
    width = value.shape[1]
    quarter = HEAD_FEATURES // 2
    lane = lax.broadcasted_iota(jnp.int32, value.shape, 1)
    ahead = pltpu.roll(value, width - quarter, 1)
    behind = pltpu.roll(value, quarter, 1)
    return jnp.where(lax.rem(lane, HEAD_FEATURES) < quarter, ahead, behind)


def causal_scores(query_block, key_block, row_start):
    scores = score_scale * matmul_nt(query_block, key_block)
    row = lax.broadcasted_iota(jnp.int32, scores.shape, 0) + row_start
    column = lax.broadcasted_iota(jnp.int32, scores.shape, 1)
    return jnp.where(row >= column, scores, masked_score)


def store_slots(slots, values):
    for group in range(values.shape[1] // HEAD_FEATURES):
        pair = group // 2
        low, high = lane_halves(values[:, pair * 128 : pair * 128 + 128])
        if group % 2:
            low = pltpu.roll(high, HEAD_FEATURES, 1)
        else:
            high = pltpu.roll(low, HEAD_FEATURES, 1)
        slots[2 * group] = low.astype(jnp.bfloat16)
        slots[2 * group + 1] = high.astype(jnp.bfloat16)


def front_kernel(*refs):
    tiles = 2 * PLANE
    refs = list(refs)

    def take(count):
        taken = refs[:count]
        del refs[:count]
        return taken

    stream, cotangent, gain_first, gain_second, query_weight, key_weight = take(6)
    value_weight, out_weight, router, routes, cosine, sine = take(6)
    weights = take(3)
    out_parts = take(LINES)
    grow_sum, weighting_sum = take(2)
    kept = take(3)
    landed = take(3)
    mixer_own, probs_own, normed_out, queries_out, keys_out, values_out, mixed_out = take(7)
    attended = take(1)[0]
    mixer, cots, probs, gates, ups, downs = take(6)
    scaled, ggate, gup, grow, grow_in, outs, weighting, weighting_in = take(8)
    part_send, part_recv = take(2)
    load_sem, own_sem, weight_send, weight_recv = take(4)
    relay_send, relay_recv, probs_send, probs_recv, part_sem = take(5)
    result_sem, store_sem, kept_sem = take(3)
    grow_send, grow_recv, weighting_send, weighting_recv = take(4)
    core_send, core_recv, plane_send, plane_recv, ready_sem = take(5)
    held = (gates, ups, downs)
    rows_all, width = mixer.shape
    half = rows_all // LINES
    tokens = 2 * half
    span = gates.shape[2]
    column_tiles = width // span
    heads_width = query_weight.shape[1]
    pieces = heads_width // span
    tall = scaled.shape[1]

    place = lax.axis_index("ep")
    core = lax.axis_index("tp")
    line = lax.div(place, PLANE)
    sibling = (place, 1 - core)
    across = [(flip(place, 1), core), (flip(place, 2), core)]
    partners = [(flip_line(place, step), core) for step in range(LINES)]
    own_rows = pl.ds(pl.multiple_of(core * half, half), half)
    stream_v, normed = outs.at[pl.ds(0, tokens)], outs.at[pl.ds(tokens, tokens)]

    def block_rows_of(block):
        return pl.ds(pl.multiple_of(block * half, half), half)

    line_rows = block_rows_of(line)

    barrier = pltpu.get_barrier_semaphore()
    for other in across + partners[1:] + [sibling]:
        pl.semaphore_signal(barrier, inc=1, device_id=other, device_id_type=MESH)

    def tall_loads(source, column, target, tile, index):
        return [
            pltpu.make_async_copy(
                source.at[pl.ds(start, size), pl.ds(column * span, span)],
                target.at[tile + part, pl.ds(0, size)],
                load_sem.at[index + part],
            )
            for part, (start, size) in enumerate(((0, tall), (tall, width - tall)))
        ]

    loads = [pltpu.make_async_copy(stream, stream_v, load_sem.at[0])]
    for piece in range(pieces):
        loads += tall_loads(query_weight, piece, scaled, 2 * piece, 1 + 2 * piece)
    loads += tall_loads(key_weight, 0, ggate, 0, 1 + 2 * pieces)
    loads += tall_loads(value_weight, 0, ggate, tiles - 2, 3 + 2 * pieces)
    out_loads = [
        pltpu.make_async_copy(
            out_weight.at[:, pl.ds(column * span, span)],
            grow.at[column, pl.ds(0, heads_width)],
            load_sem.at[5 + 2 * pieces + column],
        )
        for column in range(column_tiles)
    ]
    for copy in loads + out_loads:
        copy.start()
    pl.semaphore_wait(barrier, LINES + 2)

    def send(source, target, sems, index, device):
        return pltpu.make_async_remote_copy(
            src_ref=source,
            dst_ref=target,
            send_sem=sems[0].at[index],
            recv_sem=sems[1].at[index],
            device_id=device,
            device_id_type=MESH,
        )

    weight_sems = (weight_send, weight_recv)

    def direct(kind, axis):
        return send(
            weights[kind], held[kind].at[axis + 1], weight_sems, (kind, axis), across[axis]
        )

    def to_sibling(kind, slot):
        source = weights[kind] if slot == 0 else held[kind].at[slot]
        return send(source, held[kind].at[PLANE + slot], weight_sems, (kind, 2 + slot), sibling)

    def onward(kind, axis):
        source, target = held[kind].at[2 - axis], held[kind].at[3]
        if kind == 1:
            part = pl.ds(axis * (width // 2), width // 2)
            source, target = held[kind].at[2 - axis, part], held[kind].at[3, part]
        return send(source, target, weight_sems, (kind, 6 + axis), across[axis])

    onwards = {0: (0,), 1: (0, 1), 2: (1,)}

    def relay(array, hop, downward):
        gathered = (cots, mixer)[array]
        shift = -1 if downward else 1
        block = block_rows_of(jnp.clip(line - shift * hop, 0, LINES - 1))
        source = gathered.at[block]
        if hop == 0 and array == 0:
            source = cotangent.at[own_rows]
        return send(
            source,
            gathered.at[block],
            (relay_send, relay_recv),
            (array, downward, hop),
            (place + shift * PLANE, core),
        )

    def arriving(array, hop, downward):
        gathered = (cots, mixer)[array]
        shift = -1 if downward else 1
        block = block_rows_of(jnp.clip(line - shift * (hop + 1), 0, LINES - 1))
        return send(
            gathered.at[block],
            gathered.at[block],
            (relay_send, relay_recv),
            (array, downward, hop),
            (place + shift * PLANE, core),
        )

    def relay_sends(hop, downward):
        if downward:
            return jnp.logical_and(line > 0, line + hop < LINES)
        return jnp.logical_and(line < LINES - 1, line - hop >= 0)

    def relay_receives(hop, downward):
        if downward:
            return line + 1 + hop < LINES
        return line - 1 - hop >= 0

    def start_relay(array, hop):
        for downward in (0, 1):

            @pl.when(relay_sends(hop, downward))
            def _():
                relay(array, hop, downward).start()

    def receive_relay(array, hop):
        for downward in (0, 1):

            @pl.when(relay_receives(hop, downward))
            def _():
                arriving(array, hop, downward).wait_recv()

    def finish_relay(array, hop):
        for downward in (0, 1):

            @pl.when(relay_sends(hop, downward))
            def _():
                relay(array, hop, downward).wait_send()

    for kind in range(3):
        for axis in (0, 1):
            direct(kind, axis).start()
    start_relay(0, 0)
    own_copies = [
        pltpu.make_async_copy(weights[kind], held[kind].at[0], own_sem.at[kind])
        for kind in range(3)
    ]
    own_copies.append(
        pltpu.make_async_copy(cotangent.at[own_rows], cots.at[line_rows], own_sem.at[3])
    )
    for kind in range(3):
        to_sibling(kind, 0).start()
    for copy in own_copies:
        copy.start()
    weighting[...] = jnp.zeros_like(weighting)

    loads[0].wait()
    stream_f = stream_v[...].astype(jnp.float32)
    inverse = lax.rsqrt(jnp.mean(stream_f * stream_f, axis=-1, keepdims=True) + epsilon)
    normed[...] = (stream_f * inverse * gain_first[...].astype(jnp.float32)[None, :]).astype(jnp.bfloat16)
    for copy in loads[1:]:
        copy.wait()

    def projected(target, tile):
        return matmul(normed[:, :tall], target[tile]) + matmul(
            normed[:, tall:], target[tile + 1, : width - tall, :]
        )

    def rotated(pre):
        turned = []
        for pair in range(span // 128):
            part = pre[:, pair * 128 : pair * 128 + 128]
            turned.append(part * cosine[...] + partner_lanes(part) * sine[...])
        return jnp.concatenate(turned, axis=1).astype(jnp.bfloat16)

    low_rows, high_rows = pl.ds(0, tokens), pl.ds(tokens, tokens)
    for piece in range(pieces):
        ggate[3 + piece, low_rows, :] = rotated(projected(scaled, 2 * piece))
    key_rows = rotated(projected(ggate, 0))
    ggate[2, low_rows, :] = key_rows
    value_rows = projected(ggate, tiles - 2).astype(jnp.bfloat16)
    ggate[2, high_rows, :] = value_rows

    def store_overlaid(values, rows):
        for group in range(values.shape[1] // HEAD_FEATURES):
            pair = group // 2
            low, high = lane_halves(values[:, pair * 128 : pair * 128 + 128].astype(jnp.float32))
            if group % 2:
                low = pltpu.roll(high, HEAD_FEATURES, 1)
            else:
                high = pltpu.roll(low, HEAD_FEATURES, 1)
            gup[2 * group, rows, :128] = low.astype(jnp.bfloat16)
            gup[2 * group + 1, rows, :128] = high.astype(jnp.bfloat16)

    store_overlaid(key_rows, low_rows)
    store_overlaid(value_rows, high_rows)
    results = [
        pltpu.make_async_copy(normed, normed_out, result_sem.at[0]),
        pltpu.make_async_copy(ggate.at[2, low_rows], keys_out, result_sem.at[1]),
        pltpu.make_async_copy(ggate.at[2, high_rows], values_out, result_sem.at[2]),
    ]
    for piece in range(pieces):
        results.append(
            pltpu.make_async_copy(
                ggate.at[3 + piece, low_rows],
                queries_out.at[:, pl.ds(piece * span, span)],
                result_sem.at[3 + piece],
            )
        )
    for copy in results:
        copy.start()
    group = heads_width // key_weight.shape[1]
    blocks = 2
    block_rows = tokens // blocks

    def head_pair(pair, carry):
        tile = 3 + lax.div(pair, 2)
        here = pl.ds(pl.multiple_of(lax.rem(pair, 2) * 128, 128), 128)
        for block in range(blocks):
            start = block * block_rows
            reach = start + block_rows
            total = jnp.zeros((block_rows, 128), jnp.float32)
            query_block = ggate[tile, pl.ds(start, block_rows), here]
            for parity in range(2):
                slot = 2 * lax.div(2 * pair + parity, group) + parity
                scores = causal_scores(query_block, gup[slot, pl.ds(0, reach), :128], start)
                weight = jnp.exp(scores - jnp.max(scores, axis=-1, keepdims=True))
                weight = weight / jnp.sum(weight, axis=-1, keepdims=True)
                total = total + matmul(
                    weight.astype(jnp.bfloat16), gup[slot, pl.ds(tokens, reach), :128]
                )
            ggate[tile, pl.ds(tokens + start, block_rows), here] = total.astype(jnp.bfloat16)
        return carry

    lax.fori_loop(0, heads_width // 128, head_pair, 0)
    receive_relay(0, 0)
    start_relay(0, 1)
    for piece in range(pieces):
        results.append(
            pltpu.make_async_copy(
                ggate.at[3 + piece, high_rows],
                mixed_out.at[:, pl.ds(piece * span, span)],
                result_sem.at[3 + pieces + piece],
            )
        )
    for copy in results[3 + pieces :]:
        copy.start()
    for copy in out_loads:
        copy.wait()

    def out_product(first_row):
        rows = pl.ds(pl.multiple_of(tokens + first_row * half, half), half)
        found = []
        for column in range(column_tiles):
            found.append(
                sum(
                    matmul(
                        ggate[3 + piece, rows, :],
                        grow[column, pl.ds(piece * span, span), :],
                    )
                    for piece in range(pieces)
                )
            )
        return jnp.concatenate(found, axis=1)

    part_send[...] = out_product(1 - core).astype(jnp.bfloat16)
    part_copy = pltpu.make_async_remote_copy(
        src_ref=part_send,
        dst_ref=part_recv,
        send_sem=part_sem.at[0],
        recv_sem=part_sem.at[1],
        device_id=sibling,
        device_id_type=MESH,
    )
    part_copy.start()
    own_part = out_product(core)
    part_copy.wait()
    attended_half = own_part + part_recv[...].astype(jnp.float32)
    attended[...] = attended_half.astype(jnp.bfloat16)
    middle = stream_v[own_rows, :].astype(jnp.float32) + residual_scale * attended_half
    inverse = lax.rsqrt(jnp.mean(middle * middle, axis=-1, keepdims=True) + epsilon)
    mixer[line_rows, :] = (middle * inverse * gain_second[...].astype(jnp.float32)[None, :]).astype(jnp.bfloat16)
    start_relay(1, 0)
    padding = jnp.zeros((128 - router.shape[0], width), jnp.bfloat16)
    logits = matmul_nt(
        mixer[line_rows, :], jnp.concatenate([router[...], padding], axis=0)
    )
    own_routes = routes[:, own_rows].T
    lane = lax.broadcasted_iota(jnp.int32, logits.shape, 1)
    routed = lane < 0
    for entry in range(TOP):
        routed = jnp.logical_or(routed, lane == own_routes[:, entry : entry + 1])
    largest = jnp.max(jnp.where(routed, logits, masked_score), axis=-1, keepdims=True)
    gate_exp = jnp.where(routed, jnp.exp(jnp.minimum(logits - largest, 0.0)), 0.0)
    probs[line_rows, :] = gate_exp / jnp.sum(gate_exp, axis=-1, keepdims=True)

    def probs_copy(step):
        return send(
            probs.at[line_rows],
            probs.at[line_rows],
            (probs_send, probs_recv),
            (step,),
            partners[step],
        )

    def probs_arriving(step):
        theirs = block_rows_of(lax.div(partners[step][0], PLANE))
        return send(
            probs.at[theirs],
            probs.at[theirs],
            (probs_send, probs_recv),
            (step,),
            partners[step],
        )

    for step in range(1, LINES):
        probs_copy(step).start()
    own_copies.append(pltpu.make_async_copy(probs.at[line_rows], probs_own, own_sem.at[4]))
    own_copies.append(pltpu.make_async_copy(mixer.at[line_rows], mixer_own, own_sem.at[5]))
    for copy in own_copies[4:]:
        copy.start()

    def pass_on(kind):
        for axis in (0, 1):
            direct(kind, axis).wait_recv()
        for axis in onwards[kind]:
            onward(kind, axis).start()
        for slot in (1, 2):
            to_sibling(kind, slot).start()

    def hidden_tile(block, tile):
        rows = block_rows_of(block)
        step = lax.rem(tile, PLANE)
        owner = lax.rem(place, PLANE)
        owner = jnp.where(lax.rem(step, 2) == 1, flip(owner, 1), owner)
        owner = jnp.where(lax.div(step, 2) == 1, flip(owner, 2), owner)
        chosen = lax.broadcasted_iota(jnp.int32, (half, 128), 1) == line * PLANE + owner
        prob = jnp.sum(jnp.where(chosen, probs[rows, :], 0.0), axis=1, keepdims=True)
        gate_pre = matmul(mixer[rows, :], gates[tile])
        up_pre = matmul(mixer[rows, :], ups[tile])
        grad_raw = residual_scale * matmul_nt(cots[rows, :], downs[tile])
        sigmoid_gate = 1.0 / (1.0 + jnp.exp(-gate_pre))
        silu_gate = gate_pre * sigmoid_gate
        active = silu_gate * up_pre
        share = jnp.sum(active * grad_raw, axis=1, keepdims=True)
        weighting[rows, :] += jnp.where(chosen, share, 0.0)
        grad_active = prob * grad_raw
        scaled[tile, rows, :] = (prob * active).astype(jnp.bfloat16)
        ggate[tile, rows, :] = (
            grad_active * up_pre * sigmoid_gate * (1.0 + gate_pre * (1.0 - sigmoid_gate))
        ).astype(jnp.bfloat16)
        gup[tile, rows, :] = (grad_active * silu_gate).astype(jnp.bfloat16)

    def early_tiles(block):
        def body(index, carry):
            hidden_tile(block, index + lax.div(index, 3))
            return carry

        lax.fori_loop(0, 6, body, 0)

    def late_tiles(block):
        def body(index, carry):
            hidden_tile(block, 3 + PLANE * index)
            return carry

        lax.fori_loop(0, 2, body, 0)

    def grow_tiles(block, first, last):
        rows = block_rows_of(block)

        def body(column, carry):
            here = pl.ds(pl.multiple_of(column * span, span), span)
            total = matmul_nt(ggate[0, rows, :], gates[0, here, :])
            for tile in range(1, tiles):
                total = total + matmul_nt(ggate[tile, rows, :], gates[tile, here, :])
            for tile in range(tiles):
                total = total + matmul_nt(gup[tile, rows, :], ups[tile, here, :])
            grow[column, rows, :] = total.astype(jnp.bfloat16)
            return carry

        lax.fori_loop(first, last, body, 0)

    outer = jnp.logical_or(line == 0, line == LINES - 1)
    near_line = flip(line, 1)
    far_inner = jnp.where(line < 2, 2, 1)
    far_outer = jnp.where(line < 2, 3, 0)

    def remote_block(index):
        outside = (near_line, far_inner, far_outer)[index]
        inside = (far_inner, far_outer, near_line)[index]
        return jnp.where(outer, outside, inside)

    def home_of(block):
        return (place + (block - line) * PLANE, core)

    chunks = 2
    chunk_columns = column_tiles // chunks

    def grow_copy(index, chunk):
        block = remote_block(index)
        home = jnp.where(outer, near_line, block)
        slot = jnp.where(outer, (0, 2, 3)[index], (1, 1, 0)[index])
        columns = pl.ds(chunk * chunk_columns, chunk_columns)
        return pltpu.make_async_remote_copy(
            src_ref=grow.at[columns, block_rows_of(block)],
            dst_ref=grow_in.at[slot, columns],
            send_sem=grow_send.at[index, chunk],
            recv_sem=grow_recv.at[slot, chunk],
            device_id=home_of(home),
            device_id_type=MESH,
        )

    def grow_arriving(slot, chunk):
        columns = pl.ds(chunk * chunk_columns, chunk_columns)
        return pltpu.make_async_remote_copy(
            src_ref=grow_in.at[slot, columns],
            dst_ref=grow_in.at[slot, columns],
            send_sem=grow_send.at[0, chunk],
            recv_sem=grow_recv.at[slot, chunk],
            device_id=home_of(near_line),
            device_id_type=MESH,
        )

    def combine(index, chunk):
        @pl.when(jnp.logical_not(outer))
        def _():
            grow_arriving(2 + index, chunk).wait_recv()
            rows = block_rows_of(remote_block(index))
            for column in range(chunk * chunk_columns, (chunk + 1) * chunk_columns):
                grow[column, rows, :] = (
                    grow[column, rows, :].astype(jnp.float32)
                    + grow_in[2 + index, column].astype(jnp.float32)
                ).astype(jnp.bfloat16)
            grow_copy(index, chunk).start()

    def weighting_copy(index):
        block = remote_block(index)
        return pltpu.make_async_remote_copy(
            src_ref=weighting.at[block_rows_of(block)],
            dst_ref=weighting_in.at[line],
            send_sem=weighting_send.at[index],
            recv_sem=weighting_recv.at[line],
            device_id=home_of(block),
            device_id_type=MESH,
        )

    def weighting_arriving(index):
        block = remote_block(index)
        return pltpu.make_async_remote_copy(
            src_ref=weighting_in.at[block],
            dst_ref=weighting_in.at[block],
            send_sem=weighting_send.at[index],
            recv_sem=weighting_recv.at[block],
            device_id=home_of(block),
            device_id_type=MESH,
        )

    def send_back(index):
        weighting_copy(index).start()
        for chunk in range(chunks):
            grow_tiles(
                remote_block(index), chunk * chunk_columns, (chunk + 1) * chunk_columns
            )
            if index == 2:
                grow_copy(index, chunk).start()
            else:

                @pl.when(outer)
                def _():
                    grow_copy(index, chunk).start()

    pass_on(0)
    receive_relay(1, 0)
    start_relay(1, 1)
    receive_relay(0, 1)
    start_relay(0, 2)
    pass_on(1)
    pass_on(2)
    for copy in results:
        copy.wait()
    for copy in own_copies:
        copy.wait()
    for step in range(1, LINES):
        probs_copy(step).wait_send()
        probs_arriving(step).wait_recv()
    for kind in range(3):
        for slot in range(3):
            to_sibling(kind, slot).wait_recv()
    early_tiles(remote_block(0))
    receive_relay(1, 1)
    start_relay(1, 2)
    for kind in range(3):
        for axis in onwards[kind]:
            onward(kind, axis).wait_recv()
        to_sibling(kind, 3).start()
    early_tiles(line)
    early_tiles(remote_block(1))
    for kind in range(3):
        to_sibling(kind, 3).wait_recv()
    late_tiles(remote_block(0))
    send_back(0)
    late_tiles(remote_block(1))
    send_back(1)
    late_tiles(line)
    grow_tiles(line, 0, column_tiles)
    receive_relay(0, 2)
    receive_relay(1, 2)
    early_tiles(remote_block(2))
    late_tiles(remote_block(2))
    send_back(2)
    combine(0, 0)
    combine(0, 1)
    for kind in range(3):
        for slot in range(PLANE):
            to_sibling(kind, slot).wait_send()
        for axis in (0, 1):
            direct(kind, axis).wait_send()
        for axis in onwards[kind]:
            onward(kind, axis).wait_send()
    for array in (0, 1):
        for hop in range(LINES - 1):
            finish_relay(array, hop)

    def out_tile(column, carry):
        here = pl.ds(pl.multiple_of(column * span, span), span)
        total = matmul(scaled[0], downs[0, :, here])
        for tile in range(1, tiles):
            total = total + matmul(scaled[tile], downs[tile, :, here])
        outs[:, here] = total.astype(jnp.bfloat16)
        return carry

    stores = [
        pltpu.make_async_copy(
            outs.at[block_rows_of(lax.div(partners[step][0], PLANE))],
            out_parts[step],
            store_sem.at[step],
        )
        for step in range(LINES)
    ]
    pl.semaphore_signal(ready_sem, inc=1, device_id=sibling, device_id_type=MESH)
    pl.semaphore_wait(ready_sem, 1)
    def tile_order(index):
        return jnp.where(index == 0, 3, jnp.where(index == 3, 0, index))

    def tile_grads(tile, kinds):
        for kind in kinds:
            if kind == 2:
                yield kind, residual_scale * matmul_tn(scaled[tile], cots[...])
            else:
                yield kind, matmul_tn(mixer[...], (ggate, gup)[kind][tile])

    def core_copy(kind, step):
        return pltpu.make_async_remote_copy(
            src_ref=held[kind].at[PLANE + step],
            dst_ref=held[kind].at[step],
            send_sem=core_send.at[kind, step],
            recv_sem=core_recv.at[kind, step],
            device_id=sibling,
            device_id_type=MESH,
        )

    def sibling_tile(index, kinds):
        step = tile_order(index)
        for kind, grad in tile_grads(PLANE + step, kinds):
            held[kind][PLANE + step] = grad.astype(jnp.bfloat16)
            core_copy(kind, step).start()

    def plane_copy(kind, axis, passing):
        span_rows = held[kind].shape[1] // 2
        step = 3 if passing else axis + 1
        return pltpu.make_async_remote_copy(
            src_ref=held[kind].at[step, pl.ds(axis * span_rows, span_rows)],
            dst_ref=landed[kind].at[axis, passing],
            send_sem=plane_send.at[kind, axis, passing],
            recv_sem=plane_recv.at[kind, axis, passing],
            device_id=across[axis],
            device_id_type=MESH,
        )

    def kept_copy(kind, step):
        return pltpu.make_async_copy(
            held[kind].at[step], kept[kind].at[step], kept_sem.at[kind, step]
        )

    def own_tile(index, kinds):
        @pl.when(index < PLANE - 1)
        def _():
            sibling_tile(index + 1, kinds)

        step = tile_order(index)
        for kind, grad in tile_grads(step, kinds):
            core_copy(kind, step).wait_recv()
            held[kind][step] = (grad + held[kind][step].astype(jnp.float32)).astype(jnp.bfloat16)

            @pl.when(step == 3)
            def _():
                for axis in (0, 1):
                    plane_copy(kind, axis, 1).start()

            for axis in (0, 1):

                if kind in DEFERRED:
                    continue

                @pl.when(step == axis + 1)
                def _():
                    plane_copy(kind, axis, 0).start()

            @pl.when(step < 3)
            def _():
                kept_copy(kind, step).start()

        return kinds

    def gate_and_up(index, carry):
        own_tile(index, (0, 1))
        return carry

    def down_only(index, carry):
        own_tile(index, (2,))
        return carry

    sibling_tile(0, (0, 1))
    lax.fori_loop(0, 2, gate_and_up, 0)
    combine(1, 0)
    lax.fori_loop(2, 3, gate_and_up, 0)
    combine(1, 1)
    lax.fori_loop(3, PLANE, gate_and_up, 0)
    lax.fori_loop(0, column_tiles, out_tile, 0)
    for copy in stores:
        copy.start()
    pl.semaphore_signal(ready_sem, inc=1, device_id=sibling, device_id_type=MESH)
    pl.semaphore_wait(ready_sem, 1)
    sibling_tile(0, (2,))
    lax.fori_loop(0, PLANE, down_only, 0)
    for index in range(LINES - 1):
        weighting_copy(index).wait_send()
        for chunk in range(chunks):
            grow_copy(index, chunk).wait_send()
        weighting_arriving(index).wait_recv()
    for slot in (0, 1):
        for chunk in range(chunks):
            grow_arriving(slot, chunk).wait_recv()
    total = weighting[line_rows, :]
    for index in range(LINES - 1):
        total = total + weighting_in[remote_block(index)]
    weighting_sum[...] = total
    for column in range(column_tiles):
        here = pl.ds(column * span, span)
        total = grow[column, line_rows, :].astype(jnp.float32)
        for slot in (0, 1):
            total = total + grow_in[slot, column].astype(jnp.float32)
        grow_sum[:, here] = total
    for copy in stores:
        copy.wait()
    for kind in range(3):
        for step in range(PLANE):
            core_copy(kind, step).wait_send()
        for step in range(3):
            kept_copy(kind, step).wait()
        for axis in (0, 1):
            for passing in (1,) if kind in DEFERRED else (0, 1):
                plane_copy(kind, axis, passing).wait()


def run_front(operands, weights):
    low, wide = jnp.bfloat16, jnp.float32
    shape = jax.ShapeDtypeStruct
    vmem = pltpu.VMEM
    far = pl.BlockSpec(memory_space=pl.ANY)
    near = pl.BlockSpec(memory_space=pltpu.VMEM)
    tokens, width = operands[0].shape
    half = tokens // 2
    rows = LINES * half
    query_width, key_width = operands[4].shape[1], operands[5].shape[1]
    span = weights[0].shape[1]
    tiles = 2 * PLANE
    dma = pltpu.SemaphoreType.DMA
    pieces = query_width // span
    columns = width // span
    return pl.pallas_call(
        front_kernel,
        name="front",
        out_shape=(
            *[shape((half, width), low)] * LINES,
            shape((half, width), wide),
            shape((half, 128), wide),
            shape((3, width, span), low),
            shape((3, width, span), low),
            shape((3, span, width), low),
            shape((2, 2, width // 2, span), low),
            shape((2, 2, width // 2, span), low),
            shape((2, 2, span // 2, width), low),
            shape((half, width), low),
            shape((half, 128), wide),
            shape((tokens, width), low),
            shape((tokens, query_width), low),
            shape((tokens, key_width), low),
            shape((tokens, key_width), low),
            shape((tokens, query_width), low),
            shape((half, width), low),
        ),
        in_specs=[far, far, near, near, far, far, far, far, near, near, near, near] + [far] * 3,
        out_specs=(*[far] * LINES, near, near, *[far] * 13, near),
        scratch_shapes=[
            vmem((rows, width), low),
            vmem((rows, width), low),
            vmem((rows, 128), wide),
            vmem((tiles, width, span), low),
            vmem((tiles, width, span), low),
            vmem((tiles, span, width), low),
            vmem((tiles, rows, span), low),
            vmem((tiles, rows, span), low),
            vmem((tiles, rows, span), low),
            vmem((columns, rows, span), low),
            vmem((LINES, columns, half, span), low),
            vmem((rows, width), low),
            vmem((rows, 128), wide),
            vmem((LINES, half, 128), wide),
            vmem((half, width), low),
            vmem((half, width), low),
            dma((5 + 2 * pieces + columns,)),
            dma((6,)),
            dma((3, 8)),
            dma((3, 8)),
            dma((2, 2, LINES - 1)),
            dma((2, 2, LINES - 1)),
            dma((LINES,)),
            dma((LINES,)),
            dma((2,)),
            dma((3 + 2 * pieces,)),
            dma((LINES,)),
            dma((3, 3)),
            dma((LINES - 1, 2)),
            dma((LINES, 2)),
            dma((LINES - 1,)),
            dma((LINES,)),
            dma((3, PLANE)),
            dma((3, PLANE)),
            dma((3, 2, 2)),
            dma((3, 2, 2)),
            pltpu.SemaphoreType.REGULAR,
        ],
        compiler_params=pltpu.CompilerParams(
            collective_id=0, has_side_effects=True, vmem_limit_bytes=63 << 20
        ),
        cost_estimate=pl.CostEstimate(
            flops=18 * rows * width * span * tiles,
            bytes_accessed=12 * width * span * tiles,
            transcendentals=0,
        ),
    )(*operands, *weights)


def back_kernel(*refs):
    refs = list(refs)

    def take(count):
        taken = refs[:count]
        del refs[:count]
        return taken

    out_parts = take(LINES)
    grow_sum, weighting_sum = take(2)
    kept, landed = take(3), take(3)
    stream, cotangent, gain_first, gain_second, query_weight, key_weight = take(6)
    value_weight, out_weight, router, cosine, sine = take(5)
    mixer_own, probs_own, normed, queries, keys, values, mixed, attended = take(8)
    layer_out, grad_stream, out_result_a, out_result_b, query_result, rest_result = take(6)
    expert_grads = take(3)
    small_out = take(1)[0]
    stream_v, cot_v, query_v, key_v, value_v, out_v, normed_v, queries_v = take(8)
    mixed_v, grow_v, attended_v, out_in, layer_v = take(5)
    key_v2, value_v2, mixer_v, probs_v, weighting_v = take(5)
    key_slots, value_slots, key_totals, value_totals = take(4)
    middle_grads, attended_grads, mixed_grads = take(3)
    key_grads, value_grads, normed_recv = take(3)
    normed_send, first_terms = attended_grads, layer_v
    second_terms, query_grads = cot_v, mixed_v
    own_parts, landed_v, plane_in = take(3), take(3), take(3)
    out_source_a, out_source_b, query_source, rest_source = take(4)
    scatter_scratch = [take(5) for _ in range(4)]
    last_send, last_recv = take(2)
    load_sem, part_sem, out_send, out_recv, pair_sem, plane_send, plane_recv = take(7)
    store_sem, deferred_send, deferred_recv = take(3)
    tokens, width = stream_v.shape
    half = tokens // 2

    place = lax.axis_index("ep")
    core = lax.axis_index("tp")
    sibling = (place, 1 - core)
    across = [flip(place, 1), flip(place, 2)]
    partners = [flip_line(place, step) for step in range(LINES)]
    bits = [lax.rem(place, 2), lax.rem(lax.div(place, 2), 2)]
    own_rows = pl.ds(pl.multiple_of(core * half, half), half)

    barrier = pltpu.get_barrier_semaphore()
    for other in across + partners[1:]:
        pl.semaphore_signal(barrier, inc=1, device_id=(other, core), device_id_type=MESH)
    pl.semaphore_signal(barrier, inc=1, device_id=sibling, device_id_type=MESH)

    pairs = [
        (grow_sum, grow_v),
        (weighting_sum, weighting_v),
        (attended, attended_v),
        (probs_own, probs_v),
        (stream, stream_v),
        (cotangent.at[own_rows], cot_v),
        (out_weight, out_v),
        (mixed, mixed_v),
        (queries, queries_v),
        (keys, key_v2),
        (values, value_v2),
        (normed, normed_v),
        (query_weight, query_v),
        (key_weight, key_v),
        (value_weight, value_v),
        (mixer_own, mixer_v),
        (out_parts[0], mixer_v),
    ]
    loads = [
        pltpu.make_async_copy(source, target, load_sem.at[index])
        for index, (source, target) in enumerate(pairs)
    ]

    def part_copies(kind, final):
        rows = own_parts[kind].shape[1]
        low, high = pl.ds(0, rows), pl.ds(rows, rows)
        first, second = (0, 0) if final else (2, 1)
        return [
            pltpu.make_async_copy(source, target, part_sem.at[kind, index])
            for index, (source, target) in enumerate(
                (
                    (kept[kind].at[first, low], own_parts[kind].at[0]),
                    (kept[kind].at[second, high], own_parts[kind].at[1]),
                )
            )
        ]

    def landed_copies(kind):
        if kind in DEFERRED:
            return [
                pltpu.make_async_copy(
                    landed[kind].at[axis, 1],
                    landed_v[kind].at[axis, 1],
                    part_sem.at[kind, 2 + axis],
                )
                for axis in (0, 1)
            ]
        return [pltpu.make_async_copy(landed[kind], landed_v[kind], part_sem.at[kind, 2])]

    def deferred_copy(kind, axis):
        rows = own_parts[kind].shape[1]
        return pltpu.make_async_remote_copy(
            src_ref=kept[kind].at[axis + 1, pl.ds(axis * rows, rows)],
            dst_ref=landed_v[kind].at[axis, 0],
            send_sem=deferred_send.at[kind, axis],
            recv_sem=deferred_recv.at[kind, axis],
            device_id=(across[axis], core),
            device_id_type=MESH,
        )

    for copy in loads[:6]:
        copy.start()
    for kind in range(3):
        for copy in landed_copies(kind):
            copy.start()
        for copy in part_copies(kind, False):
            copy.start()
    for copy in loads[6:-1]:
        copy.start()
    pl.semaphore_wait(barrier, LINES + 2)

    def send(source, target, sems, index, device):
        return pltpu.make_async_remote_copy(
            src_ref=source,
            dst_ref=target,
            send_sem=sems[0].at[index],
            recv_sem=sems[1].at[index],
            device_id=device,
            device_id_type=MESH,
        )

    def out_copy(step):
        return send(
            out_parts[step],
            out_in.at[step - 1],
            (out_send, out_recv),
            (step - 1,),
            (partners[step], core),
        )

    for kind in DEFERRED:
        for axis in (0, 1):
            deferred_copy(kind, axis).start()
    for step in (3, 2, 1):
        out_copy(step).start()

    for copy in loads[:6]:
        copy.wait()
    middle = stream_v[own_rows, :].astype(jnp.float32) + residual_scale * attended_v[...].astype(jnp.float32)
    inverse = lax.rsqrt(jnp.mean(middle * middle, axis=-1, keepdims=True) + epsilon)
    probs = probs_v[...]
    weighting = weighting_v[...]
    grad_chosen = probs * (weighting - jnp.sum(probs * weighting, axis=-1, keepdims=True))
    grad_logits = grad_chosen.astype(jnp.bfloat16)
    padding = jnp.zeros((128 - router.shape[0], width), jnp.bfloat16)
    grad_mixer = (
        matmul(grad_logits, jnp.concatenate([router[...], padding], axis=0)) + grow_v[...]
    )
    weighted = grad_mixer * gain_second[...].astype(jnp.float32)[None, :]
    grad_middle = (
        cot_v[...].astype(jnp.float32)
        + inverse * weighted
        - middle * (inverse * inverse * inverse)
        * jnp.mean(middle * weighted, axis=-1, keepdims=True)
    )
    middle_grads[own_rows, :] = grad_middle.astype(jnp.bfloat16)
    second_terms[...] = (grad_mixer * middle * inverse).astype(jnp.bfloat16)

    def pair_copy(source, target, index):
        return pltpu.make_async_remote_copy(
            src_ref=source,
            dst_ref=target,
            send_sem=pair_sem.at[0, index],
            recv_sem=pair_sem.at[1, index],
            device_id=sibling,
            device_id_type=MESH,
        )

    middle_copy = pair_copy(middle_grads.at[own_rows], middle_grads.at[own_rows], 0)
    middle_copy.start()

    def plane_copy(kind, axis):
        return send(
            landed_v[kind].at[axis, 1],
            plane_in[kind].at[axis],
            (plane_send, plane_recv),
            (kind, axis),
            (across[1 - axis], core),
        )

    for kind in range(3):
        for copy in landed_copies(kind):
            copy.wait()
        for copy in part_copies(kind, False):
            copy.wait()
        for axis in (0, 1):
            landed_v[kind][axis, 1] = (
                own_parts[kind][axis].astype(jnp.float32)
                + landed_v[kind][axis, 1].astype(jnp.float32)
            ).astype(jnp.bfloat16)
            plane_copy(kind, axis).start()
        for copy in part_copies(kind, True):
            copy.start()

    slab = out_result_a.shape[0]
    order = (3, 2, 1, 0)
    plans = list(
        zip(
            (out_source_a, out_source_b, query_source, rest_source),
            (out_result_a, out_result_b, query_result, rest_result),
            scatter_scratch,
        )
    )

    def rows_of(step, first, second_same, first_same):
        other_line = lax.div(partners[step], PLANE)
        first_bit = bits[first] if first_same else 1 - bits[first]
        second_bit = bits[1 - first] if second_same else 1 - bits[1 - first]
        index = other_line * PLANE + first_bit * (1 + first) + second_bit * (2 - first)
        return pl.ds(pl.multiple_of(index * slab, slab), slab)

    def first_copy(number, step, same):
        source, _, scratch = plans[number]
        first = number % 2
        index = step * 2 + same
        return send(
            source.at[rows_of(step, first, same, False)],
            scratch[0].at[index],
            (scratch[4].at[0], scratch[4].at[1]),
            (index,),
            (across[first], core),
        )

    def second_copy(number, step):
        scratch = plans[number][2]
        return send(
            scratch[1].at[step],
            scratch[2].at[step],
            (scratch[4].at[2], scratch[4].at[3]),
            (step,),
            (across[1 - number % 2], core),
        )

    def line_copy(number, step):
        scratch = plans[number][2]
        return send(
            scratch[1].at[step],
            scratch[3].at[step],
            (scratch[4].at[4], scratch[4].at[5]),
            (step,),
            (partners[step], core),
        )

    def start_scatter(number):
        for step in order:
            for same in (0, 1):
                first_copy(number, step, same).start()

    def add_first(number, step, same):
        source, _, scratch = plans[number]
        first_copy(number, step, same).wait()
        mine = source[rows_of(step, number % 2, same, True), :].astype(jnp.float32)
        return mine + scratch[0][step * 2 + same].astype(jnp.float32)

    def finish_first(number, step):
        plans[number][2][1][step] = add_first(number, step, 0).astype(jnp.bfloat16)
        second_copy(number, step).start()

    def finish_second(number, step):
        _, result, scratch = plans[number]
        total = add_first(number, step, 1)
        second_copy(number, step).wait()
        total = total + scratch[2][step].astype(jnp.float32)
        if step:
            scratch[1][step] = total.astype(jnp.bfloat16)
            line_copy(number, step).start()
        else:
            result[...] = total

    def finish_line(number):
        _, result, scratch = plans[number]
        for step in order[:-1]:
            line_copy(number, step).wait()
            result[...] += scratch[3][step].astype(jnp.float32)

    middle_copy.wait()
    attended_grads[...] = (residual_scale * middle_grads[...].astype(jnp.float32)).astype(
        jnp.bfloat16
    )
    loads[6].wait()
    loads[7].wait()
    columns = out_source_a.shape[1]
    out_source_a[...] = matmul_tn(attended_grads[...], mixed_v[:, :columns]).astype(jnp.bfloat16)
    start_scatter(0)
    out_source_b[...] = matmul_tn(attended_grads[...], mixed_v[:, columns:]).astype(jnp.bfloat16)
    start_scatter(1)
    mixed_grads[...] = matmul_nt(attended_grads[...], out_v[...]).astype(jnp.bfloat16)
    for copy in loads[8:11]:
        copy.wait()
    store_slots(key_slots, key_v2[...].astype(jnp.float32))
    store_slots(value_slots, value_v2[...].astype(jnp.float32))
    key_totals[...] = jnp.zeros_like(key_totals)
    value_totals[...] = jnp.zeros_like(value_totals)
    group = query_v.shape[1] // key_v.shape[1]
    blocks = 2
    block_rows = tokens // blocks

    def turned_back(value, cosines, sines):
        return (value * cosines - partner_lanes(value) * sines).astype(jnp.bfloat16)

    def head_pair(pair, carry):
        here = pl.ds(pl.multiple_of(pair * 128, 128), 128)
        for block in range(blocks):
            rows = slice(block * block_rows, (block + 1) * block_rows)
            reach = (block + 1) * block_rows
            total = jnp.zeros((block_rows, 128), jnp.float32)
            query_block = queries_v[rows, here]
            grad_block = mixed_grads[rows, here]
            for parity in range(2):
                slot = 2 * lax.div(2 * pair + parity, group) + parity
                key_block = key_slots[slot, :reach, :]
                scores = causal_scores(query_block, key_block, block * block_rows)
                weight = jnp.exp(scores - jnp.max(scores, axis=-1, keepdims=True))
                weight = weight / jnp.sum(weight, axis=-1, keepdims=True)
                grad_probs = matmul_nt(grad_block, value_slots[slot, :reach, :])
                inner = jnp.sum(weight * grad_probs, axis=-1, keepdims=True)
                grad_scores = (weight * (grad_probs - inner)).astype(jnp.bfloat16)
                total = total + matmul(grad_scores, key_block)
                key_totals[slot, :reach, :] += matmul_tn(grad_scores, query_block)
                value_totals[slot, :reach, :] += matmul_tn(
                    weight.astype(jnp.bfloat16), grad_block
                )
            query_grads[rows, here] = turned_back(
                score_scale * total, cosine[rows, :], sine[rows, :]
            )
        return carry

    lax.fori_loop(0, query_v.shape[1] // 128, head_pair, 0)

    def gathered_pairs(totals):
        found = []
        for pair in range(key_v.shape[1] // 128):
            first, second = 4 * pair, 4 * pair + 2
            low = lane_halves(totals[first])[0] + pltpu.roll(
                lane_halves(totals[first + 1])[1], HEAD_FEATURES, 1
            )
            high = lane_halves(totals[second + 1])[1] + pltpu.roll(
                lane_halves(totals[second])[0], HEAD_FEATURES, 1
            )
            found.append(low + high)
        return found

    for pair, value in enumerate(gathered_pairs(key_totals)):
        key_grads[:, pair * 128 : pair * 128 + 128] = turned_back(
            score_scale * value, cosine[...], sine[...]
        )
    for pair, value in enumerate(gathered_pairs(value_totals)):
        value_grads[:, pair * 128 : pair * 128 + 128] = value.astype(jnp.bfloat16)
    for copy in loads[11:-1]:
        copy.wait()
    query_source[...] = matmul_tn(normed_v[...], query_grads[...]).astype(jnp.bfloat16)
    start_scatter(2)
    normed_send[...] = (
        matmul_nt(query_grads[...], query_v[...])
        + matmul_nt(key_grads[...], key_v[...])
        + matmul_nt(value_grads[...], value_v[...])
    ).astype(jnp.bfloat16)
    normed_copy = pair_copy(normed_send, normed_recv, 1)
    normed_copy.start()
    key_width = key_grads.shape[1]
    rest_source[:, :key_width] = matmul_tn(normed_v[...], key_grads[...]).astype(jnp.bfloat16)
    rest_source[:, key_width : 2 * key_width] = matmul_tn(
        normed_v[...], value_grads[...]
    ).astype(jnp.bfloat16)
    for step in order:
        finish_first(0, step)
        finish_first(1, step)
    normed_copy.wait()

    def stream_rows(rows):
        grad_normed = normed_send[rows, :].astype(jnp.float32) + normed_recv[rows, :].astype(
            jnp.float32
        )
        stream_f = stream_v[rows, :].astype(jnp.float32)
        inverse = lax.rsqrt(jnp.mean(stream_f * stream_f, axis=-1, keepdims=True) + epsilon)
        weighted = grad_normed * gain_first[...].astype(jnp.float32)[None, :]
        total = (
            middle_grads[rows, :].astype(jnp.float32)
            + inverse * weighted
            - stream_f * (inverse * inverse * inverse)
            * jnp.mean(stream_f * weighted, axis=-1, keepdims=True)
        )
        return grad_normed * stream_f * inverse, total

    first_terms[...] = stream_rows(own_rows)[0].astype(jnp.bfloat16)
    lane = lax.broadcasted_iota(jnp.int32, (half, 128), 1)
    experts = LINES * PLANE
    rest_source[:, 2 * key_width :] = (
        matmul_tn(mixer_v[...], grad_logits)
        + matmul_tn(second_terms[...], (lane == experts).astype(jnp.bfloat16))
        + matmul_tn(first_terms[...], (lane == experts + 1).astype(jnp.bfloat16))
    ).astype(jnp.bfloat16)
    loads[-1].start()
    start_scatter(3)
    for position in range(2):
        rows = slice(position * half, position * half + half)
        normed_recv[rows, :] = stream_rows(rows)[1].astype(jnp.bfloat16)
    stream_copy = pltpu.make_async_copy(normed_recv, grad_stream, store_sem.at[4])
    stream_copy.start()
    for step in order:
        finish_second(0, step)
        finish_second(1, step)
    for step in order:
        finish_first(2, step)
        finish_first(3, step)
    for step in (1, 2, 3):
        out_copy(step).wait()
    loads[-1].wait()
    mixture = mixer_v[...].astype(jnp.float32)
    for step in range(1, LINES):
        mixture = mixture + out_in[step - 1].astype(jnp.float32)
    middle = stream_v[own_rows, :].astype(jnp.float32) + residual_scale * attended_v[...].astype(jnp.float32)
    result = middle + residual_scale * mixture
    layer_v[...] = result.astype(jnp.bfloat16)
    layer_pair = pair_copy(layer_v, layer_out.at[own_rows], 2)
    layer_pair.start()
    layer_own = pltpu.make_async_copy(layer_v, layer_out.at[own_rows], store_sem.at[0])
    layer_own.start()
    row_lane = lax.broadcasted_iota(jnp.int32, (8, 128), 1)
    squares = jnp.zeros((8, 128), jnp.float32)
    for index, value in enumerate((result, attended_v[...].astype(jnp.float32), mixture)):
        total = jnp.sum(jnp.sum(value * value, axis=1, keepdims=True), axis=0, keepdims=True)
        squares = jnp.where(row_lane == index, total, squares)
    for step in order:
        finish_second(2, step)
        finish_second(3, step)
    def expert_copy(kind):
        return pltpu.make_async_copy(own_parts[kind], expert_grads[kind], store_sem.at[1 + kind])

    for kind in range(3):
        for copy in part_copies(kind, True):
            copy.wait()
        for axis in (0, 1):
            plane_copy(kind, axis).wait()
            if kind in DEFERRED:
                deferred_copy(kind, axis).wait()
            own_parts[kind][axis] = (
                own_parts[kind][axis].astype(jnp.float32)
                + landed_v[kind][axis, 0].astype(jnp.float32)
                + plane_in[kind][axis].astype(jnp.float32)
            ).astype(jnp.bfloat16)
        expert_copy(kind).start()
    finish_line(3)
    last_send[:slab, :] = rest_result[:, 2 * key_width :]
    last_send[slab:, :] = squares
    last_copy = pair_copy(last_send, last_recv, 3)
    last_copy.start()
    for number in range(3):
        finish_line(number)
    last_copy.wait()
    small_out[...] = last_send[...] + last_recv[...]
    layer_pair.wait()
    layer_own.wait()
    stream_copy.wait()
    for kind in range(3):
        expert_copy(kind).wait()


def run_back(expert_results, operands, front_results):
    low, wide = jnp.bfloat16, jnp.float32
    shape = jax.ShapeDtypeStruct
    vmem = pltpu.VMEM
    far = pl.BlockSpec(memory_space=pl.ANY)
    near = pl.BlockSpec(memory_space=pltpu.VMEM)
    tokens, width = operands[0].shape
    half = tokens // 2
    query_width, key_width = operands[4].shape[1], operands[5].shape[1]
    kept = expert_results[LINES + 2 : LINES + 5]
    tile_shapes = [value.shape[1:] for value in kept]
    half_shapes = [(value[0] // 2, value[1]) for value in tile_shapes]
    slab = width // (LINES * PLANE)
    slots = 2 * key_width // HEAD_FEATURES
    rest_width = 2 * key_width + 128
    widths = (query_width // 2, query_width // 2, query_width, rest_width)
    dma = pltpu.SemaphoreType.DMA
    scatter_scratch = []
    for columns in widths:
        scatter_scratch += [
            vmem((2 * LINES, slab, columns), low),
            vmem((LINES, slab, columns), low),
            vmem((LINES, slab, columns), low),
            vmem((LINES, slab, columns), low),
            dma((6, 2 * LINES)),
        ]
    return pl.pallas_call(
        back_kernel,
        name="back",
        out_shape=(
            shape((tokens, width), low),
            shape((tokens, width), low),
            *[shape((slab, columns), wide) for columns in widths],
            *[shape((2, *value), low) for value in half_shapes],
            shape((slab + 8, 128), wide),
        ),
        in_specs=[far] * (LINES + 8)
        + [far, far, near, near, far, far, far, far, near, near, near]
        + [far] * 8,
        out_specs=(far,) * 2 + (near,) * 4 + (far,) * 3 + (near,),
        scratch_shapes=[
            vmem((tokens, width), low),
            vmem((half, width), low),
            vmem((width, query_width), low),
            vmem((width, key_width), low),
            vmem((width, key_width), low),
            vmem((query_width, width), low),
            vmem((tokens, width), low),
            vmem((tokens, query_width), low),
            vmem((tokens, query_width), low),
            vmem((half, width), wide),
            vmem((half, width), low),
            vmem((LINES - 1, half, width), low),
            vmem((half, width), low),
            vmem((tokens, key_width), low),
            vmem((tokens, key_width), low),
            vmem((half, width), low),
            vmem((half, 128), wide),
            vmem((half, 128), wide),
            vmem((slots, tokens, 128), low),
            vmem((slots, tokens, 128), low),
            vmem((slots, tokens, 128), wide),
            vmem((slots, tokens, 128), wide),
            vmem((tokens, width), low),
            vmem((tokens, width), low),
            vmem((tokens, query_width), low),
            vmem((tokens, key_width), low),
            vmem((tokens, key_width), low),
            vmem((tokens, width), low),
            *[vmem((2, *value), low) for value in half_shapes],
            *[vmem((2, 2, *value), low) for value in half_shapes],
            *[vmem((2, *value), low) for value in half_shapes],
            *[vmem((width, columns), low) for columns in widths],
            *scatter_scratch,
            vmem((slab + 8, 128), wide),
            vmem((slab + 8, 128), wide),
            dma((17,)),
            dma((3, 4)),
            dma((LINES - 1,)),
            dma((LINES - 1,)),
            dma((2, 4)),
            dma((3, 2)),
            dma((3, 2)),
            dma((5,)),
            dma((3, 2)),
            dma((3, 2)),
        ],
        compiler_params=pltpu.CompilerParams(
            collective_id=1, has_side_effects=True, vmem_limit_bytes=63 << 20
        ),
    )(*expert_results, *operands, *front_results)


def finish_kernel(*refs):
    layer_in, sources, refs = refs[0], refs[1:10], refs[10:]
    layer_out, refs = refs[0], refs[1:]
    grad_stream, out_grad, query_grad, key_grad, value_grad = refs[:5]
    gate_grad, up_grad, down_grad, router_grad, second_gain, first_gain, rms = refs[5:12]
    loaded, load_sem = refs[12:21], refs[21]
    layer_copy = pltpu.make_async_copy(layer_in, layer_out, load_sem.at[9])
    layer_copy.start()
    stream_low, out_first, out_second, query_low, rest, gate_low, up_low, down_low, small = loaded
    copies = [
        pltpu.make_async_copy(source, target, load_sem.at[index])
        for index, (source, target) in enumerate(zip(sources, loaded))
    ]
    for copy in copies:
        copy.start()
    copies[0].wait()
    grad_stream[...] = stream_low[...].astype(jnp.float32)
    for copy in copies[1:]:
        copy.wait()
    half = out_first.shape[1]
    out_grad[:, :half] = out_first[...]
    out_grad[:, half:] = out_second[...]
    query_grad[...] = query_low[...]
    width = key_grad.shape[1]
    key_grad[...] = rest[:, :width]
    value_grad[...] = rest[:, width : 2 * width]
    for low, grad in ((gate_low, gate_grad), (up_low, up_grad), (down_low, down_grad)):
        rows = low.shape[1]
        grad[0, :rows, :] = low[0].astype(jnp.float32)
        grad[0, rows:, :] = low[1].astype(jnp.float32)
    experts, slab = router_grad.shape
    turned = small[:slab, :].T
    router_grad[...] = turned[:experts, :]
    second_gain[...] = turned[experts, :]
    first_gain[...] = turned[experts + 1, :]
    total = grad_stream.shape[0] * grad_stream.shape[1]
    rms[...] = jnp.sqrt(small[slab : slab + 1, :3] / total)
    layer_copy.wait()


def run_finish(layer, values, tokens, width, experts):
    shape = jax.ShapeDtypeStruct
    wide = jnp.float32
    far = pl.BlockSpec(memory_space=pl.ANY)
    near = pl.BlockSpec(memory_space=pltpu.VMEM)
    slab, query_width = values[3].shape
    key_width = (values[4].shape[1] - 128) // 2
    tiles = [(1, 2 * value.shape[1], value.shape[2]) for value in values[5:8]]
    return pl.pallas_call(
        finish_kernel,
        name="finish",
        out_shape=(
            shape(layer.shape, layer.dtype),
            shape((tokens, width), wide),
            shape((slab, query_width), wide),
            shape((slab, query_width), wide),
            shape((slab, key_width), wide),
            shape((slab, key_width), wide),
            *[shape(tile, wide) for tile in tiles],
            shape((experts, slab), wide),
            shape((slab,), wide),
            shape((slab,), wide),
            shape((1, 3), wide),
        ),
        in_specs=[far] * 10,
        out_specs=(near,) * 13,
        scratch_shapes=[pltpu.VMEM(value.shape, value.dtype) for value in values]
        + [pltpu.SemaphoreType.DMA((10,))],
        compiler_params=pltpu.CompilerParams(vmem_limit_bytes=63 << 20),
    )(layer, *values)


def dense_shards(
    stream,
    cotangent,
    attention_gain,
    query_weight,
    key_matrix,
    value_matrix,
    out_weight,
    mixture_gain,
    router_weight,
    gate_weight,
    up_weight,
    down_weight,
    routes,
):
    tok_rows, model_width = stream.shape
    experts = router_weight.shape[1]
    steps_up = np.arange(HEAD_FEATURES // 2, dtype=np.float32) * np.float32(2.0 / HEAD_FEATURES)
    turns = np.exp(-steps_up * np.log(np.float32(rope_base)))
    angles = np.arange(SEQ_LEN, dtype=np.float32)[:, None] * turns[None, :]
    cosines, sines = np.cos(angles), np.sin(angles)
    operands = [
        stream,
        cotangent,
        attention_gain,
        mixture_gain,
        query_weight,
        key_matrix,
        value_matrix,
        out_weight,
        router_weight.T,
        routes.T,
        jnp.asarray(np.tile(cosines, (1, 4))),
        jnp.asarray(np.tile(np.concatenate([-sines, sines], axis=1), (1, 2))),
    ]
    front = run_front(operands, [gate_weight[0], up_weight[0], down_weight[0]])
    layer_part, *partial = run_back(
        front[: LINES + 8], operands[:9] + operands[10:], front[LINES + 8 :]
    )
    (
        layer_out,
        grad_stream,
        out_grad,
        query_grad,
        key_grad,
        value_grad,
        gate_grad,
        up_grad,
        down_grad,
        router_grad,
        second_gain,
        first_gain,
        rms_stats,
    ) = run_finish(layer_part, partial, tok_rows, model_width, experts)
    return (
        layer_out,
        grad_stream,
        first_gain,
        query_grad,
        key_grad,
        value_grad,
        out_grad.T,
        second_gain,
        router_grad.T,
        gate_grad,
        up_grad,
        down_grad,
        rms_stats,
    )


def solution(mesh):
    in_specs = (
        P("ep", None),
        P("ep", None),
        P(),
        P(None, "tp"),
        P(None, "tp"),
        P(None, "tp"),
        P("tp", None),
        P(),
        P(),
        P("ep", None, "tp"),
        P("ep", None, "tp"),
        P("ep", "tp", None),
        P("ep", None),
    )
    out_specs = (
        P("ep", None),
        P("ep", None),
        P("ep"),
        P("ep", "tp"),
        P("ep", "tp"),
        P("ep", "tp"),
        P("tp", "ep"),
        P("ep"),
        P("ep", None),
        P("ep", None, "tp"),
        P("ep", None, "tp"),
        P("ep", "tp", None),
        P("ep", None),
    )
    ep_size = mesh.shape["ep"]
    dense = mesh.shape["tp"] == 2 and ep_size <= 2 * TOP and ep_size == 16
    shards = dense_shards if dense else routed_shards
    return jax.shard_map(shards, mesh=mesh, in_specs=in_specs, out_specs=out_specs, check_vma=False)
```

```python
import functools

import jax
import jax.numpy as jnp
import numpy as np
from jax import lax
from jax.experimental import pallas as pl
from jax.experimental.pallas import tpu as pltpu
from jax.sharding import PartitionSpec as P

HEAD_FEATURES = 64
TOP = 8
SEQ_LEN = 512


epsilon = 1e-06
score_scale = 0.015625
residual_scale = 0.22
rope_base = 10000.0
masked_score = -1e30


def rope_tables(sequence_length):
    half_dim = HEAD_FEATURES // 2
    steps_up = jnp.arange(half_dim).astype(jnp.float32) * (2.0 / HEAD_FEATURES)
    inverse = jnp.exp(-steps_up * jnp.log(rope_base))
    places = jnp.arange(sequence_length).astype(jnp.float32)
    angles = places[:, None] * inverse[None, :]
    return (jnp.cos(angles), jnp.sin(angles))


def apply_rotation(value_rows, cosine_table, sine_values):
    half_dim = value_rows.shape[-1] // 2
    first_half = value_rows[..., :half_dim]
    second_half = value_rows[..., half_dim:]
    cos_rows = cosine_table[:, None, :]
    sin_rows = sine_values[:, None, :]
    return jnp.concatenate(
        [
            first_half * cos_rows - second_half * sin_rows,
            second_half * cos_rows + first_half * sin_rows,
        ],
        axis=-1,
    )


def rotary_back(grads_in, cosine_table, sine_values):
    half_dim = grads_in.shape[-1] // 2
    first_half = grads_in[..., :half_dim]
    second_half = grads_in[..., half_dim:]
    cos_rows = cosine_table[:, None, :]
    sin_rows = sine_values[:, None, :]
    return jnp.concatenate(
        [
            first_half * cos_rows + second_half * sin_rows,
            second_half * cos_rows - first_half * sin_rows,
        ],
        axis=-1,
    )


def block_scores(query_block, rotated_keys, row_start, block_rows, row_stop):
    scores = score_scale * jnp.einsum(
        "qhgd,khd->hgqk", query_block, rotated_keys, preferred_element_type=jnp.float32
    )
    causal = (row_start + jnp.arange(block_rows))[:, None] >= jnp.arange(row_stop)[None, :]
    return jnp.where(causal, scores, masked_score)


def attention_forward(query_rows, rotated_keys, value_rows):
    sequence_length = query_rows.shape[0]
    block_rows = min(512, sequence_length)
    scores = block_scores(query_rows, rotated_keys, 0, block_rows, block_rows)
    largest = jnp.max(scores, axis=-1, keepdims=True)
    weights_exp = jnp.exp(scores - largest)
    totals = jnp.sum(weights_exp, axis=-1, keepdims=True)
    probs_low = (weights_exp / totals).astype(jnp.bfloat16)
    outputs = jnp.einsum(
        "hgqk,khd->qhgd", probs_low, value_rows, preferred_element_type=jnp.float32
    )
    normalizers = [largest + jnp.log(totals)]
    return (outputs, normalizers)


def attention_backward(query_rows, rotated_keys, value_rows, normalizers, grad_mixed):
    sequence_length = query_rows.shape[0]
    block_rows = min(512, sequence_length)
    grad_keys = jnp.zeros(rotated_keys.shape, jnp.float32)
    grad_values = jnp.zeros(value_rows.shape, jnp.float32)
    grad_queries = []
    for block_index, row_start in enumerate(range(0, sequence_length, block_rows)):
        row_stop = row_start + block_rows
        scores = block_scores(query_rows, rotated_keys, row_start, block_rows, row_stop)
        probs = jnp.exp(scores - normalizers[block_index])
        probs_low = probs.astype(jnp.bfloat16)
        grad_probs = jnp.einsum(
            "qhgd,khd->hgqk", grad_mixed, value_rows, preferred_element_type=jnp.float32
        )
        inner = jnp.sum(probs * grad_probs, axis=-1, keepdims=True)
        grad_scores = (probs * (grad_probs - inner)).astype(jnp.bfloat16)
        grad_queries.append(
            score_scale
            * jnp.einsum(
                "hgqk,khd->qhgd", grad_scores, rotated_keys, preferred_element_type=jnp.float32
            )
        )
        grad_keys = grad_keys.at[:row_stop].add(
            score_scale
            * jnp.einsum(
                "hgqk,qhgd->khd", grad_scores, query_rows, preferred_element_type=jnp.float32
            )
        )
        grad_values = grad_values.at[:row_stop].add(
            jnp.einsum("hgqk,qhgd->khd", probs_low, grad_mixed, preferred_element_type=jnp.float32)
        )
    return (grad_queries[0], grad_keys, grad_values)


def to_owners(packed):
    return lax.all_to_all(packed, "ep", split_axis=1, concat_axis=1, tiled=True)


def back_to_tokens(rows_low, slot_count, model_width):
    returned = lax.all_to_all(rows_low, "ep", split_axis=1, concat_axis=1, tiled=True)
    joined = lax.all_gather(returned, "tp", axis=0, tiled=True)
    return joined.reshape(slot_count, model_width)


def from_owners(term_fn, slot_count, experts, model_width):
    share_rows = slot_count // lax.axis_size("tp")
    summed = lax.psum_scatter(
        term_fn(jnp.int32(0), lax.axis_size("tp") * share_rows).astype(jnp.bfloat16),
        "tp",
        scatter_dimension=0,
        tiled=True,
    ).astype(jnp.float32)
    summed = summed.astype(jnp.bfloat16).reshape(share_rows // experts, experts, model_width)
    return back_to_tokens(summed, slot_count, model_width)


def seq_rms(value_rows, seq_count):
    return jnp.sqrt(jnp.mean((value_rows * value_rows).reshape(seq_count, -1), axis=1))


def routed_shards(
    stream,
    cotangent,
    attention_gain,
    query_weight,
    key_matrix,
    value_matrix,
    out_weight,
    mixture_gain,
    router_weight,
    gate_weight,
    up_weight,
    down_weight,
    routes,
):
    tok_rows, model_width = stream.shape
    experts = router_weight.shape[1]
    cap_slots = tok_rows * TOP * 5 // (4 * experts)
    slot_count = cap_slots * experts
    query_heads = query_weight.shape[1] // HEAD_FEATURES
    key_heads = key_matrix.shape[1] // HEAD_FEATURES
    group_width = query_heads // key_heads
    seq_count = tok_rows // SEQ_LEN
    stream_f = stream.astype(jnp.float32)
    grad_result = cotangent.astype(jnp.float32)
    gain_first = attention_gain.astype(jnp.float32)
    gain_second = mixture_gain.astype(jnp.float32)
    cosine_table, sine_values = rope_tables(SEQ_LEN)
    cosine_rows = jnp.tile(cosine_table, (seq_count, 1))
    sine_rows = jnp.tile(sine_values, (seq_count, 1))
    zero_low = jnp.zeros((), jnp.bfloat16)
    inv_first = lax.rsqrt(jnp.mean(stream_f * stream_f, axis=-1, keepdims=True) + epsilon)
    normalized_input = (stream_f * inv_first * gain_first).astype(jnp.bfloat16)
    query_pre = jnp.dot(normalized_input, query_weight, preferred_element_type=jnp.float32).reshape(
        tok_rows, query_heads, HEAD_FEATURES
    )
    key_pre = jnp.dot(normalized_input, key_matrix, preferred_element_type=jnp.float32).reshape(
        tok_rows, key_heads, HEAD_FEATURES
    )
    query_rows = (
        apply_rotation(query_pre, cosine_rows, sine_rows)
        .astype(jnp.bfloat16)
        .reshape(tok_rows, key_heads, group_width, HEAD_FEATURES)
    )
    rotated_keys = apply_rotation(key_pre, cosine_rows, sine_rows).astype(jnp.bfloat16)
    value_rows = (
        jnp.dot(normalized_input, value_matrix, preferred_element_type=jnp.float32)
        .astype(jnp.bfloat16)
        .reshape(tok_rows, key_heads, HEAD_FEATURES)
    )
    mixed_seq, norms_seq = attention_forward(query_rows, rotated_keys, value_rows)
    mixed_low = mixed_seq.reshape(tok_rows, query_heads * HEAD_FEATURES).astype(jnp.bfloat16)
    attended = lax.psum(
        jnp.dot(mixed_low, out_weight, preferred_element_type=jnp.float32).astype(jnp.bfloat16),
        "tp",
    ).astype(jnp.float32)
    middle = stream_f + residual_scale * attended
    inv_second = lax.rsqrt(jnp.mean(middle * middle, axis=-1, keepdims=True) + epsilon)
    mixer_in = (middle * inv_second * gain_second).astype(jnp.bfloat16)
    logits = jnp.dot(mixer_in, router_weight, preferred_element_type=jnp.float32)
    expert_ids = jnp.arange(experts, dtype=jnp.int32)
    route_hot = routes[:, :, None] == expert_ids[None, None, :]
    chosen = jnp.sum(jnp.where(route_hot, logits[:, None, :], 0.0), axis=-1)
    chosen_exp = jnp.exp(chosen - jnp.max(chosen, axis=-1, keepdims=True))
    gate_probs = chosen_exp / jnp.sum(chosen_exp, axis=-1, keepdims=True)
    flat_routes = routes.reshape(-1)
    flat_hot = route_hot.reshape(tok_rows * TOP, experts).astype(jnp.int32)
    ranks = jnp.sum((jnp.cumsum(flat_hot, axis=0) - 1) * flat_hot, axis=1)
    slot_index = ranks * experts + flat_routes
    source_pair = (
        jnp.zeros((slot_count,), jnp.int32)
        .at[slot_index]
        .set(jnp.arange(tok_rows * TOP, dtype=jnp.int32))
    )
    filled = jnp.zeros((slot_count,), jnp.bool_).at[slot_index].set(True)
    source_token = source_pair // TOP
    sent_rows = jnp.where(filled[:, None], mixer_in[source_token], zero_low).reshape(
        cap_slots, experts, model_width
    )
    received = to_owners(sent_rows).reshape(slot_count, model_width)
    gate_matrix = gate_weight[0]
    up_matrix = up_weight[0]
    down_matrix = down_weight[0]
    gate_pre = jnp.dot(received, gate_matrix, preferred_element_type=jnp.float32)
    up_pre = jnp.dot(received, up_matrix, preferred_element_type=jnp.float32)
    sigmoid_gate = jax.nn.sigmoid(gate_pre)
    silu_gate = gate_pre * sigmoid_gate
    active = (silu_gate * up_pre).astype(jnp.bfloat16)

    def down_term(row_start, row_count):
        return jnp.dot(active, down_matrix, preferred_element_type=jnp.float32)

    expert_rows = from_owners(down_term, slot_count, experts, model_width)
    picked_rows = expert_rows[slot_index].reshape(tok_rows, TOP, model_width)
    mixture = jnp.sum(gate_probs[:, :, None] * picked_rows, axis=1)
    result = middle + residual_scale * mixture
    layer_out = result.astype(jnp.bfloat16)
    rms_stats = jnp.stack(
        [seq_rms(result, seq_count), seq_rms(attended, seq_count), seq_rms(mixture, seq_count)],
        axis=1,
    )
    grad_mix = residual_scale * grad_result
    grad_weighting = jnp.sum(picked_rows * grad_mix[:, None, :], axis=-1)
    grad_chosen = gate_probs * (
        grad_weighting - jnp.sum(gate_probs * grad_weighting, axis=-1, keepdims=True)
    )
    grad_logits = jnp.sum(jnp.where(route_hot, grad_chosen[:, :, None], 0.0), axis=1).astype(
        jnp.bfloat16
    )
    router_grad = jnp.dot(mixer_in.T, grad_logits, preferred_element_type=jnp.float32)
    flat_gates = gate_probs.reshape(-1)
    grad_sent = jnp.where(
        filled[:, None],
        (flat_gates[source_pair][:, None] * grad_mix[source_token]).astype(jnp.bfloat16),
        zero_low,
    ).reshape(cap_slots, experts, model_width)
    grad_received = to_owners(grad_sent).reshape(slot_count, model_width)
    grad_active = jnp.dot(grad_received, down_matrix.T, preferred_element_type=jnp.float32)
    down_grad = jnp.dot(active.T, grad_received, preferred_element_type=jnp.float32)
    grad_gate_pre = (
        grad_active * up_pre * sigmoid_gate * (1.0 + gate_pre * (1.0 - sigmoid_gate))
    ).astype(jnp.bfloat16)
    grad_up_pre = (grad_active * silu_gate).astype(jnp.bfloat16)
    gate_grad = jnp.dot(received.T, grad_gate_pre, preferred_element_type=jnp.float32)
    up_grad = jnp.dot(received.T, grad_up_pre, preferred_element_type=jnp.float32)

    def input_term(row_start, row_count):
        return jnp.dot(grad_gate_pre, gate_matrix.T, preferred_element_type=jnp.float32) + jnp.dot(
            grad_up_pre, up_matrix.T, preferred_element_type=jnp.float32
        )

    grad_rows = from_owners(input_term, slot_count, experts, model_width)
    grad_mixer = jnp.dot(
        grad_logits, router_weight.T, preferred_element_type=jnp.float32
    ) + jnp.sum(
        grad_rows[slot_index].reshape(tok_rows, TOP, model_width), axis=1, dtype=jnp.float32
    )
    weighted_second = grad_mixer * gain_second
    second_grad = jnp.sum(grad_mixer * middle * inv_second, axis=0)
    grad_middle = (
        grad_result
        + inv_second * weighted_second
        - middle * inv_second**3 * jnp.mean(middle * weighted_second, axis=-1, keepdims=True)
    )
    grad_attended = (residual_scale * grad_middle).astype(jnp.bfloat16)
    out_grad_t = jnp.dot(grad_attended.T, mixed_low, preferred_element_type=jnp.float32)
    grad_mixed = (
        jnp.dot(grad_attended, out_weight.T, preferred_element_type=jnp.float32)
        .astype(jnp.bfloat16)
        .reshape(tok_rows, key_heads, group_width, HEAD_FEATURES)
    )
    grad_query_seq, grad_key_seq, grad_value_seq = attention_backward(
        query_rows, rotated_keys, value_rows, norms_seq, grad_mixed
    )
    grad_queries_rot = grad_query_seq.reshape(tok_rows, query_heads, HEAD_FEATURES)
    grad_query_pre = (
        rotary_back(grad_queries_rot, cosine_rows, sine_rows)
        .astype(jnp.bfloat16)
        .reshape(tok_rows, query_heads * HEAD_FEATURES)
    )
    grad_key_pre = (
        rotary_back(grad_key_seq, cosine_rows, sine_rows)
        .astype(jnp.bfloat16)
        .reshape(tok_rows, key_heads * HEAD_FEATURES)
    )
    grad_values_low = grad_value_seq.astype(jnp.bfloat16).reshape(
        tok_rows, key_heads * HEAD_FEATURES
    )
    query_grad = jnp.dot(normalized_input.T, grad_query_pre, preferred_element_type=jnp.float32)
    key_grad = jnp.dot(normalized_input.T, grad_key_pre, preferred_element_type=jnp.float32)
    value_grad = jnp.dot(normalized_input.T, grad_values_low, preferred_element_type=jnp.float32)
    normed_term = jnp.dot(grad_query_pre, query_weight.T, preferred_element_type=jnp.float32)
    normed_term = normed_term + jnp.dot(
        grad_key_pre, key_matrix.T, preferred_element_type=jnp.float32
    )
    normed_term = normed_term + jnp.dot(
        grad_values_low, value_matrix.T, preferred_element_type=jnp.float32
    )
    grad_normed = lax.psum(normed_term.astype(jnp.bfloat16), "tp").astype(jnp.float32)
    weighted_first = grad_normed * gain_first
    first_grad = jnp.sum(grad_normed * stream_f * inv_first, axis=0)
    grad_stream = (
        grad_middle
        + inv_first * weighted_first
        - stream_f * inv_first**3 * jnp.mean(stream_f * weighted_first, axis=-1, keepdims=True)
    )
    reduced = (
        lax.psum_scatter(query_grad, "ep", scatter_dimension=0, tiled=True),
        lax.psum_scatter(key_grad, "ep", scatter_dimension=0, tiled=True),
        lax.psum_scatter(value_grad, "ep", scatter_dimension=0, tiled=True),
        lax.psum_scatter(out_grad_t, "ep", scatter_dimension=0, tiled=True),
        lax.psum_scatter(router_grad, "ep", scatter_dimension=0, tiled=True),
        lax.psum_scatter(first_grad, "ep", scatter_dimension=0, tiled=True),
        lax.psum_scatter(second_grad, "ep", scatter_dimension=0, tiled=True),
    )
    return (
        layer_out,
        grad_stream,
        reduced[5],
        reduced[0],
        reduced[1],
        reduced[2],
        reduced[3].T,
        reduced[6],
        reduced[4],
        gate_grad[None],
        up_grad[None],
        down_grad[None],
        rms_stats,
    )


MESH = pl.DeviceIdType.MESH
PLANE = 4
LINES = 4
CHUNK = 64
DEFERRED = (2,)


def flip(place, unit):
    return place + unit * (1 - 2 * lax.rem(lax.div(place, unit), 2))


def flip_line(place, step):
    if step % 2:
        place = flip(place, PLANE)
    if step // 2:
        place = flip(place, 2 * PLANE)
    return place


def matmul(left, right):
    return jnp.dot(left, right, preferred_element_type=jnp.float32)


def matmul_nt(left, right):
    return lax.dot_general(
        left, right, (((1,), (1,)), ((), ())), preferred_element_type=jnp.float32
    )


def matmul_tn(left, right):
    return lax.dot_general(
        left, right, (((0,), (0,)), ((), ())), preferred_element_type=jnp.float32
    )


def lane_halves(value):
    lane = lax.broadcasted_iota(jnp.int32, value.shape, 1)
    low = jnp.where(lane < HEAD_FEATURES, value, 0.0)
    high = jnp.where(lane < HEAD_FEATURES, 0.0, value)
    return low, high


def partner_lanes(value):
    width = value.shape[1]
    quarter = HEAD_FEATURES // 2
    lane = lax.broadcasted_iota(jnp.int32, value.shape, 1)
    ahead = pltpu.roll(value, width - quarter, 1)
    behind = pltpu.roll(value, quarter, 1)
    return jnp.where(lax.rem(lane, HEAD_FEATURES) < quarter, ahead, behind)


def causal_scores(query_block, key_block, row_start):
    scores = score_scale * matmul_nt(query_block, key_block)
    row = lax.broadcasted_iota(jnp.int32, scores.shape, 0) + row_start
    column = lax.broadcasted_iota(jnp.int32, scores.shape, 1)
    return jnp.where(row >= column, scores, masked_score)


def store_slots(slots, values):
    for group in range(values.shape[1] // HEAD_FEATURES):
        pair = group // 2
        low, high = lane_halves(values[:, pair * 128 : pair * 128 + 128])
        if group % 2:
            low = pltpu.roll(high, HEAD_FEATURES, 1)
        else:
            high = pltpu.roll(low, HEAD_FEATURES, 1)
        slots[2 * group] = low.astype(jnp.bfloat16)
        slots[2 * group + 1] = high.astype(jnp.bfloat16)


def front_kernel(*refs):
    tiles = 2 * PLANE
    refs = list(refs)

    def take(count):
        taken = refs[:count]
        del refs[:count]
        return taken

    stream, cotangent, gain_first, gain_second, query_weight, key_weight = take(6)
    value_weight, out_weight, router, routes, cosine, sine = take(6)
    weights = take(3)
    out_parts = take(LINES)
    grow_sum, weighting_sum = take(2)
    kept = take(3)
    landed = take(3)
    mixer_own, probs_own, normed_out, queries_out, keys_out, values_out, mixed_out = take(7)
    attended = take(1)[0]
    mixer, cots, probs, gates, ups, downs = take(6)
    scaled, ggate, gup, grow, grow_in, outs, weighting, weighting_in = take(8)
    part_send, part_recv = take(2)
    load_sem, own_sem, weight_send, weight_recv = take(4)
    relay_send, relay_recv, probs_send, probs_recv, part_sem = take(5)
    result_sem, store_sem, kept_sem = take(3)
    grow_send, grow_recv, weighting_send, weighting_recv = take(4)
    core_send, core_recv, plane_send, plane_recv, ready_sem = take(5)
    held = (gates, ups, downs)
    rows_all, width = mixer.shape
    half = rows_all // LINES
    tokens = 2 * half
    span = gates.shape[2]
    column_tiles = width // span
    heads_width = query_weight.shape[1]
    pieces = heads_width // span
    tall = scaled.shape[1]

    place = lax.axis_index("ep")
    core = lax.axis_index("tp")
    line = lax.div(place, PLANE)
    sibling = (place, 1 - core)
    across = [(flip(place, 1), core), (flip(place, 2), core)]
    partners = [(flip_line(place, step), core) for step in range(LINES)]
    own_rows = pl.ds(pl.multiple_of(core * half, half), half)
    stream_v, normed = outs.at[pl.ds(0, tokens)], outs.at[pl.ds(tokens, tokens)]

    def block_rows_of(block):
        return pl.ds(pl.multiple_of(block * half, half), half)

    line_rows = block_rows_of(line)

    barrier = pltpu.get_barrier_semaphore()
    for other in across + partners[1:] + [sibling]:
        pl.semaphore_signal(barrier, inc=1, device_id=other, device_id_type=MESH)

    def tall_loads(source, column, target, tile, index):
        return [
            pltpu.make_async_copy(
                source.at[pl.ds(start, size), pl.ds(column * span, span)],
                target.at[tile + part, pl.ds(0, size)],
                load_sem.at[index + part],
            )
            for part, (start, size) in enumerate(((0, tall), (tall, width - tall)))
        ]

    loads = [pltpu.make_async_copy(stream, stream_v, load_sem.at[0])]
    for piece in range(pieces):
        loads += tall_loads(query_weight, piece, scaled, 2 * piece, 1 + 2 * piece)
    loads += tall_loads(key_weight, 0, ggate, 0, 1 + 2 * pieces)
    loads += tall_loads(value_weight, 0, ggate, tiles - 2, 3 + 2 * pieces)
    out_loads = [
        pltpu.make_async_copy(
            out_weight.at[:, pl.ds(column * span, span)],
            grow.at[column, pl.ds(0, heads_width)],
            load_sem.at[5 + 2 * pieces + column],
        )
        for column in range(column_tiles)
    ]
    for copy in loads + out_loads:
        copy.start()
    pl.semaphore_wait(barrier, LINES + 2)

    def send(source, target, sems, index, device):
        return pltpu.make_async_remote_copy(
            src_ref=source,
            dst_ref=target,
            send_sem=sems[0].at[index],
            recv_sem=sems[1].at[index],
            device_id=device,
            device_id_type=MESH,
        )

    weight_sems = (weight_send, weight_recv)

    def direct(kind, axis):
        return send(
            weights[kind], held[kind].at[axis + 1], weight_sems, (kind, axis), across[axis]
        )

    def to_sibling(kind, slot):
        source = weights[kind] if slot == 0 else held[kind].at[slot]
        return send(source, held[kind].at[PLANE + slot], weight_sems, (kind, 2 + slot), sibling)

    def onward(kind, axis):
        source, target = held[kind].at[2 - axis], held[kind].at[3]
        if kind == 1:
            part = pl.ds(axis * (width // 2), width // 2)
            source, target = held[kind].at[2 - axis, part], held[kind].at[3, part]
        return send(source, target, weight_sems, (kind, 6 + axis), across[axis])

    onwards = {0: (0,), 1: (0, 1), 2: (1,)}

    def relay(array, hop, downward):
        gathered = (cots, mixer)[array]
        shift = -1 if downward else 1
        block = block_rows_of(jnp.clip(line - shift * hop, 0, LINES - 1))
        source = gathered.at[block]
        if hop == 0 and array == 0:
            source = cotangent.at[own_rows]
        return send(
            source,
            gathered.at[block],
            (relay_send, relay_recv),
            (array, downward, hop),
            (place + shift * PLANE, core),
        )

    def arriving(array, hop, downward):
        gathered = (cots, mixer)[array]
        shift = -1 if downward else 1
        block = block_rows_of(jnp.clip(line - shift * (hop + 1), 0, LINES - 1))
        return send(
            gathered.at[block],
            gathered.at[block],
            (relay_send, relay_recv),
            (array, downward, hop),
            (place + shift * PLANE, core),
        )

    def relay_sends(hop, downward):
        if downward:
            return jnp.logical_and(line > 0, line + hop < LINES)
        return jnp.logical_and(line < LINES - 1, line - hop >= 0)

    def relay_receives(hop, downward):
        if downward:
            return line + 1 + hop < LINES
        return line - 1 - hop >= 0

    def start_relay(array, hop):
        for downward in (0, 1):

            @pl.when(relay_sends(hop, downward))
            def _():
                relay(array, hop, downward).start()

    def receive_relay(array, hop):
        for downward in (0, 1):

            @pl.when(relay_receives(hop, downward))
            def _():
                arriving(array, hop, downward).wait_recv()

    def finish_relay(array, hop):
        for downward in (0, 1):

            @pl.when(relay_sends(hop, downward))
            def _():
                relay(array, hop, downward).wait_send()

    for kind in range(3):
        for axis in (0, 1):
            direct(kind, axis).start()
    start_relay(0, 0)
    own_copies = [
        pltpu.make_async_copy(weights[kind], held[kind].at[0], own_sem.at[kind])
        for kind in range(3)
    ]
    own_copies.append(
        pltpu.make_async_copy(cotangent.at[own_rows], cots.at[line_rows], own_sem.at[3])
    )
    for kind in range(3):
        to_sibling(kind, 0).start()
    for copy in own_copies:
        copy.start()
    weighting[...] = jnp.zeros_like(weighting)

    loads[0].wait()

    def normed_chunk(index, carry):
        rows = pl.ds(pl.multiple_of(index * CHUNK, CHUNK), CHUNK)
        stream_f = stream_v[rows, :].astype(jnp.float32)
        inverse = lax.rsqrt(jnp.mean(stream_f * stream_f, axis=-1, keepdims=True) + epsilon)
        normed[rows, :] = (
            stream_f * inverse * gain_first[...].astype(jnp.float32)[None, :]
        ).astype(jnp.bfloat16)
        return carry

    lax.fori_loop(0, tokens // CHUNK, normed_chunk, 0)
    for copy in loads[1:]:
        copy.wait()

    def projected(target, tile):
        return matmul(normed[:, :tall], target[tile]) + matmul(
            normed[:, tall:], target[tile + 1, : width - tall, :]
        )

    def rotated(pre):
        turned = []
        for pair in range(span // 128):
            part = pre[:, pair * 128 : pair * 128 + 128]
            turned.append(part * cosine[...] + partner_lanes(part) * sine[...])
        return jnp.concatenate(turned, axis=1).astype(jnp.bfloat16)

    low_rows, high_rows = pl.ds(0, tokens), pl.ds(tokens, tokens)
    for piece in range(pieces):
        ggate[3 + piece, low_rows, :] = rotated(projected(scaled, 2 * piece))
    key_rows = rotated(projected(ggate, 0))
    ggate[2, low_rows, :] = key_rows
    value_rows = projected(ggate, tiles - 2).astype(jnp.bfloat16)
    ggate[2, high_rows, :] = value_rows

    def store_overlaid(values, rows):
        for group in range(values.shape[1] // HEAD_FEATURES):
            pair = group // 2
            low, high = lane_halves(values[:, pair * 128 : pair * 128 + 128].astype(jnp.float32))
            if group % 2:
                low = pltpu.roll(high, HEAD_FEATURES, 1)
            else:
                high = pltpu.roll(low, HEAD_FEATURES, 1)
            gup[2 * group, rows, :128] = low.astype(jnp.bfloat16)
            gup[2 * group + 1, rows, :128] = high.astype(jnp.bfloat16)

    store_overlaid(key_rows, low_rows)
    store_overlaid(value_rows, high_rows)
    results = [
        pltpu.make_async_copy(normed, normed_out, result_sem.at[0]),
        pltpu.make_async_copy(ggate.at[2, low_rows], keys_out, result_sem.at[1]),
        pltpu.make_async_copy(ggate.at[2, high_rows], values_out, result_sem.at[2]),
    ]
    for piece in range(pieces):
        results.append(
            pltpu.make_async_copy(
                ggate.at[3 + piece, low_rows],
                queries_out.at[:, pl.ds(piece * span, span)],
                result_sem.at[3 + piece],
            )
        )
    for copy in results:
        copy.start()
    group = heads_width // key_weight.shape[1]
    blocks = 2
    block_rows = tokens // blocks

    def head_pair(pair, carry):
        tile = 3 + lax.div(pair, 2)
        here = pl.ds(pl.multiple_of(lax.rem(pair, 2) * 128, 128), 128)
        for block in range(blocks):
            start = block * block_rows
            reach = start + block_rows
            total = jnp.zeros((block_rows, 128), jnp.float32)
            query_block = ggate[tile, pl.ds(start, block_rows), here]
            for parity in range(2):
                slot = 2 * lax.div(2 * pair + parity, group) + parity
                scores = causal_scores(query_block, gup[slot, pl.ds(0, reach), :128], start)
                weight = jnp.exp(scores - jnp.max(scores, axis=-1, keepdims=True))
                weight = weight / jnp.sum(weight, axis=-1, keepdims=True)
                total = total + matmul(
                    weight.astype(jnp.bfloat16), gup[slot, pl.ds(tokens, reach), :128]
                )
            ggate[tile, pl.ds(tokens + start, block_rows), here] = total.astype(jnp.bfloat16)
        return carry

    lax.fori_loop(0, heads_width // 128, head_pair, 0)
    receive_relay(0, 0)
    start_relay(0, 1)
    for piece in range(pieces):
        results.append(
            pltpu.make_async_copy(
                ggate.at[3 + piece, high_rows],
                mixed_out.at[:, pl.ds(piece * span, span)],
                result_sem.at[3 + pieces + piece],
            )
        )
    for copy in results[3 + pieces :]:
        copy.start()
    for copy in out_loads:
        copy.wait()

    def out_product(first_row, column):
        rows = pl.ds(pl.multiple_of(tokens + first_row * half, half), half)
        return sum(
            matmul(ggate[3 + piece, rows, :], grow[column, pl.ds(piece * span, span), :])
            for piece in range(pieces)
        )

    def send_column(column, carry):
        here = pl.ds(pl.multiple_of(column * span, span), span)
        part_send[:, here] = out_product(1 - core, column).astype(jnp.bfloat16)
        return carry

    def own_column(column, carry):
        here = pl.ds(pl.multiple_of(column * span, span), span)
        grow_sum[:, here] = out_product(core, column)
        return carry

    lax.fori_loop(0, column_tiles, send_column, 0)
    part_copy = pltpu.make_async_remote_copy(
        src_ref=part_send,
        dst_ref=part_recv,
        send_sem=part_sem.at[0],
        recv_sem=part_sem.at[1],
        device_id=sibling,
        device_id_type=MESH,
    )
    part_copy.start()
    lax.fori_loop(0, column_tiles, own_column, 0)
    part_copy.wait()

    def mixer_chunk(index, carry):
        rows = pl.ds(pl.multiple_of(index * CHUNK, CHUNK), CHUNK)
        stream_part = pl.ds(pl.multiple_of(core * half + index * CHUNK, CHUNK), CHUNK)
        mixer_part = pl.ds(pl.multiple_of(line * half + index * CHUNK, CHUNK), CHUNK)
        attended_f = grow_sum[rows, :] + part_recv[rows, :].astype(jnp.float32)
        attended[rows, :] = attended_f.astype(jnp.bfloat16)
        middle = stream_v[stream_part, :].astype(jnp.float32) + residual_scale * attended_f
        inverse = lax.rsqrt(jnp.mean(middle * middle, axis=-1, keepdims=True) + epsilon)
        mixer[mixer_part, :] = (
            middle * inverse * gain_second[...].astype(jnp.float32)[None, :]
        ).astype(jnp.bfloat16)
        return carry

    lax.fori_loop(0, half // CHUNK, mixer_chunk, 0)
    start_relay(1, 0)
    padding = jnp.zeros((128 - router.shape[0], width), jnp.bfloat16)
    logits = matmul_nt(
        mixer[line_rows, :], jnp.concatenate([router[...], padding], axis=0)
    )
    own_routes = routes[:, own_rows].T
    lane = lax.broadcasted_iota(jnp.int32, logits.shape, 1)
    routed = lane < 0
    for entry in range(TOP):
        routed = jnp.logical_or(routed, lane == own_routes[:, entry : entry + 1])
    largest = jnp.max(jnp.where(routed, logits, masked_score), axis=-1, keepdims=True)
    gate_exp = jnp.where(routed, jnp.exp(jnp.minimum(logits - largest, 0.0)), 0.0)
    probs[line_rows, :] = gate_exp / jnp.sum(gate_exp, axis=-1, keepdims=True)

    def probs_copy(step):
        return send(
            probs.at[line_rows],
            probs.at[line_rows],
            (probs_send, probs_recv),
            (step,),
            partners[step],
        )

    def probs_arriving(step):
        theirs = block_rows_of(lax.div(partners[step][0], PLANE))
        return send(
            probs.at[theirs],
            probs.at[theirs],
            (probs_send, probs_recv),
            (step,),
            partners[step],
        )

    for step in range(1, LINES):
        probs_copy(step).start()
    own_copies.append(pltpu.make_async_copy(probs.at[line_rows], probs_own, own_sem.at[4]))
    own_copies.append(pltpu.make_async_copy(mixer.at[line_rows], mixer_own, own_sem.at[5]))
    for copy in own_copies[4:]:
        copy.start()

    def pass_on(kind):
        for axis in (0, 1):
            direct(kind, axis).wait_recv()
        for axis in onwards[kind]:
            onward(kind, axis).start()
        for slot in (1, 2):
            to_sibling(kind, slot).start()

    def hidden_tile(block, tile):
        rows = block_rows_of(block)
        step = lax.rem(tile, PLANE)
        owner = lax.rem(place, PLANE)
        owner = jnp.where(lax.rem(step, 2) == 1, flip(owner, 1), owner)
        owner = jnp.where(lax.div(step, 2) == 1, flip(owner, 2), owner)
        chosen = lax.broadcasted_iota(jnp.int32, (half, 128), 1) == line * PLANE + owner
        prob = jnp.sum(jnp.where(chosen, probs[rows, :], 0.0), axis=1, keepdims=True)
        gate_pre = matmul(mixer[rows, :], gates[tile])
        up_pre = matmul(mixer[rows, :], ups[tile])
        grad_raw = residual_scale * matmul_nt(cots[rows, :], downs[tile])
        sigmoid_gate = 1.0 / (1.0 + jnp.exp(-gate_pre))
        silu_gate = gate_pre * sigmoid_gate
        active = silu_gate * up_pre
        share = jnp.sum(active * grad_raw, axis=1, keepdims=True)
        weighting[rows, :] += jnp.where(chosen, share, 0.0)
        grad_active = prob * grad_raw
        scaled[tile, rows, :] = (prob * active).astype(jnp.bfloat16)
        ggate[tile, rows, :] = (
            grad_active * up_pre * sigmoid_gate * (1.0 + gate_pre * (1.0 - sigmoid_gate))
        ).astype(jnp.bfloat16)
        gup[tile, rows, :] = (grad_active * silu_gate).astype(jnp.bfloat16)

    def early_tiles(block):
        def body(index, carry):
            hidden_tile(block, index + lax.div(index, 3))
            return carry

        lax.fori_loop(0, 6, body, 0)

    def late_tiles(block):
        def body(index, carry):
            hidden_tile(block, 3 + PLANE * index)
            return carry

        lax.fori_loop(0, 2, body, 0)

    def grow_tiles(block, first, last):
        rows = block_rows_of(block)

        def body(column, carry):
            here = pl.ds(pl.multiple_of(column * span, span), span)
            total = matmul_nt(ggate[0, rows, :], gates[0, here, :])
            for tile in range(1, tiles):
                total = total + matmul_nt(ggate[tile, rows, :], gates[tile, here, :])
            for tile in range(tiles):
                total = total + matmul_nt(gup[tile, rows, :], ups[tile, here, :])
            grow[column, rows, :] = total.astype(jnp.bfloat16)
            return carry

        lax.fori_loop(first, last, body, 0)

    outer = jnp.logical_or(line == 0, line == LINES - 1)
    near_line = flip(line, 1)
    far_inner = jnp.where(line < 2, 2, 1)
    far_outer = jnp.where(line < 2, 3, 0)

    def remote_block(index):
        outside = (near_line, far_inner, far_outer)[index]
        inside = (far_inner, far_outer, near_line)[index]
        return jnp.where(outer, outside, inside)

    def home_of(block):
        return (place + (block - line) * PLANE, core)

    chunks = 2
    chunk_columns = column_tiles // chunks

    def grow_copy(index, chunk):
        block = remote_block(index)
        home = jnp.where(outer, near_line, block)
        slot = jnp.where(outer, (0, 2, 3)[index], (1, 1, 0)[index])
        columns = pl.ds(chunk * chunk_columns, chunk_columns)
        return pltpu.make_async_remote_copy(
            src_ref=grow.at[columns, block_rows_of(block)],
            dst_ref=grow_in.at[slot, columns],
            send_sem=grow_send.at[index, chunk],
            recv_sem=grow_recv.at[slot, chunk],
            device_id=home_of(home),
            device_id_type=MESH,
        )

    def grow_arriving(slot, chunk):
        columns = pl.ds(chunk * chunk_columns, chunk_columns)
        return pltpu.make_async_remote_copy(
            src_ref=grow_in.at[slot, columns],
            dst_ref=grow_in.at[slot, columns],
            send_sem=grow_send.at[0, chunk],
            recv_sem=grow_recv.at[slot, chunk],
            device_id=home_of(near_line),
            device_id_type=MESH,
        )

    def combine(index, chunk):
        @pl.when(jnp.logical_not(outer))
        def _():
            grow_arriving(2 + index, chunk).wait_recv()
            rows = block_rows_of(remote_block(index))

            def add_column(column, carry):
                grow[column, rows, :] = (
                    grow[column, rows, :].astype(jnp.float32)
                    + grow_in[2 + index, column].astype(jnp.float32)
                ).astype(jnp.bfloat16)
                return carry

            first = chunk * chunk_columns
            lax.fori_loop(first, first + chunk_columns, add_column, 0)
            grow_copy(index, chunk).start()

    def weighting_copy(index):
        block = remote_block(index)
        return pltpu.make_async_remote_copy(
            src_ref=weighting.at[block_rows_of(block)],
            dst_ref=weighting_in.at[line],
            send_sem=weighting_send.at[index],
            recv_sem=weighting_recv.at[line],
            device_id=home_of(block),
            device_id_type=MESH,
        )

    def weighting_arriving(index):
        block = remote_block(index)
        return pltpu.make_async_remote_copy(
            src_ref=weighting_in.at[block],
            dst_ref=weighting_in.at[block],
            send_sem=weighting_send.at[index],
            recv_sem=weighting_recv.at[block],
            device_id=home_of(block),
            device_id_type=MESH,
        )

    def send_back(index):
        weighting_copy(index).start()
        for chunk in range(chunks):
            grow_tiles(
                remote_block(index), chunk * chunk_columns, (chunk + 1) * chunk_columns
            )
            if index == 2:
                grow_copy(index, chunk).start()
            elif index == 1:

                @pl.when(outer)
                def _():
                    grow_copy(index, chunk).start()

        if index == 2:

            @pl.when(outer)
            def _():
                for chunk in range(chunks):
                    grow_copy(0, chunk).start()

    pass_on(0)
    receive_relay(1, 0)
    start_relay(1, 1)
    receive_relay(0, 1)
    start_relay(0, 2)
    pass_on(1)
    pass_on(2)
    for copy in results:
        copy.wait()
    for copy in own_copies:
        copy.wait()
    for step in range(1, LINES):
        probs_copy(step).wait_send()
        probs_arriving(step).wait_recv()
    for kind in range(3):
        for slot in range(3):
            to_sibling(kind, slot).wait_recv()
    early_tiles(remote_block(0))
    receive_relay(1, 1)
    start_relay(1, 2)
    for kind in range(3):
        for axis in onwards[kind]:
            onward(kind, axis).wait_recv()
        to_sibling(kind, 3).start()
    early_tiles(line)
    early_tiles(remote_block(1))
    for kind in range(3):
        to_sibling(kind, 3).wait_recv()
    late_tiles(remote_block(0))
    send_back(0)
    late_tiles(remote_block(1))
    send_back(1)
    late_tiles(line)
    grow_tiles(line, 0, column_tiles)
    receive_relay(0, 2)
    receive_relay(1, 2)
    early_tiles(remote_block(2))
    late_tiles(remote_block(2))
    send_back(2)
    combine(0, 0)
    combine(0, 1)
    for kind in range(3):
        for slot in range(PLANE):
            to_sibling(kind, slot).wait_send()
        for axis in (0, 1):
            direct(kind, axis).wait_send()
        for axis in onwards[kind]:
            onward(kind, axis).wait_send()
    for array in (0, 1):
        for hop in range(LINES - 1):
            finish_relay(array, hop)

    def out_tile(column, carry):
        here = pl.ds(pl.multiple_of(column * span, span), span)
        total = matmul(scaled[0], downs[0, :, here])
        for tile in range(1, tiles):
            total = total + matmul(scaled[tile], downs[tile, :, here])
        outs[:, here] = total.astype(jnp.bfloat16)
        return carry

    stores = [
        pltpu.make_async_copy(
            outs.at[block_rows_of(lax.div(partners[step][0], PLANE))],
            out_parts[step],
            store_sem.at[step],
        )
        for step in range(LINES)
    ]
    pl.semaphore_signal(ready_sem, inc=1, device_id=sibling, device_id_type=MESH)
    pl.semaphore_wait(ready_sem, 1)
    def tile_order(index):
        return jnp.where(index == 0, 3, jnp.where(index == 3, 0, index))

    def tile_grads(tile, kinds):
        for kind in kinds:
            if kind == 2:
                yield kind, residual_scale * matmul_tn(scaled[tile], cots[...])
            else:
                yield kind, matmul_tn(mixer[...], (ggate, gup)[kind][tile])

    def core_copy(kind, step):
        return pltpu.make_async_remote_copy(
            src_ref=held[kind].at[PLANE + step],
            dst_ref=held[kind].at[step],
            send_sem=core_send.at[kind, step],
            recv_sem=core_recv.at[kind, step],
            device_id=sibling,
            device_id_type=MESH,
        )

    def sibling_tile(index, kinds):
        step = tile_order(index)
        for kind, grad in tile_grads(PLANE + step, kinds):
            held[kind][PLANE + step] = grad.astype(jnp.bfloat16)
            core_copy(kind, step).start()

    def plane_copy(kind, axis, passing):
        span_rows = held[kind].shape[1] // 2
        step = 3 if passing else axis + 1
        return pltpu.make_async_remote_copy(
            src_ref=held[kind].at[step, pl.ds(axis * span_rows, span_rows)],
            dst_ref=landed[kind].at[axis, passing],
            send_sem=plane_send.at[kind, axis, passing],
            recv_sem=plane_recv.at[kind, axis, passing],
            device_id=across[axis],
            device_id_type=MESH,
        )

    def kept_copy(kind, step):
        return pltpu.make_async_copy(
            held[kind].at[step], kept[kind].at[step], kept_sem.at[kind, step]
        )

    def own_tile(index, kinds):
        @pl.when(index < PLANE - 1)
        def _():
            sibling_tile(index + 1, kinds)

        step = tile_order(index)
        for kind, grad in tile_grads(step, kinds):
            core_copy(kind, step).wait_recv()
            held[kind][step] = (grad + held[kind][step].astype(jnp.float32)).astype(jnp.bfloat16)

            @pl.when(step == 3)
            def _():
                for axis in (0, 1):
                    plane_copy(kind, axis, 1).start()

            for axis in (0, 1):

                if kind in DEFERRED:
                    continue

                @pl.when(step == axis + 1)
                def _():
                    plane_copy(kind, axis, 0).start()

            @pl.when(step < 3)
            def _():
                kept_copy(kind, step).start()

        return kinds

    def gate_and_up(index, carry):
        own_tile(index, (0, 1))
        return carry

    def down_only(index, carry):
        own_tile(index, (2,))
        return carry

    sibling_tile(0, (0, 1))
    lax.fori_loop(0, PLANE, gate_and_up, 0)
    combine(1, 0)
    lax.fori_loop(0, column_tiles, out_tile, 0)
    combine(1, 1)
    for copy in stores:
        copy.start()
    pl.semaphore_signal(ready_sem, inc=1, device_id=sibling, device_id_type=MESH)
    pl.semaphore_wait(ready_sem, 1)
    sibling_tile(0, (2,))
    lax.fori_loop(0, PLANE, down_only, 0)
    for index in range(LINES - 1):
        weighting_copy(index).wait_send()
        for chunk in range(chunks):
            grow_copy(index, chunk).wait_send()
        weighting_arriving(index).wait_recv()
    for slot in (0, 1):
        for chunk in range(chunks):
            grow_arriving(slot, chunk).wait_recv()
    total = weighting[line_rows, :]
    for index in range(LINES - 1):
        total = total + weighting_in[remote_block(index)]
    weighting_sum[...] = total

    def sum_column(column, carry):
        here = pl.ds(pl.multiple_of(column * span, span), span)
        total = grow[column, line_rows, :].astype(jnp.float32)
        for slot in (0, 1):
            total = total + grow_in[slot, column].astype(jnp.float32)
        grow_sum[:, here] = total
        return carry

    lax.fori_loop(0, column_tiles, sum_column, 0)
    for copy in stores:
        copy.wait()
    for kind in range(3):
        for step in range(PLANE):
            core_copy(kind, step).wait_send()
        for step in range(3):
            kept_copy(kind, step).wait()
        for axis in (0, 1):
            for passing in (1,) if kind in DEFERRED else (0, 1):
                plane_copy(kind, axis, passing).wait()


def run_front(operands, weights):
    low, wide = jnp.bfloat16, jnp.float32
    shape = jax.ShapeDtypeStruct
    vmem = pltpu.VMEM
    far = pl.BlockSpec(memory_space=pl.ANY)
    near = pl.BlockSpec(memory_space=pltpu.VMEM)
    tokens, width = operands[0].shape
    half = tokens // 2
    rows = LINES * half
    query_width, key_width = operands[4].shape[1], operands[5].shape[1]
    span = weights[0].shape[1]
    tiles = 2 * PLANE
    dma = pltpu.SemaphoreType.DMA
    pieces = query_width // span
    columns = width // span
    return pl.pallas_call(
        front_kernel,
        name="front",
        out_shape=(
            *[shape((half, width), low)] * LINES,
            shape((half, width), wide),
            shape((half, 128), wide),
            shape((3, width, span), low),
            shape((3, width, span), low),
            shape((3, span, width), low),
            shape((2, 2, width // 2, span), low),
            shape((2, 2, width // 2, span), low),
            shape((2, 2, span // 2, width), low),
            shape((half, width), low),
            shape((half, 128), wide),
            shape((tokens, width), low),
            shape((tokens, query_width), low),
            shape((tokens, key_width), low),
            shape((tokens, key_width), low),
            shape((tokens, query_width), low),
            shape((half, width), low),
        ),
        in_specs=[far, far, near, near, far, far, far, far, near, near, near, near] + [far] * 3,
        out_specs=(*[far] * LINES, near, near, *[far] * 13, near),
        scratch_shapes=[
            vmem((rows, width), low),
            vmem((rows, width), low),
            vmem((rows, 128), wide),
            vmem((tiles, width, span), low),
            vmem((tiles, width, span), low),
            vmem((tiles, span, width), low),
            vmem((tiles, rows, span), low),
            vmem((tiles, rows, span), low),
            vmem((tiles, rows, span), low),
            vmem((columns, rows, span), low),
            vmem((LINES, columns, half, span), low),
            vmem((rows, width), low),
            vmem((rows, 128), wide),
            vmem((LINES, half, 128), wide),
            vmem((half, width), low),
            vmem((half, width), low),
            dma((5 + 2 * pieces + columns,)),
            dma((6,)),
            dma((3, 8)),
            dma((3, 8)),
            dma((2, 2, LINES - 1)),
            dma((2, 2, LINES - 1)),
            dma((LINES,)),
            dma((LINES,)),
            dma((2,)),
            dma((3 + 2 * pieces,)),
            dma((LINES,)),
            dma((3, 3)),
            dma((LINES - 1, 2)),
            dma((LINES, 2)),
            dma((LINES - 1,)),
            dma((LINES,)),
            dma((3, PLANE)),
            dma((3, PLANE)),
            dma((3, 2, 2)),
            dma((3, 2, 2)),
            pltpu.SemaphoreType.REGULAR,
        ],
        compiler_params=pltpu.CompilerParams(
            collective_id=0, has_side_effects=True, vmem_limit_bytes=63 << 20
        ),
        cost_estimate=pl.CostEstimate(
            flops=18 * rows * width * span * tiles,
            bytes_accessed=12 * width * span * tiles,
            transcendentals=0,
        ),
    )(*operands, *weights)


def back_kernel(*refs):
    refs = list(refs)

    def take(count):
        taken = refs[:count]
        del refs[:count]
        return taken

    out_parts = take(LINES)
    grow_sum, weighting_sum = take(2)
    kept, landed = take(3), take(3)
    stream, cotangent, gain_first, gain_second, query_weight, key_weight = take(6)
    value_weight, out_weight, router, cosine, sine = take(5)
    mixer_own, probs_own, normed, queries, keys, values, mixed, attended = take(8)
    layer_out, grad_stream = take(2)
    scatter_results = take(6)
    expert_grads = take(3)
    small_out = take(1)[0]
    stream_v, cot_v, query_v, key_v, value_v, out_v, normed_v, queries_v = take(8)
    mixed_v, grow_v, attended_v, out_in, layer_v = take(5)
    key_v2, value_v2, mixer_v, probs_v, weighting_v = take(5)
    key_slots, value_slots, key_totals, value_totals = take(4)
    middle_grads, attended_grads, mixed_grads = take(3)
    key_grads, value_grads, normed_recv = take(3)
    normed_send, first_terms = attended_grads, layer_v
    second_terms, query_grads = cot_v, mixed_v
    own_parts, landed_v, plane_in = take(3), take(3), take(3)
    scatter_sources = take(6)
    scatter_scratch = [take(5) for _ in range(6)]
    out_source_a, out_source_b, query_first, pair_first, pair_second, query_second = (
        scatter_sources
    )
    last_send, last_recv = take(2)
    load_sem, part_sem, out_send, out_recv, pair_sem, plane_send, plane_recv = take(7)
    store_sem, deferred_send, deferred_recv = take(3)
    tokens, width = stream_v.shape
    half = tokens // 2

    place = lax.axis_index("ep")
    core = lax.axis_index("tp")
    sibling = (place, 1 - core)
    across = [flip(place, 1), flip(place, 2)]
    partners = [flip_line(place, step) for step in range(LINES)]
    bits = [lax.rem(place, 2), lax.rem(lax.div(place, 2), 2)]
    own_rows = pl.ds(pl.multiple_of(core * half, half), half)

    barrier = pltpu.get_barrier_semaphore()
    for other in across + partners[1:]:
        pl.semaphore_signal(barrier, inc=1, device_id=(other, core), device_id_type=MESH)
    pl.semaphore_signal(barrier, inc=1, device_id=sibling, device_id_type=MESH)

    pairs = [
        (grow_sum, grow_v),
        (weighting_sum, weighting_v),
        (attended, attended_v),
        (probs_own, probs_v),
        (stream, stream_v),
        (cotangent.at[own_rows], cot_v),
        (out_weight, out_v),
        (mixed, mixed_v),
        (queries, queries_v),
        (keys, key_v2),
        (values, value_v2),
        (normed, normed_v),
        (query_weight, query_v),
        (key_weight, key_v),
        (value_weight, value_v),
        (mixer_own, mixer_v),
        (out_parts[0], mixer_v),
    ]
    loads = [
        pltpu.make_async_copy(source, target, load_sem.at[index])
        for index, (source, target) in enumerate(pairs)
    ]

    def part_copies(kind, final):
        rows = own_parts[kind].shape[1]
        low, high = pl.ds(0, rows), pl.ds(rows, rows)
        first, second = (0, 0) if final else (2, 1)
        return [
            pltpu.make_async_copy(source, target, part_sem.at[kind, index])
            for index, (source, target) in enumerate(
                (
                    (kept[kind].at[first, low], own_parts[kind].at[0]),
                    (kept[kind].at[second, high], own_parts[kind].at[1]),
                )
            )
        ]

    def landed_copies(kind):
        if kind in DEFERRED:
            return [
                pltpu.make_async_copy(
                    landed[kind].at[axis, 1],
                    landed_v[kind].at[axis, 1],
                    part_sem.at[kind, 2 + axis],
                )
                for axis in (0, 1)
            ]
        return [pltpu.make_async_copy(landed[kind], landed_v[kind], part_sem.at[kind, 2])]

    def deferred_copy(kind, axis):
        rows = own_parts[kind].shape[1]
        return pltpu.make_async_remote_copy(
            src_ref=kept[kind].at[axis + 1, pl.ds(axis * rows, rows)],
            dst_ref=landed_v[kind].at[axis, 0],
            send_sem=deferred_send.at[kind, axis],
            recv_sem=deferred_recv.at[kind, axis],
            device_id=(across[axis], core),
            device_id_type=MESH,
        )

    for copy in loads[:6]:
        copy.start()
    for kind in range(3):
        for copy in landed_copies(kind):
            copy.start()
        for copy in part_copies(kind, False):
            copy.start()
    for copy in loads[6:-1]:
        copy.start()
    pl.semaphore_wait(barrier, LINES + 2)

    def send(source, target, sems, index, device):
        return pltpu.make_async_remote_copy(
            src_ref=source,
            dst_ref=target,
            send_sem=sems[0].at[index],
            recv_sem=sems[1].at[index],
            device_id=device,
            device_id_type=MESH,
        )

    def out_copy(step):
        return send(
            out_parts[step],
            out_in.at[step - 1],
            (out_send, out_recv),
            (step - 1,),
            (partners[step], core),
        )

    for kind in DEFERRED:
        for axis in (0, 1):
            deferred_copy(kind, axis).start()
    for step in (3, 2, 1):
        out_copy(step).start()

    for copy in loads[:6]:
        copy.wait()
    padding = jnp.zeros((128 - router.shape[0], width), jnp.bfloat16)
    router_rows = jnp.concatenate([router[...], padding], axis=0)
    own_start = core * half

    def own_chunk(index):
        rows = pl.ds(pl.multiple_of(index * CHUNK, CHUNK), CHUNK)
        return rows, pl.ds(pl.multiple_of(own_start + index * CHUNK, CHUNK), CHUNK)

    def middle_chunk(index, carry):
        rows, stream_rows = own_chunk(index)
        middle = stream_v[stream_rows, :].astype(jnp.float32) + residual_scale * attended_v[
            rows, :
        ].astype(jnp.float32)
        inverse = lax.rsqrt(jnp.mean(middle * middle, axis=-1, keepdims=True) + epsilon)
        probs = probs_v[rows, :]
        weighting = weighting_v[rows, :]
        grad_chosen = probs * (weighting - jnp.sum(probs * weighting, axis=-1, keepdims=True))
        weighting_v[rows, :] = grad_chosen
        grad_mixer = matmul(grad_chosen.astype(jnp.bfloat16), router_rows) + grow_v[rows, :]
        weighted = grad_mixer * gain_second[...].astype(jnp.float32)[None, :]
        grad_middle = (
            cot_v[rows, :].astype(jnp.float32)
            + inverse * weighted
            - middle * (inverse * inverse * inverse)
            * jnp.mean(middle * weighted, axis=-1, keepdims=True)
        )
        middle_grads[stream_rows, :] = grad_middle.astype(jnp.bfloat16)
        second_terms[rows, :] = (grad_mixer * middle * inverse).astype(jnp.bfloat16)
        return carry

    lax.fori_loop(0, half // CHUNK, middle_chunk, 0)

    def pair_copy(source, target, index):
        return pltpu.make_async_remote_copy(
            src_ref=source,
            dst_ref=target,
            send_sem=pair_sem.at[0, index],
            recv_sem=pair_sem.at[1, index],
            device_id=sibling,
            device_id_type=MESH,
        )

    middle_copy = pair_copy(middle_grads.at[own_rows], middle_grads.at[own_rows], 0)
    middle_copy.start()

    def plane_copy(kind, axis):
        return send(
            landed_v[kind].at[axis, 1],
            plane_in[kind].at[axis],
            (plane_send, plane_recv),
            (kind, axis),
            (across[1 - axis], core),
        )

    for kind in range(3):
        for copy in landed_copies(kind):
            copy.wait()
        for copy in part_copies(kind, False):
            copy.wait()
        for axis in (0, 1):

            def add_passing(index, carry):
                rows = pl.ds(pl.multiple_of(index * CHUNK, CHUNK), CHUNK)
                landed_v[kind][axis, 1, rows, :] = (
                    own_parts[kind][axis, rows, :].astype(jnp.float32)
                    + landed_v[kind][axis, 1, rows, :].astype(jnp.float32)
                ).astype(jnp.bfloat16)
                return carry

            lax.fori_loop(0, own_parts[kind].shape[1] // CHUNK, add_passing, 0)
            plane_copy(kind, axis).start()
        for copy in part_copies(kind, True):
            copy.start()

    slab = scatter_results[0].shape[0]
    order = (3, 2, 1, 0)
    plans = list(zip(scatter_sources, scatter_results, scatter_scratch))

    def rows_of(step, first, second_same, first_same):
        other_line = lax.div(partners[step], PLANE)
        first_bit = bits[first] if first_same else 1 - bits[first]
        second_bit = bits[1 - first] if second_same else 1 - bits[1 - first]
        index = other_line * PLANE + first_bit * (1 + first) + second_bit * (2 - first)
        return pl.ds(pl.multiple_of(index * slab, slab), slab)

    def first_copy(number, step, same):
        source, _, scratch = plans[number]
        first = number % 2
        index = step * 2 + same
        return send(
            source.at[rows_of(step, first, same, False)],
            scratch[0].at[index],
            (scratch[4].at[0], scratch[4].at[1]),
            (index,),
            (across[first], core),
        )

    def second_copy(number, step):
        scratch = plans[number][2]
        return send(
            scratch[1].at[step],
            scratch[2].at[step],
            (scratch[4].at[2], scratch[4].at[3]),
            (step,),
            (across[1 - number % 2], core),
        )

    def line_copy(number, step):
        scratch = plans[number][2]
        return send(
            scratch[1].at[step],
            scratch[3].at[step],
            (scratch[4].at[4], scratch[4].at[5]),
            (step,),
            (partners[step], core),
        )

    def start_scatter(number):
        for step in order:
            for same in (0, 1):
                first_copy(number, step, same).start()

    def add_first(number, step, same):
        source, _, scratch = plans[number]
        first_copy(number, step, same).wait()
        mine = source[rows_of(step, number % 2, same, True), :].astype(jnp.float32)
        return mine + scratch[0][step * 2 + same].astype(jnp.float32)

    def finish_first(number, step):
        plans[number][2][1][step] = add_first(number, step, 0).astype(jnp.bfloat16)
        second_copy(number, step).start()

    def finish_second(number, step):
        _, result, scratch = plans[number]
        total = add_first(number, step, 1)
        second_copy(number, step).wait()
        total = total + scratch[2][step].astype(jnp.float32)
        if step:
            scratch[1][step] = total.astype(jnp.bfloat16)
            line_copy(number, step).start()
        else:
            result[...] = total

    def finish_line(number):
        _, result, scratch = plans[number]
        for step in order[:-1]:
            line_copy(number, step).wait()
            result[...] += scratch[3][step].astype(jnp.float32)

    middle_copy.wait()

    def attended_chunk(index, carry):
        rows = pl.ds(pl.multiple_of(index * CHUNK, CHUNK), CHUNK)
        attended_grads[rows, :] = (
            residual_scale * middle_grads[rows, :].astype(jnp.float32)
        ).astype(jnp.bfloat16)
        return carry

    lax.fori_loop(0, tokens // CHUNK, attended_chunk, 0)
    loads[6].wait()
    loads[7].wait()
    columns = out_source_a.shape[1]
    out_source_a[...] = matmul_tn(attended_grads[...], mixed_v[:, :columns]).astype(jnp.bfloat16)
    start_scatter(0)
    out_source_b[...] = matmul_tn(attended_grads[...], mixed_v[:, columns:]).astype(jnp.bfloat16)
    start_scatter(1)
    mixed_grads[...] = matmul_nt(attended_grads[...], out_v[...]).astype(jnp.bfloat16)
    for copy in loads[8:11]:
        copy.wait()
    store_slots(key_slots, key_v2[...].astype(jnp.float32))
    store_slots(value_slots, value_v2[...].astype(jnp.float32))
    key_totals[...] = jnp.zeros_like(key_totals)
    value_totals[...] = jnp.zeros_like(value_totals)
    group = query_v.shape[1] // key_v.shape[1]
    blocks = 2
    block_rows = tokens // blocks

    def turned_back(value, cosines, sines):
        return (value * cosines - partner_lanes(value) * sines).astype(jnp.bfloat16)

    def head_pair(pair, carry):
        here = pl.ds(pl.multiple_of(pair * 128, 128), 128)
        for block in range(blocks):
            rows = slice(block * block_rows, (block + 1) * block_rows)
            reach = (block + 1) * block_rows
            total = jnp.zeros((block_rows, 128), jnp.float32)
            query_block = queries_v[rows, here]
            grad_block = mixed_grads[rows, here]
            for parity in range(2):
                slot = 2 * lax.div(2 * pair + parity, group) + parity
                key_block = key_slots[slot, :reach, :]
                scores = causal_scores(query_block, key_block, block * block_rows)
                weight = jnp.exp(scores - jnp.max(scores, axis=-1, keepdims=True))
                weight = weight / jnp.sum(weight, axis=-1, keepdims=True)
                grad_probs = matmul_nt(grad_block, value_slots[slot, :reach, :])
                inner = jnp.sum(weight * grad_probs, axis=-1, keepdims=True)
                grad_scores = (weight * (grad_probs - inner)).astype(jnp.bfloat16)
                total = total + matmul(grad_scores, key_block)
                key_totals[slot, :reach, :] += matmul_tn(grad_scores, query_block)
                value_totals[slot, :reach, :] += matmul_tn(
                    weight.astype(jnp.bfloat16), grad_block
                )
            query_grads[rows, here] = turned_back(
                score_scale * total, cosine[rows, :], sine[rows, :]
            )
        return carry

    def gathered_pair(totals, pair):
        first, second = 4 * pair, 4 * pair + 2
        low = lane_halves(totals[first])[0] + pltpu.roll(
            lane_halves(totals[first + 1])[1], HEAD_FEATURES, 1
        )
        high = lane_halves(totals[second + 1])[1] + pltpu.roll(
            lane_halves(totals[second])[0], HEAD_FEATURES, 1
        )
        return low + high

    def half_of_heads(pair, query_target, number, pair_target):
        lanes = slice(pair * 128, pair * 128 + 128)
        columns = query_target.shape[1]
        mine = slice(pair * columns, (pair + 1) * columns)
        lax.fori_loop(3 * pair, 3 * pair + 3, head_pair, 0)
        query_target[...] = matmul_tn(normed_v[...], query_grads[:, mine]).astype(jnp.bfloat16)
        start_scatter(number)
        key_grads[:, lanes] = turned_back(
            score_scale * gathered_pair(key_totals, pair), cosine[...], sine[...]
        )
        value_grads[:, lanes] = gathered_pair(value_totals, pair).astype(jnp.bfloat16)
        pair_target[:, :128] = matmul_tn(normed_v[...], key_grads[:, lanes]).astype(jnp.bfloat16)
        pair_target[:, 128:256] = matmul_tn(normed_v[...], value_grads[:, lanes]).astype(
            jnp.bfloat16
        )

    for copy in loads[11:-1]:
        copy.wait()
    half_of_heads(0, query_first, 2, pair_first)
    start_scatter(3)
    half_of_heads(1, query_second, 5, pair_second)
    normed_send[...] = (
        matmul_nt(query_grads[...], query_v[...])
        + matmul_nt(key_grads[...], key_v[...])
        + matmul_nt(value_grads[...], value_v[...])
    ).astype(jnp.bfloat16)
    normed_copy = pair_copy(normed_send, normed_recv, 1)
    normed_copy.start()
    for step in order:
        finish_first(0, step)
        finish_first(1, step)
    normed_copy.wait()

    def stream_rows(rows):
        grad_normed = normed_send[rows, :].astype(jnp.float32) + normed_recv[rows, :].astype(
            jnp.float32
        )
        stream_f = stream_v[rows, :].astype(jnp.float32)
        inverse = lax.rsqrt(jnp.mean(stream_f * stream_f, axis=-1, keepdims=True) + epsilon)
        weighted = grad_normed * gain_first[...].astype(jnp.float32)[None, :]
        total = (
            middle_grads[rows, :].astype(jnp.float32)
            + inverse * weighted
            - stream_f * (inverse * inverse * inverse)
            * jnp.mean(stream_f * weighted, axis=-1, keepdims=True)
        )
        return grad_normed * stream_f * inverse, total

    def first_chunk(index, carry):
        rows, mine = own_chunk(index)
        first_terms[rows, :] = stream_rows(mine)[0].astype(jnp.bfloat16)
        return carry

    lax.fori_loop(0, half // CHUNK, first_chunk, 0)
    lane = lax.broadcasted_iota(jnp.int32, (half, 128), 1)
    experts = LINES * PLANE
    pair_second[:, 256:] = (
        matmul_tn(mixer_v[...], weighting_v[...].astype(jnp.bfloat16))
        + matmul_tn(second_terms[...], (lane == experts).astype(jnp.bfloat16))
        + matmul_tn(first_terms[...], (lane == experts + 1).astype(jnp.bfloat16))
    ).astype(jnp.bfloat16)
    loads[-1].start()
    start_scatter(4)

    def stream_chunk(index, carry):
        rows = pl.ds(pl.multiple_of(index * CHUNK, CHUNK), CHUNK)
        normed_recv[rows, :] = stream_rows(rows)[1].astype(jnp.bfloat16)
        return carry

    lax.fori_loop(0, tokens // CHUNK, stream_chunk, 0)
    stream_copy = pltpu.make_async_copy(normed_recv, grad_stream, store_sem.at[4])
    stream_copy.start()
    for step in order:
        finish_second(0, step)
        finish_second(1, step)
    for step in order:
        finish_first(2, step)
        finish_first(3, step)
    for step in order:
        finish_second(2, step)
        finish_second(3, step)
    for step in order:
        finish_first(4, step)
        finish_first(5, step)
    for step in (1, 2, 3):
        out_copy(step).wait()
    loads[-1].wait()

    def result_chunk(index, carry):
        rows, stream_part = own_chunk(index)
        attended_f = attended_v[rows, :].astype(jnp.float32)
        mixture = mixer_v[rows, :].astype(jnp.float32)
        for step in range(1, LINES):
            mixture = mixture + out_in[step - 1, rows, :].astype(jnp.float32)
        middle = stream_v[stream_part, :].astype(jnp.float32) + residual_scale * attended_f
        result = middle + residual_scale * mixture
        layer_v[rows, :] = result.astype(jnp.bfloat16)
        return tuple(
            total + jnp.sum(value * value, axis=0, keepdims=True)
            for total, value in zip(carry, (result, attended_f, mixture))
        )

    totals = lax.fori_loop(
        0, half // CHUNK, result_chunk, (jnp.zeros((1, width), jnp.float32),) * 3
    )
    layer_pair = pair_copy(layer_v, layer_out.at[own_rows], 2)
    layer_pair.start()
    layer_own = pltpu.make_async_copy(layer_v, layer_out.at[own_rows], store_sem.at[0])
    layer_own.start()
    row_lane = lax.broadcasted_iota(jnp.int32, (8, 128), 1)
    squares = jnp.zeros((8, 128), jnp.float32)
    for index, value in enumerate(totals):
        total = jnp.sum(value, axis=1, keepdims=True)
        squares = jnp.where(row_lane == index, total, squares)
    for step in order:
        finish_second(4, step)
        finish_second(5, step)
    def expert_copy(kind):
        return pltpu.make_async_copy(own_parts[kind], expert_grads[kind], store_sem.at[1 + kind])

    for kind in range(3):
        for copy in part_copies(kind, True):
            copy.wait()
        for axis in (0, 1):
            plane_copy(kind, axis).wait()
            if kind in DEFERRED:
                deferred_copy(kind, axis).wait()

            def add_final(index, carry):
                rows = pl.ds(pl.multiple_of(index * CHUNK, CHUNK), CHUNK)
                own_parts[kind][axis, rows, :] = (
                    own_parts[kind][axis, rows, :].astype(jnp.float32)
                    + landed_v[kind][axis, 0, rows, :].astype(jnp.float32)
                    + plane_in[kind][axis, rows, :].astype(jnp.float32)
                ).astype(jnp.bfloat16)
                return carry

            lax.fori_loop(0, own_parts[kind].shape[1] // CHUNK, add_final, 0)
        expert_copy(kind).start()
    finish_line(4)
    last_send[:slab, :] = scatter_results[4][:, 256:]
    last_send[slab:, :] = squares
    last_copy = pair_copy(last_send, last_recv, 3)
    last_copy.start()
    for number in (0, 1, 2, 3, 5):
        finish_line(number)
    last_copy.wait()
    small_out[...] = last_send[...] + last_recv[...]
    layer_pair.wait()
    layer_own.wait()
    stream_copy.wait()
    for kind in range(3):
        expert_copy(kind).wait()


def run_back(expert_results, operands, front_results):
    low, wide = jnp.bfloat16, jnp.float32
    shape = jax.ShapeDtypeStruct
    vmem = pltpu.VMEM
    far = pl.BlockSpec(memory_space=pl.ANY)
    near = pl.BlockSpec(memory_space=pltpu.VMEM)
    tokens, width = operands[0].shape
    half = tokens // 2
    query_width, key_width = operands[4].shape[1], operands[5].shape[1]
    kept = expert_results[LINES + 2 : LINES + 5]
    tile_shapes = [value.shape[1:] for value in kept]
    half_shapes = [(value[0] // 2, value[1]) for value in tile_shapes]
    slab = width // (LINES * PLANE)
    slots = 2 * key_width // HEAD_FEATURES
    part = query_width // 2
    widths = (part, part, part, key_width, key_width + 128, part)
    dma = pltpu.SemaphoreType.DMA
    scatter_scratch = []
    for columns in widths:
        scatter_scratch += [
            vmem((2 * LINES, slab, columns), low),
            vmem((LINES, slab, columns), low),
            vmem((LINES, slab, columns), low),
            vmem((LINES, slab, columns), low),
            dma((6, 2 * LINES)),
        ]
    return pl.pallas_call(
        back_kernel,
        name="back",
        out_shape=(
            shape((tokens, width), low),
            shape((tokens, width), low),
            *[shape((slab, columns), wide) for columns in widths],
            *[shape((2, *value), low) for value in half_shapes],
            shape((slab + 8, 128), wide),
        ),
        in_specs=[far] * (LINES + 8)
        + [far, far, near, near, far, far, far, far, near, near, near]
        + [far] * 8,
        out_specs=(far,) * 2 + (near,) * 6 + (far,) * 3 + (near,),
        scratch_shapes=[
            vmem((tokens, width), low),
            vmem((half, width), low),
            vmem((width, query_width), low),
            vmem((width, key_width), low),
            vmem((width, key_width), low),
            vmem((query_width, width), low),
            vmem((tokens, width), low),
            vmem((tokens, query_width), low),
            vmem((tokens, query_width), low),
            vmem((half, width), wide),
            vmem((half, width), low),
            vmem((LINES - 1, half, width), low),
            vmem((half, width), low),
            vmem((tokens, key_width), low),
            vmem((tokens, key_width), low),
            vmem((half, width), low),
            vmem((half, 128), wide),
            vmem((half, 128), wide),
            vmem((slots, tokens, 128), low),
            vmem((slots, tokens, 128), low),
            vmem((slots, tokens, 128), wide),
            vmem((slots, tokens, 128), wide),
            vmem((tokens, width), low),
            vmem((tokens, width), low),
            vmem((tokens, query_width), low),
            vmem((tokens, key_width), low),
            vmem((tokens, key_width), low),
            vmem((tokens, width), low),
            *[vmem((2, *value), low) for value in half_shapes],
            *[vmem((2, 2, *value), low) for value in half_shapes],
            *[vmem((2, *value), low) for value in half_shapes],
            *[vmem((width, columns), low) for columns in widths],
            *scatter_scratch,
            vmem((slab + 8, 128), wide),
            vmem((slab + 8, 128), wide),
            dma((17,)),
            dma((3, 4)),
            dma((LINES - 1,)),
            dma((LINES - 1,)),
            dma((2, 4)),
            dma((3, 2)),
            dma((3, 2)),
            dma((5,)),
            dma((3, 2)),
            dma((3, 2)),
        ],
        compiler_params=pltpu.CompilerParams(
            collective_id=1, has_side_effects=True, vmem_limit_bytes=63 << 20
        ),
    )(*expert_results, *operands, *front_results)


def finish_kernel(*refs):
    layer_in, sources, refs = refs[0], refs[1:12], refs[12:]
    layer_out, refs = refs[0], refs[1:]
    grad_stream, out_grad, query_grad, key_grad, value_grad = refs[:5]
    gate_grad, up_grad, down_grad, router_grad, second_gain, first_gain, rms = refs[5:12]
    loaded, load_sem = refs[12:23], refs[23]
    layer_copy = pltpu.make_async_copy(layer_in, layer_out, load_sem.at[11])
    layer_copy.start()
    stream_low, out_first, out_second, query_first, pair_first, pair_second, query_second = (
        loaded[:7]
    )
    gate_low, up_low, down_low, small = loaded[7:]
    copies = [
        pltpu.make_async_copy(source, target, load_sem.at[index])
        for index, (source, target) in enumerate(zip(sources, loaded))
    ]
    for copy in copies:
        copy.start()
    copies[0].wait()

    def widen_stream(index, carry):
        rows = pl.ds(pl.multiple_of(index * CHUNK, CHUNK), CHUNK)
        grad_stream[rows, :] = stream_low[rows, :].astype(jnp.float32)
        return carry

    lax.fori_loop(0, grad_stream.shape[0] // CHUNK, widen_stream, 0)
    for copy in copies[1:]:
        copy.wait()
    half = out_first.shape[1]
    out_grad[:, :half] = out_first[...]
    out_grad[:, half:] = out_second[...]
    query_grad[:, :half] = query_first[...]
    query_grad[:, half:] = query_second[...]
    for place, part in enumerate((pair_first, pair_second)):
        lanes = slice(place * 128, place * 128 + 128)
        key_grad[:, lanes] = part[:, :128]
        value_grad[:, lanes] = part[:, 128:256]
    for low, grad in ((gate_low, gate_grad), (up_low, up_grad), (down_low, down_grad)):
        for part in range(2):

            def widen(index, carry):
                rows = pl.multiple_of(index * CHUNK, CHUNK)
                start = pl.multiple_of(part * low.shape[1] + rows, CHUNK)
                grad[0, pl.ds(start, CHUNK), :] = low[part, pl.ds(rows, CHUNK), :].astype(
                    jnp.float32
                )
                return carry

            lax.fori_loop(0, low.shape[1] // CHUNK, widen, 0)
    experts, slab = router_grad.shape
    turned = small[:slab, :].T
    router_grad[...] = turned[:experts, :]
    second_gain[...] = turned[experts, :]
    first_gain[...] = turned[experts + 1, :]
    total = grad_stream.shape[0] * grad_stream.shape[1]
    rms[...] = jnp.sqrt(small[slab : slab + 1, :3] / total)
    layer_copy.wait()


def run_finish(layer, values, tokens, width, experts):
    shape = jax.ShapeDtypeStruct
    wide = jnp.float32
    far = pl.BlockSpec(memory_space=pl.ANY)
    near = pl.BlockSpec(memory_space=pltpu.VMEM)
    slab, part = values[3].shape
    query_width, key_width = 2 * part, values[4].shape[1]
    tiles = [(1, 2 * value.shape[1], value.shape[2]) for value in values[7:10]]
    return pl.pallas_call(
        finish_kernel,
        name="finish",
        out_shape=(
            shape(layer.shape, layer.dtype),
            shape((tokens, width), wide),
            shape((slab, query_width), wide),
            shape((slab, query_width), wide),
            shape((slab, key_width), wide),
            shape((slab, key_width), wide),
            *[shape(tile, wide) for tile in tiles],
            shape((experts, slab), wide),
            shape((slab,), wide),
            shape((slab,), wide),
            shape((1, 3), wide),
        ),
        in_specs=[far] * 12,
        out_specs=(near,) * 13,
        scratch_shapes=[pltpu.VMEM(value.shape, value.dtype) for value in values]
        + [pltpu.SemaphoreType.DMA((12,))],
        compiler_params=pltpu.CompilerParams(vmem_limit_bytes=63 << 20),
    )(layer, *values)


def dense_shards(
    stream,
    cotangent,
    attention_gain,
    query_weight,
    key_matrix,
    value_matrix,
    out_weight,
    mixture_gain,
    router_weight,
    gate_weight,
    up_weight,
    down_weight,
    routes,
):
    tok_rows, model_width = stream.shape
    experts = router_weight.shape[1]
    steps_up = np.arange(HEAD_FEATURES // 2, dtype=np.float32) * np.float32(2.0 / HEAD_FEATURES)
    turns = np.exp(-steps_up * np.log(np.float32(rope_base)))
    angles = np.arange(SEQ_LEN, dtype=np.float32)[:, None] * turns[None, :]
    cosines, sines = np.cos(angles), np.sin(angles)
    operands = [
        stream,
        cotangent,
        attention_gain,
        mixture_gain,
        query_weight,
        key_matrix,
        value_matrix,
        out_weight,
        router_weight.T,
        routes.T,
        jnp.asarray(np.tile(cosines, (1, 4))),
        jnp.asarray(np.tile(np.concatenate([-sines, sines], axis=1), (1, 2))),
    ]
    front = run_front(operands, [gate_weight[0], up_weight[0], down_weight[0]])
    layer_part, *partial = run_back(
        front[: LINES + 8], operands[:9] + operands[10:], front[LINES + 8 :]
    )
    (
        layer_out,
        grad_stream,
        out_grad,
        query_grad,
        key_grad,
        value_grad,
        gate_grad,
        up_grad,
        down_grad,
        router_grad,
        second_gain,
        first_gain,
        rms_stats,
    ) = run_finish(layer_part, partial, tok_rows, model_width, experts)
    return (
        layer_out,
        grad_stream,
        first_gain,
        query_grad,
        key_grad,
        value_grad,
        out_grad.T,
        second_gain,
        router_grad.T,
        gate_grad,
        up_grad,
        down_grad,
        rms_stats,
    )


def solution(mesh):
    in_specs = (
        P("ep", None),
        P("ep", None),
        P(),
        P(None, "tp"),
        P(None, "tp"),
        P(None, "tp"),
        P("tp", None),
        P(),
        P(),
        P("ep", None, "tp"),
        P("ep", None, "tp"),
        P("ep", "tp", None),
        P("ep", None),
    )
    out_specs = (
        P("ep", None),
        P("ep", None),
        P("ep"),
        P("ep", "tp"),
        P("ep", "tp"),
        P("ep", "tp"),
        P("tp", "ep"),
        P("ep"),
        P("ep", None),
        P("ep", None, "tp"),
        P("ep", None, "tp"),
        P("ep", "tp", None),
        P("ep", None),
    )
    ep_size = mesh.shape["ep"]
    dense = mesh.shape["tp"] == 2 and ep_size <= 2 * TOP and ep_size == 16
    shards = dense_shards if dense else routed_shards
    return jax.shard_map(shards, mesh=mesh, in_specs=in_specs, out_specs=out_specs, check_vma=False)
```

```python
import functools

import jax
import jax.numpy as jnp
import numpy as np
from jax import lax
from jax.experimental import pallas as pl
from jax.experimental.pallas import tpu as pltpu
from jax.sharding import PartitionSpec as P

HEAD_FEATURES = 64
TOP = 8
SEQ_LEN = 512


epsilon = 1e-06
score_scale = 0.015625
residual_scale = 0.22
rope_base = 10000.0
masked_score = -1e30


def rope_tables(sequence_length):
    half_dim = HEAD_FEATURES // 2
    steps_up = jnp.arange(half_dim).astype(jnp.float32) * (2.0 / HEAD_FEATURES)
    inverse = jnp.exp(-steps_up * jnp.log(rope_base))
    places = jnp.arange(sequence_length).astype(jnp.float32)
    angles = places[:, None] * inverse[None, :]
    return (jnp.cos(angles), jnp.sin(angles))


def apply_rotation(value_rows, cosine_table, sine_values):
    half_dim = value_rows.shape[-1] // 2
    first_half = value_rows[..., :half_dim]
    second_half = value_rows[..., half_dim:]
    cos_rows = cosine_table[:, None, :]
    sin_rows = sine_values[:, None, :]
    return jnp.concatenate(
        [
            first_half * cos_rows - second_half * sin_rows,
            second_half * cos_rows + first_half * sin_rows,
        ],
        axis=-1,
    )


def rotary_back(grads_in, cosine_table, sine_values):
    half_dim = grads_in.shape[-1] // 2
    first_half = grads_in[..., :half_dim]
    second_half = grads_in[..., half_dim:]
    cos_rows = cosine_table[:, None, :]
    sin_rows = sine_values[:, None, :]
    return jnp.concatenate(
        [
            first_half * cos_rows + second_half * sin_rows,
            second_half * cos_rows - first_half * sin_rows,
        ],
        axis=-1,
    )


def block_scores(query_block, rotated_keys, row_start, block_rows, row_stop):
    scores = score_scale * jnp.einsum(
        "qhgd,khd->hgqk", query_block, rotated_keys, preferred_element_type=jnp.float32
    )
    causal = (row_start + jnp.arange(block_rows))[:, None] >= jnp.arange(row_stop)[None, :]
    return jnp.where(causal, scores, masked_score)


def attention_forward(query_rows, rotated_keys, value_rows):
    sequence_length = query_rows.shape[0]
    block_rows = min(512, sequence_length)
    scores = block_scores(query_rows, rotated_keys, 0, block_rows, block_rows)
    largest = jnp.max(scores, axis=-1, keepdims=True)
    weights_exp = jnp.exp(scores - largest)
    totals = jnp.sum(weights_exp, axis=-1, keepdims=True)
    probs_low = (weights_exp / totals).astype(jnp.bfloat16)
    outputs = jnp.einsum(
        "hgqk,khd->qhgd", probs_low, value_rows, preferred_element_type=jnp.float32
    )
    normalizers = [largest + jnp.log(totals)]
    return (outputs, normalizers)


def attention_backward(query_rows, rotated_keys, value_rows, normalizers, grad_mixed):
    sequence_length = query_rows.shape[0]
    block_rows = min(512, sequence_length)
    grad_keys = jnp.zeros(rotated_keys.shape, jnp.float32)
    grad_values = jnp.zeros(value_rows.shape, jnp.float32)
    grad_queries = []
    for block_index, row_start in enumerate(range(0, sequence_length, block_rows)):
        row_stop = row_start + block_rows
        scores = block_scores(query_rows, rotated_keys, row_start, block_rows, row_stop)
        probs = jnp.exp(scores - normalizers[block_index])
        probs_low = probs.astype(jnp.bfloat16)
        grad_probs = jnp.einsum(
            "qhgd,khd->hgqk", grad_mixed, value_rows, preferred_element_type=jnp.float32
        )
        inner = jnp.sum(probs * grad_probs, axis=-1, keepdims=True)
        grad_scores = (probs * (grad_probs - inner)).astype(jnp.bfloat16)
        grad_queries.append(
            score_scale
            * jnp.einsum(
                "hgqk,khd->qhgd", grad_scores, rotated_keys, preferred_element_type=jnp.float32
            )
        )
        grad_keys = grad_keys.at[:row_stop].add(
            score_scale
            * jnp.einsum(
                "hgqk,qhgd->khd", grad_scores, query_rows, preferred_element_type=jnp.float32
            )
        )
        grad_values = grad_values.at[:row_stop].add(
            jnp.einsum("hgqk,qhgd->khd", probs_low, grad_mixed, preferred_element_type=jnp.float32)
        )
    return (grad_queries[0], grad_keys, grad_values)


def to_owners(packed):
    return lax.all_to_all(packed, "ep", split_axis=1, concat_axis=1, tiled=True)


def back_to_tokens(rows_low, slot_count, model_width):
    returned = lax.all_to_all(rows_low, "ep", split_axis=1, concat_axis=1, tiled=True)
    joined = lax.all_gather(returned, "tp", axis=0, tiled=True)
    return joined.reshape(slot_count, model_width)


def from_owners(term_fn, slot_count, experts, model_width):
    share_rows = slot_count // lax.axis_size("tp")
    summed = lax.psum_scatter(
        term_fn(jnp.int32(0), lax.axis_size("tp") * share_rows).astype(jnp.bfloat16),
        "tp",
        scatter_dimension=0,
        tiled=True,
    ).astype(jnp.float32)
    summed = summed.astype(jnp.bfloat16).reshape(share_rows // experts, experts, model_width)
    return back_to_tokens(summed, slot_count, model_width)


def seq_rms(value_rows, seq_count):
    return jnp.sqrt(jnp.mean((value_rows * value_rows).reshape(seq_count, -1), axis=1))


def routed_shards(
    stream,
    cotangent,
    attention_gain,
    query_weight,
    key_matrix,
    value_matrix,
    out_weight,
    mixture_gain,
    router_weight,
    gate_weight,
    up_weight,
    down_weight,
    routes,
):
    tok_rows, model_width = stream.shape
    experts = router_weight.shape[1]
    cap_slots = tok_rows * TOP * 5 // (4 * experts)
    slot_count = cap_slots * experts
    query_heads = query_weight.shape[1] // HEAD_FEATURES
    key_heads = key_matrix.shape[1] // HEAD_FEATURES
    group_width = query_heads // key_heads
    seq_count = tok_rows // SEQ_LEN
    stream_f = stream.astype(jnp.float32)
    grad_result = cotangent.astype(jnp.float32)
    gain_first = attention_gain.astype(jnp.float32)
    gain_second = mixture_gain.astype(jnp.float32)
    cosine_table, sine_values = rope_tables(SEQ_LEN)
    cosine_rows = jnp.tile(cosine_table, (seq_count, 1))
    sine_rows = jnp.tile(sine_values, (seq_count, 1))
    zero_low = jnp.zeros((), jnp.bfloat16)
    inv_first = lax.rsqrt(jnp.mean(stream_f * stream_f, axis=-1, keepdims=True) + epsilon)
    normalized_input = (stream_f * inv_first * gain_first).astype(jnp.bfloat16)
    query_pre = jnp.dot(normalized_input, query_weight, preferred_element_type=jnp.float32).reshape(
        tok_rows, query_heads, HEAD_FEATURES
    )
    key_pre = jnp.dot(normalized_input, key_matrix, preferred_element_type=jnp.float32).reshape(
        tok_rows, key_heads, HEAD_FEATURES
    )
    query_rows = (
        apply_rotation(query_pre, cosine_rows, sine_rows)
        .astype(jnp.bfloat16)
        .reshape(tok_rows, key_heads, group_width, HEAD_FEATURES)
    )
    rotated_keys = apply_rotation(key_pre, cosine_rows, sine_rows).astype(jnp.bfloat16)
    value_rows = (
        jnp.dot(normalized_input, value_matrix, preferred_element_type=jnp.float32)
        .astype(jnp.bfloat16)
        .reshape(tok_rows, key_heads, HEAD_FEATURES)
    )
    mixed_seq, norms_seq = attention_forward(query_rows, rotated_keys, value_rows)
    mixed_low = mixed_seq.reshape(tok_rows, query_heads * HEAD_FEATURES).astype(jnp.bfloat16)
    attended = lax.psum(
        jnp.dot(mixed_low, out_weight, preferred_element_type=jnp.float32).astype(jnp.bfloat16),
        "tp",
    ).astype(jnp.float32)
    middle = stream_f + residual_scale * attended
    inv_second = lax.rsqrt(jnp.mean(middle * middle, axis=-1, keepdims=True) + epsilon)
    mixer_in = (middle * inv_second * gain_second).astype(jnp.bfloat16)
    logits = jnp.dot(mixer_in, router_weight, preferred_element_type=jnp.float32)
    expert_ids = jnp.arange(experts, dtype=jnp.int32)
    route_hot = routes[:, :, None] == expert_ids[None, None, :]
    chosen = jnp.sum(jnp.where(route_hot, logits[:, None, :], 0.0), axis=-1)
    chosen_exp = jnp.exp(chosen - jnp.max(chosen, axis=-1, keepdims=True))
    gate_probs = chosen_exp / jnp.sum(chosen_exp, axis=-1, keepdims=True)
    flat_routes = routes.reshape(-1)
    flat_hot = route_hot.reshape(tok_rows * TOP, experts).astype(jnp.int32)
    ranks = jnp.sum((jnp.cumsum(flat_hot, axis=0) - 1) * flat_hot, axis=1)
    slot_index = ranks * experts + flat_routes
    source_pair = (
        jnp.zeros((slot_count,), jnp.int32)
        .at[slot_index]
        .set(jnp.arange(tok_rows * TOP, dtype=jnp.int32))
    )
    filled = jnp.zeros((slot_count,), jnp.bool_).at[slot_index].set(True)
    source_token = source_pair // TOP
    sent_rows = jnp.where(filled[:, None], mixer_in[source_token], zero_low).reshape(
        cap_slots, experts, model_width
    )
    received = to_owners(sent_rows).reshape(slot_count, model_width)
    gate_matrix = gate_weight[0]
    up_matrix = up_weight[0]
    down_matrix = down_weight[0]
    gate_pre = jnp.dot(received, gate_matrix, preferred_element_type=jnp.float32)
    up_pre = jnp.dot(received, up_matrix, preferred_element_type=jnp.float32)
    sigmoid_gate = jax.nn.sigmoid(gate_pre)
    silu_gate = gate_pre * sigmoid_gate
    active = (silu_gate * up_pre).astype(jnp.bfloat16)

    def down_term(row_start, row_count):
        return jnp.dot(active, down_matrix, preferred_element_type=jnp.float32)

    expert_rows = from_owners(down_term, slot_count, experts, model_width)
    picked_rows = expert_rows[slot_index].reshape(tok_rows, TOP, model_width)
    mixture = jnp.sum(gate_probs[:, :, None] * picked_rows, axis=1)
    result = middle + residual_scale * mixture
    layer_out = result.astype(jnp.bfloat16)
    rms_stats = jnp.stack(
        [seq_rms(result, seq_count), seq_rms(attended, seq_count), seq_rms(mixture, seq_count)],
        axis=1,
    )
    grad_mix = residual_scale * grad_result
    grad_weighting = jnp.sum(picked_rows * grad_mix[:, None, :], axis=-1)
    grad_chosen = gate_probs * (
        grad_weighting - jnp.sum(gate_probs * grad_weighting, axis=-1, keepdims=True)
    )
    grad_logits = jnp.sum(jnp.where(route_hot, grad_chosen[:, :, None], 0.0), axis=1).astype(
        jnp.bfloat16
    )
    router_grad = jnp.dot(mixer_in.T, grad_logits, preferred_element_type=jnp.float32)
    flat_gates = gate_probs.reshape(-1)
    grad_sent = jnp.where(
        filled[:, None],
        (flat_gates[source_pair][:, None] * grad_mix[source_token]).astype(jnp.bfloat16),
        zero_low,
    ).reshape(cap_slots, experts, model_width)
    grad_received = to_owners(grad_sent).reshape(slot_count, model_width)
    grad_active = jnp.dot(grad_received, down_matrix.T, preferred_element_type=jnp.float32)
    down_grad = jnp.dot(active.T, grad_received, preferred_element_type=jnp.float32)
    grad_gate_pre = (
        grad_active * up_pre * sigmoid_gate * (1.0 + gate_pre * (1.0 - sigmoid_gate))
    ).astype(jnp.bfloat16)
    grad_up_pre = (grad_active * silu_gate).astype(jnp.bfloat16)
    gate_grad = jnp.dot(received.T, grad_gate_pre, preferred_element_type=jnp.float32)
    up_grad = jnp.dot(received.T, grad_up_pre, preferred_element_type=jnp.float32)

    def input_term(row_start, row_count):
        return jnp.dot(grad_gate_pre, gate_matrix.T, preferred_element_type=jnp.float32) + jnp.dot(
            grad_up_pre, up_matrix.T, preferred_element_type=jnp.float32
        )

    grad_rows = from_owners(input_term, slot_count, experts, model_width)
    grad_mixer = jnp.dot(
        grad_logits, router_weight.T, preferred_element_type=jnp.float32
    ) + jnp.sum(
        grad_rows[slot_index].reshape(tok_rows, TOP, model_width), axis=1, dtype=jnp.float32
    )
    weighted_second = grad_mixer * gain_second
    second_grad = jnp.sum(grad_mixer * middle * inv_second, axis=0)
    grad_middle = (
        grad_result
        + inv_second * weighted_second
        - middle * inv_second**3 * jnp.mean(middle * weighted_second, axis=-1, keepdims=True)
    )
    grad_attended = (residual_scale * grad_middle).astype(jnp.bfloat16)
    out_grad_t = jnp.dot(grad_attended.T, mixed_low, preferred_element_type=jnp.float32)
    grad_mixed = (
        jnp.dot(grad_attended, out_weight.T, preferred_element_type=jnp.float32)
        .astype(jnp.bfloat16)
        .reshape(tok_rows, key_heads, group_width, HEAD_FEATURES)
    )
    grad_query_seq, grad_key_seq, grad_value_seq = attention_backward(
        query_rows, rotated_keys, value_rows, norms_seq, grad_mixed
    )
    grad_queries_rot = grad_query_seq.reshape(tok_rows, query_heads, HEAD_FEATURES)
    grad_query_pre = (
        rotary_back(grad_queries_rot, cosine_rows, sine_rows)
        .astype(jnp.bfloat16)
        .reshape(tok_rows, query_heads * HEAD_FEATURES)
    )
    grad_key_pre = (
        rotary_back(grad_key_seq, cosine_rows, sine_rows)
        .astype(jnp.bfloat16)
        .reshape(tok_rows, key_heads * HEAD_FEATURES)
    )
    grad_values_low = grad_value_seq.astype(jnp.bfloat16).reshape(
        tok_rows, key_heads * HEAD_FEATURES
    )
    query_grad = jnp.dot(normalized_input.T, grad_query_pre, preferred_element_type=jnp.float32)
    key_grad = jnp.dot(normalized_input.T, grad_key_pre, preferred_element_type=jnp.float32)
    value_grad = jnp.dot(normalized_input.T, grad_values_low, preferred_element_type=jnp.float32)
    normed_term = jnp.dot(grad_query_pre, query_weight.T, preferred_element_type=jnp.float32)
    normed_term = normed_term + jnp.dot(
        grad_key_pre, key_matrix.T, preferred_element_type=jnp.float32
    )
    normed_term = normed_term + jnp.dot(
        grad_values_low, value_matrix.T, preferred_element_type=jnp.float32
    )
    grad_normed = lax.psum(normed_term.astype(jnp.bfloat16), "tp").astype(jnp.float32)
    weighted_first = grad_normed * gain_first
    first_grad = jnp.sum(grad_normed * stream_f * inv_first, axis=0)
    grad_stream = (
        grad_middle
        + inv_first * weighted_first
        - stream_f * inv_first**3 * jnp.mean(stream_f * weighted_first, axis=-1, keepdims=True)
    )
    reduced = (
        lax.psum_scatter(query_grad, "ep", scatter_dimension=0, tiled=True),
        lax.psum_scatter(key_grad, "ep", scatter_dimension=0, tiled=True),
        lax.psum_scatter(value_grad, "ep", scatter_dimension=0, tiled=True),
        lax.psum_scatter(out_grad_t, "ep", scatter_dimension=0, tiled=True),
        lax.psum_scatter(router_grad, "ep", scatter_dimension=0, tiled=True),
        lax.psum_scatter(first_grad, "ep", scatter_dimension=0, tiled=True),
        lax.psum_scatter(second_grad, "ep", scatter_dimension=0, tiled=True),
    )
    return (
        layer_out,
        grad_stream,
        reduced[5],
        reduced[0],
        reduced[1],
        reduced[2],
        reduced[3].T,
        reduced[6],
        reduced[4],
        gate_grad[None],
        up_grad[None],
        down_grad[None],
        rms_stats,
    )


MESH = pl.DeviceIdType.MESH
PLANE = 4
LINES = 4
CHUNK = 32
DEFERRED = (2,)


def flip(place, unit):
    return place + unit * (1 - 2 * lax.rem(lax.div(place, unit), 2))


def flip_line(place, step):
    if step % 2:
        place = flip(place, PLANE)
    if step // 2:
        place = flip(place, 2 * PLANE)
    return place


def matmul(left, right):
    return jnp.dot(left, right, preferred_element_type=jnp.float32)


def matmul_nt(left, right):
    return lax.dot_general(
        left, right, (((1,), (1,)), ((), ())), preferred_element_type=jnp.float32
    )


def matmul_tn(left, right):
    return lax.dot_general(
        left, right, (((0,), (0,)), ((), ())), preferred_element_type=jnp.float32
    )


def lane_halves(value):
    lane = lax.broadcasted_iota(jnp.int32, value.shape, 1)
    low = jnp.where(lane < HEAD_FEATURES, value, 0.0)
    high = jnp.where(lane < HEAD_FEATURES, 0.0, value)
    return low, high


def partner_lanes(value):
    width = value.shape[1]
    quarter = HEAD_FEATURES // 2
    lane = lax.broadcasted_iota(jnp.int32, value.shape, 1)
    ahead = pltpu.roll(value, width - quarter, 1)
    behind = pltpu.roll(value, quarter, 1)
    return jnp.where(lax.rem(lane, HEAD_FEATURES) < quarter, ahead, behind)


def causal_scores(query_block, key_block, row_start):
    scores = score_scale * matmul_nt(query_block, key_block)
    row = lax.broadcasted_iota(jnp.int32, scores.shape, 0) + row_start
    column = lax.broadcasted_iota(jnp.int32, scores.shape, 1)
    return jnp.where(row >= column, scores, masked_score)


def store_slots(slots, values):
    for group in range(values.shape[1] // HEAD_FEATURES):
        pair = group // 2
        low, high = lane_halves(values[:, pair * 128 : pair * 128 + 128])
        if group % 2:
            low = pltpu.roll(high, HEAD_FEATURES, 1)
        else:
            high = pltpu.roll(low, HEAD_FEATURES, 1)
        slots[2 * group] = low.astype(jnp.bfloat16)
        slots[2 * group + 1] = high.astype(jnp.bfloat16)


def front_kernel(*refs):
    tiles = 2 * PLANE
    refs = list(refs)

    def take(count):
        taken = refs[:count]
        del refs[:count]
        return taken

    stream, cotangent, gain_first, gain_second, query_weight, key_weight = take(6)
    value_weight, out_weight, router, routes, cosine, sine = take(6)
    weights = take(3)
    out_parts = take(LINES)
    grow_sum, weighting_sum = take(2)
    kept = take(3)
    landed = take(3)
    mixer_own, probs_own, normed_out, queries_out, keys_out, values_out, mixed_out = take(7)
    attended = take(1)[0]
    mixer, cots, probs, gates, ups, downs = take(6)
    scaled, ggate, gup, grow, grow_in, outs, weighting, weighting_in = take(8)
    part_send, part_recv = take(2)
    load_sem, own_sem, weight_send, weight_recv = take(4)
    relay_send, relay_recv, probs_send, probs_recv, part_sem = take(5)
    result_sem, store_sem, kept_sem = take(3)
    grow_send, grow_recv, weighting_send, weighting_recv = take(4)
    core_send, core_recv, plane_send, plane_recv, ready_sem = take(5)
    held = (gates, ups, downs)
    rows_all, width = mixer.shape
    half = rows_all // LINES
    tokens = 2 * half
    span = gates.shape[2]
    column_tiles = width // span
    heads_width = query_weight.shape[1]
    pieces = heads_width // span
    tall = scaled.shape[1]

    place = lax.axis_index("ep")
    core = lax.axis_index("tp")
    line = lax.div(place, PLANE)
    sibling = (place, 1 - core)
    across = [(flip(place, 1), core), (flip(place, 2), core)]
    partners = [(flip_line(place, step), core) for step in range(LINES)]
    own_rows = pl.ds(pl.multiple_of(core * half, half), half)
    stream_v, normed = outs.at[pl.ds(0, tokens)], outs.at[pl.ds(tokens, tokens)]

    def block_rows_of(block):
        return pl.ds(pl.multiple_of(block * half, half), half)

    line_rows = block_rows_of(line)

    barrier = pltpu.get_barrier_semaphore()
    for other in across + partners[1:] + [sibling]:
        pl.semaphore_signal(barrier, inc=1, device_id=other, device_id_type=MESH)

    def tall_loads(source, column, target, tile, index):
        return [
            pltpu.make_async_copy(
                source.at[pl.ds(start, size), pl.ds(column * span, span)],
                target.at[tile + part, pl.ds(0, size)],
                load_sem.at[index + part],
            )
            for part, (start, size) in enumerate(((0, tall), (tall, width - tall)))
        ]

    loads = [pltpu.make_async_copy(stream, stream_v, load_sem.at[0])]
    for piece in range(pieces):
        loads += tall_loads(query_weight, piece, scaled, 2 * piece, 1 + 2 * piece)
    loads += tall_loads(key_weight, 0, ggate, 0, 1 + 2 * pieces)
    loads += tall_loads(value_weight, 0, ggate, tiles - 2, 3 + 2 * pieces)
    out_loads = [
        pltpu.make_async_copy(
            out_weight.at[:, pl.ds(column * span, span)],
            grow.at[column, pl.ds(0, heads_width)],
            load_sem.at[5 + 2 * pieces + column],
        )
        for column in range(column_tiles)
    ]
    for copy in loads + out_loads:
        copy.start()
    pl.semaphore_wait(barrier, LINES + 2)

    def send(source, target, sems, index, device):
        return pltpu.make_async_remote_copy(
            src_ref=source,
            dst_ref=target,
            send_sem=sems[0].at[index],
            recv_sem=sems[1].at[index],
            device_id=device,
            device_id_type=MESH,
        )

    weight_sems = (weight_send, weight_recv)

    def direct(kind, axis):
        return send(
            weights[kind], held[kind].at[axis + 1], weight_sems, (kind, axis), across[axis]
        )

    def to_sibling(kind, slot):
        source = weights[kind] if slot == 0 else held[kind].at[slot]
        return send(source, held[kind].at[PLANE + slot], weight_sems, (kind, 2 + slot), sibling)

    def onward(kind, axis):
        source, target = held[kind].at[2 - axis], held[kind].at[3]
        if kind == 1:
            part = pl.ds(axis * (width // 2), width // 2)
            source, target = held[kind].at[2 - axis, part], held[kind].at[3, part]
        return send(source, target, weight_sems, (kind, 6 + axis), across[axis])

    onwards = {0: (0,), 1: (0, 1), 2: (1,)}

    def relay(array, hop, downward):
        gathered = (cots, mixer)[array]
        shift = -1 if downward else 1
        block = block_rows_of(jnp.clip(line - shift * hop, 0, LINES - 1))
        source = gathered.at[block]
        if hop == 0 and array == 0:
            source = cotangent.at[own_rows]
        return send(
            source,
            gathered.at[block],
            (relay_send, relay_recv),
            (array, downward, hop),
            (place + shift * PLANE, core),
        )

    def arriving(array, hop, downward):
        gathered = (cots, mixer)[array]
        shift = -1 if downward else 1
        block = block_rows_of(jnp.clip(line - shift * (hop + 1), 0, LINES - 1))
        return send(
            gathered.at[block],
            gathered.at[block],
            (relay_send, relay_recv),
            (array, downward, hop),
            (place + shift * PLANE, core),
        )

    def relay_sends(hop, downward):
        if downward:
            return jnp.logical_and(line > 0, line + hop < LINES)
        return jnp.logical_and(line < LINES - 1, line - hop >= 0)

    def relay_receives(hop, downward):
        if downward:
            return line + 1 + hop < LINES
        return line - 1 - hop >= 0

    def start_relay(array, hop):
        for downward in (0, 1):

            @pl.when(relay_sends(hop, downward))
            def _():
                relay(array, hop, downward).start()

    def receive_relay(array, hop):
        for downward in (0, 1):

            @pl.when(relay_receives(hop, downward))
            def _():
                arriving(array, hop, downward).wait_recv()

    def finish_relay(array, hop):
        for downward in (0, 1):

            @pl.when(relay_sends(hop, downward))
            def _():
                relay(array, hop, downward).wait_send()

    for kind in range(3):
        for axis in (0, 1):
            direct(kind, axis).start()
    start_relay(0, 0)
    own_copies = [
        pltpu.make_async_copy(weights[kind], held[kind].at[0], own_sem.at[kind])
        for kind in range(3)
    ]
    own_copies.append(
        pltpu.make_async_copy(cotangent.at[own_rows], cots.at[line_rows], own_sem.at[3])
    )
    for kind in range(3):
        to_sibling(kind, 0).start()
    for copy in own_copies:
        copy.start()
    weighting[...] = jnp.zeros_like(weighting)

    loads[0].wait()

    def normed_chunk(index, carry):
        rows = pl.ds(pl.multiple_of(index * CHUNK, CHUNK), CHUNK)
        stream_f = stream_v[rows, :].astype(jnp.float32)
        inverse = lax.rsqrt(jnp.mean(stream_f * stream_f, axis=-1, keepdims=True) + epsilon)
        normed[rows, :] = (
            stream_f * inverse * gain_first[...].astype(jnp.float32)[None, :]
        ).astype(jnp.bfloat16)
        return carry

    lax.fori_loop(0, tokens // CHUNK, normed_chunk, 0)
    for copy in loads[1:]:
        copy.wait()

    def projected(target, tile):
        return matmul(normed[:, :tall], target[tile]) + matmul(
            normed[:, tall:], target[tile + 1, : width - tall, :]
        )

    def rotated(pre):
        turned = []
        for pair in range(span // 128):
            part = pre[:, pair * 128 : pair * 128 + 128]
            turned.append(part * cosine[...] + partner_lanes(part) * sine[...])
        return jnp.concatenate(turned, axis=1).astype(jnp.bfloat16)

    low_rows, high_rows = pl.ds(0, tokens), pl.ds(tokens, tokens)
    for piece in range(pieces):
        ggate[3 + piece, low_rows, :] = rotated(projected(scaled, 2 * piece))
    key_rows = rotated(projected(ggate, 0))
    ggate[2, low_rows, :] = key_rows
    value_rows = projected(ggate, tiles - 2).astype(jnp.bfloat16)
    ggate[2, high_rows, :] = value_rows

    def store_overlaid(values, rows):
        for group in range(values.shape[1] // HEAD_FEATURES):
            pair = group // 2
            low, high = lane_halves(values[:, pair * 128 : pair * 128 + 128].astype(jnp.float32))
            if group % 2:
                low = pltpu.roll(high, HEAD_FEATURES, 1)
            else:
                high = pltpu.roll(low, HEAD_FEATURES, 1)
            gup[2 * group, rows, :128] = low.astype(jnp.bfloat16)
            gup[2 * group + 1, rows, :128] = high.astype(jnp.bfloat16)

    store_overlaid(key_rows, low_rows)
    store_overlaid(value_rows, high_rows)
    results = [
        pltpu.make_async_copy(normed, normed_out, result_sem.at[0]),
        pltpu.make_async_copy(ggate.at[2, low_rows], keys_out, result_sem.at[1]),
        pltpu.make_async_copy(ggate.at[2, high_rows], values_out, result_sem.at[2]),
    ]
    for piece in range(pieces):
        results.append(
            pltpu.make_async_copy(
                ggate.at[3 + piece, low_rows],
                queries_out.at[:, pl.ds(piece * span, span)],
                result_sem.at[3 + piece],
            )
        )
    for copy in results:
        copy.start()
    group = heads_width // key_weight.shape[1]
    blocks = 2
    block_rows = tokens // blocks

    def head_pair(pair, carry):
        tile = 3 + lax.div(pair, 2)
        here = pl.ds(pl.multiple_of(lax.rem(pair, 2) * 128, 128), 128)
        for block in range(blocks):
            start = block * block_rows
            reach = start + block_rows
            total = jnp.zeros((block_rows, 128), jnp.float32)
            query_block = ggate[tile, pl.ds(start, block_rows), here]
            for parity in range(2):
                slot = 2 * lax.div(2 * pair + parity, group) + parity
                scores = causal_scores(query_block, gup[slot, pl.ds(0, reach), :128], start)
                weight = jnp.exp(scores - jnp.max(scores, axis=-1, keepdims=True))
                weight = weight / jnp.sum(weight, axis=-1, keepdims=True)
                total = total + matmul(
                    weight.astype(jnp.bfloat16), gup[slot, pl.ds(tokens, reach), :128]
                )
            ggate[tile, pl.ds(tokens + start, block_rows), here] = total.astype(jnp.bfloat16)
        return carry

    lax.fori_loop(0, heads_width // 128, head_pair, 0)
    receive_relay(0, 0)
    start_relay(0, 1)
    for piece in range(pieces):
        results.append(
            pltpu.make_async_copy(
                ggate.at[3 + piece, high_rows],
                mixed_out.at[:, pl.ds(piece * span, span)],
                result_sem.at[3 + pieces + piece],
            )
        )
    for copy in results[3 + pieces :]:
        copy.start()
    for copy in out_loads:
        copy.wait()

    def out_product(first_row, column):
        rows = pl.ds(pl.multiple_of(tokens + first_row * half, half), half)
        return sum(
            matmul(ggate[3 + piece, rows, :], grow[column, pl.ds(piece * span, span), :])
            for piece in range(pieces)
        )

    def send_column(column, carry):
        here = pl.ds(pl.multiple_of(column * span, span), span)
        part_send[:, here] = out_product(1 - core, column).astype(jnp.bfloat16)
        return carry

    def own_column(column, carry):
        here = pl.ds(pl.multiple_of(column * span, span), span)
        grow_sum[:, here] = out_product(core, column)
        return carry

    lax.fori_loop(0, column_tiles, send_column, 0)
    part_copy = pltpu.make_async_remote_copy(
        src_ref=part_send,
        dst_ref=part_recv,
        send_sem=part_sem.at[0],
        recv_sem=part_sem.at[1],
        device_id=sibling,
        device_id_type=MESH,
    )
    part_copy.start()
    lax.fori_loop(0, column_tiles, own_column, 0)
    part_copy.wait()

    def mixer_chunk(index, carry):
        rows = pl.ds(pl.multiple_of(index * CHUNK, CHUNK), CHUNK)
        stream_part = pl.ds(pl.multiple_of(core * half + index * CHUNK, CHUNK), CHUNK)
        mixer_part = pl.ds(pl.multiple_of(line * half + index * CHUNK, CHUNK), CHUNK)
        attended_f = grow_sum[rows, :] + part_recv[rows, :].astype(jnp.float32)
        attended[rows, :] = attended_f.astype(jnp.bfloat16)
        middle = stream_v[stream_part, :].astype(jnp.float32) + residual_scale * attended_f
        inverse = lax.rsqrt(jnp.mean(middle * middle, axis=-1, keepdims=True) + epsilon)
        mixer[mixer_part, :] = (
            middle * inverse * gain_second[...].astype(jnp.float32)[None, :]
        ).astype(jnp.bfloat16)
        return carry

    lax.fori_loop(0, half // CHUNK, mixer_chunk, 0)
    start_relay(1, 0)
    padding = jnp.zeros((128 - router.shape[0], width), jnp.bfloat16)
    logits = matmul_nt(
        mixer[line_rows, :], jnp.concatenate([router[...], padding], axis=0)
    )
    own_routes = routes[:, own_rows].T
    lane = lax.broadcasted_iota(jnp.int32, logits.shape, 1)
    routed = lane < 0
    for entry in range(TOP):
        routed = jnp.logical_or(routed, lane == own_routes[:, entry : entry + 1])
    largest = jnp.max(jnp.where(routed, logits, masked_score), axis=-1, keepdims=True)
    gate_exp = jnp.where(routed, jnp.exp(jnp.minimum(logits - largest, 0.0)), 0.0)
    probs[line_rows, :] = gate_exp / jnp.sum(gate_exp, axis=-1, keepdims=True)

    def probs_copy(step):
        return send(
            probs.at[line_rows],
            probs.at[line_rows],
            (probs_send, probs_recv),
            (step,),
            partners[step],
        )

    def probs_arriving(step):
        theirs = block_rows_of(lax.div(partners[step][0], PLANE))
        return send(
            probs.at[theirs],
            probs.at[theirs],
            (probs_send, probs_recv),
            (step,),
            partners[step],
        )

    for step in range(1, LINES):
        probs_copy(step).start()
    own_copies.append(pltpu.make_async_copy(probs.at[line_rows], probs_own, own_sem.at[4]))
    own_copies.append(pltpu.make_async_copy(mixer.at[line_rows], mixer_own, own_sem.at[5]))
    for copy in own_copies[4:]:
        copy.start()

    def pass_on(kind):
        for axis in (0, 1):
            direct(kind, axis).wait_recv()
        for axis in onwards[kind]:
            onward(kind, axis).start()
        for slot in (1, 2):
            to_sibling(kind, slot).start()

    def hidden_tile(block, tile):
        rows = block_rows_of(block)
        step = lax.rem(tile, PLANE)
        owner = lax.rem(place, PLANE)
        owner = jnp.where(lax.rem(step, 2) == 1, flip(owner, 1), owner)
        owner = jnp.where(lax.div(step, 2) == 1, flip(owner, 2), owner)
        chosen = lax.broadcasted_iota(jnp.int32, (half, 128), 1) == line * PLANE + owner
        prob = jnp.sum(jnp.where(chosen, probs[rows, :], 0.0), axis=1, keepdims=True)
        gate_pre = matmul(mixer[rows, :], gates[tile])
        up_pre = matmul(mixer[rows, :], ups[tile])
        grad_raw = residual_scale * matmul_nt(cots[rows, :], downs[tile])
        sigmoid_gate = 1.0 / (1.0 + jnp.exp(-gate_pre))
        silu_gate = gate_pre * sigmoid_gate
        active = silu_gate * up_pre
        share = jnp.sum(active * grad_raw, axis=1, keepdims=True)
        weighting[rows, :] += jnp.where(chosen, share, 0.0)
        grad_active = prob * grad_raw
        scaled[tile, rows, :] = (prob * active).astype(jnp.bfloat16)
        ggate[tile, rows, :] = (
            grad_active * up_pre * sigmoid_gate * (1.0 + gate_pre * (1.0 - sigmoid_gate))
        ).astype(jnp.bfloat16)
        gup[tile, rows, :] = (grad_active * silu_gate).astype(jnp.bfloat16)

    def early_tiles(block):
        def body(index, carry):
            hidden_tile(block, index + lax.div(index, 3))
            return carry

        lax.fori_loop(0, 6, body, 0)

    def late_tiles(block):
        def body(index, carry):
            hidden_tile(block, 3 + PLANE * index)
            return carry

        lax.fori_loop(0, 2, body, 0)

    def grow_tiles(block, first, last):
        rows = block_rows_of(block)

        def body(column, carry):
            here = pl.ds(pl.multiple_of(column * span, span), span)
            total = matmul_nt(ggate[0, rows, :], gates[0, here, :])
            for tile in range(1, tiles):
                total = total + matmul_nt(ggate[tile, rows, :], gates[tile, here, :])
            for tile in range(tiles):
                total = total + matmul_nt(gup[tile, rows, :], ups[tile, here, :])
            grow[column, rows, :] = total.astype(jnp.bfloat16)
            return carry

        lax.fori_loop(first, last, body, 0)

    outer = jnp.logical_or(line == 0, line == LINES - 1)
    near_line = flip(line, 1)
    far_inner = jnp.where(line < 2, 2, 1)
    far_outer = jnp.where(line < 2, 3, 0)

    def remote_block(index):
        outside = (near_line, far_inner, far_outer)[index]
        inside = (far_inner, far_outer, near_line)[index]
        return jnp.where(outer, outside, inside)

    def home_of(block):
        return (place + (block - line) * PLANE, core)

    chunks = 2
    chunk_columns = column_tiles // chunks

    def grow_copy(index, chunk):
        block = remote_block(index)
        home = jnp.where(outer, near_line, block)
        slot = jnp.where(outer, (0, 2, 3)[index], (1, 1, 0)[index])
        columns = pl.ds(chunk * chunk_columns, chunk_columns)
        return pltpu.make_async_remote_copy(
            src_ref=grow.at[columns, block_rows_of(block)],
            dst_ref=grow_in.at[slot, columns],
            send_sem=grow_send.at[index, chunk],
            recv_sem=grow_recv.at[slot, chunk],
            device_id=home_of(home),
            device_id_type=MESH,
        )

    def grow_arriving(slot, chunk):
        columns = pl.ds(chunk * chunk_columns, chunk_columns)
        return pltpu.make_async_remote_copy(
            src_ref=grow_in.at[slot, columns],
            dst_ref=grow_in.at[slot, columns],
            send_sem=grow_send.at[0, chunk],
            recv_sem=grow_recv.at[slot, chunk],
            device_id=home_of(near_line),
            device_id_type=MESH,
        )

    def combine(index, chunk):
        @pl.when(jnp.logical_not(outer))
        def _():
            grow_arriving(2 + index, chunk).wait_recv()
            rows = block_rows_of(remote_block(index))

            def add_column(column, carry):
                grow[column, rows, :] = (
                    grow[column, rows, :].astype(jnp.float32)
                    + grow_in[2 + index, column].astype(jnp.float32)
                ).astype(jnp.bfloat16)
                return carry

            first = chunk * chunk_columns
            lax.fori_loop(first, first + chunk_columns, add_column, 0)
            grow_copy(index, chunk).start()

    def weighting_copy(index):
        block = remote_block(index)
        return pltpu.make_async_remote_copy(
            src_ref=weighting.at[block_rows_of(block)],
            dst_ref=weighting_in.at[line],
            send_sem=weighting_send.at[index],
            recv_sem=weighting_recv.at[line],
            device_id=home_of(block),
            device_id_type=MESH,
        )

    def weighting_arriving(index):
        block = remote_block(index)
        return pltpu.make_async_remote_copy(
            src_ref=weighting_in.at[block],
            dst_ref=weighting_in.at[block],
            send_sem=weighting_send.at[index],
            recv_sem=weighting_recv.at[block],
            device_id=home_of(block),
            device_id_type=MESH,
        )

    def send_back(index):
        weighting_copy(index).start()
        for chunk in range(chunks):
            grow_tiles(
                remote_block(index), chunk * chunk_columns, (chunk + 1) * chunk_columns
            )
            if index == 2:
                grow_copy(index, chunk).start()
            elif index == 1:

                @pl.when(outer)
                def _():
                    grow_copy(index, chunk).start()

        if index == 2:

            @pl.when(outer)
            def _():
                for chunk in range(chunks):
                    grow_copy(0, chunk).start()

    pass_on(0)
    receive_relay(1, 0)
    start_relay(1, 1)
    receive_relay(0, 1)
    start_relay(0, 2)
    pass_on(1)
    pass_on(2)
    for copy in results:
        copy.wait()
    for copy in own_copies:
        copy.wait()
    for step in range(1, LINES):
        probs_copy(step).wait_send()
        probs_arriving(step).wait_recv()
    for kind in range(3):
        for slot in range(3):
            to_sibling(kind, slot).wait_recv()
    early_tiles(remote_block(0))
    receive_relay(1, 1)
    start_relay(1, 2)
    for kind in range(3):
        for axis in onwards[kind]:
            onward(kind, axis).wait_recv()
        to_sibling(kind, 3).start()
    early_tiles(line)
    early_tiles(remote_block(1))
    for kind in range(3):
        to_sibling(kind, 3).wait_recv()
    late_tiles(remote_block(0))
    send_back(0)
    late_tiles(remote_block(1))
    send_back(1)
    late_tiles(line)
    grow_tiles(line, 0, column_tiles)
    receive_relay(0, 2)
    receive_relay(1, 2)
    early_tiles(remote_block(2))
    late_tiles(remote_block(2))
    send_back(2)
    for kind in range(3):
        for slot in range(PLANE):
            to_sibling(kind, slot).wait_send()
        for axis in (0, 1):
            direct(kind, axis).wait_send()
        for axis in onwards[kind]:
            onward(kind, axis).wait_send()
    for array in (0, 1):
        for hop in range(LINES - 1):
            finish_relay(array, hop)

    def out_tile(column, carry):
        here = pl.ds(pl.multiple_of(column * span, span), span)
        total = matmul(scaled[0], downs[0, :, here])
        for tile in range(1, tiles):
            total = total + matmul(scaled[tile], downs[tile, :, here])
        outs[:, here] = total.astype(jnp.bfloat16)
        return carry

    stores = [
        pltpu.make_async_copy(
            outs.at[block_rows_of(lax.div(partners[step][0], PLANE))],
            out_parts[step],
            store_sem.at[step],
        )
        for step in range(LINES)
    ]
    pl.semaphore_signal(ready_sem, inc=1, device_id=sibling, device_id_type=MESH)
    pl.semaphore_wait(ready_sem, 1)
    def tile_order(index):
        return jnp.where(index == 0, 3, jnp.where(index == 3, 0, index))

    def tile_grads(tile, kinds):
        for kind in kinds:
            if kind == 2:
                yield kind, residual_scale * matmul_tn(scaled[tile], cots[...])
            else:
                yield kind, matmul_tn(mixer[...], (ggate, gup)[kind][tile])

    def core_copy(kind, step):
        return pltpu.make_async_remote_copy(
            src_ref=held[kind].at[PLANE + step],
            dst_ref=held[kind].at[step],
            send_sem=core_send.at[kind, step],
            recv_sem=core_recv.at[kind, step],
            device_id=sibling,
            device_id_type=MESH,
        )

    def sibling_tile(index, kinds):
        step = tile_order(index)
        for kind, grad in tile_grads(PLANE + step, kinds):
            held[kind][PLANE + step] = grad.astype(jnp.bfloat16)
            core_copy(kind, step).start()

    def plane_copy(kind, axis, passing):
        span_rows = held[kind].shape[1] // 2
        step = 3 if passing else axis + 1
        return pltpu.make_async_remote_copy(
            src_ref=held[kind].at[step, pl.ds(axis * span_rows, span_rows)],
            dst_ref=landed[kind].at[axis, passing],
            send_sem=plane_send.at[kind, axis, passing],
            recv_sem=plane_recv.at[kind, axis, passing],
            device_id=across[axis],
            device_id_type=MESH,
        )

    def kept_copy(kind, step):
        return pltpu.make_async_copy(
            held[kind].at[step], kept[kind].at[step], kept_sem.at[kind, step]
        )

    def own_tile(index, kinds):
        @pl.when(index < PLANE - 1)
        def _():
            sibling_tile(index + 1, kinds)

        step = tile_order(index)
        for kind, grad in tile_grads(step, kinds):
            core_copy(kind, step).wait_recv()
            held[kind][step] = (grad + held[kind][step].astype(jnp.float32)).astype(jnp.bfloat16)

            @pl.when(step == 3)
            def _():
                for axis in (0, 1):
                    plane_copy(kind, axis, 1).start()

            for axis in (0, 1):

                if kind in DEFERRED:
                    continue

                @pl.when(step == axis + 1)
                def _():
                    plane_copy(kind, axis, 0).start()

            @pl.when(step < 3)
            def _():
                kept_copy(kind, step).start()

        return kinds

    def gate_and_up(index, carry):
        own_tile(index, (0, 1))
        return carry

    def down_only(index, carry):
        own_tile(index, (2,))
        return carry

    sibling_tile(0, (0, 1))
    lax.fori_loop(0, 1, gate_and_up, 0)
    combine(0, 0)
    combine(0, 1)
    lax.fori_loop(1, PLANE, gate_and_up, 0)
    combine(1, 0)
    lax.fori_loop(0, column_tiles, out_tile, 0)
    combine(1, 1)
    for copy in stores:
        copy.start()
    pl.semaphore_signal(ready_sem, inc=1, device_id=sibling, device_id_type=MESH)
    pl.semaphore_wait(ready_sem, 1)
    sibling_tile(0, (2,))
    lax.fori_loop(0, PLANE, down_only, 0)
    for index in range(LINES - 1):
        weighting_copy(index).wait_send()
        for chunk in range(chunks):
            grow_copy(index, chunk).wait_send()
        weighting_arriving(index).wait_recv()
    for slot in (0, 1):
        for chunk in range(chunks):
            grow_arriving(slot, chunk).wait_recv()
    total = weighting[line_rows, :]
    for index in range(LINES - 1):
        total = total + weighting_in[remote_block(index)]
    weighting_sum[...] = total

    def sum_column(column, carry):
        here = pl.ds(pl.multiple_of(column * span, span), span)
        total = grow[column, line_rows, :].astype(jnp.float32)
        for slot in (0, 1):
            total = total + grow_in[slot, column].astype(jnp.float32)
        grow_sum[:, here] = total
        return carry

    lax.fori_loop(0, column_tiles, sum_column, 0)
    for copy in stores:
        copy.wait()
    for kind in range(3):
        for step in range(PLANE):
            core_copy(kind, step).wait_send()
        for step in range(3):
            kept_copy(kind, step).wait()
        for axis in (0, 1):
            for passing in (1,) if kind in DEFERRED else (0, 1):
                plane_copy(kind, axis, passing).wait()


def run_front(operands, weights):
    low, wide = jnp.bfloat16, jnp.float32
    shape = jax.ShapeDtypeStruct
    vmem = pltpu.VMEM
    far = pl.BlockSpec(memory_space=pl.ANY)
    near = pl.BlockSpec(memory_space=pltpu.VMEM)
    tokens, width = operands[0].shape
    half = tokens // 2
    rows = LINES * half
    query_width, key_width = operands[4].shape[1], operands[5].shape[1]
    span = weights[0].shape[1]
    tiles = 2 * PLANE
    dma = pltpu.SemaphoreType.DMA
    pieces = query_width // span
    columns = width // span
    return pl.pallas_call(
        front_kernel,
        name="front",
        out_shape=(
            *[shape((half, width), low)] * LINES,
            shape((half, width), wide),
            shape((half, 128), wide),
            shape((3, width, span), low),
            shape((3, width, span), low),
            shape((3, span, width), low),
            shape((2, 2, width // 2, span), low),
            shape((2, 2, width // 2, span), low),
            shape((2, 2, span // 2, width), low),
            shape((half, width), low),
            shape((half, 128), wide),
            shape((tokens, width), low),
            shape((tokens, query_width), low),
            shape((tokens, key_width), low),
            shape((tokens, key_width), low),
            shape((tokens, query_width), low),
            shape((half, width), low),
        ),
        in_specs=[far, far, near, near, far, far, far, far, near, near, near, near] + [far] * 3,
        out_specs=(*[far] * LINES, near, near, *[far] * 13, near),
        scratch_shapes=[
            vmem((rows, width), low),
            vmem((rows, width), low),
            vmem((rows, 128), wide),
            vmem((tiles, width, span), low),
            vmem((tiles, width, span), low),
            vmem((tiles, span, width), low),
            vmem((tiles, rows, span), low),
            vmem((tiles, rows, span), low),
            vmem((tiles, rows, span), low),
            vmem((columns, rows, span), low),
            vmem((LINES, columns, half, span), low),
            vmem((rows, width), low),
            vmem((rows, 128), wide),
            vmem((LINES, half, 128), wide),
            vmem((half, width), low),
            vmem((half, width), low),
            dma((5 + 2 * pieces + columns,)),
            dma((6,)),
            dma((3, 8)),
            dma((3, 8)),
            dma((2, 2, LINES - 1)),
            dma((2, 2, LINES - 1)),
            dma((LINES,)),
            dma((LINES,)),
            dma((2,)),
            dma((3 + 2 * pieces,)),
            dma((LINES,)),
            dma((3, 3)),
            dma((LINES - 1, 2)),
            dma((LINES, 2)),
            dma((LINES - 1,)),
            dma((LINES,)),
            dma((3, PLANE)),
            dma((3, PLANE)),
            dma((3, 2, 2)),
            dma((3, 2, 2)),
            pltpu.SemaphoreType.REGULAR,
        ],
        compiler_params=pltpu.CompilerParams(
            collective_id=0, has_side_effects=True, vmem_limit_bytes=63 << 20
        ),
        cost_estimate=pl.CostEstimate(
            flops=18 * rows * width * span * tiles,
            bytes_accessed=12 * width * span * tiles,
            transcendentals=0,
        ),
    )(*operands, *weights)


def back_kernel(*refs):
    refs = list(refs)

    def take(count):
        taken = refs[:count]
        del refs[:count]
        return taken

    out_parts = take(LINES)
    grow_sum, weighting_sum = take(2)
    kept, landed = take(3), take(3)
    stream, cotangent, gain_first, gain_second, query_weight, key_weight = take(6)
    value_weight, out_weight, router, cosine, sine = take(5)
    mixer_own, probs_own, normed, queries, keys, values, mixed, attended = take(8)
    layer_out, grad_stream = take(2)
    scatter_results = take(6)
    expert_grads = take(3)
    small_out = take(1)[0]
    stream_v, cot_v, query_v, key_v, value_v, out_v, normed_v, queries_v = take(8)
    mixed_v, grow_v, attended_v, out_in, layer_v = take(5)
    key_v2, value_v2, mixer_v, probs_v, weighting_v = take(5)
    key_slots, value_slots, key_totals, value_totals = take(4)
    middle_grads, attended_grads, mixed_grads = take(3)
    key_grads, value_grads, normed_recv = take(3)
    normed_send, first_terms = attended_grads, layer_v
    second_terms, query_grads = cot_v, mixed_v
    own_parts, landed_v, plane_in = take(3), take(3), take(3)
    scatter_sources = take(6)
    scatter_scratch = [take(5) for _ in range(6)]
    out_source_a, out_source_b, query_first, pair_first, pair_second, query_second = (
        scatter_sources
    )
    last_send, last_recv = take(2)
    load_sem, part_sem, out_send, out_recv, pair_sem, plane_send, plane_recv = take(7)
    store_sem, deferred_send, deferred_recv = take(3)
    tokens, width = stream_v.shape
    half = tokens // 2

    place = lax.axis_index("ep")
    core = lax.axis_index("tp")
    sibling = (place, 1 - core)
    across = [flip(place, 1), flip(place, 2)]
    partners = [flip_line(place, step) for step in range(LINES)]
    bits = [lax.rem(place, 2), lax.rem(lax.div(place, 2), 2)]
    own_rows = pl.ds(pl.multiple_of(core * half, half), half)

    barrier = pltpu.get_barrier_semaphore()
    for other in across + partners[1:]:
        pl.semaphore_signal(barrier, inc=1, device_id=(other, core), device_id_type=MESH)
    pl.semaphore_signal(barrier, inc=1, device_id=sibling, device_id_type=MESH)

    pairs = [
        (grow_sum, grow_v),
        (weighting_sum, weighting_v),
        (attended, attended_v),
        (probs_own, probs_v),
        (stream, stream_v),
        (cotangent.at[own_rows], cot_v),
        (out_weight, out_v),
        (mixed, mixed_v),
        (queries, queries_v),
        (keys, key_v2),
        (values, value_v2),
        (normed, normed_v),
        (query_weight, query_v),
        (key_weight, key_v),
        (value_weight, value_v),
        (mixer_own, mixer_v),
        (out_parts[0], mixer_v),
    ]
    loads = [
        pltpu.make_async_copy(source, target, load_sem.at[index])
        for index, (source, target) in enumerate(pairs)
    ]

    def part_copies(kind, final):
        rows = own_parts[kind].shape[1]
        low, high = pl.ds(0, rows), pl.ds(rows, rows)
        first, second = (0, 0) if final else (2, 1)
        return [
            pltpu.make_async_copy(source, target, part_sem.at[kind, index])
            for index, (source, target) in enumerate(
                (
                    (kept[kind].at[first, low], own_parts[kind].at[0]),
                    (kept[kind].at[second, high], own_parts[kind].at[1]),
                )
            )
        ]

    def landed_copies(kind):
        if kind in DEFERRED:
            return [
                pltpu.make_async_copy(
                    landed[kind].at[axis, 1],
                    landed_v[kind].at[axis, 1],
                    part_sem.at[kind, 2 + axis],
                )
                for axis in (0, 1)
            ]
        return [pltpu.make_async_copy(landed[kind], landed_v[kind], part_sem.at[kind, 2])]

    def deferred_copy(kind, axis):
        rows = own_parts[kind].shape[1]
        return pltpu.make_async_remote_copy(
            src_ref=kept[kind].at[axis + 1, pl.ds(axis * rows, rows)],
            dst_ref=landed_v[kind].at[axis, 0],
            send_sem=deferred_send.at[kind, axis],
            recv_sem=deferred_recv.at[kind, axis],
            device_id=(across[axis], core),
            device_id_type=MESH,
        )

    for copy in loads[:6]:
        copy.start()
    for kind in range(3):
        for copy in landed_copies(kind):
            copy.start()
        for copy in part_copies(kind, False):
            copy.start()
    for copy in loads[6:-1]:
        copy.start()
    pl.semaphore_wait(barrier, LINES + 2)

    def send(source, target, sems, index, device):
        return pltpu.make_async_remote_copy(
            src_ref=source,
            dst_ref=target,
            send_sem=sems[0].at[index],
            recv_sem=sems[1].at[index],
            device_id=device,
            device_id_type=MESH,
        )

    def out_copy(step):
        return send(
            out_parts[step],
            out_in.at[step - 1],
            (out_send, out_recv),
            (step - 1,),
            (partners[step], core),
        )

    for kind in DEFERRED:
        for axis in (0, 1):
            deferred_copy(kind, axis).start()
    for step in (3, 2, 1):
        out_copy(step).start()

    for copy in loads[:6]:
        copy.wait()
    padding = jnp.zeros((128 - router.shape[0], width), jnp.bfloat16)
    router_rows = jnp.concatenate([router[...], padding], axis=0)
    own_start = core * half

    def own_chunk(index):
        rows = pl.ds(pl.multiple_of(index * CHUNK, CHUNK), CHUNK)
        return rows, pl.ds(pl.multiple_of(own_start + index * CHUNK, CHUNK), CHUNK)

    def middle_chunk(index, carry):
        rows, stream_rows = own_chunk(index)
        middle = stream_v[stream_rows, :].astype(jnp.float32) + residual_scale * attended_v[
            rows, :
        ].astype(jnp.float32)
        inverse = lax.rsqrt(jnp.mean(middle * middle, axis=-1, keepdims=True) + epsilon)
        probs = probs_v[rows, :]
        weighting = weighting_v[rows, :]
        grad_chosen = probs * (weighting - jnp.sum(probs * weighting, axis=-1, keepdims=True))
        weighting_v[rows, :] = grad_chosen
        grad_mixer = matmul(grad_chosen.astype(jnp.bfloat16), router_rows) + grow_v[rows, :]
        weighted = grad_mixer * gain_second[...].astype(jnp.float32)[None, :]
        grad_middle = (
            cot_v[rows, :].astype(jnp.float32)
            + inverse * weighted
            - middle * (inverse * inverse * inverse)
            * jnp.mean(middle * weighted, axis=-1, keepdims=True)
        )
        middle_grads[stream_rows, :] = grad_middle.astype(jnp.bfloat16)
        second_terms[rows, :] = (grad_mixer * middle * inverse).astype(jnp.bfloat16)
        return carry

    lax.fori_loop(0, half // CHUNK, middle_chunk, 0)

    def pair_copy(source, target, index):
        return pltpu.make_async_remote_copy(
            src_ref=source,
            dst_ref=target,
            send_sem=pair_sem.at[0, index],
            recv_sem=pair_sem.at[1, index],
            device_id=sibling,
            device_id_type=MESH,
        )

    middle_copy = pair_copy(middle_grads.at[own_rows], middle_grads.at[own_rows], 0)
    middle_copy.start()

    def plane_copy(kind, axis):
        return send(
            landed_v[kind].at[axis, 1],
            plane_in[kind].at[axis],
            (plane_send, plane_recv),
            (kind, axis),
            (across[1 - axis], core),
        )

    for kind in range(3):
        for copy in landed_copies(kind):
            copy.wait()
        for copy in part_copies(kind, False):
            copy.wait()
        for axis in (0, 1):

            def add_passing(index, carry):
                rows = pl.ds(pl.multiple_of(index * CHUNK, CHUNK), CHUNK)
                landed_v[kind][axis, 1, rows, :] = (
                    own_parts[kind][axis, rows, :].astype(jnp.float32)
                    + landed_v[kind][axis, 1, rows, :].astype(jnp.float32)
                ).astype(jnp.bfloat16)
                return carry

            lax.fori_loop(0, own_parts[kind].shape[1] // CHUNK, add_passing, 0)
            plane_copy(kind, axis).start()
        for copy in part_copies(kind, True):
            copy.start()

    slab = scatter_results[0].shape[0]
    order = (3, 2, 1, 0)
    plans = list(zip(scatter_sources, scatter_results, scatter_scratch))

    def rows_of(step, first, second_same, first_same):
        other_line = lax.div(partners[step], PLANE)
        first_bit = bits[first] if first_same else 1 - bits[first]
        second_bit = bits[1 - first] if second_same else 1 - bits[1 - first]
        index = other_line * PLANE + first_bit * (1 + first) + second_bit * (2 - first)
        return pl.ds(pl.multiple_of(index * slab, slab), slab)

    def first_copy(number, step, same):
        source, _, scratch = plans[number]
        first = number % 2
        index = step * 2 + same
        return send(
            source.at[rows_of(step, first, same, False)],
            scratch[0].at[index],
            (scratch[4].at[0], scratch[4].at[1]),
            (index,),
            (across[first], core),
        )

    def second_copy(number, step):
        scratch = plans[number][2]
        return send(
            scratch[1].at[step],
            scratch[2].at[step],
            (scratch[4].at[2], scratch[4].at[3]),
            (step,),
            (across[1 - number % 2], core),
        )

    def line_copy(number, step):
        scratch = plans[number][2]
        return send(
            scratch[1].at[step],
            scratch[3].at[step],
            (scratch[4].at[4], scratch[4].at[5]),
            (step,),
            (partners[step], core),
        )

    def start_scatter(number):
        for step in order:
            for same in (0, 1):
                first_copy(number, step, same).start()

    def add_first(number, step, same):
        source, _, scratch = plans[number]
        first_copy(number, step, same).wait()
        mine = source[rows_of(step, number % 2, same, True), :].astype(jnp.float32)
        return mine + scratch[0][step * 2 + same].astype(jnp.float32)

    def finish_first(number, step):
        plans[number][2][1][step] = add_first(number, step, 0).astype(jnp.bfloat16)
        second_copy(number, step).start()

    def finish_second(number, step):
        _, result, scratch = plans[number]
        total = add_first(number, step, 1)
        second_copy(number, step).wait()
        total = total + scratch[2][step].astype(jnp.float32)
        if step:
            scratch[1][step] = total.astype(jnp.bfloat16)
            line_copy(number, step).start()
        else:
            result[...] = total

    def finish_line(number):
        _, result, scratch = plans[number]
        for step in order[:-1]:
            line_copy(number, step).wait()
            result[...] += scratch[3][step].astype(jnp.float32)

    middle_copy.wait()

    def attended_chunk(index, carry):
        rows = pl.ds(pl.multiple_of(index * CHUNK, CHUNK), CHUNK)
        attended_grads[rows, :] = (
            residual_scale * middle_grads[rows, :].astype(jnp.float32)
        ).astype(jnp.bfloat16)
        return carry

    lax.fori_loop(0, tokens // CHUNK, attended_chunk, 0)
    loads[6].wait()
    loads[7].wait()
    columns = out_source_a.shape[1]
    out_source_a[...] = matmul_tn(attended_grads[...], mixed_v[:, :columns]).astype(jnp.bfloat16)
    start_scatter(0)
    out_source_b[...] = matmul_tn(attended_grads[...], mixed_v[:, columns:]).astype(jnp.bfloat16)
    start_scatter(1)
    mixed_grads[...] = matmul_nt(attended_grads[...], out_v[...]).astype(jnp.bfloat16)
    for copy in loads[8:11]:
        copy.wait()
    store_slots(key_slots, key_v2[...].astype(jnp.float32))
    store_slots(value_slots, value_v2[...].astype(jnp.float32))
    key_totals[...] = jnp.zeros_like(key_totals)
    value_totals[...] = jnp.zeros_like(value_totals)
    group = query_v.shape[1] // key_v.shape[1]
    blocks = 2
    block_rows = tokens // blocks

    def turned_back(value, cosines, sines):
        return (value * cosines - partner_lanes(value) * sines).astype(jnp.bfloat16)

    def head_pair(pair, carry):
        here = pl.ds(pl.multiple_of(pair * 128, 128), 128)
        for block in range(blocks):
            rows = slice(block * block_rows, (block + 1) * block_rows)
            reach = (block + 1) * block_rows
            total = jnp.zeros((block_rows, 128), jnp.float32)
            query_block = queries_v[rows, here]
            grad_block = mixed_grads[rows, here]
            for parity in range(2):
                slot = 2 * lax.div(2 * pair + parity, group) + parity
                key_block = key_slots[slot, :reach, :]
                scores = causal_scores(query_block, key_block, block * block_rows)
                weight = jnp.exp(scores - jnp.max(scores, axis=-1, keepdims=True))
                weight = weight / jnp.sum(weight, axis=-1, keepdims=True)
                grad_probs = matmul_nt(grad_block, value_slots[slot, :reach, :])
                inner = jnp.sum(weight * grad_probs, axis=-1, keepdims=True)
                grad_scores = (weight * (grad_probs - inner)).astype(jnp.bfloat16)
                total = total + matmul(grad_scores, key_block)
                key_totals[slot, :reach, :] += matmul_tn(grad_scores, query_block)
                value_totals[slot, :reach, :] += matmul_tn(
                    weight.astype(jnp.bfloat16), grad_block
                )
            query_grads[rows, here] = turned_back(
                score_scale * total, cosine[rows, :], sine[rows, :]
            )
        return carry

    def gathered_pair(totals, pair):
        first, second = 4 * pair, 4 * pair + 2
        low = lane_halves(totals[first])[0] + pltpu.roll(
            lane_halves(totals[first + 1])[1], HEAD_FEATURES, 1
        )
        high = lane_halves(totals[second + 1])[1] + pltpu.roll(
            lane_halves(totals[second])[0], HEAD_FEATURES, 1
        )
        return low + high

    def half_of_heads(pair, query_target, number, pair_target):
        lanes = slice(pair * 128, pair * 128 + 128)
        columns = query_target.shape[1]
        mine = slice(pair * columns, (pair + 1) * columns)
        lax.fori_loop(3 * pair, 3 * pair + 3, head_pair, 0)
        query_target[...] = matmul_tn(normed_v[...], query_grads[:, mine]).astype(jnp.bfloat16)
        start_scatter(number)
        key_grads[:, lanes] = turned_back(
            score_scale * gathered_pair(key_totals, pair), cosine[...], sine[...]
        )
        value_grads[:, lanes] = gathered_pair(value_totals, pair).astype(jnp.bfloat16)
        pair_target[:, :128] = matmul_tn(normed_v[...], key_grads[:, lanes]).astype(jnp.bfloat16)
        pair_target[:, 128:256] = matmul_tn(normed_v[...], value_grads[:, lanes]).astype(
            jnp.bfloat16
        )

    for copy in loads[11:-1]:
        copy.wait()
    half_of_heads(0, query_first, 2, pair_first)
    start_scatter(3)
    half_of_heads(1, query_second, 5, pair_second)
    normed_send[...] = (
        matmul_nt(query_grads[...], query_v[...])
        + matmul_nt(key_grads[...], key_v[...])
        + matmul_nt(value_grads[...], value_v[...])
    ).astype(jnp.bfloat16)
    normed_copy = pair_copy(normed_send, normed_recv, 1)
    normed_copy.start()
    for step in order:
        finish_first(0, step)
        finish_first(1, step)
    normed_copy.wait()

    def stream_rows(rows):
        grad_normed = normed_send[rows, :].astype(jnp.float32) + normed_recv[rows, :].astype(
            jnp.float32
        )
        stream_f = stream_v[rows, :].astype(jnp.float32)
        inverse = lax.rsqrt(jnp.mean(stream_f * stream_f, axis=-1, keepdims=True) + epsilon)
        weighted = grad_normed * gain_first[...].astype(jnp.float32)[None, :]
        total = (
            middle_grads[rows, :].astype(jnp.float32)
            + inverse * weighted
            - stream_f * (inverse * inverse * inverse)
            * jnp.mean(stream_f * weighted, axis=-1, keepdims=True)
        )
        return grad_normed * stream_f * inverse, total

    def first_chunk(index, carry):
        rows, mine = own_chunk(index)
        first_terms[rows, :] = stream_rows(mine)[0].astype(jnp.bfloat16)
        return carry

    lax.fori_loop(0, half // CHUNK, first_chunk, 0)
    lane = lax.broadcasted_iota(jnp.int32, (half, 128), 1)
    experts = LINES * PLANE
    pair_second[:, 256:] = (
        matmul_tn(mixer_v[...], weighting_v[...].astype(jnp.bfloat16))
        + matmul_tn(second_terms[...], (lane == experts).astype(jnp.bfloat16))
        + matmul_tn(first_terms[...], (lane == experts + 1).astype(jnp.bfloat16))
    ).astype(jnp.bfloat16)
    loads[-1].start()
    start_scatter(4)

    def stream_chunk(index, carry):
        rows = pl.ds(pl.multiple_of(index * CHUNK, CHUNK), CHUNK)
        normed_recv[rows, :] = stream_rows(rows)[1].astype(jnp.bfloat16)
        return carry

    lax.fori_loop(0, tokens // CHUNK, stream_chunk, 0)
    stream_copy = pltpu.make_async_copy(normed_recv, grad_stream, store_sem.at[4])
    stream_copy.start()
    for step in order:
        finish_second(0, step)
        finish_second(1, step)
    for step in order:
        finish_first(2, step)
        finish_first(3, step)
    for step in order:
        finish_second(2, step)
        finish_second(3, step)
    for step in order:
        finish_first(4, step)
        finish_first(5, step)
    for step in (1, 2, 3):
        out_copy(step).wait()
    loads[-1].wait()

    def result_chunk(index, carry):
        rows, stream_part = own_chunk(index)
        attended_f = attended_v[rows, :].astype(jnp.float32)
        mixture = mixer_v[rows, :].astype(jnp.float32)
        for step in range(1, LINES):
            mixture = mixture + out_in[step - 1, rows, :].astype(jnp.float32)
        middle = stream_v[stream_part, :].astype(jnp.float32) + residual_scale * attended_f
        result = middle + residual_scale * mixture
        layer_v[rows, :] = result.astype(jnp.bfloat16)
        return tuple(
            total + jnp.sum(value * value, axis=0, keepdims=True)
            for total, value in zip(carry, (result, attended_f, mixture))
        )

    totals = lax.fori_loop(
        0, half // CHUNK, result_chunk, (jnp.zeros((1, width), jnp.float32),) * 3
    )
    layer_pair = pair_copy(layer_v, layer_out.at[own_rows], 2)
    layer_pair.start()
    layer_own = pltpu.make_async_copy(layer_v, layer_out.at[own_rows], store_sem.at[0])
    layer_own.start()
    row_lane = lax.broadcasted_iota(jnp.int32, (8, 128), 1)
    squares = jnp.zeros((8, 128), jnp.float32)
    for index, value in enumerate(totals):
        total = jnp.sum(value, axis=1, keepdims=True)
        squares = jnp.where(row_lane == index, total, squares)
    for step in order:
        finish_second(4, step)
        finish_second(5, step)
    def expert_copy(kind):
        return pltpu.make_async_copy(own_parts[kind], expert_grads[kind], store_sem.at[1 + kind])

    for kind in range(3):
        for copy in part_copies(kind, True):
            copy.wait()
        for axis in (0, 1):
            plane_copy(kind, axis).wait()
            if kind in DEFERRED:
                deferred_copy(kind, axis).wait()

            def add_final(index, carry):
                rows = pl.ds(pl.multiple_of(index * CHUNK, CHUNK), CHUNK)
                own_parts[kind][axis, rows, :] = (
                    own_parts[kind][axis, rows, :].astype(jnp.float32)
                    + landed_v[kind][axis, 0, rows, :].astype(jnp.float32)
                    + plane_in[kind][axis, rows, :].astype(jnp.float32)
                ).astype(jnp.bfloat16)
                return carry

            lax.fori_loop(0, own_parts[kind].shape[1] // CHUNK, add_final, 0)
        expert_copy(kind).start()
    finish_line(4)
    last_send[:slab, :] = scatter_results[4][:, 256:]
    last_send[slab:, :] = squares
    last_copy = pair_copy(last_send, last_recv, 3)
    last_copy.start()
    for number in (0, 1, 2, 3, 5):
        finish_line(number)
    last_copy.wait()
    small_out[...] = last_send[...] + last_recv[...]
    layer_pair.wait()
    layer_own.wait()
    stream_copy.wait()
    for kind in range(3):
        expert_copy(kind).wait()


def run_back(expert_results, operands, front_results):
    low, wide = jnp.bfloat16, jnp.float32
    shape = jax.ShapeDtypeStruct
    vmem = pltpu.VMEM
    far = pl.BlockSpec(memory_space=pl.ANY)
    near = pl.BlockSpec(memory_space=pltpu.VMEM)
    tokens, width = operands[0].shape
    half = tokens // 2
    query_width, key_width = operands[4].shape[1], operands[5].shape[1]
    kept = expert_results[LINES + 2 : LINES + 5]
    tile_shapes = [value.shape[1:] for value in kept]
    half_shapes = [(value[0] // 2, value[1]) for value in tile_shapes]
    slab = width // (LINES * PLANE)
    slots = 2 * key_width // HEAD_FEATURES
    part = query_width // 2
    widths = (part, part, part, key_width, key_width + 128, part)
    dma = pltpu.SemaphoreType.DMA
    scatter_scratch = []
    for columns in widths:
        scatter_scratch += [
            vmem((2 * LINES, slab, columns), low),
            vmem((LINES, slab, columns), low),
            vmem((LINES, slab, columns), low),
            vmem((LINES, slab, columns), low),
            dma((6, 2 * LINES)),
        ]
    return pl.pallas_call(
        back_kernel,
        name="back",
        out_shape=(
            shape((tokens, width), low),
            shape((tokens, width), low),
            *[shape((slab, columns), wide) for columns in widths],
            *[shape((2, *value), low) for value in half_shapes],
            shape((slab + 8, 128), wide),
        ),
        in_specs=[far] * (LINES + 8)
        + [far, far, near, near, far, far, far, far, near, near, near]
        + [far] * 8,
        out_specs=(far,) * 2 + (near,) * 6 + (far,) * 3 + (near,),
        scratch_shapes=[
            vmem((tokens, width), low),
            vmem((half, width), low),
            vmem((width, query_width), low),
            vmem((width, key_width), low),
            vmem((width, key_width), low),
            vmem((query_width, width), low),
            vmem((tokens, width), low),
            vmem((tokens, query_width), low),
            vmem((tokens, query_width), low),
            vmem((half, width), wide),
            vmem((half, width), low),
            vmem((LINES - 1, half, width), low),
            vmem((half, width), low),
            vmem((tokens, key_width), low),
            vmem((tokens, key_width), low),
            vmem((half, width), low),
            vmem((half, 128), wide),
            vmem((half, 128), wide),
            vmem((slots, tokens, 128), low),
            vmem((slots, tokens, 128), low),
            vmem((slots, tokens, 128), wide),
            vmem((slots, tokens, 128), wide),
            vmem((tokens, width), low),
            vmem((tokens, width), low),
            vmem((tokens, query_width), low),
            vmem((tokens, key_width), low),
            vmem((tokens, key_width), low),
            vmem((tokens, width), low),
            *[vmem((2, *value), low) for value in half_shapes],
            *[vmem((2, 2, *value), low) for value in half_shapes],
            *[vmem((2, *value), low) for value in half_shapes],
            *[vmem((width, columns), low) for columns in widths],
            *scatter_scratch,
            vmem((slab + 8, 128), wide),
            vmem((slab + 8, 128), wide),
            dma((17,)),
            dma((3, 4)),
            dma((LINES - 1,)),
            dma((LINES - 1,)),
            dma((2, 4)),
            dma((3, 2)),
            dma((3, 2)),
            dma((5,)),
            dma((3, 2)),
            dma((3, 2)),
        ],
        compiler_params=pltpu.CompilerParams(
            collective_id=1, has_side_effects=True, vmem_limit_bytes=63 << 20
        ),
    )(*expert_results, *operands, *front_results)


def finish_kernel(*refs):
    layer_in, sources, refs = refs[0], refs[1:12], refs[12:]
    layer_out, refs = refs[0], refs[1:]
    grad_stream, out_grad, query_grad, key_grad, value_grad = refs[:5]
    gate_grad, up_grad, down_grad, router_grad, second_gain, first_gain, rms = refs[5:12]
    loaded, load_sem = refs[12:23], refs[23]
    layer_copy = pltpu.make_async_copy(layer_in, layer_out, load_sem.at[11])
    layer_copy.start()
    stream_low, out_first, out_second, query_first, pair_first, pair_second, query_second = (
        loaded[:7]
    )
    gate_low, up_low, down_low, small = loaded[7:]
    copies = [
        pltpu.make_async_copy(source, target, load_sem.at[index])
        for index, (source, target) in enumerate(zip(sources, loaded))
    ]
    for copy in copies:
        copy.start()
    copies[0].wait()

    def widen_stream(index, carry):
        rows = pl.ds(pl.multiple_of(index * CHUNK, CHUNK), CHUNK)
        grad_stream[rows, :] = stream_low[rows, :].astype(jnp.float32)
        return carry

    lax.fori_loop(0, grad_stream.shape[0] // CHUNK, widen_stream, 0)
    for copy in copies[1:]:
        copy.wait()
    half = out_first.shape[1]
    out_grad[:, :half] = out_first[...]
    out_grad[:, half:] = out_second[...]
    query_grad[:, :half] = query_first[...]
    query_grad[:, half:] = query_second[...]
    for place, part in enumerate((pair_first, pair_second)):
        lanes = slice(place * 128, place * 128 + 128)
        key_grad[:, lanes] = part[:, :128]
        value_grad[:, lanes] = part[:, 128:256]
    for low, grad in ((gate_low, gate_grad), (up_low, up_grad), (down_low, down_grad)):
        for part in range(2):

            def widen(index, carry):
                rows = pl.multiple_of(index * CHUNK, CHUNK)
                start = pl.multiple_of(part * low.shape[1] + rows, CHUNK)
                grad[0, pl.ds(start, CHUNK), :] = low[part, pl.ds(rows, CHUNK), :].astype(
                    jnp.float32
                )
                return carry

            lax.fori_loop(0, low.shape[1] // CHUNK, widen, 0)
    experts, slab = router_grad.shape
    turned = small[:slab, :].T
    router_grad[...] = turned[:experts, :]
    second_gain[...] = turned[experts, :]
    first_gain[...] = turned[experts + 1, :]
    total = grad_stream.shape[0] * grad_stream.shape[1]
    rms[...] = jnp.sqrt(small[slab : slab + 1, :3] / total)
    layer_copy.wait()


def run_finish(layer, values, tokens, width, experts):
    shape = jax.ShapeDtypeStruct
    wide = jnp.float32
    far = pl.BlockSpec(memory_space=pl.ANY)
    near = pl.BlockSpec(memory_space=pltpu.VMEM)
    slab, part = values[3].shape
    query_width, key_width = 2 * part, values[4].shape[1]
    tiles = [(1, 2 * value.shape[1], value.shape[2]) for value in values[7:10]]
    return pl.pallas_call(
        finish_kernel,
        name="finish",
        out_shape=(
            shape(layer.shape, layer.dtype),
            shape((tokens, width), wide),
            shape((slab, query_width), wide),
            shape((slab, query_width), wide),
            shape((slab, key_width), wide),
            shape((slab, key_width), wide),
            *[shape(tile, wide) for tile in tiles],
            shape((experts, slab), wide),
            shape((slab,), wide),
            shape((slab,), wide),
            shape((1, 3), wide),
        ),
        in_specs=[far] * 12,
        out_specs=(near,) * 13,
        scratch_shapes=[pltpu.VMEM(value.shape, value.dtype) for value in values]
        + [pltpu.SemaphoreType.DMA((12,))],
        compiler_params=pltpu.CompilerParams(vmem_limit_bytes=63 << 20),
    )(layer, *values)


def dense_shards(
    stream,
    cotangent,
    attention_gain,
    query_weight,
    key_matrix,
    value_matrix,
    out_weight,
    mixture_gain,
    router_weight,
    gate_weight,
    up_weight,
    down_weight,
    routes,
):
    tok_rows, model_width = stream.shape
    experts = router_weight.shape[1]
    steps_up = np.arange(HEAD_FEATURES // 2, dtype=np.float32) * np.float32(2.0 / HEAD_FEATURES)
    turns = np.exp(-steps_up * np.log(np.float32(rope_base)))
    angles = np.arange(SEQ_LEN, dtype=np.float32)[:, None] * turns[None, :]
    cosines, sines = np.cos(angles), np.sin(angles)
    operands = [
        stream,
        cotangent,
        attention_gain,
        mixture_gain,
        query_weight,
        key_matrix,
        value_matrix,
        out_weight,
        router_weight.T,
        routes.T,
        jnp.asarray(np.tile(cosines, (1, 4))),
        jnp.asarray(np.tile(np.concatenate([-sines, sines], axis=1), (1, 2))),
    ]
    front = run_front(operands, [gate_weight[0], up_weight[0], down_weight[0]])
    layer_part, *partial = run_back(
        front[: LINES + 8], operands[:9] + operands[10:], front[LINES + 8 :]
    )
    (
        layer_out,
        grad_stream,
        out_grad,
        query_grad,
        key_grad,
        value_grad,
        gate_grad,
        up_grad,
        down_grad,
        router_grad,
        second_gain,
        first_gain,
        rms_stats,
    ) = run_finish(layer_part, partial, tok_rows, model_width, experts)
    return (
        layer_out,
        grad_stream,
        first_gain,
        query_grad,
        key_grad,
        value_grad,
        out_grad.T,
        second_gain,
        router_grad.T,
        gate_grad,
        up_grad,
        down_grad,
        rms_stats,
    )


def solution(mesh):
    in_specs = (
        P("ep", None),
        P("ep", None),
        P(),
        P(None, "tp"),
        P(None, "tp"),
        P(None, "tp"),
        P("tp", None),
        P(),
        P(),
        P("ep", None, "tp"),
        P("ep", None, "tp"),
        P("ep", "tp", None),
        P("ep", None),
    )
    out_specs = (
        P("ep", None),
        P("ep", None),
        P("ep"),
        P("ep", "tp"),
        P("ep", "tp"),
        P("ep", "tp"),
        P("tp", "ep"),
        P("ep"),
        P("ep", None),
        P("ep", None, "tp"),
        P("ep", None, "tp"),
        P("ep", "tp", None),
        P("ep", None),
    )
    ep_size = mesh.shape["ep"]
    dense = mesh.shape["tp"] == 2 and ep_size <= 2 * TOP and ep_size == 16
    shards = dense_shards if dense else routed_shards
    return jax.shard_map(shards, mesh=mesh, in_specs=in_specs, out_specs=out_specs, check_vma=False)
```
